32 devices in a mesh: rep: 8 (over z, x), shard: 4 (over y, core).
Axes of the slice: x: 2, y: 2, z: 4, core: 2. Of those that a mesh axis runs over, the one named last changes fastest.
Arguments:
- inputs: bfloat16 [8, 512, 768], P('rep', 'shard'), may hold values from -6 to 6
- encoder: bfloat16 [8, 512, 768], P('rep', 'shard'), may hold values from -6 to 6
- segments: int32 [8, 512], P('rep'), may hold values from 0 to 1, as said below
- enc_segments: int32 [8, 512], P('rep'), may hold values from 0 to 1, as said below
- self_query: bfloat16 [768, 768], P('shard'), may hold values from -0.109375 to 0.109375
- self_key: bfloat16 [768, 768], P('shard'), may hold values from -0.109375 to 0.109375
- self_value: bfloat16 [768, 768], P('shard'), may hold values from -0.21875 to 0.21875
- self_output: bfloat16 [768, 768], P('shard'), may hold values from -0.625 to 0.625
- cross_query: bfloat16 [768, 768], P('shard'), may hold values from -0.109375 to 0.109375
- cross_key: bfloat16 [768, 768], P('shard'), may hold values from -0.109375 to 0.109375
- cross_value: bfloat16 [768, 768], P('shard'), may hold values from -0.21875 to 0.21875
- cross_output: bfloat16 [768, 768], P('shard'), may hold values from -0.625 to 0.625
- gate_weight: bfloat16 [768, 2048], P('shard'), may hold values from -0.21875 to 0.21875
- up_weight: bfloat16 [768, 2048], P('shard'), may hold values from -0.21875 to 0.21875
- down_weight: bfloat16 [2048, 768], P('shard'), may hold values from -0.125 to 0.125
- self_gain: bfloat16 [768], P('shard'), may hold values from 0.5 to 1.5
- cross_gain: bfloat16 [768], P('shard'), may hold values from 0.5 to 1.5
- feed_gain: bfloat16 [768], P('shard'), may hold values from 0.5 to 1.5
- bias_table: bfloat16 [32, 12], P('shard'), may hold values from -4 to 4
- cotangent: bfloat16 [8, 512, 768], P('rep', 'shard'), may hold values from -6 to 6
Outputs:
- result: bfloat16 [8, 512, 768], P('rep', 'shard')
- grad_inputs: float32 [8, 512, 768], P('rep', 'shard')
- grad_encoder: float32 [8, 512, 768], P('rep', 'shard')
- grad_self_query: float32 [768, 768], P('shard')
- grad_self_key: float32 [768, 768], P('shard')
- grad_self_value: float32 [768, 768], P('shard')
- grad_self_output: float32 [768, 768], P('shard')
- grad_cross_query: float32 [768, 768], P('shard')
- grad_cross_key: float32 [768, 768], P('shard')
- grad_cross_value: float32 [768, 768], P('shard')
- grad_cross_output: float32 [768, 768], P('shard')
- grad_gate_weight: float32 [768, 2048], P('shard')
- grad_up_weight: float32 [768, 2048], P('shard')
- grad_down_weight: float32 [2048, 768], P('shard')
- grad_self_gain: float32 [768], P('shard')
- grad_cross_gain: float32 [768], P('shard')
- grad_feed_gain: float32 [768], P('shard')
- grad_bias_table: float32 [32, 12], P('shard')
The draws below stay inside these ranges and needn't reach their ends.
Inputs may be any that keep to these rules, and one draw needn't show every extreme that they name: `segments`: in each sequence the decoder tokens carry document numbers 0 to 1 without falling, every number present, each document on 200 or more neighbouring tokens and one on exactly 200. `enc_segments`: in each sequence the encoder states carry document numbers 0 to 1 without falling, every number present, each document on 32 or more neighbouring states and one on exactly 32.
All inputs are finite; a program needn't handle non-finite values.
Results may differ from the reference program's by a relative error of at most 0.03.
Values may be sent and summed in bfloat16 or wider, within the bound.
No kernel may reach another device: no remote copies, remote signals or barrier semaphores. Data moves between devices by JAX's collectives and lax.ppermute only.
A program may use at most 192 MiB of HBM per device.

```python
import math
import jax
import jax.numpy as jnp
from jax import lax

D = 768
HEADS = 12
HEAD_DIM = 64
FF = 2048
NB = 32
ENC = 512
MIN_DOC = 200
MIN_ENC = 32
SEQ = 512
DOCS = 2
SEQS = 8


def document_ids(key, length, documents, shortest):
    shares = jax.random.randint(key, (documents,), 1, 1000, dtype=jnp.int32)
    chosen = jax.random.randint(jax.random.fold_in(key, 7), (), 0, documents, dtype=jnp.int32)
    shares = jnp.where(jnp.arange(documents, dtype=jnp.int32) == chosen, 0, shares)
    spare = length - documents * shortest
    running = jnp.cumsum(shares)
    extras = spare * running // running[-1]
    starts = jnp.arange(1, documents, dtype=jnp.int32) * shortest + extras[:-1]
    places = jnp.arange(length, dtype=jnp.int32)
    return jnp.sum((places[:, None] >= starts[None, :]).astype(jnp.int32), axis=1).astype(jnp.int32)


def draw_segments(key, part):
    subkeys = jax.random.split(jax.random.fold_in(key, 3), SEQS)
    return jax.vmap(lambda single: document_ids(single, SEQ, DOCS, MIN_DOC))(subkeys)


def draw_enc_segments(key, part):
    subkeys = jax.random.split(jax.random.fold_in(key, 11), SEQS)
    return jax.vmap(lambda single: document_ids(single, ENC, DOCS, MIN_ENC))(subkeys)


def level_of(own_key, shape, cuts, smallest, top_value):
    level = 1.0
    for dim, blocks in cuts:
        steps = jax.random.uniform(jax.random.fold_in(jax.random.fold_in(own_key, 6), dim), (blocks,), jnp.float32, smallest / len(cuts), top_value / len(cuts))
        level = level * jnp.repeat(jnp.exp(steps), shape[dim] // blocks).reshape((-1,) + (1,) * (len(shape) - 1 - dim))
    return level


def noise(key, extent, spread, limit, pieces=(), kind=jnp.bfloat16):
    level = level_of(key, extent, pieces, -0.22, 0.18) if pieces else 1.0
    values = jax.random.normal(key, extent, jnp.float32) * spread * level
    return jnp.minimum(jnp.maximum(values, -limit), limit).astype(kind)


def setup_inputs(seed: int = 0) -> dict:
    streams_of = jax.random.split(jax.random.key(seed), 21)
    return {
        "inputs": noise(streams_of[0], (SEQS, SEQ, D), 1.0, 6.0, ((0, 8), (1, 4))),
        "encoder": noise(streams_of[1], (SEQS, ENC, D), 1.0, 6.0, ((0, 8), (1, 4))),
        "segments": draw_segments(jax.random.fold_in(streams_of[20], 71), 0),
        "enc_segments": draw_enc_segments(jax.random.fold_in(streams_of[20], 71), 0),
        "self_query": noise(streams_of[4], (D, D), (4 * D) ** -0.5, 0.109375, ((0, 4),)),
        "self_key": noise(streams_of[5], (D, D), (4 * D) ** -0.5, 0.109375, ((0, 4),)),
        "self_value": noise(streams_of[6], (D, D), D ** -0.5, 0.21875, ((0, 4),)),
        "self_output": noise(streams_of[7], (D, D), (D // 8) ** -0.5, 0.625, ((0, 4),)),
        "cross_query": noise(streams_of[8], (D, D), (4 * D) ** -0.5, 0.109375, ((0, 4),)),
        "cross_key": noise(streams_of[9], (D, D), (4 * D) ** -0.5, 0.109375, ((0, 4),)),
        "cross_value": noise(streams_of[10], (D, D), D ** -0.5, 0.21875, ((0, 4),)),
        "cross_output": noise(streams_of[11], (D, D), (D // 8) ** -0.5, 0.625, ((0, 4),)),
        "gate_weight": noise(streams_of[12], (D, FF), D ** -0.5, 0.21875, ((0, 4),)),
        "up_weight": noise(streams_of[13], (D, FF), D ** -0.5, 0.21875, ((0, 4),)),
        "down_weight": noise(streams_of[14], (FF, D), FF ** -0.5, 0.125, ((0, 4),)),
        "self_gain": jnp.clip(1.0 + 0.1 * jax.random.normal(streams_of[15], (D,), jnp.float32), 0.5, 1.5).astype(jnp.bfloat16),
        "cross_gain": jnp.clip(1.0 + 0.1 * jax.random.normal(streams_of[16], (D,), jnp.float32), 0.5, 1.5).astype(jnp.bfloat16),
        "feed_gain": jnp.clip(1.0 + 0.1 * jax.random.normal(streams_of[17], (D,), jnp.float32), 0.5, 1.5).astype(jnp.bfloat16),
        "bias_table": noise(streams_of[18], (NB, HEADS), 1.0, 4.0, ((0, 4),)),
        "cotangent": noise(streams_of[19], (SEQS, SEQ, D), 1.0, 6.0, ((0, 8), (1, 4))),
    }


@jax.custom_vjp
def low(v):
    return lax.optimization_barrier(v.astype(jnp.bfloat16)).astype(jnp.float32)

@jax.custom_vjp
def low_back(v):
    return v

def low_keep(v):
    return (low(v), None)

def low_pass(kept, grad):
    return (grad,)

def back_keep(v):
    return (v, None)

def back_low(kept, grad):
    return (low(grad),)
low.defvjp(low_keep, low_pass)
low_back.defvjp(back_keep, back_low)
bucket_edges = [math.ceil(16 * 8 ** (number / 16)) for number in range(1, 16)]
epsilon = 1e-06
masked_score = -1000000000.0

def bucket_of(distance):
    far_part = sum(((distance >= border).astype(jnp.int32) for border in bucket_edges))
    return jnp.where(distance < 16, distance, 16 + far_part)

def rms_scale(values, scales):
    return values * lax.rsqrt(lax.optimization_barrier(jnp.mean(values * values, axis=-1, keepdims=True)) + epsilon) * scales

def matmul(former, latter):
    return jnp.dot(former, latter, precision=lax.Precision.HIGHEST)

def split_heads(matrix):
    return matrix.reshape(matrix.shape[0], HEADS, HEAD_DIM).transpose(1, 0, 2)

def join_heads(stacked):
    return stacked.transpose(1, 0, 2).reshape(stacked.shape[1], HEADS * HEAD_DIM)

def attend(queries, key_heads, value_heads, extra, allowed):
    raw_scores = low_back(jnp.einsum('hqd,hkd->hqk', queries, key_heads, precision=lax.Precision.HIGHEST))
    scores = jnp.where(allowed, raw_scores + extra, masked_score)
    weights = low(jax.nn.softmax(scores, axis=-1))
    return jnp.einsum('hqk,hkd->hqd', weights, value_heads, precision=lax.Precision.HIGHEST)

def self_attend(query_self, key_self, value_self, seg_rows, bias_rows):
    block_size = math.gcd(SEQ, 512)
    block_count = SEQ // block_size
    query_blocks = split_heads(query_self).reshape(HEADS, block_count, block_size, HEAD_DIM).transpose(1, 0, 2, 3)
    key_heads = split_heads(key_self)
    value_heads = split_heads(value_self)
    key_places = jnp.arange(SEQ, dtype=jnp.int32)

    def one_block(packed):
        query_rows, first_row = packed
        query_places = first_row + jnp.arange(block_size, dtype=jnp.int32)
        query_ids = lax.dynamic_slice_in_dim(seg_rows, first_row, block_size)
        distance = jnp.maximum(query_places[:, None] - key_places[None, :], 0)
        bias_block = jnp.transpose(bias_rows[bucket_of(distance)], (2, 0, 1))
        allowed = (query_places[:, None] >= key_places[None, :]) & (query_ids[:, None] == seg_rows[None, :])
        return attend(query_rows, key_heads, value_heads, bias_block, allowed[None])
    first_rows = jnp.arange(block_count, dtype=jnp.int32) * block_size
    mixed = lax.map(jax.checkpoint(one_block), (query_blocks, first_rows))
    return mixed.transpose(1, 0, 2, 3).reshape(HEADS, SEQ, HEAD_DIM)

def sequence_forward(source, memory, seg_rows, enc_rows, params):
    w_query, w_key, w_value, w_output, c_query, c_key, c_value, c_output, w_gate, w_up, w_down, g_self, g_cross, g_feed, bias_rows = params
    allowed_cross = seg_rows[:, None] == enc_rows[None, :]
    normed_self = low(rms_scale(source, g_self))
    query_self = low(low_back(matmul(normed_self, w_query)))
    key_self = low(low_back(matmul(normed_self, w_key)))
    value_self = low(low_back(matmul(normed_self, w_value)))
    mixed_self = self_attend(query_self, key_self, value_self, seg_rows, bias_rows)
    mixed_self = low(low_back(join_heads(mixed_self)))
    after_self = source + low_back(matmul(mixed_self, w_output))
    normed_cross = low(rms_scale(after_self, g_cross))
    query_cross = low(low_back(matmul(normed_cross, c_query)))
    key_cross = low(low_back(matmul(memory, c_key)))
    value_cross = low(low_back(matmul(memory, c_value)))
    mixed_cross = attend(split_heads(query_cross), split_heads(key_cross), split_heads(value_cross), 0.0, allowed_cross[None])
    mixed_cross = low(low_back(join_heads(mixed_cross)))
    after_cross = after_self + low_back(matmul(mixed_cross, c_output))
    normed_feed = low(rms_scale(after_cross, g_feed))
    gate_act = low_back(matmul(normed_feed, w_gate))
    up_act = low_back(matmul(normed_feed, w_up))
    hidden = low(jax.nn.gelu(gate_act, approximate=True) * up_act)
    return after_cross + low_back(matmul(hidden, w_down))

def reference(inputs, encoder, segments, enc_segments, self_query, self_key, self_value, self_output, cross_query, cross_key, cross_value, cross_output, gate_weight, up_weight, down_weight, self_gain, cross_gain, feed_gain, bias_table, cotangent):
    params = tuple((weight.astype(jnp.float32) for weight in (self_query, self_key, self_value, self_output, cross_query, cross_key, cross_value, cross_output, gate_weight, up_weight, down_weight, self_gain, cross_gain, feed_gain, bias_table)))

    def forward(source_all, memory_all, weights):

        def one_sequence(packed):
            return sequence_forward(packed[0], packed[1], packed[2], packed[3], weights)
        return lax.map(jax.checkpoint(one_sequence), (source_all, memory_all, segments, enc_segments))
    outcome, pull = jax.vjp(forward, inputs.astype(jnp.float32), encoder.astype(jnp.float32), params)
    grad_in, grad_memory, grad_params = pull(cotangent.astype(jnp.float32))
    return (outcome.astype(jnp.bfloat16), grad_in, grad_memory, grad_params[0], grad_params[1], grad_params[2], grad_params[3], grad_params[4], grad_params[5], grad_params[6], grad_params[7], grad_params[8], grad_params[9], grad_params[10], grad_params[11], grad_params[12], grad_params[13], grad_params[14])
```

```python
import functools
import math

import jax
import jax.numpy as jnp
from jax import lax
from jax.sharding import PartitionSpec as P

HEADS = 12
HEAD_DIM = 64


bucket_edges = [math.ceil(16 * 8 ** (number / 16)) for number in range(1, 16)]
epsilon = 1e-06
masked_score = -1000000000.0


def bucket_of(distance):
    far_part = sum(((distance >= border).astype(jnp.int32) for border in bucket_edges))
    return jnp.where(distance < 16, distance, 16 + far_part)


def rms_scale(values, scales):
    return values * lax.rsqrt(jnp.mean(values * values, axis=-1, keepdims=True) + epsilon) * scales


def product(former, latter):
    return jnp.dot(former, latter, preferred_element_type=jnp.float32)


def product_rows(former, latter):
    return lax.dot_general(
        former, latter, (((0,), (0,)), ((), ())), preferred_element_type=jnp.float32
    )


def product_cols(former, latter):
    return lax.dot_general(
        former, latter, (((1,), (1,)), ((), ())), preferred_element_type=jnp.float32
    )


def split_heads(matrix):
    return matrix.reshape(matrix.shape[0], HEADS, HEAD_DIM).transpose(1, 0, 2)


def join_heads(stacked):
    return stacked.transpose(1, 0, 2).reshape(stacked.shape[1], HEADS * HEAD_DIM)


def to_blocks(matrix, block_count):
    return matrix.reshape(block_count, -1, HEADS, HEAD_DIM).transpose(0, 2, 1, 3)


def from_blocks(stacked):
    return stacked.transpose(0, 2, 1, 3).reshape(-1, HEADS * HEAD_DIM)


def self_scores(queries, query_start, query_ids, table_full, key_rows, key_start, key_ids):
    query_count = queries.shape[1]
    key_count = key_rows.shape[1]
    query_places = query_start + jnp.arange(query_count, dtype=jnp.int32)
    key_places = key_start + jnp.arange(key_count, dtype=jnp.int32)
    buckets = bucket_of(jnp.maximum(query_places[:, None] - key_places[None, :], 0))
    one_hot = (
        buckets.reshape(1, -1) == jnp.arange(table_full.shape[0], dtype=jnp.int32)[:, None]
    ).astype(jnp.bfloat16)
    bias_block = jnp.einsum(
        "bn,bh->hn", one_hot, table_full, preferred_element_type=jnp.float32
    ).reshape(HEADS, query_count, key_count)
    scores = (
        jnp.einsum("hqd,hkd->hqk", queries, key_rows, preferred_element_type=jnp.float32)
        + bias_block
    )
    allowed = (query_places[:, None] >= key_places[None, :]) & (
        query_ids[:, None] == key_ids[None, :]
    )
    return (jnp.where(allowed[None], scores, masked_score), one_hot)


def self_logsum(queries, query_start, query_ids, table_full, key_blocks, id_blocks, key_starts):
    query_count = queries.shape[1]

    def advance(running, packed):
        largest, totals = running
        key_rows, key_ids, key_start = packed
        scores, unused = self_scores(
            queries, query_start, query_ids, table_full, key_rows, key_start, key_ids
        )
        newest = jnp.maximum(largest, jnp.max(scores, axis=-1, keepdims=True))
        totals = totals * jnp.exp(largest - newest) + jnp.sum(
            jnp.exp(scores - newest), axis=-1, keepdims=True
        )
        return ((newest, totals), None)

    initial = (
        jnp.full((HEADS, query_count, 1), -jnp.inf, jnp.float32),
        jnp.zeros((HEADS, query_count, 1), jnp.float32),
    )
    (largest, totals), unused = lax.scan(advance, initial, (key_blocks, id_blocks, key_starts))
    return largest + jnp.log(totals)


def self_mix(
    queries,
    query_start,
    query_ids,
    table_full,
    key_blocks,
    value_blocks,
    id_blocks,
    key_starts,
    logsum,
):

    def advance(accum, packed):
        key_rows, value_rows, key_ids, key_start = packed
        scores, unused = self_scores(
            queries, query_start, query_ids, table_full, key_rows, key_start, key_ids
        )
        weights = jnp.exp(scores - logsum).astype(jnp.bfloat16)
        return (
            accum
            + jnp.einsum("hqk,hkd->hqd", weights, value_rows, preferred_element_type=jnp.float32),
            None,
        )

    initial = jnp.zeros((HEADS, queries.shape[1], HEAD_DIM), jnp.float32)
    accum, unused = lax.scan(advance, initial, (key_blocks, value_blocks, id_blocks, key_starts))
    return accum


def self_backward(
    queries,
    query_start,
    query_ids,
    table_full,
    key_blocks,
    value_blocks,
    id_blocks,
    key_starts,
    logsum,
    grad_mixed,
):
    query_count = queries.shape[1]

    def dots(accum, packed):
        key_rows, value_rows, key_ids, key_start = packed
        scores, unused = self_scores(
            queries, query_start, query_ids, table_full, key_rows, key_start, key_ids
        )
        chances = jnp.exp(scores - logsum)
        grad_chances = jnp.einsum(
            "hqd,hkd->hqk", grad_mixed, value_rows, preferred_element_type=jnp.float32
        )
        return (accum + jnp.sum(chances * grad_chances, axis=-1, keepdims=True), None)

    row_dots, unused = lax.scan(
        dots,
        jnp.zeros((HEADS, query_count, 1), jnp.float32),
        (key_blocks, value_blocks, id_blocks, key_starts),
    )

    def advance(running, packed):
        grad_queries, grad_table = running
        key_rows, value_rows, key_ids, key_start = packed
        scores, one_hot = self_scores(
            queries, query_start, query_ids, table_full, key_rows, key_start, key_ids
        )
        chances = jnp.exp(scores - logsum)
        grad_chances = jnp.einsum(
            "hqd,hkd->hqk", grad_mixed, value_rows, preferred_element_type=jnp.float32
        )
        grad_scores = chances * (grad_chances - row_dots)
        rounded = grad_scores.astype(jnp.bfloat16)
        grad_values = jnp.einsum(
            "hqk,hqd->hkd",
            chances.astype(jnp.bfloat16),
            grad_mixed,
            preferred_element_type=jnp.float32,
        )
        grad_keys = jnp.einsum("hqk,hqd->hkd", rounded, queries, preferred_element_type=jnp.float32)
        grad_queries = grad_queries + jnp.einsum(
            "hqk,hkd->hqd", rounded, key_rows, preferred_element_type=jnp.float32
        )
        grad_table = grad_table + jnp.einsum(
            "bn,hn->bh",
            one_hot,
            grad_scores.reshape(HEADS, -1),
            precision=lax.Precision.HIGHEST,
            preferred_element_type=jnp.float32,
        )
        return ((grad_queries, grad_table), (grad_keys, grad_values))

    initial = (
        jnp.zeros((HEADS, query_count, HEAD_DIM), jnp.float32),
        jnp.zeros((table_full.shape[0], HEADS), jnp.float32),
    )
    (grad_queries, grad_table), (grad_keys, grad_values) = lax.scan(
        advance, initial, (key_blocks, value_blocks, id_blocks, key_starts)
    )
    return (join_heads(grad_queries), grad_table, from_blocks(grad_keys), from_blocks(grad_values))


def cross_forward(queries, key_heads, value_heads, allowed):
    scores = jnp.where(
        allowed,
        jnp.einsum("hqd,hkd->hqk", queries, key_heads, preferred_element_type=jnp.float32),
        masked_score,
    )
    largest = jnp.max(scores, axis=-1, keepdims=True)
    logsum = largest + jnp.log(jnp.sum(jnp.exp(scores - largest), axis=-1, keepdims=True))
    weights = jnp.exp(scores - logsum).astype(jnp.bfloat16)
    mixed = jnp.einsum("hqk,hkd->hqd", weights, value_heads, preferred_element_type=jnp.float32)
    return (mixed, logsum)


def cross_backward(queries, key_heads, value_heads, allowed, logsum, grad_mixed):
    scores = jnp.where(
        allowed,
        jnp.einsum("hqd,hkd->hqk", queries, key_heads, preferred_element_type=jnp.float32),
        masked_score,
    )
    chances = jnp.exp(scores - logsum)
    grad_values = jnp.einsum(
        "hqk,hqd->hkd", chances.astype(jnp.bfloat16), grad_mixed, preferred_element_type=jnp.float32
    )
    grad_chances = jnp.einsum(
        "hqd,hkd->hqk", grad_mixed, value_heads, preferred_element_type=jnp.float32
    )
    grad_scores = chances * (grad_chances - jnp.sum(chances * grad_chances, axis=-1, keepdims=True))
    rounded = grad_scores.astype(jnp.bfloat16)
    grad_queries = jnp.einsum(
        "hqk,hkd->hqd", rounded, key_heads, preferred_element_type=jnp.float32
    )
    grad_keys = jnp.einsum("hqk,hqd->hkd", rounded, queries, preferred_element_type=jnp.float32)
    return (join_heads(grad_queries), join_heads(grad_keys), join_heads(grad_values))


def shards(
    inputs,
    encoder,
    segments,
    enc_segments,
    self_query,
    self_key,
    self_value,
    self_output,
    cross_query,
    cross_key,
    cross_value,
    cross_output,
    gate_weight,
    up_weight,
    down_weight,
    self_gain,
    cross_gain,
    feed_gain,
    bias_table,
    cotangent,
):
    fetched = (
        lax.all_gather(self_query, "shard", axis=0, tiled=True),
        lax.all_gather(self_key, "shard", axis=0, tiled=True),
        lax.all_gather(self_value, "shard", axis=0, tiled=True),
        lax.all_gather(self_output, "shard", axis=0, tiled=True),
        lax.all_gather(cross_query, "shard", axis=0, tiled=True),
        lax.all_gather(cross_key, "shard", axis=0, tiled=True),
        lax.all_gather(cross_value, "shard", axis=0, tiled=True),
        lax.all_gather(cross_output, "shard", axis=0, tiled=True),
        lax.all_gather(gate_weight, "shard", axis=0, tiled=True),
        lax.all_gather(up_weight, "shard", axis=0, tiled=True),
        lax.all_gather(down_weight, "shard", axis=0, tiled=True),
        lax.all_gather(self_gain, "shard", axis=0, tiled=True),
        lax.all_gather(cross_gain, "shard", axis=0, tiled=True),
        lax.all_gather(feed_gain, "shard", axis=0, tiled=True),
        lax.all_gather(bias_table, "shard", axis=0, tiled=True),
    )
    (
        w_query,
        w_key,
        w_value,
        w_output,
        c_query,
        c_key,
        c_value,
        c_output,
        w_gate,
        w_up,
        w_down,
        g_self,
        g_cross,
        g_feed,
        table_full,
    ) = fetched
    gain_self = g_self.astype(jnp.float32)
    gain_cross = g_cross.astype(jnp.float32)
    gain_feed = g_feed.astype(jnp.float32)
    source = inputs[0].astype(jnp.float32)
    memory = encoder[0]
    segment_ids = segments[0]
    memory_ids = enc_segments[0]
    tokens_here = source.shape[0]
    length = segment_ids.shape[0]
    block_size = math.gcd(length, 512)
    block_count = length // block_size
    query_start = lax.axis_index("shard") * tokens_here
    query_ids = lax.dynamic_slice_in_dim(segment_ids, query_start, tokens_here)
    id_blocks = segment_ids.reshape(block_count, block_size)
    key_starts = jnp.arange(block_count, dtype=jnp.int32) * block_size
    cross_allowed = (query_ids[:, None] == memory_ids[None, :])[None]
    normed_self = rms_scale(source, gain_self).astype(jnp.bfloat16)
    query_heads = split_heads(product(normed_self, w_query).astype(jnp.bfloat16))
    key_local = product(normed_self, w_key).astype(jnp.bfloat16)
    value_local = product(normed_self, w_value).astype(jnp.bfloat16)
    keys_all, values_all = (
        lax.all_gather(key_local, "shard", axis=0, tiled=True),
        lax.all_gather(value_local, "shard", axis=0, tiled=True),
    )
    key_blocks = to_blocks(keys_all, block_count)
    value_blocks = to_blocks(values_all, block_count)
    logsum_self = self_logsum(
        query_heads, query_start, query_ids, table_full, key_blocks, id_blocks, key_starts
    )
    mixed_self = self_mix(
        query_heads,
        query_start,
        query_ids,
        table_full,
        key_blocks,
        value_blocks,
        id_blocks,
        key_starts,
        logsum_self,
    )
    joined_self = join_heads(mixed_self).astype(jnp.bfloat16)
    after_self = source + product(joined_self, w_output)
    normed_cross = rms_scale(after_self, gain_cross).astype(jnp.bfloat16)
    query_cross = split_heads(product(normed_cross, c_query).astype(jnp.bfloat16))
    key_cross_local = product(memory, c_key).astype(jnp.bfloat16)
    value_cross_local = product(memory, c_value).astype(jnp.bfloat16)
    keys_cross, values_cross = (
        lax.all_gather(key_cross_local, "shard", axis=0, tiled=True),
        lax.all_gather(value_cross_local, "shard", axis=0, tiled=True),
    )
    key_cross = split_heads(keys_cross)
    value_cross = split_heads(values_cross)
    mixed_cross, logsum_cross = cross_forward(query_cross, key_cross, value_cross, cross_allowed)
    joined_cross = join_heads(mixed_cross).astype(jnp.bfloat16)
    after_cross = after_self + product(joined_cross, c_output)
    normed_feed = rms_scale(after_cross, gain_feed).astype(jnp.bfloat16)
    gate_act = product(normed_feed, w_gate)
    up_act = product(normed_feed, w_up)
    hidden = (jax.nn.gelu(gate_act, approximate=True) * up_act).astype(jnp.bfloat16)
    outcome = after_cross + product(hidden, w_down)
    fetched = (
        lax.all_gather(self_query, "shard", axis=0, tiled=True),
        lax.all_gather(self_key, "shard", axis=0, tiled=True),
        lax.all_gather(self_value, "shard", axis=0, tiled=True),
        lax.all_gather(self_output, "shard", axis=0, tiled=True),
        lax.all_gather(cross_query, "shard", axis=0, tiled=True),
        lax.all_gather(cross_key, "shard", axis=0, tiled=True),
        lax.all_gather(cross_value, "shard", axis=0, tiled=True),
        lax.all_gather(cross_output, "shard", axis=0, tiled=True),
        lax.all_gather(gate_weight, "shard", axis=0, tiled=True),
        lax.all_gather(up_weight, "shard", axis=0, tiled=True),
        lax.all_gather(down_weight, "shard", axis=0, tiled=True),
        lax.all_gather(self_gain, "shard", axis=0, tiled=True),
        lax.all_gather(cross_gain, "shard", axis=0, tiled=True),
        lax.all_gather(feed_gain, "shard", axis=0, tiled=True),
        lax.all_gather(bias_table, "shard", axis=0, tiled=True),
    )
    (
        w_query,
        w_key,
        w_value,
        w_output,
        c_query,
        c_key,
        c_value,
        c_output,
        w_gate,
        w_up,
        w_down,
        g_self,
        g_cross,
        g_feed,
        table_full,
    ) = fetched
    gain_self = g_self.astype(jnp.float32)
    gain_cross = g_cross.astype(jnp.float32)
    gain_feed = g_feed.astype(jnp.float32)
    keys_all, values_all = (
        lax.all_gather(key_local, "shard", axis=0, tiled=True),
        lax.all_gather(value_local, "shard", axis=0, tiled=True),
    )
    key_blocks = to_blocks(keys_all, block_count)
    value_blocks = to_blocks(values_all, block_count)
    grad_out = cotangent[0].astype(jnp.float32)
    grad_down_in = cotangent[0]
    d_down = product_rows(hidden, grad_down_in)
    grad_hidden = product_cols(grad_down_in, w_down)

    def activation(gate_in, up_in):
        return jax.nn.gelu(gate_in, approximate=True) * up_in

    unused, pull = jax.vjp(activation, gate_act, up_act)
    grad_gate, grad_up = pull(grad_hidden)
    grad_gate = grad_gate.astype(jnp.bfloat16)
    grad_up = grad_up.astype(jnp.bfloat16)
    d_gate = product_rows(normed_feed, grad_gate)
    d_up = product_rows(normed_feed, grad_up)
    grad_normed_feed = product_cols(grad_gate, w_gate) + product_cols(grad_up, w_up)
    unused, pull = jax.vjp(rms_scale, after_cross, gain_feed)
    norm_part, d_feed_gain = pull(grad_normed_feed)
    grad_cross_total = grad_out + norm_part
    grad_cross_in = grad_cross_total.astype(jnp.bfloat16)
    d_c_output = product_rows(joined_cross, grad_cross_in)
    grad_mixed_cross = split_heads(product_cols(grad_cross_in, c_output).astype(jnp.bfloat16))
    grad_query_cross, grad_keys_cross, grad_values_cross = cross_backward(
        query_cross, key_cross, value_cross, cross_allowed, logsum_cross, grad_mixed_cross
    )
    grad_query_cross = grad_query_cross.astype(jnp.bfloat16)
    key_part, value_part = (
        lax.psum_scatter(
            grad_keys_cross.astype(jnp.bfloat16), "shard", scatter_dimension=0, tiled=True
        ).astype(jnp.float32),
        lax.psum_scatter(
            grad_values_cross.astype(jnp.bfloat16), "shard", scatter_dimension=0, tiled=True
        ).astype(jnp.float32),
    )
    grad_key_cross = key_part.astype(jnp.bfloat16)
    grad_value_cross = value_part.astype(jnp.bfloat16)
    d_c_query = product_rows(normed_cross, grad_query_cross)
    d_c_key = product_rows(memory, grad_key_cross)
    d_c_value = product_rows(memory, grad_value_cross)
    grad_memory = product_cols(grad_key_cross, c_key) + product_cols(grad_value_cross, c_value)
    grad_normed_cross = product_cols(grad_query_cross, c_query)
    unused, pull = jax.vjp(rms_scale, after_self, gain_cross)
    norm_part, d_cross_gain = pull(grad_normed_cross)
    grad_self_total = grad_cross_total + norm_part
    grad_self_in = grad_self_total.astype(jnp.bfloat16)
    d_output = product_rows(joined_self, grad_self_in)
    grad_mixed_self = split_heads(product_cols(grad_self_in, w_output).astype(jnp.bfloat16))
    grad_queries, d_table, grad_keys_full, grad_values_full = self_backward(
        query_heads,
        query_start,
        query_ids,
        table_full,
        key_blocks,
        value_blocks,
        id_blocks,
        key_starts,
        logsum_self,
        grad_mixed_self,
    )
    grad_query_self = grad_queries.astype(jnp.bfloat16)
    key_part, value_part = (
        lax.psum_scatter(
            grad_keys_full.astype(jnp.bfloat16), "shard", scatter_dimension=0, tiled=True
        ).astype(jnp.float32),
        lax.psum_scatter(
            grad_values_full.astype(jnp.bfloat16), "shard", scatter_dimension=0, tiled=True
        ).astype(jnp.float32),
    )
    grad_key_self = key_part.astype(jnp.bfloat16)
    grad_value_self = value_part.astype(jnp.bfloat16)
    d_query = product_rows(normed_self, grad_query_self)
    d_key = product_rows(normed_self, grad_key_self)
    d_value = product_rows(normed_self, grad_value_self)
    grad_normed_self = (
        product_cols(grad_query_self, w_query)
        + product_cols(grad_key_self, w_key)
        + product_cols(grad_value_self, w_value)
    )
    unused, pull = jax.vjp(rms_scale, source, gain_self)
    norm_part, d_self_gain = pull(grad_normed_self)
    grad_source = grad_self_total + norm_part
    summed = (
        lax.psum_scatter(
            d_query.astype(jnp.bfloat16), "shard", scatter_dimension=0, tiled=True
        ).astype(jnp.float32),
        lax.psum_scatter(
            d_key.astype(jnp.bfloat16), "shard", scatter_dimension=0, tiled=True
        ).astype(jnp.float32),
        lax.psum_scatter(
            d_value.astype(jnp.bfloat16), "shard", scatter_dimension=0, tiled=True
        ).astype(jnp.float32),
        lax.psum_scatter(
            d_output.astype(jnp.bfloat16), "shard", scatter_dimension=0, tiled=True
        ).astype(jnp.float32),
        lax.psum_scatter(
            d_c_query.astype(jnp.bfloat16), "shard", scatter_dimension=0, tiled=True
        ).astype(jnp.float32),
        lax.psum_scatter(
            d_c_key.astype(jnp.bfloat16), "shard", scatter_dimension=0, tiled=True
        ).astype(jnp.float32),
        lax.psum_scatter(
            d_c_value.astype(jnp.bfloat16), "shard", scatter_dimension=0, tiled=True
        ).astype(jnp.float32),
        lax.psum_scatter(
            d_c_output.astype(jnp.bfloat16), "shard", scatter_dimension=0, tiled=True
        ).astype(jnp.float32),
        lax.psum_scatter(
            d_gate.astype(jnp.bfloat16), "shard", scatter_dimension=0, tiled=True
        ).astype(jnp.float32),
        lax.psum_scatter(
            d_up.astype(jnp.bfloat16), "shard", scatter_dimension=0, tiled=True
        ).astype(jnp.float32),
        lax.psum_scatter(
            d_down.astype(jnp.bfloat16), "shard", scatter_dimension=0, tiled=True
        ).astype(jnp.float32),
        lax.psum_scatter(
            d_self_gain.astype(jnp.bfloat16), "shard", scatter_dimension=0, tiled=True
        ).astype(jnp.float32),
        lax.psum_scatter(
            d_cross_gain.astype(jnp.bfloat16), "shard", scatter_dimension=0, tiled=True
        ).astype(jnp.float32),
        lax.psum_scatter(
            d_feed_gain.astype(jnp.bfloat16), "shard", scatter_dimension=0, tiled=True
        ).astype(jnp.float32),
        lax.psum_scatter(
            d_table.astype(jnp.bfloat16), "shard", scatter_dimension=0, tiled=True
        ).astype(jnp.float32),
    )
    totals = (
        lax.psum(summed[0].astype(jnp.bfloat16), "rep").astype(jnp.float32),
        lax.psum(summed[1].astype(jnp.bfloat16), "rep").astype(jnp.float32),
        lax.psum(summed[2].astype(jnp.bfloat16), "rep").astype(jnp.float32),
        lax.psum(summed[3].astype(jnp.bfloat16), "rep").astype(jnp.float32),
        lax.psum(summed[4].astype(jnp.bfloat16), "rep").astype(jnp.float32),
        lax.psum(summed[5].astype(jnp.bfloat16), "rep").astype(jnp.float32),
        lax.psum(summed[6].astype(jnp.bfloat16), "rep").astype(jnp.float32),
        lax.psum(summed[7].astype(jnp.bfloat16), "rep").astype(jnp.float32),
        lax.psum(summed[8].astype(jnp.bfloat16), "rep").astype(jnp.float32),
        lax.psum(summed[9].astype(jnp.bfloat16), "rep").astype(jnp.float32),
        lax.psum(summed[10].astype(jnp.bfloat16), "rep").astype(jnp.float32),
        lax.psum(summed[11].astype(jnp.bfloat16), "rep").astype(jnp.float32),
        lax.psum(summed[12].astype(jnp.bfloat16), "rep").astype(jnp.float32),
        lax.psum(summed[13].astype(jnp.bfloat16), "rep").astype(jnp.float32),
        lax.psum(summed[14].astype(jnp.bfloat16), "rep").astype(jnp.float32),
    )
    return (
        outcome.astype(jnp.bfloat16)[None],
        grad_source[None],
        grad_memory[None],
        totals[0],
        totals[1],
        totals[2],
        totals[3],
        totals[4],
        totals[5],
        totals[6],
        totals[7],
        totals[8],
        totals[9],
        totals[10],
        totals[11],
        totals[12],
        totals[13],
        totals[14],
    )


def swap(value, axis, size, step):
    return lax.ppermute(value, axis, [(place, place ^ step) for place in range(size)])


def after(value, *others):
    return lax.optimization_barrier((value, *others))[0]


def spread_columns(weight, count):
    rows = weight.shape[0]
    return weight.reshape(rows, count, -1).transpose(1, 0, 2)


def place_blocks(own, received, index, axis=0):
    stacked = jnp.zeros(own.shape[:axis] + (len(received) + 1,) + own.shape[axis:], own.dtype)
    stacked = lax.dynamic_update_index_in_dim(stacked, own, index, axis)
    for step, block in received:
        stacked = lax.dynamic_update_index_in_dim(stacked, block, index ^ step, axis)
    return stacked


def exchange(blocks, index, axis, size, unit=1):
    received = []
    for number in range(1, size):
        step = number * unit
        part = lax.dynamic_index_in_dim(blocks, index ^ number, 0, keepdims=False)
        received.append((number, swap(part, axis, size * unit, step)))
    own = lax.dynamic_index_in_dim(blocks, index, 0, keepdims=False)
    return own, received


def gather_rows(value, index):
    far = swap(value, "shard", 4, 2)
    near = swap(value, "shard", 4, 1)
    last = swap(far, "shard", 4, 1)
    stacked = place_blocks(value, [(1, near), (2, far), (3, last)], index)
    return stacked.reshape((-1,) + value.shape[1:])


def halves_sum(partial, index):
    core = index & 1
    view = partial.reshape((2, 2, -1) + partial.shape[1:])
    mine = lax.dynamic_index_in_dim(view, core, 1, keepdims=False)
    other = lax.dynamic_index_in_dim(view, 1 - core, 1, keepdims=False)
    arrived = swap(other.astype(jnp.bfloat16), "shard", 4, 1)
    return mine + arrived.astype(jnp.float32)


def sum_all(partial, index):
    pair = halves_sum(partial, index).astype(jnp.bfloat16)
    far = swap(pair, "shard", 4, 2)
    total = (pair.astype(jnp.float32) + far.astype(jnp.float32)).astype(jnp.bfloat16)
    near = swap(total, "shard", 4, 1)
    stacked = place_blocks(total, [(1, near)], index & 1, axis=1)
    return stacked.reshape(partial.shape).astype(jnp.float32)


def sum_scatter(partial, index):
    chip = index >> 1
    pair = halves_sum(partial, index)
    mine = lax.dynamic_index_in_dim(pair, chip, 0, keepdims=False)
    other = lax.dynamic_index_in_dim(pair, 1 - chip, 0, keepdims=False)
    far = swap(other.astype(jnp.bfloat16), "shard", 4, 2)
    return mine + far.astype(jnp.float32)


def rep_scatter(chunks, rep, count):
    depth = count // 2
    view = chunks.reshape((depth, 2) + chunks.shape[1:])
    column = rep & 1
    row = rep >> 1
    mine = lax.dynamic_index_in_dim(view, column, 1, keepdims=False)
    other = lax.dynamic_index_in_dim(view, 1 - column, 1, keepdims=False)
    arrived = swap(other.astype(jnp.bfloat16), "rep", count, 1)
    pair = mine.astype(jnp.float32) + arrived.astype(jnp.float32)
    low = pair.astype(jnp.bfloat16)
    own = lax.dynamic_index_in_dim(pair, row, 0, keepdims=False)
    for number in range(1, depth):
        part = lax.dynamic_index_in_dim(low, row ^ number, 0, keepdims=False)
        own = own + swap(part, "rep", count, number * 2).astype(jnp.float32)
    return own


def rep_gather(piece, rep, count):
    depth = count // 2
    column = rep & 1
    row = rep >> 1
    received = [
        (number, swap(piece, "rep", count, number * 2)) for number in range(1, depth)
    ]
    line = place_blocks(piece, received, row)
    arrived = swap(line, "rep", count, 1)
    stacked = place_blocks(line, [(1, arrived)], column, axis=1)
    return stacked.reshape((count,) + piece.shape)


def reduce_columns(gradient, index, rep, count):
    rows, width = gradient.shape
    small = rows // (4 * count)
    chunks = gradient.reshape(4, count, small, width).transpose(1, 0, 2, 3)
    piece = rep_scatter(chunks, rep, count).astype(jnp.bfloat16)
    own, received = exchange(piece, index, "shard", 4)
    return rep_gather(place_blocks(own, received, index), rep, count)


def unpack_columns(gathered, start, width):
    count, parts, small, unused = gathered.shape
    part = gathered[..., start : start + width]
    return part.transpose(0, 2, 1, 3).reshape(count * small, parts * width).astype(jnp.float32)


def reduce_rows(gradient, rep, count):
    rows, width = gradient.shape
    piece = rep_scatter(gradient.reshape(count, rows // count, width), rep, count)
    gathered = rep_gather(piece.astype(jnp.bfloat16), rep, count)
    return gathered.reshape(rows, width).astype(jnp.float32)


def sum_everywhere(vector, count):
    for step in (1, 2):
        vector = vector + swap(vector, "shard", 4, step)
    step = 1
    while step < count:
        vector = vector + swap(vector, "rep", count, step)
        step *= 2
    return vector


def local_heads(matrix):
    return matrix.reshape(matrix.shape[0], -1, HEAD_DIM).transpose(1, 0, 2)


def merge_heads(stacked):
    return stacked.transpose(1, 0, 2).reshape(stacked.shape[1], -1)


def attend_forward(queries, keys, values, bias, allowed):
    scores = jnp.einsum("hqd,hkd->hqk", queries, keys, preferred_element_type=jnp.float32)
    if bias is not None:
        scores = scores + bias
    scores = jnp.where(allowed, scores, masked_score)
    largest = jnp.max(scores, axis=-1, keepdims=True)
    logsum = largest + jnp.log(jnp.sum(jnp.exp(scores - largest), axis=-1, keepdims=True))
    chances = jnp.exp(scores - logsum)
    mixed = jnp.einsum(
        "hqk,hkd->hqd", chances.astype(jnp.bfloat16), values, preferred_element_type=jnp.float32
    )
    return merge_heads(mixed).astype(jnp.bfloat16), chances


def attend_backward(queries, keys, values, chances, grad_mixed):
    grad_values = jnp.einsum(
        "hqk,hqd->hkd", chances.astype(jnp.bfloat16), grad_mixed, preferred_element_type=jnp.float32
    )
    grad_chances = jnp.einsum(
        "hqd,hkd->hqk", grad_mixed, values, preferred_element_type=jnp.float32
    )
    grad_scores = chances * (grad_chances - jnp.sum(chances * grad_chances, axis=-1, keepdims=True))
    rounded = grad_scores.astype(jnp.bfloat16)
    grad_queries = jnp.einsum("hqk,hkd->hqd", rounded, keys, preferred_element_type=jnp.float32)
    grad_keys = jnp.einsum("hqk,hqd->hkd", rounded, queries, preferred_element_type=jnp.float32)
    merged = [
        merge_heads(part).astype(jnp.bfloat16) for part in (grad_queries, grad_keys, grad_values)
    ]
    return merged, grad_scores


def split_shards(
    count,
    inputs,
    encoder,
    segments,
    enc_segments,
    self_query,
    self_key,
    self_value,
    self_output,
    cross_query,
    cross_key,
    cross_value,
    cross_output,
    gate_weight,
    up_weight,
    down_weight,
    self_gain,
    cross_gain,
    feed_gain,
    bias_table,
    cotangent,
):
    index = lax.axis_index("shard")
    rep = lax.axis_index("rep")
    tokens_here, model = inputs.shape[1:]
    heads_here = HEADS // 4
    wide = heads_here * HEAD_DIM
    small_rows = bias_table.shape[0]
    table_size = small_rows * HEADS
    small = jnp.concatenate([self_gain, cross_gain, feed_gain, bias_table.reshape(-1)])
    extra = jnp.zeros((8, model), jnp.bfloat16).at[0, : small.shape[0]].set(small)

    def whole_weight(columns):
        own, received = exchange(columns, index, "shard", 4)
        stacked = place_blocks(own, received, index)
        return stacked.reshape(-1, columns.shape[-1])

    packed = jnp.concatenate([inputs[0], extra])
    packed_all = gather_rows(packed, index).reshape(4, tokens_here + 8, model)
    w_self = whole_weight(
        jnp.concatenate([spread_columns(w, 4) for w in (self_query, self_key, self_value)], axis=-1)
    )
    source_low = packed_all[:, :tokens_here].reshape(-1, model)
    small_all = packed_all[:, tokens_here].astype(jnp.float32)
    part = self_gain.shape[0]
    gain_self = small_all[:, :part].reshape(-1)
    gain_cross = small_all[:, part : 2 * part].reshape(-1)
    gain_feed = small_all[:, 2 * part : 3 * part].reshape(-1)
    table_full = small_all[:, 3 * part : 3 * part + table_size].reshape(-1, HEADS)
    memory = gather_rows(after(encoder[0], w_self), index)
    w_cross = whole_weight(
        after(
            jnp.concatenate(
                [spread_columns(w, 4) for w in (cross_query, cross_key, cross_value)], axis=-1
            ),
            w_self,
        )
    )
    w_feed = whole_weight(
        after(
            jnp.concatenate([spread_columns(w, 4) for w in (gate_weight, up_weight)], axis=-1),
            w_cross,
        )
    )
    grad_out = gather_rows(after(cotangent[0], w_feed), index)

    source = source_low.astype(jnp.float32)
    segment_ids = segments[0]
    memory_ids = enc_segments[0]
    length = source.shape[0]
    places = jnp.arange(length, dtype=jnp.int32)
    gap = places[:, None] - places[None, :]
    allowed_self = ((gap >= 0) & (segment_ids[:, None] == segment_ids[None, :]))[None]
    allowed_cross = (segment_ids[:, None] == memory_ids[None, :])[None]
    table_here = lax.dynamic_slice_in_dim(table_full, index * heads_here, heads_here, 1)
    buckets = bucket_of(jnp.maximum(gap, 0))
    one_hot = (
        buckets.reshape(1, -1) == jnp.arange(table_full.shape[0], dtype=jnp.int32)[:, None]
    ).astype(jnp.bfloat16)
    bias = jnp.einsum(
        "bn,bh->hn", one_hot, table_here.astype(jnp.bfloat16), preferred_element_type=jnp.float32
    ).reshape(heads_here, length, length)

    normed_self = rms_scale(source, gain_self).astype(jnp.bfloat16)
    mapped = product(normed_self, w_self).astype(jnp.bfloat16)
    query_self, key_self, value_self = (
        local_heads(mapped[:, start * wide : (start + 1) * wide]) for start in range(3)
    )
    mixed_self, chances_self = attend_forward(query_self, key_self, value_self, bias, allowed_self)
    after_self = source + sum_all(product(mixed_self, self_output), index)
    normed_cross = rms_scale(after_self, gain_cross).astype(jnp.bfloat16)
    query_cross = local_heads(product(normed_cross, w_cross[:, :wide]).astype(jnp.bfloat16))
    mapped = product(memory, w_cross[:, wide:]).astype(jnp.bfloat16)
    key_cross, value_cross = (
        local_heads(mapped[:, start * wide : (start + 1) * wide]) for start in range(2)
    )
    mixed_cross, chances_cross = attend_forward(
        query_cross, key_cross, value_cross, None, allowed_cross
    )
    after_cross = after_self + sum_all(product(mixed_cross, cross_output), index)
    normed_feed = rms_scale(after_cross, gain_feed).astype(jnp.bfloat16)
    acts = product(normed_feed, w_feed)
    hidden_size = acts.shape[1] // 2
    gate_act, up_act = acts[:, :hidden_size], acts[:, hidden_size:]

    def activation(gate_in, up_in):
        return jax.nn.gelu(gate_in, approximate=True) * up_in

    hidden, pull = jax.vjp(activation, gate_act, up_act)
    hidden = hidden.astype(jnp.bfloat16)
    own_start = index * tokens_here
    outcome = lax.dynamic_slice_in_dim(after_cross, own_start, tokens_here) + sum_scatter(
        product(hidden, down_weight), index
    )

    d_down = product_rows(hidden, grad_out)
    grad_gate, grad_up = pull(product_cols(grad_out, down_weight))
    grad_acts = jnp.concatenate([grad_gate, grad_up], axis=1).astype(jnp.bfloat16)
    d_feed = product_rows(normed_feed, grad_acts)
    grad_normed_feed = sum_all(product_cols(grad_acts, w_feed), index)
    unused, pull = jax.vjp(rms_scale, after_cross, gain_feed)
    norm_part, d_feed_gain = pull(grad_normed_feed)
    grad_cross_total = grad_out.astype(jnp.float32) + norm_part
    grad_cross_in = grad_cross_total.astype(jnp.bfloat16)
    d_c_output = product_rows(mixed_cross, grad_cross_in)
    grad_mixed_cross = local_heads(product_cols(grad_cross_in, cross_output).astype(jnp.bfloat16))
    merged, unused = attend_backward(
        query_cross, key_cross, value_cross, chances_cross, grad_mixed_cross
    )
    d_cross = jnp.concatenate(
        [
            product_rows(normed_cross, merged[0]),
            product_rows(memory, jnp.concatenate(merged[1:], axis=1)),
        ],
        axis=1,
    )
    grad_normed_cross = sum_all(product_cols(merged[0], w_cross[:, :wide]), index)
    grad_memory = sum_scatter(
        product_cols(jnp.concatenate(merged[1:], axis=1), w_cross[:, wide:]), index
    )
    unused, pull = jax.vjp(rms_scale, after_self, gain_cross)
    norm_part, d_cross_gain = pull(grad_normed_cross)
    grad_self_total = grad_cross_total + norm_part
    grad_self_in = grad_self_total.astype(jnp.bfloat16)
    d_output = product_rows(mixed_self, grad_self_in)
    grad_mixed_self = local_heads(product_cols(grad_self_in, self_output).astype(jnp.bfloat16))
    merged, grad_scores = attend_backward(
        query_self, key_self, value_self, chances_self, grad_mixed_self
    )
    d_table = jnp.einsum(
        "bn,hn->bh",
        one_hot,
        grad_scores.reshape(heads_here, -1),
        precision=lax.Precision.HIGHEST,
        preferred_element_type=jnp.float32,
    )
    merged = jnp.concatenate(merged, axis=1)
    d_self = product_rows(normed_self, merged)
    grad_normed_self = sum_scatter(product_cols(merged, w_self), index)
    source_here = inputs[0].astype(jnp.float32)
    unused, pull = jax.vjp(rms_scale, source_here, gain_self)
    norm_part, d_self_gain = pull(grad_normed_self)
    grad_source = lax.dynamic_slice_in_dim(grad_self_total, own_start, tokens_here) + norm_part

    def only_here(gradient):
        own = lax.dynamic_slice_in_dim(gradient, index * part, part)
        return lax.dynamic_update_slice_in_dim(jnp.zeros_like(gradient), own, index * part, 0)

    table_sparse = lax.dynamic_update_slice_in_dim(
        jnp.zeros(table_full.shape, jnp.float32), d_table, index * heads_here, 1
    )
    vector = jnp.concatenate(
        [
            d_self_gain,
            only_here(d_cross_gain),
            only_here(d_feed_gain),
            table_sparse.reshape(-1),
        ]
    )
    vector = sum_everywhere(vector, count)
    gains = vector[: 3 * model].reshape(3, model)
    gains_here = lax.dynamic_slice_in_dim(gains, index * part, part, 1)
    table_grad = lax.dynamic_slice_in_dim(
        vector[3 * model :].reshape(-1, HEADS), index * small_rows, small_rows
    )
    feed_sum = reduce_columns(d_feed, index, rep, count)
    down_sum = reduce_rows(d_down, rep, count)
    cross_sum = reduce_columns(d_cross, index, rep, count)
    c_output_sum = reduce_rows(d_c_output, rep, count)
    output_sum = reduce_rows(d_output, rep, count)
    self_sum = reduce_columns(d_self, index, rep, count)
    return (
        outcome.astype(jnp.bfloat16)[None],
        grad_source[None],
        grad_memory[None],
        unpack_columns(self_sum, 0, wide),
        unpack_columns(self_sum, wide, wide),
        unpack_columns(self_sum, 2 * wide, wide),
        output_sum,
        unpack_columns(cross_sum, 0, wide),
        unpack_columns(cross_sum, wide, wide),
        unpack_columns(cross_sum, 2 * wide, wide),
        c_output_sum,
        unpack_columns(feed_sum, 0, hidden_size),
        unpack_columns(feed_sum, hidden_size, hidden_size),
        down_sum,
        gains_here[0],
        gains_here[1],
        gains_here[2],
        table_grad,
    )


def solution(mesh):
    in_specs = (
        P("rep", "shard", None),
        P("rep", "shard", None),
        P("rep", None),
        P("rep", None),
        P("shard", None),
        P("shard", None),
        P("shard", None),
        P("shard", None),
        P("shard", None),
        P("shard", None),
        P("shard", None),
        P("shard", None),
        P("shard", None),
        P("shard", None),
        P("shard", None),
        P("shard"),
        P("shard"),
        P("shard"),
        P("shard", None),
        P("rep", "shard", None),
    )
    out_specs = (
        P("rep", "shard", None),
        P("rep", "shard", None),
        P("rep", "shard", None),
        P("shard", None),
        P("shard", None),
        P("shard", None),
        P("shard", None),
        P("shard", None),
        P("shard", None),
        P("shard", None),
        P("shard", None),
        P("shard", None),
        P("shard", None),
        P("shard", None),
        P("shard"),
        P("shard"),
        P("shard"),
        P("shard", None),
    )
    count = mesh.shape["rep"]
    split = mesh.shape["shard"] == 4 and count >= 2 and count & (count - 1) == 0
    body = functools.partial(split_shards, count) if split else shards
    return jax.shard_map(body, mesh=mesh, in_specs=in_specs, out_specs=out_specs, check_vma=False)
```

```python
import functools
import math

import jax
import jax.numpy as jnp
from jax import lax
from jax.experimental import pallas as pl
from jax.experimental.pallas import tpu as pltpu
from jax.sharding import PartitionSpec as P

HEADS = 12
HEAD_DIM = 64


bucket_edges = [math.ceil(16 * 8 ** (number / 16)) for number in range(1, 16)]
epsilon = 1e-06
masked_score = -1000000000.0


def bucket_of(distance):
    far_part = sum(((distance >= border).astype(jnp.int32) for border in bucket_edges))
    return jnp.where(distance < 16, distance, 16 + far_part)


def rms_scale(values, scales):
    return values * lax.rsqrt(jnp.mean(values * values, axis=-1, keepdims=True) + epsilon) * scales


def product(former, latter):
    return jnp.dot(former, latter, preferred_element_type=jnp.float32)


def product_rows(former, latter):
    return lax.dot_general(
        former, latter, (((0,), (0,)), ((), ())), preferred_element_type=jnp.float32
    )


def product_cols(former, latter):
    return lax.dot_general(
        former, latter, (((1,), (1,)), ((), ())), preferred_element_type=jnp.float32
    )


def split_heads(matrix):
    return matrix.reshape(matrix.shape[0], HEADS, HEAD_DIM).transpose(1, 0, 2)


def join_heads(stacked):
    return stacked.transpose(1, 0, 2).reshape(stacked.shape[1], HEADS * HEAD_DIM)


def to_blocks(matrix, block_count):
    return matrix.reshape(block_count, -1, HEADS, HEAD_DIM).transpose(0, 2, 1, 3)


def from_blocks(stacked):
    return stacked.transpose(0, 2, 1, 3).reshape(-1, HEADS * HEAD_DIM)


def self_scores(queries, query_start, query_ids, table_full, key_rows, key_start, key_ids):
    query_count = queries.shape[1]
    key_count = key_rows.shape[1]
    query_places = query_start + jnp.arange(query_count, dtype=jnp.int32)
    key_places = key_start + jnp.arange(key_count, dtype=jnp.int32)
    buckets = bucket_of(jnp.maximum(query_places[:, None] - key_places[None, :], 0))
    one_hot = (
        buckets.reshape(1, -1) == jnp.arange(table_full.shape[0], dtype=jnp.int32)[:, None]
    ).astype(jnp.bfloat16)
    bias_block = jnp.einsum(
        "bn,bh->hn", one_hot, table_full, preferred_element_type=jnp.float32
    ).reshape(HEADS, query_count, key_count)
    scores = (
        jnp.einsum("hqd,hkd->hqk", queries, key_rows, preferred_element_type=jnp.float32)
        + bias_block
    )
    allowed = (query_places[:, None] >= key_places[None, :]) & (
        query_ids[:, None] == key_ids[None, :]
    )
    return (jnp.where(allowed[None], scores, masked_score), one_hot)


def self_logsum(queries, query_start, query_ids, table_full, key_blocks, id_blocks, key_starts):
    query_count = queries.shape[1]

    def advance(running, packed):
        largest, totals = running
        key_rows, key_ids, key_start = packed
        scores, unused = self_scores(
            queries, query_start, query_ids, table_full, key_rows, key_start, key_ids
        )
        newest = jnp.maximum(largest, jnp.max(scores, axis=-1, keepdims=True))
        totals = totals * jnp.exp(largest - newest) + jnp.sum(
            jnp.exp(scores - newest), axis=-1, keepdims=True
        )
        return ((newest, totals), None)

    initial = (
        jnp.full((HEADS, query_count, 1), -jnp.inf, jnp.float32),
        jnp.zeros((HEADS, query_count, 1), jnp.float32),
    )
    (largest, totals), unused = lax.scan(advance, initial, (key_blocks, id_blocks, key_starts))
    return largest + jnp.log(totals)


def self_mix(
    queries,
    query_start,
    query_ids,
    table_full,
    key_blocks,
    value_blocks,
    id_blocks,
    key_starts,
    logsum,
):

    def advance(accum, packed):
        key_rows, value_rows, key_ids, key_start = packed
        scores, unused = self_scores(
            queries, query_start, query_ids, table_full, key_rows, key_start, key_ids
        )
        weights = jnp.exp(scores - logsum).astype(jnp.bfloat16)
        return (
            accum
            + jnp.einsum("hqk,hkd->hqd", weights, value_rows, preferred_element_type=jnp.float32),
            None,
        )

    initial = jnp.zeros((HEADS, queries.shape[1], HEAD_DIM), jnp.float32)
    accum, unused = lax.scan(advance, initial, (key_blocks, value_blocks, id_blocks, key_starts))
    return accum


def self_backward(
    queries,
    query_start,
    query_ids,
    table_full,
    key_blocks,
    value_blocks,
    id_blocks,
    key_starts,
    logsum,
    grad_mixed,
):
    query_count = queries.shape[1]

    def dots(accum, packed):
        key_rows, value_rows, key_ids, key_start = packed
        scores, unused = self_scores(
            queries, query_start, query_ids, table_full, key_rows, key_start, key_ids
        )
        chances = jnp.exp(scores - logsum)
        grad_chances = jnp.einsum(
            "hqd,hkd->hqk", grad_mixed, value_rows, preferred_element_type=jnp.float32
        )
        return (accum + jnp.sum(chances * grad_chances, axis=-1, keepdims=True), None)

    row_dots, unused = lax.scan(
        dots,
        jnp.zeros((HEADS, query_count, 1), jnp.float32),
        (key_blocks, value_blocks, id_blocks, key_starts),
    )

    def advance(running, packed):
        grad_queries, grad_table = running
        key_rows, value_rows, key_ids, key_start = packed
        scores, one_hot = self_scores(
            queries, query_start, query_ids, table_full, key_rows, key_start, key_ids
        )
        chances = jnp.exp(scores - logsum)
        grad_chances = jnp.einsum(
            "hqd,hkd->hqk", grad_mixed, value_rows, preferred_element_type=jnp.float32
        )
        grad_scores = chances * (grad_chances - row_dots)
        rounded = grad_scores.astype(jnp.bfloat16)
        grad_values = jnp.einsum(
            "hqk,hqd->hkd",
            chances.astype(jnp.bfloat16),
            grad_mixed,
            preferred_element_type=jnp.float32,
        )
        grad_keys = jnp.einsum("hqk,hqd->hkd", rounded, queries, preferred_element_type=jnp.float32)
        grad_queries = grad_queries + jnp.einsum(
            "hqk,hkd->hqd", rounded, key_rows, preferred_element_type=jnp.float32
        )
        grad_table = grad_table + jnp.einsum(
            "bn,hn->bh",
            one_hot,
            grad_scores.reshape(HEADS, -1),
            precision=lax.Precision.HIGHEST,
            preferred_element_type=jnp.float32,
        )
        return ((grad_queries, grad_table), (grad_keys, grad_values))

    initial = (
        jnp.zeros((HEADS, query_count, HEAD_DIM), jnp.float32),
        jnp.zeros((table_full.shape[0], HEADS), jnp.float32),
    )
    (grad_queries, grad_table), (grad_keys, grad_values) = lax.scan(
        advance, initial, (key_blocks, value_blocks, id_blocks, key_starts)
    )
    return (join_heads(grad_queries), grad_table, from_blocks(grad_keys), from_blocks(grad_values))


def cross_forward(queries, key_heads, value_heads, allowed):
    scores = jnp.where(
        allowed,
        jnp.einsum("hqd,hkd->hqk", queries, key_heads, preferred_element_type=jnp.float32),
        masked_score,
    )
    largest = jnp.max(scores, axis=-1, keepdims=True)
    logsum = largest + jnp.log(jnp.sum(jnp.exp(scores - largest), axis=-1, keepdims=True))
    weights = jnp.exp(scores - logsum).astype(jnp.bfloat16)
    mixed = jnp.einsum("hqk,hkd->hqd", weights, value_heads, preferred_element_type=jnp.float32)
    return (mixed, logsum)


def cross_backward(queries, key_heads, value_heads, allowed, logsum, grad_mixed):
    scores = jnp.where(
        allowed,
        jnp.einsum("hqd,hkd->hqk", queries, key_heads, preferred_element_type=jnp.float32),
        masked_score,
    )
    chances = jnp.exp(scores - logsum)
    grad_values = jnp.einsum(
        "hqk,hqd->hkd", chances.astype(jnp.bfloat16), grad_mixed, preferred_element_type=jnp.float32
    )
    grad_chances = jnp.einsum(
        "hqd,hkd->hqk", grad_mixed, value_heads, preferred_element_type=jnp.float32
    )
    grad_scores = chances * (grad_chances - jnp.sum(chances * grad_chances, axis=-1, keepdims=True))
    rounded = grad_scores.astype(jnp.bfloat16)
    grad_queries = jnp.einsum(
        "hqk,hkd->hqd", rounded, key_heads, preferred_element_type=jnp.float32
    )
    grad_keys = jnp.einsum("hqk,hqd->hkd", rounded, queries, preferred_element_type=jnp.float32)
    return (join_heads(grad_queries), join_heads(grad_keys), join_heads(grad_values))


def shards(
    inputs,
    encoder,
    segments,
    enc_segments,
    self_query,
    self_key,
    self_value,
    self_output,
    cross_query,
    cross_key,
    cross_value,
    cross_output,
    gate_weight,
    up_weight,
    down_weight,
    self_gain,
    cross_gain,
    feed_gain,
    bias_table,
    cotangent,
):
    fetched = (
        lax.all_gather(self_query, "shard", axis=0, tiled=True),
        lax.all_gather(self_key, "shard", axis=0, tiled=True),
        lax.all_gather(self_value, "shard", axis=0, tiled=True),
        lax.all_gather(self_output, "shard", axis=0, tiled=True),
        lax.all_gather(cross_query, "shard", axis=0, tiled=True),
        lax.all_gather(cross_key, "shard", axis=0, tiled=True),
        lax.all_gather(cross_value, "shard", axis=0, tiled=True),
        lax.all_gather(cross_output, "shard", axis=0, tiled=True),
        lax.all_gather(gate_weight, "shard", axis=0, tiled=True),
        lax.all_gather(up_weight, "shard", axis=0, tiled=True),
        lax.all_gather(down_weight, "shard", axis=0, tiled=True),
        lax.all_gather(self_gain, "shard", axis=0, tiled=True),
        lax.all_gather(cross_gain, "shard", axis=0, tiled=True),
        lax.all_gather(feed_gain, "shard", axis=0, tiled=True),
        lax.all_gather(bias_table, "shard", axis=0, tiled=True),
    )
    (
        w_query,
        w_key,
        w_value,
        w_output,
        c_query,
        c_key,
        c_value,
        c_output,
        w_gate,
        w_up,
        w_down,
        g_self,
        g_cross,
        g_feed,
        table_full,
    ) = fetched
    gain_self = g_self.astype(jnp.float32)
    gain_cross = g_cross.astype(jnp.float32)
    gain_feed = g_feed.astype(jnp.float32)
    source = inputs[0].astype(jnp.float32)
    memory = encoder[0]
    segment_ids = segments[0]
    memory_ids = enc_segments[0]
    tokens_here = source.shape[0]
    length = segment_ids.shape[0]
    block_size = math.gcd(length, 512)
    block_count = length // block_size
    query_start = lax.axis_index("shard") * tokens_here
    query_ids = lax.dynamic_slice_in_dim(segment_ids, query_start, tokens_here)
    id_blocks = segment_ids.reshape(block_count, block_size)
    key_starts = jnp.arange(block_count, dtype=jnp.int32) * block_size
    cross_allowed = (query_ids[:, None] == memory_ids[None, :])[None]
    normed_self = rms_scale(source, gain_self).astype(jnp.bfloat16)
    query_heads = split_heads(product(normed_self, w_query).astype(jnp.bfloat16))
    key_local = product(normed_self, w_key).astype(jnp.bfloat16)
    value_local = product(normed_self, w_value).astype(jnp.bfloat16)
    keys_all, values_all = (
        lax.all_gather(key_local, "shard", axis=0, tiled=True),
        lax.all_gather(value_local, "shard", axis=0, tiled=True),
    )
    key_blocks = to_blocks(keys_all, block_count)
    value_blocks = to_blocks(values_all, block_count)
    logsum_self = self_logsum(
        query_heads, query_start, query_ids, table_full, key_blocks, id_blocks, key_starts
    )
    mixed_self = self_mix(
        query_heads,
        query_start,
        query_ids,
        table_full,
        key_blocks,
        value_blocks,
        id_blocks,
        key_starts,
        logsum_self,
    )
    joined_self = join_heads(mixed_self).astype(jnp.bfloat16)
    after_self = source + product(joined_self, w_output)
    normed_cross = rms_scale(after_self, gain_cross).astype(jnp.bfloat16)
    query_cross = split_heads(product(normed_cross, c_query).astype(jnp.bfloat16))
    key_cross_local = product(memory, c_key).astype(jnp.bfloat16)
    value_cross_local = product(memory, c_value).astype(jnp.bfloat16)
    keys_cross, values_cross = (
        lax.all_gather(key_cross_local, "shard", axis=0, tiled=True),
        lax.all_gather(value_cross_local, "shard", axis=0, tiled=True),
    )
    key_cross = split_heads(keys_cross)
    value_cross = split_heads(values_cross)
    mixed_cross, logsum_cross = cross_forward(query_cross, key_cross, value_cross, cross_allowed)
    joined_cross = join_heads(mixed_cross).astype(jnp.bfloat16)
    after_cross = after_self + product(joined_cross, c_output)
    normed_feed = rms_scale(after_cross, gain_feed).astype(jnp.bfloat16)
    gate_act = product(normed_feed, w_gate)
    up_act = product(normed_feed, w_up)
    hidden = (jax.nn.gelu(gate_act, approximate=True) * up_act).astype(jnp.bfloat16)
    outcome = after_cross + product(hidden, w_down)
    fetched = (
        lax.all_gather(self_query, "shard", axis=0, tiled=True),
        lax.all_gather(self_key, "shard", axis=0, tiled=True),
        lax.all_gather(self_value, "shard", axis=0, tiled=True),
        lax.all_gather(self_output, "shard", axis=0, tiled=True),
        lax.all_gather(cross_query, "shard", axis=0, tiled=True),
        lax.all_gather(cross_key, "shard", axis=0, tiled=True),
        lax.all_gather(cross_value, "shard", axis=0, tiled=True),
        lax.all_gather(cross_output, "shard", axis=0, tiled=True),
        lax.all_gather(gate_weight, "shard", axis=0, tiled=True),
        lax.all_gather(up_weight, "shard", axis=0, tiled=True),
        lax.all_gather(down_weight, "shard", axis=0, tiled=True),
        lax.all_gather(self_gain, "shard", axis=0, tiled=True),
        lax.all_gather(cross_gain, "shard", axis=0, tiled=True),
        lax.all_gather(feed_gain, "shard", axis=0, tiled=True),
        lax.all_gather(bias_table, "shard", axis=0, tiled=True),
    )
    (
        w_query,
        w_key,
        w_value,
        w_output,
        c_query,
        c_key,
        c_value,
        c_output,
        w_gate,
        w_up,
        w_down,
        g_self,
        g_cross,
        g_feed,
        table_full,
    ) = fetched
    gain_self = g_self.astype(jnp.float32)
    gain_cross = g_cross.astype(jnp.float32)
    gain_feed = g_feed.astype(jnp.float32)
    keys_all, values_all = (
        lax.all_gather(key_local, "shard", axis=0, tiled=True),
        lax.all_gather(value_local, "shard", axis=0, tiled=True),
    )
    key_blocks = to_blocks(keys_all, block_count)
    value_blocks = to_blocks(values_all, block_count)
    grad_out = cotangent[0].astype(jnp.float32)
    grad_down_in = cotangent[0]
    d_down = product_rows(hidden, grad_down_in)
    grad_hidden = product_cols(grad_down_in, w_down)

    def activation(gate_in, up_in):
        return jax.nn.gelu(gate_in, approximate=True) * up_in

    unused, pull = jax.vjp(activation, gate_act, up_act)
    grad_gate, grad_up = pull(grad_hidden)
    grad_gate = grad_gate.astype(jnp.bfloat16)
    grad_up = grad_up.astype(jnp.bfloat16)
    d_gate = product_rows(normed_feed, grad_gate)
    d_up = product_rows(normed_feed, grad_up)
    grad_normed_feed = product_cols(grad_gate, w_gate) + product_cols(grad_up, w_up)
    unused, pull = jax.vjp(rms_scale, after_cross, gain_feed)
    norm_part, d_feed_gain = pull(grad_normed_feed)
    grad_cross_total = grad_out + norm_part
    grad_cross_in = grad_cross_total.astype(jnp.bfloat16)
    d_c_output = product_rows(joined_cross, grad_cross_in)
    grad_mixed_cross = split_heads(product_cols(grad_cross_in, c_output).astype(jnp.bfloat16))
    grad_query_cross, grad_keys_cross, grad_values_cross = cross_backward(
        query_cross, key_cross, value_cross, cross_allowed, logsum_cross, grad_mixed_cross
    )
    grad_query_cross = grad_query_cross.astype(jnp.bfloat16)
    key_part, value_part = (
        lax.psum_scatter(
            grad_keys_cross.astype(jnp.bfloat16), "shard", scatter_dimension=0, tiled=True
        ).astype(jnp.float32),
        lax.psum_scatter(
            grad_values_cross.astype(jnp.bfloat16), "shard", scatter_dimension=0, tiled=True
        ).astype(jnp.float32),
    )
    grad_key_cross = key_part.astype(jnp.bfloat16)
    grad_value_cross = value_part.astype(jnp.bfloat16)
    d_c_query = product_rows(normed_cross, grad_query_cross)
    d_c_key = product_rows(memory, grad_key_cross)
    d_c_value = product_rows(memory, grad_value_cross)
    grad_memory = product_cols(grad_key_cross, c_key) + product_cols(grad_value_cross, c_value)
    grad_normed_cross = product_cols(grad_query_cross, c_query)
    unused, pull = jax.vjp(rms_scale, after_self, gain_cross)
    norm_part, d_cross_gain = pull(grad_normed_cross)
    grad_self_total = grad_cross_total + norm_part
    grad_self_in = grad_self_total.astype(jnp.bfloat16)
    d_output = product_rows(joined_self, grad_self_in)
    grad_mixed_self = split_heads(product_cols(grad_self_in, w_output).astype(jnp.bfloat16))
    grad_queries, d_table, grad_keys_full, grad_values_full = self_backward(
        query_heads,
        query_start,
        query_ids,
        table_full,
        key_blocks,
        value_blocks,
        id_blocks,
        key_starts,
        logsum_self,
        grad_mixed_self,
    )
    grad_query_self = grad_queries.astype(jnp.bfloat16)
    key_part, value_part = (
        lax.psum_scatter(
            grad_keys_full.astype(jnp.bfloat16), "shard", scatter_dimension=0, tiled=True
        ).astype(jnp.float32),
        lax.psum_scatter(
            grad_values_full.astype(jnp.bfloat16), "shard", scatter_dimension=0, tiled=True
        ).astype(jnp.float32),
    )
    grad_key_self = key_part.astype(jnp.bfloat16)
    grad_value_self = value_part.astype(jnp.bfloat16)
    d_query = product_rows(normed_self, grad_query_self)
    d_key = product_rows(normed_self, grad_key_self)
    d_value = product_rows(normed_self, grad_value_self)
    grad_normed_self = (
        product_cols(grad_query_self, w_query)
        + product_cols(grad_key_self, w_key)
        + product_cols(grad_value_self, w_value)
    )
    unused, pull = jax.vjp(rms_scale, source, gain_self)
    norm_part, d_self_gain = pull(grad_normed_self)
    grad_source = grad_self_total + norm_part
    summed = (
        lax.psum_scatter(
            d_query.astype(jnp.bfloat16), "shard", scatter_dimension=0, tiled=True
        ).astype(jnp.float32),
        lax.psum_scatter(
            d_key.astype(jnp.bfloat16), "shard", scatter_dimension=0, tiled=True
        ).astype(jnp.float32),
        lax.psum_scatter(
            d_value.astype(jnp.bfloat16), "shard", scatter_dimension=0, tiled=True
        ).astype(jnp.float32),
        lax.psum_scatter(
            d_output.astype(jnp.bfloat16), "shard", scatter_dimension=0, tiled=True
        ).astype(jnp.float32),
        lax.psum_scatter(
            d_c_query.astype(jnp.bfloat16), "shard", scatter_dimension=0, tiled=True
        ).astype(jnp.float32),
        lax.psum_scatter(
            d_c_key.astype(jnp.bfloat16), "shard", scatter_dimension=0, tiled=True
        ).astype(jnp.float32),
        lax.psum_scatter(
            d_c_value.astype(jnp.bfloat16), "shard", scatter_dimension=0, tiled=True
        ).astype(jnp.float32),
        lax.psum_scatter(
            d_c_output.astype(jnp.bfloat16), "shard", scatter_dimension=0, tiled=True
        ).astype(jnp.float32),
        lax.psum_scatter(
            d_gate.astype(jnp.bfloat16), "shard", scatter_dimension=0, tiled=True
        ).astype(jnp.float32),
        lax.psum_scatter(
            d_up.astype(jnp.bfloat16), "shard", scatter_dimension=0, tiled=True
        ).astype(jnp.float32),
        lax.psum_scatter(
            d_down.astype(jnp.bfloat16), "shard", scatter_dimension=0, tiled=True
        ).astype(jnp.float32),
        lax.psum_scatter(
            d_self_gain.astype(jnp.bfloat16), "shard", scatter_dimension=0, tiled=True
        ).astype(jnp.float32),
        lax.psum_scatter(
            d_cross_gain.astype(jnp.bfloat16), "shard", scatter_dimension=0, tiled=True
        ).astype(jnp.float32),
        lax.psum_scatter(
            d_feed_gain.astype(jnp.bfloat16), "shard", scatter_dimension=0, tiled=True
        ).astype(jnp.float32),
        lax.psum_scatter(
            d_table.astype(jnp.bfloat16), "shard", scatter_dimension=0, tiled=True
        ).astype(jnp.float32),
    )
    totals = (
        lax.psum(summed[0].astype(jnp.bfloat16), "rep").astype(jnp.float32),
        lax.psum(summed[1].astype(jnp.bfloat16), "rep").astype(jnp.float32),
        lax.psum(summed[2].astype(jnp.bfloat16), "rep").astype(jnp.float32),
        lax.psum(summed[3].astype(jnp.bfloat16), "rep").astype(jnp.float32),
        lax.psum(summed[4].astype(jnp.bfloat16), "rep").astype(jnp.float32),
        lax.psum(summed[5].astype(jnp.bfloat16), "rep").astype(jnp.float32),
        lax.psum(summed[6].astype(jnp.bfloat16), "rep").astype(jnp.float32),
        lax.psum(summed[7].astype(jnp.bfloat16), "rep").astype(jnp.float32),
        lax.psum(summed[8].astype(jnp.bfloat16), "rep").astype(jnp.float32),
        lax.psum(summed[9].astype(jnp.bfloat16), "rep").astype(jnp.float32),
        lax.psum(summed[10].astype(jnp.bfloat16), "rep").astype(jnp.float32),
        lax.psum(summed[11].astype(jnp.bfloat16), "rep").astype(jnp.float32),
        lax.psum(summed[12].astype(jnp.bfloat16), "rep").astype(jnp.float32),
        lax.psum(summed[13].astype(jnp.bfloat16), "rep").astype(jnp.float32),
        lax.psum(summed[14].astype(jnp.bfloat16), "rep").astype(jnp.float32),
    )
    return (
        outcome.astype(jnp.bfloat16)[None],
        grad_source[None],
        grad_memory[None],
        totals[0],
        totals[1],
        totals[2],
        totals[3],
        totals[4],
        totals[5],
        totals[6],
        totals[7],
        totals[8],
        totals[9],
        totals[10],
        totals[11],
        totals[12],
        totals[13],
        totals[14],
    )


def swap(value, axis, size, step):
    return lax.ppermute(value, axis, [(place, place ^ step) for place in range(size)])


def after(value, *others):
    return lax.optimization_barrier((value, *others))[0]


def spread_columns(weight, count):
    rows = weight.shape[0]
    return weight.reshape(rows, count, -1).transpose(1, 0, 2)


def place_blocks(own, received, index, axis=0):
    stacked = jnp.zeros(own.shape[:axis] + (len(received) + 1,) + own.shape[axis:], own.dtype)
    stacked = lax.dynamic_update_index_in_dim(stacked, own, index, axis)
    for step, block in received:
        stacked = lax.dynamic_update_index_in_dim(stacked, block, index ^ step, axis)
    return stacked


def exchange(blocks, index, axis, size, unit=1):
    received = []
    for number in range(1, size):
        step = number * unit
        part = lax.dynamic_index_in_dim(blocks, index ^ number, 0, keepdims=False)
        received.append((number, swap(part, axis, size * unit, step)))
    own = lax.dynamic_index_in_dim(blocks, index, 0, keepdims=False)
    return own, received


def gather_rows(value, index):
    far = swap(value, "shard", 4, 2)
    near = swap(value, "shard", 4, 1)
    last = swap(far, "shard", 4, 1)
    stacked = place_blocks(value, [(1, near), (2, far), (3, last)], index)
    return stacked.reshape((-1,) + value.shape[1:])


def halves_sum(partial, index):
    core = index & 1
    view = partial.reshape((2, 2, -1) + partial.shape[1:])
    mine = lax.dynamic_index_in_dim(view, core, 1, keepdims=False)
    other = lax.dynamic_index_in_dim(view, 1 - core, 1, keepdims=False)
    arrived = swap(other.astype(jnp.bfloat16), "shard", 4, 1)
    return mine + arrived.astype(jnp.float32)


def sum_all(partial, index):
    pair = halves_sum(partial, index).astype(jnp.bfloat16)
    far = swap(pair, "shard", 4, 2)
    total = (pair.astype(jnp.float32) + far.astype(jnp.float32)).astype(jnp.bfloat16)
    near = swap(total, "shard", 4, 1)
    stacked = place_blocks(total, [(1, near)], index & 1, axis=1)
    return stacked.reshape(partial.shape).astype(jnp.float32)


def sum_scatter(partial, index):
    chip = index >> 1
    pair = halves_sum(partial, index)
    mine = lax.dynamic_index_in_dim(pair, chip, 0, keepdims=False)
    other = lax.dynamic_index_in_dim(pair, 1 - chip, 0, keepdims=False)
    far = swap(other.astype(jnp.bfloat16), "shard", 4, 2)
    return mine + far.astype(jnp.float32)


def rep_scatter(chunks, rep, count):
    depth = count // 2
    view = chunks.reshape((depth, 2) + chunks.shape[1:])
    column = rep & 1
    row = rep >> 1
    mine = lax.dynamic_index_in_dim(view, column, 1, keepdims=False)
    other = lax.dynamic_index_in_dim(view, 1 - column, 1, keepdims=False)
    arrived = swap(other.astype(jnp.bfloat16), "rep", count, 1)
    pair = mine.astype(jnp.float32) + arrived.astype(jnp.float32)
    low = pair.astype(jnp.bfloat16)
    own = lax.dynamic_index_in_dim(pair, row, 0, keepdims=False)
    for number in range(1, depth):
        part = lax.dynamic_index_in_dim(low, row ^ number, 0, keepdims=False)
        own = own + swap(part, "rep", count, number * 2).astype(jnp.float32)
    return own


def rep_gather(piece, rep, count):
    depth = count // 2
    column = rep & 1
    row = rep >> 1
    received = [
        (number, swap(piece, "rep", count, number * 2)) for number in range(1, depth)
    ]
    line = place_blocks(piece, received, row)
    arrived = swap(line, "rep", count, 1)
    stacked = place_blocks(line, [(1, arrived)], column, axis=1)
    return stacked.reshape((count,) + piece.shape)


def reduce_columns(gradient, index, rep, count):
    rows, width = gradient.shape
    small = rows // (4 * count)
    chunks = gradient.reshape(4, count, small, width).transpose(1, 0, 2, 3)
    piece = rep_scatter(chunks, rep, count).astype(jnp.bfloat16)
    own, received = exchange(piece, index, "shard", 4)
    return rep_gather(place_blocks(own, received, index), rep, count)


def unpack_columns(gathered, start, width):
    count, parts, small, unused = gathered.shape
    part = gathered[..., start : start + width]
    return part.transpose(0, 2, 1, 3).reshape(count * small, parts * width).astype(jnp.float32)


def reduce_rows(gradient, rep, count):
    rows, width = gradient.shape
    piece = rep_scatter(gradient.reshape(count, rows // count, width), rep, count)
    gathered = rep_gather(piece.astype(jnp.bfloat16), rep, count)
    return gathered.reshape(rows, width).astype(jnp.float32)


def sum_everywhere(vector, count):
    for step in (1, 2):
        vector = vector + swap(vector, "shard", 4, step)
    step = 1
    while step < count:
        vector = vector + swap(vector, "rep", count, step)
        step *= 2
    return vector


def run_kernel(name, body, ids, operands, results, scratch=()):
    whole = pl.BlockSpec(memory_space=pltpu.VMEM)
    return pl.pallas_call(
        body,
        out_shape=[jax.ShapeDtypeStruct(shape, kind) for shape, kind in results],
        in_specs=[pl.BlockSpec(memory_space=pltpu.SMEM)] + [whole] * len(operands),
        out_specs=[whole] * len(results),
        scratch_shapes=[pltpu.VMEM(shape, kind) for shape, kind in scratch],
        name=name,
    )(ids, *operands)


low_kind = jnp.bfloat16
full_kind = jnp.float32


def rows_at(place, size):
    return pl.ds(pl.multiple_of(place * size, size), size)


def put_blocks(index, blocks, target):
    size = blocks[0].shape[0]
    for step, block in enumerate(blocks):
        target[rows_at(index ^ step, size), :] = block[...]


def split_cores(index, partial, room, send, keep):
    core = index & 1
    size = send.shape[0]
    room[...] = partial
    keep[...] = room[rows_at(core, size), :]
    send[...] = room[rows_at(1 - core, size), :].astype(low_kind)


def join_cores(index, own, other, room):
    core = index & 1
    size = own.shape[0]
    room[rows_at(core, size), :] = own[...].astype(full_kind)
    room[rows_at(1 - core, size), :] = other[...].astype(full_kind)
    return room[...]


def inverse_rms(values):
    return lax.rsqrt(jnp.mean(values * values, axis=-1, keepdims=True) + epsilon)


def norm_backward(grad, values, gain):
    scale = inverse_rms(values)
    row = jnp.sum(grad * values * scale, axis=0, keepdims=True)
    scaled = grad * gain
    inner = jnp.mean(scaled * values, axis=-1, keepdims=True)
    return scale * scaled - values * (scale * scale * scale * inner), row


def bucket_rows(buckets, length):
    lanes = lax.broadcasted_iota(jnp.int32, (buckets, length), 1)
    distance = jnp.where(lanes == 0, 0, length - lanes)
    return (bucket_of(distance) == lax.broadcasted_iota(jnp.int32, (buckets, length), 0)).astype(
        full_kind
    )


def columns_body(ids, *refs):
    count = len(refs) - 4
    sources, targets = refs[:count], refs[count:]
    for place in range(4):

        @pl.when(ids[0] == place)
        def _():
            for step in range(4):
                start = 0
                for source in sources:
                    width = source.shape[1] // 4
                    begin = (place ^ step) * width
                    targets[step][:, start : start + width] = source[:, begin : begin + width]
                    start += width


def heads_of(matrix, number, part, wide):
    start = part * wide + number * HEAD_DIM
    return matrix[:, start : start + HEAD_DIM]


def softmax_rows(scores, allowed):
    scores = jnp.where(allowed, scores, masked_score)
    powers = jnp.exp(scores - jnp.max(scores, axis=-1, keepdims=True))
    return powers * (1.0 / jnp.sum(powers, axis=-1, keepdims=True))


def self_half(half, ids, source, weight, gains, rows, mapped_before, output, seg_col, seg_row, outs):
    normed_out, mapped_out, chances_out, mixed_out, send, keep, room = outs
    size = normed_out.shape[0]
    wide = output.shape[0]
    normed = (source * inverse_rms(source) * gains[0:1, :]).astype(low_kind)
    normed_out[...] = normed
    mapped = product(normed, weight).astype(low_kind)
    mapped_out[...] = mapped
    every = mapped if half == 0 else jnp.concatenate([mapped_before, mapped], axis=0)
    keys = every.shape[0]
    places = lax.broadcasted_iota(jnp.int32, (size, keys), 0) + half * size
    others = lax.broadcasted_iota(jnp.int32, (size, keys), 1)
    allowed = (places >= others) & (seg_col == seg_row[:, :keys])
    mixed = []
    for number in range(wide // HEAD_DIM):
        line = jnp.broadcast_to(rows[number : number + 1, :], (size, rows.shape[1]))
        bias = pltpu.roll(line, half * size, 1, stride=1, stride_axis=0)[:, :keys]
        scores = product_cols(heads_of(mapped, number, 0, wide), heads_of(every, number, 1, wide))
        chances = softmax_rows(scores + bias, allowed).astype(low_kind)
        chances_out[number] = chances
        mixed.append(product(chances, heads_of(every, number, 2, wide)))
    mixed = jnp.concatenate(mixed, axis=1).astype(low_kind)
    mixed_out[...] = mixed
    split_cores(ids[0], product(mixed, output), room, send, keep)


def self_first_body(
    ids, x0, x1, x2, x3, w0, w1, w2, w3, s0, s1, s2, s3, output, seg_col, seg_row,
    source_out, weight_out, gains_out, rows_out,
    normed_out, mapped_out, chances_out, mixed_out, send, keep,
    room, small, lines,
):
    index = ids[0]
    put_blocks(index, (x0, x1, x2, x3), source_out)
    put_blocks(index, (w0, w1, w2, w3), weight_out)
    put_blocks(index, (s0, s1, s2, s3), small)
    model = source_out.shape[1]
    part = model // 4
    for place in range(3):
        gains_out[place : place + 1, :] = jnp.concatenate(
            [small[16 * t : 16 * t + 1, part * place : part * (place + 1)] for t in range(4)],
            axis=1,
        )
    gains_out[3:8, :] = jnp.zeros((5, model), full_kind)
    table = jnp.concatenate([small[16 * t + 8 : 16 * t + 16, :128] for t in range(4)], axis=0)
    hot = bucket_rows(table.shape[0], rows_out.shape[1])
    lines[...] = product_rows(table.astype(low_kind), hot.astype(low_kind))
    heads_here = chances_out.shape[0]
    for number in range(heads_here):
        rows_out[number : number + 1, :] = lines[pl.ds(index * heads_here + number, 1), :]
    rows_out[heads_here:8, :] = jnp.zeros((8 - heads_here, rows_out.shape[1]), full_kind)
    size = normed_out.shape[0]
    self_half(
        0, ids, source_out[:size, :].astype(full_kind), weight_out[...], gains_out, rows_out, None,
        output[...], seg_col[:size, :], seg_row[...],
        (normed_out, mapped_out, chances_out, mixed_out, send, keep, room),
    )


def self_second_body(
    ids, source, weight, gains, rows, mapped_before, output, seg_col, seg_row,
    normed_out, mapped_out, chances_out, mixed_out, send, keep, room,
):
    size = normed_out.shape[0]
    self_half(
        1, ids, source[size:, :].astype(full_kind), weight[...], gains, rows, mapped_before[...],
        output[...], seg_col[size:, :], seg_row[...],
        (normed_out, mapped_out, chances_out, mixed_out, send, keep, room),
    )


def cross_keys_body(ids, e0, e1, e2, e3, w0, w1, w2, w3, memory_out, weight_out, mapped_out):
    put_blocks(ids[0], (e0, e1, e2, e3), memory_out)
    put_blocks(ids[0], (w0, w1, w2, w3), weight_out)
    wide = weight_out.shape[1] // 3
    mapped_out[...] = product(memory_out[...], weight_out[:, wide:]).astype(low_kind)


def cross_body(
    half, ids, source, own, other, gains, weight, mapped, output, seg_col, enc_row,
    after_out, normed_out, query_out, chances_out, mixed_out, send, keep, room,
):
    size = after_out.shape[0]
    wide = output.shape[0]
    start = half * size
    values = source[start : start + size, :].astype(full_kind) + join_cores(
        ids[0], own, other, room
    )
    after_out[...] = values
    normed = (values * inverse_rms(values) * gains[1:2, :]).astype(low_kind)
    normed_out[...] = normed
    query = product(normed, weight[:, :wide]).astype(low_kind)
    query_out[...] = query
    allowed = seg_col[start : start + size, :] == enc_row[...]
    every = mapped[...]
    mixed = []
    for number in range(wide // HEAD_DIM):
        scores = product_cols(heads_of(query, number, 0, wide), heads_of(every, number, 0, wide))
        chances = softmax_rows(scores, allowed).astype(low_kind)
        chances_out[number] = chances
        mixed.append(product(chances, heads_of(every, number, 1, wide)))
    mixed = jnp.concatenate(mixed, axis=1).astype(low_kind)
    mixed_out[...] = mixed
    split_cores(ids[0], product(mixed, output[...]), room, send, keep)


def feed_join_body(ids, w0, w1, w2, w3, g0, g1, g2, g3, weight_out, grad_out):
    put_blocks(ids[0], (w0, w1, w2, w3), weight_out)
    put_blocks(ids[0], (g0, g1, g2, g3), grad_out)


def feed_body(
    half, ids, before, own, other, gains, weight, down, grad_out,
    after_out, normed_out, hidden_out, acts_out, out_send, out_keep, send, keep, room,
):
    size = after_out.shape[0]
    start = half * size
    units = down.shape[0]
    values = before[...] + join_cores(ids[0], own, other, room)
    after_out[...] = values
    normed = (values * inverse_rms(values) * gains[2:3, :]).astype(low_kind)
    normed_out[...] = normed
    acts = product(normed, weight[...])
    gate, up = acts[:, :units], acts[:, units:]
    root = math.sqrt(2 / math.pi)
    square = gate * gate
    bend = jnp.tanh(root * gate * (1.0 + 0.044715 * square))
    curve = 0.5 * gate * (1.0 + bend)
    slope = 0.5 * (1.0 + bend) + 0.5 * gate * (1.0 - bend * bend) * root * (
        1.0 + 3 * 0.044715 * square
    )
    hidden = (curve * up).astype(low_kind)
    hidden_out[...] = hidden
    grad_hidden = product_cols(grad_out[start : start + size, :], down[...])
    acts_out[:, :units] = (grad_hidden * up * slope).astype(low_kind)
    acts_out[:, units:] = (grad_hidden * curve).astype(low_kind)
    split_cores(ids[0], product_cols(acts_out[...], weight[...]), room, send, keep)
    split_cores(ids[0], product(hidden, down[...]), room, out_send, out_keep)


def feed_weights_body(ids, normed0, normed1, acts0, acts1, hidden0, hidden1, grad_out, feed, down):
    size = normed0.shape[0]
    feed[...] = (
        product_rows(normed0[...], acts0[...]) + product_rows(normed1[...], acts1[...])
    ).astype(low_kind)
    down[...] = (
        product_rows(hidden0[...], grad_out[:size, :])
        + product_rows(hidden1[...], grad_out[size:, :])
    ).astype(low_kind)


def attention_backward(half, grads, query, keys, values, chances, grad_query, sums):
    everything = []
    heads_here = chances.shape[0]
    wide = heads_here * HEAD_DIM
    for number in range(heads_here):
        grad = heads_of(grads, number, 0, wide)
        key, value = heads_of(keys, number, 0, wide), heads_of(values, number, 0, wide)
        low = chances[number]
        full = low.astype(full_kind)
        grad_chances = product_cols(grad, value)
        grad_scores = full * (
            grad_chances - jnp.sum(full * grad_chances, axis=-1, keepdims=True)
        )
        rounded = grad_scores.astype(low_kind)
        start = number * HEAD_DIM
        grad_query[:, start : start + HEAD_DIM] = product(rounded, key).astype(low_kind)
        sums.append(
            (product_rows(rounded, heads_of(query, number, 0, wide)), product_rows(low, grad))
        )
        everything.append(grad_scores)
    return everything


def joined_sums(sums):
    return jnp.concatenate([pair[0] for pair in sums] + [pair[1] for pair in sums], axis=1)


def cross_back_body(
    half, ids, grad_out, own, other, values, gains, output, query, chances, mapped, weight, *refs,
):
    before = refs[:2] if half else ()
    total_out, low_out, query_out, sums_out, row_out, send, keep, room = refs[len(before) :]
    size = total_out.shape[0]
    wide = output.shape[0]
    start = half * size
    grad, row = norm_backward(join_cores(ids[0], own, other, room), values[...], gains[2:3, :])
    total = grad_out[start : start + size, :].astype(full_kind) + grad
    total_out[...] = total
    low = total.astype(low_kind)
    low_out[...] = low
    grad_mixed = product_cols(low, output[...]).astype(low_kind)
    every = mapped[...]
    sums = []
    attention_backward(
        half, grad_mixed, query[...], every[:, :wide], every[:, wide:], chances, query_out, sums
    )
    sums = joined_sums(sums)
    if half:
        sums_out[...] = (sums + before[0][...]).astype(low_kind)
        row_out[...] = jnp.broadcast_to(row + before[1][0:1, :], row_out.shape)
    else:
        sums_out[...] = sums
        row_out[...] = jnp.broadcast_to(row, row_out.shape)
    split_cores(ids[0], product_cols(query_out[...], weight[:, :wide]), room, send, keep)


def cross_weights_body(
    ids, normed0, normed1, query0, query1, memory, sums, mixed0, mixed1, low0, low1, weight,
    cross, output, send, keep, room,
):
    wide = query0.shape[1]
    cross[:, :wide] = (
        product_rows(normed0[...], query0[...]) + product_rows(normed1[...], query1[...])
    ).astype(low_kind)
    cross[:, wide:] = product_rows(memory[...], sums[...]).astype(low_kind)
    output[...] = (
        product_rows(mixed0[...], low0[...]) + product_rows(mixed1[...], low1[...])
    ).astype(low_kind)
    scatter_cores(ids[0], product_cols(sums[...], weight[:, wide:]), room, send, keep)


def scatter_cores(index, partial, room, send, keep):
    core = index & 1
    size = send.shape[1]
    room[...] = partial
    for chip in range(2):
        keep[chip] = room[rows_at(core + 2 * chip, size), :]
        send[chip] = room[rows_at(1 - core + 2 * chip, size), :].astype(low_kind)


def diagonal_sums(matrix):
    width = matrix.shape[1]
    size = matrix.shape[0]
    while size > 1:
        size //= 2
        matrix = matrix[:size] + pltpu.roll(matrix[size:], width - size, 1)
    return matrix


def self_back_body(
    half, ids, total, own, other, values, gains, output, mapped0, mapped1, chances, *refs,
):
    before = refs[:3] if half else ()
    total_out, low_out, query_out, sums_out, row_out, table_out, room = refs[len(before) :]
    size = total_out.shape[0]
    wide = output.shape[0]
    grad, row = norm_backward(join_cores(ids[0], own, other, room), values[...], gains[1:2, :])
    new_total = total[...] + grad
    total_out[...] = new_total
    low = new_total.astype(low_kind)
    low_out[...] = low
    grad_mixed = product_cols(low, output[...]).astype(low_kind)
    mapped = mapped1[...] if half else mapped0[...]
    every = jnp.concatenate([mapped0[...], mapped], axis=0) if half else mapped
    sums = []
    everything = attention_backward(
        half, grad_mixed, mapped[:, :wide], every[:, wide : 2 * wide], every[:, 2 * wide :],
        chances, query_out, sums,
    )
    sums = joined_sums(sums)
    length = 2 * size
    buckets = table_out.shape[0]
    hot = bucket_rows(buckets, length)
    columns = []
    for grad_scores in everything:
        if half == 0:
            grad_scores = jnp.concatenate(
                [grad_scores, jnp.zeros((size, length - size), full_kind)], axis=1
            )
        line = diagonal_sums(grad_scores)
        if half:
            line = pltpu.roll(line, length - size, 1)
        columns.append(jnp.sum(hot * line, axis=1, keepdims=True))
    columns.append(jnp.zeros((buckets, 128 - len(columns)), full_kind))
    table = jnp.concatenate(columns, axis=1)
    if half:
        sums_out[:size, :] = (sums[:size] + before[0][...]).astype(low_kind)
        sums_out[size:, :] = sums[size:].astype(low_kind)
        row_out[...] = jnp.broadcast_to(row + before[1][0:1, :], row_out.shape)
        table_out[...] = table + before[2][...]
    else:
        sums_out[...] = sums
        row_out[...] = jnp.broadcast_to(row, row_out.shape)
        table_out[...] = table


def self_weights_body(
    ids, normed0, normed1, query0, query1, sums, mixed0, mixed1, low0, low1, weight,
    gradient, output, send, keep, room, merged,
):
    size, wide = query0.shape
    merged[:size, :wide] = query0[...]
    merged[size:, :wide] = query1[...]
    merged[:, wide:] = sums[...]
    gradient[...] = (
        product_rows(normed0[...], merged[:size, :]) + product_rows(normed1[...], merged[size:, :])
    ).astype(low_kind)
    output[...] = (
        product_rows(mixed0[...], low0[...]) + product_rows(mixed1[...], low1[...])
    ).astype(low_kind)
    scatter_cores(ids[0], product_cols(merged[...], weight[...]), room, send, keep)


def finish_body(ids, source, mine, far, gains, total0, total1, grad_out, row_out):
    index = ids[0]
    size = source.shape[0]
    grad, row = norm_backward(
        mine[...] + far[...].astype(full_kind), source[...].astype(full_kind), gains[0:1, :]
    )
    row_out[...] = jnp.broadcast_to(row, row_out.shape)

    @pl.when(index < 2)
    def _():
        grad_out[...] = total0[rows_at(index & 1, size), :] + grad

    @pl.when(index >= 2)
    def _():
        grad_out[...] = total1[rows_at(index & 1, size), :] + grad


def chip_pair_body(ids, keep, arrived, mine, other):
    chip = ids[0] >> 1
    mine[...] = keep[chip] + arrived[chip].astype(full_kind)
    other[...] = (keep[1 - chip] + arrived[1 - chip].astype(full_kind)).astype(low_kind)


def scatter_pair(ids, send, keep):
    arrived = swap(send, "shard", 4, 1)
    shape = keep.shape[1:]
    mine, other = run_kernel(
        "chip_pair", chip_pair_body, ids, (keep, arrived), [(shape, full_kind), (shape, low_kind)]
    )
    return mine, swap(other, "shard", 4, 2)


def sum_half(send, keep):
    arrived = swap(send, "shard", 4, 1)
    pair = (keep + arrived.astype(full_kind)).astype(low_kind)
    far = swap(pair, "shard", 4, 2)
    total = (pair.astype(full_kind) + far.astype(full_kind)).astype(low_kind)
    return total, swap(total, "shard", 4, 1)


def split_shards(
    count,
    inputs,
    encoder,
    segments,
    enc_segments,
    self_query,
    self_key,
    self_value,
    self_output,
    cross_query,
    cross_key,
    cross_value,
    cross_output,
    gate_weight,
    up_weight,
    down_weight,
    self_gain,
    cross_gain,
    feed_gain,
    bias_table,
    cotangent,
):
    index = lax.axis_index("shard")
    rep = lax.axis_index("rep")
    ids = jnp.stack([index, rep])
    tokens_here, model = inputs.shape[1:]
    length = 4 * tokens_here
    half_size = 2 * tokens_here
    heads_here = HEADS // 4
    wide = heads_here * HEAD_DIM
    units = down_weight.shape[0]
    memory_length = enc_segments.shape[1]
    small_rows = bias_table.shape[0]
    buckets = 4 * small_rows
    part = self_gain.shape[0]

    def blocks_of(*weights):
        width = sum(weight.shape[1] for weight in weights) // 4
        shape = (weights[0].shape[0], width)
        return run_kernel("columns", columns_body, ids, weights, [(shape, low_kind)] * 4)

    def traded(blocks):
        return [blocks[0]] + [swap(blocks[step], "shard", 4, step) for step in range(1, 4)]

    def spread(value):
        far = swap(value, "shard", 4, 2)
        return [value, swap(value, "shard", 4, 1), far, swap(far, "shard", 4, 1)]

    small = jnp.zeros((16, model), full_kind)
    small = small.at[0, : 3 * part].set(
        jnp.concatenate([self_gain, cross_gain, feed_gain]).astype(full_kind)
    )
    small = small.at[8 : 8 + small_rows, :HEADS].set(bias_table.astype(full_kind))
    source_blocks = spread(inputs[0])
    small_blocks = spread(small)
    self_blocks = traded(blocks_of(self_query, self_key, self_value))
    memory_blocks = spread(after(encoder[0], self_blocks[2], self_blocks[3]))
    cross_blocks = blocks_of(cross_query, cross_key, cross_value)
    cross_blocks = traded(after(tuple(cross_blocks), self_blocks[2], self_blocks[3]))
    feed_blocks = blocks_of(gate_weight, up_weight)
    feed_blocks = traded(after(tuple(feed_blocks), cross_blocks[2], cross_blocks[3]))
    grad_blocks = spread(after(cotangent[0], cross_blocks[2], cross_blocks[3]))

    seg_row = segments
    seg_col = segments[0][:, None]
    enc_row = enc_segments

    room = [((half_size, model), full_kind)]
    pieces = [((tokens_here, model), low_kind), ((tokens_here, model), full_kind)]

    def self_results(keys):
        return [
            ((half_size, model), low_kind),
            ((half_size, 3 * wide), low_kind),
            ((heads_here, half_size, keys), low_kind),
            ((half_size, wide), low_kind),
        ] + pieces

    source, w_self, gains, rows, *first = run_kernel(
        "self_first",
        self_first_body,
        ids,
        (*source_blocks, *self_blocks, *small_blocks, self_output, seg_col, seg_row),
        [
            ((length, model), low_kind),
            ((model, 3 * wide), low_kind),
            ((8, model), full_kind),
            ((8, length), full_kind),
        ]
        + self_results(half_size),
        room + [((64, model), full_kind), ((128, length), full_kind)],
    )
    second = run_kernel(
        "self_second",
        self_second_body,
        ids,
        (source, w_self, gains, rows, first[1], self_output, seg_col, seg_row),
        self_results(length),
        room,
    )
    self_parts = (first, second)
    memory, w_cross, cross_mapped = run_kernel(
        "cross_keys",
        cross_keys_body,
        ids,
        (*memory_blocks, *cross_blocks),
        [
            ((memory_length, model), low_kind),
            ((model, 3 * wide), low_kind),
            ((memory_length, 2 * wide), low_kind),
        ],
    )
    w_feed, grad_out = run_kernel(
        "feed_join",
        feed_join_body,
        ids,
        (*feed_blocks, *grad_blocks),
        [((model, 2 * units), low_kind), ((length, model), low_kind)],
    )

    cross_parts = []
    for half in range(2):
        own, other = sum_half(*self_parts[half][4:])
        cross_parts.append(
            run_kernel(
                "cross",
                functools.partial(cross_body, half),
                ids,
                (source, own, other, gains, w_cross, cross_mapped, cross_output, seg_col, enc_row),
                [
                    ((half_size, model), full_kind),
                    ((half_size, model), low_kind),
                    ((half_size, wide), low_kind),
                    ((heads_here, half_size, memory_length), low_kind),
                    ((half_size, wide), low_kind),
                ]
                + pieces,
                room,
            )
        )
    feed_parts = []
    for half in range(2):
        own, other = sum_half(*cross_parts[half][5:])
        feed_parts.append(
            run_kernel(
                "feed",
                functools.partial(feed_body, half),
                ids,
                (cross_parts[half][0], own, other, gains, w_feed, down_weight, grad_out),
                [
                    ((half_size, model), full_kind),
                    ((half_size, model), low_kind),
                    ((half_size, units), low_kind),
                    ((half_size, 2 * units), low_kind),
                ]
                + pieces
                + pieces,
                room,
            )
        )
    d_feed, d_down = run_kernel(
        "feed_weights",
        feed_weights_body,
        ids,
        (
            feed_parts[0][1], feed_parts[1][1], feed_parts[0][3], feed_parts[1][3],
            feed_parts[0][2], feed_parts[1][2], grad_out,
        ),
        [((model, 2 * units), low_kind), ((units, model), low_kind)],
    )
    back_parts = []
    for half in range(2):
        own, other = sum_half(*feed_parts[half][6:])
        before = (back_parts[0][3], back_parts[0][4]) if half else ()
        back_parts.append(
            run_kernel(
                "cross_back",
                functools.partial(cross_back_body, half),
                ids,
                (
                    grad_out, own, other, feed_parts[half][0], gains, cross_output,
                    cross_parts[half][2], cross_parts[half][3], cross_mapped, w_cross,
                )
                + before,
                [
                    ((half_size, model), full_kind),
                    ((half_size, model), low_kind),
                    ((half_size, wide), low_kind),
                    ((memory_length, 2 * wide), low_kind if half else full_kind),
                    ((8, model), full_kind),
                ]
                + pieces,
                room,
            )
        )
    two_pieces = [((2,) + shape, kind) for shape, kind in pieces]
    whole_room = [((length, model), full_kind)]
    d_cross, d_c_output, send, keep = run_kernel(
        "cross_weights",
        cross_weights_body,
        ids,
        (
            cross_parts[0][1], cross_parts[1][1], back_parts[0][2], back_parts[1][2], memory,
            back_parts[1][3], cross_parts[0][4], cross_parts[1][4], back_parts[0][1],
            back_parts[1][1], w_cross,
        ),
        [((model, 3 * wide), low_kind), ((wide, model), low_kind)] + two_pieces,
        whole_room,
    )
    mine, far = scatter_pair(ids, send, keep)
    grad_memory = mine + far.astype(full_kind)
    last_parts = []
    for half in range(2):
        own, other = sum_half(*back_parts[half][5:])
        before = tuple(last_parts[0][3:6]) if half else ()
        keys = length if half else half_size
        last_parts.append(
            run_kernel(
                "self_back",
                functools.partial(self_back_body, half),
                ids,
                (
                    back_parts[half][0], own, other, cross_parts[half][0], gains, self_output,
                    first[1], second[1], self_parts[half][2],
                )
                + before,
                [
                    ((half_size, model), full_kind),
                    ((half_size, model), low_kind),
                    ((half_size, wide), low_kind),
                    ((keys, 2 * wide), low_kind if half else full_kind),
                    ((8, model), full_kind),
                    ((buckets, 128), full_kind),
                ],
                room,
            )
        )
    d_self, d_output, send, keep = run_kernel(
        "self_weights",
        self_weights_body,
        ids,
        (
            first[0], second[0], last_parts[0][2], last_parts[1][2], last_parts[1][3], first[3],
            second[3], last_parts[0][1], last_parts[1][1], w_self,
        ),
        [((model, 3 * wide), low_kind), ((wide, model), low_kind)] + two_pieces,
        whole_room + [((length, 3 * wide), low_kind)],
    )
    mine, far = scatter_pair(ids, send, keep)
    grad_source, self_row = run_kernel(
        "finish",
        finish_body,
        ids,
        (inputs[0], mine, far, gains, last_parts[0][0], last_parts[1][0]),
        [((tokens_here, model), full_kind), ((8, model), full_kind)],
    )

    out_send = jnp.stack([feed_parts[0][4], feed_parts[1][4]])
    out_keep = jnp.stack([feed_parts[0][5], feed_parts[1][5]])
    mine, far = scatter_pair(ids, out_send, out_keep)
    own_after = lax.dynamic_slice_in_dim(
        jnp.where(index < 2, feed_parts[0][0], feed_parts[1][0]), (index & 1) * tokens_here, tokens_here
    )
    outcome = own_after + mine + far.astype(full_kind)

    d_table = last_parts[1][5][:, :heads_here]

    def only_here(gradient):
        own = lax.dynamic_slice_in_dim(gradient, index * part, part)
        return lax.dynamic_update_slice_in_dim(jnp.zeros_like(gradient), own, index * part, 0)

    table_sparse = lax.dynamic_update_slice_in_dim(
        jnp.zeros((buckets, HEADS), full_kind), d_table, index * heads_here, 1
    )
    vector = jnp.concatenate(
        [
            self_row[0],
            only_here(last_parts[1][4][0]),
            only_here(back_parts[1][4][0]),
            table_sparse.reshape(-1),
        ]
    )
    vector = sum_everywhere(vector, count)
    gains_sum = vector[: 3 * model].reshape(3, model)
    gains_here = lax.dynamic_slice_in_dim(gains_sum, index * part, part, 1)
    table_grad = lax.dynamic_slice_in_dim(
        vector[3 * model :].reshape(-1, HEADS), index * small_rows, small_rows
    )
    feed_sum = reduce_columns(d_feed, index, rep, count)
    down_sum = reduce_rows(d_down, rep, count)
    cross_sum = reduce_columns(d_cross, index, rep, count)
    c_output_sum = reduce_rows(d_c_output, rep, count)
    output_sum = reduce_rows(d_output, rep, count)
    self_sum = reduce_columns(d_self, index, rep, count)
    return (
        outcome.astype(jnp.bfloat16)[None],
        grad_source[None],
        grad_memory[None],
        unpack_columns(self_sum, 0, wide),
        unpack_columns(self_sum, wide, wide),
        unpack_columns(self_sum, 2 * wide, wide),
        output_sum,
        unpack_columns(cross_sum, 0, wide),
        unpack_columns(cross_sum, wide, wide),
        unpack_columns(cross_sum, 2 * wide, wide),
        c_output_sum,
        unpack_columns(feed_sum, 0, units),
        unpack_columns(feed_sum, units, units),
        down_sum,
        gains_here[0],
        gains_here[1],
        gains_here[2],
        table_grad,
    )


def solution(mesh):
    in_specs = (
        P("rep", "shard", None),
        P("rep", "shard", None),
        P("rep", None),
        P("rep", None),
        P("shard", None),
        P("shard", None),
        P("shard", None),
        P("shard", None),
        P("shard", None),
        P("shard", None),
        P("shard", None),
        P("shard", None),
        P("shard", None),
        P("shard", None),
        P("shard", None),
        P("shard"),
        P("shard"),
        P("shard"),
        P("shard", None),
        P("rep", "shard", None),
    )
    out_specs = (
        P("rep", "shard", None),
        P("rep", "shard", None),
        P("rep", "shard", None),
        P("shard", None),
        P("shard", None),
        P("shard", None),
        P("shard", None),
        P("shard", None),
        P("shard", None),
        P("shard", None),
        P("shard", None),
        P("shard", None),
        P("shard", None),
        P("shard", None),
        P("shard"),
        P("shard"),
        P("shard"),
        P("shard", None),
    )
    count = mesh.shape["rep"]
    split = mesh.shape["shard"] == 4 and count >= 2 and count & (count - 1) == 0
    body = functools.partial(split_shards, count) if split else shards
    return jax.shard_map(body, mesh=mesh, in_specs=in_specs, out_specs=out_specs, check_vma=False)
```

```python
import functools
import math

import jax
import jax.numpy as jnp
from jax import lax
from jax.experimental import pallas as pl
from jax.experimental.pallas import tpu as pltpu
from jax.sharding import PartitionSpec as P

HEADS = 12
HEAD_DIM = 64


bucket_edges = [math.ceil(16 * 8 ** (number / 16)) for number in range(1, 16)]
epsilon = 1e-06
masked_score = -1000000000.0


def bucket_of(distance):
    far_part = sum(((distance >= border).astype(jnp.int32) for border in bucket_edges))
    return jnp.where(distance < 16, distance, 16 + far_part)


def rms_scale(values, scales):
    return values * lax.rsqrt(jnp.mean(values * values, axis=-1, keepdims=True) + epsilon) * scales


def product(former, latter):
    return jnp.dot(former, latter, preferred_element_type=jnp.float32)


def product_rows(former, latter):
    return lax.dot_general(
        former, latter, (((0,), (0,)), ((), ())), preferred_element_type=jnp.float32
    )


def product_cols(former, latter):
    return lax.dot_general(
        former, latter, (((1,), (1,)), ((), ())), preferred_element_type=jnp.float32
    )


def split_heads(matrix):
    return matrix.reshape(matrix.shape[0], HEADS, HEAD_DIM).transpose(1, 0, 2)


def join_heads(stacked):
    return stacked.transpose(1, 0, 2).reshape(stacked.shape[1], HEADS * HEAD_DIM)


def to_blocks(matrix, block_count):
    return matrix.reshape(block_count, -1, HEADS, HEAD_DIM).transpose(0, 2, 1, 3)


def from_blocks(stacked):
    return stacked.transpose(0, 2, 1, 3).reshape(-1, HEADS * HEAD_DIM)


def self_scores(queries, query_start, query_ids, table_full, key_rows, key_start, key_ids):
    query_count = queries.shape[1]
    key_count = key_rows.shape[1]
    query_places = query_start + jnp.arange(query_count, dtype=jnp.int32)
    key_places = key_start + jnp.arange(key_count, dtype=jnp.int32)
    buckets = bucket_of(jnp.maximum(query_places[:, None] - key_places[None, :], 0))
    one_hot = (
        buckets.reshape(1, -1) == jnp.arange(table_full.shape[0], dtype=jnp.int32)[:, None]
    ).astype(jnp.bfloat16)
    bias_block = jnp.einsum(
        "bn,bh->hn", one_hot, table_full, preferred_element_type=jnp.float32
    ).reshape(HEADS, query_count, key_count)
    scores = (
        jnp.einsum("hqd,hkd->hqk", queries, key_rows, preferred_element_type=jnp.float32)
        + bias_block
    )
    allowed = (query_places[:, None] >= key_places[None, :]) & (
        query_ids[:, None] == key_ids[None, :]
    )
    return (jnp.where(allowed[None], scores, masked_score), one_hot)


def self_logsum(queries, query_start, query_ids, table_full, key_blocks, id_blocks, key_starts):
    query_count = queries.shape[1]

    def advance(running, packed):
        largest, totals = running
        key_rows, key_ids, key_start = packed
        scores, unused = self_scores(
            queries, query_start, query_ids, table_full, key_rows, key_start, key_ids
        )
        newest = jnp.maximum(largest, jnp.max(scores, axis=-1, keepdims=True))
        totals = totals * jnp.exp(largest - newest) + jnp.sum(
            jnp.exp(scores - newest), axis=-1, keepdims=True
        )
        return ((newest, totals), None)

    initial = (
        jnp.full((HEADS, query_count, 1), -jnp.inf, jnp.float32),
        jnp.zeros((HEADS, query_count, 1), jnp.float32),
    )
    (largest, totals), unused = lax.scan(advance, initial, (key_blocks, id_blocks, key_starts))
    return largest + jnp.log(totals)


def self_mix(
    queries,
    query_start,
    query_ids,
    table_full,
    key_blocks,
    value_blocks,
    id_blocks,
    key_starts,
    logsum,
):

    def advance(accum, packed):
        key_rows, value_rows, key_ids, key_start = packed
        scores, unused = self_scores(
            queries, query_start, query_ids, table_full, key_rows, key_start, key_ids
        )
        weights = jnp.exp(scores - logsum).astype(jnp.bfloat16)
        return (
            accum
            + jnp.einsum("hqk,hkd->hqd", weights, value_rows, preferred_element_type=jnp.float32),
            None,
        )

    initial = jnp.zeros((HEADS, queries.shape[1], HEAD_DIM), jnp.float32)
    accum, unused = lax.scan(advance, initial, (key_blocks, value_blocks, id_blocks, key_starts))
    return accum


def self_backward(
    queries,
    query_start,
    query_ids,
    table_full,
    key_blocks,
    value_blocks,
    id_blocks,
    key_starts,
    logsum,
    grad_mixed,
):
    query_count = queries.shape[1]

    def dots(accum, packed):
        key_rows, value_rows, key_ids, key_start = packed
        scores, unused = self_scores(
            queries, query_start, query_ids, table_full, key_rows, key_start, key_ids
        )
        chances = jnp.exp(scores - logsum)
        grad_chances = jnp.einsum(
            "hqd,hkd->hqk", grad_mixed, value_rows, preferred_element_type=jnp.float32
        )
        return (accum + jnp.sum(chances * grad_chances, axis=-1, keepdims=True), None)

    row_dots, unused = lax.scan(
        dots,
        jnp.zeros((HEADS, query_count, 1), jnp.float32),
        (key_blocks, value_blocks, id_blocks, key_starts),
    )

    def advance(running, packed):
        grad_queries, grad_table = running
        key_rows, value_rows, key_ids, key_start = packed
        scores, one_hot = self_scores(
            queries, query_start, query_ids, table_full, key_rows, key_start, key_ids
        )
        chances = jnp.exp(scores - logsum)
        grad_chances = jnp.einsum(
            "hqd,hkd->hqk", grad_mixed, value_rows, preferred_element_type=jnp.float32
        )
        grad_scores = chances * (grad_chances - row_dots)
        rounded = grad_scores.astype(jnp.bfloat16)
        grad_values = jnp.einsum(
            "hqk,hqd->hkd",
            chances.astype(jnp.bfloat16),
            grad_mixed,
            preferred_element_type=jnp.float32,
        )
        grad_keys = jnp.einsum("hqk,hqd->hkd", rounded, queries, preferred_element_type=jnp.float32)
        grad_queries = grad_queries + jnp.einsum(
            "hqk,hkd->hqd", rounded, key_rows, preferred_element_type=jnp.float32
        )
        grad_table = grad_table + jnp.einsum(
            "bn,hn->bh",
            one_hot,
            grad_scores.reshape(HEADS, -1),
            precision=lax.Precision.HIGHEST,
            preferred_element_type=jnp.float32,
        )
        return ((grad_queries, grad_table), (grad_keys, grad_values))

    initial = (
        jnp.zeros((HEADS, query_count, HEAD_DIM), jnp.float32),
        jnp.zeros((table_full.shape[0], HEADS), jnp.float32),
    )
    (grad_queries, grad_table), (grad_keys, grad_values) = lax.scan(
        advance, initial, (key_blocks, value_blocks, id_blocks, key_starts)
    )
    return (join_heads(grad_queries), grad_table, from_blocks(grad_keys), from_blocks(grad_values))


def cross_forward(queries, key_heads, value_heads, allowed):
    scores = jnp.where(
        allowed,
        jnp.einsum("hqd,hkd->hqk", queries, key_heads, preferred_element_type=jnp.float32),
        masked_score,
    )
    largest = jnp.max(scores, axis=-1, keepdims=True)
    logsum = largest + jnp.log(jnp.sum(jnp.exp(scores - largest), axis=-1, keepdims=True))
    weights = jnp.exp(scores - logsum).astype(jnp.bfloat16)
    mixed = jnp.einsum("hqk,hkd->hqd", weights, value_heads, preferred_element_type=jnp.float32)
    return (mixed, logsum)


def cross_backward(queries, key_heads, value_heads, allowed, logsum, grad_mixed):
    scores = jnp.where(
        allowed,
        jnp.einsum("hqd,hkd->hqk", queries, key_heads, preferred_element_type=jnp.float32),
        masked_score,
    )
    chances = jnp.exp(scores - logsum)
    grad_values = jnp.einsum(
        "hqk,hqd->hkd", chances.astype(jnp.bfloat16), grad_mixed, preferred_element_type=jnp.float32
    )
    grad_chances = jnp.einsum(
        "hqd,hkd->hqk", grad_mixed, value_heads, preferred_element_type=jnp.float32
    )
    grad_scores = chances * (grad_chances - jnp.sum(chances * grad_chances, axis=-1, keepdims=True))
    rounded = grad_scores.astype(jnp.bfloat16)
    grad_queries = jnp.einsum(
        "hqk,hkd->hqd", rounded, key_heads, preferred_element_type=jnp.float32
    )
    grad_keys = jnp.einsum("hqk,hqd->hkd", rounded, queries, preferred_element_type=jnp.float32)
    return (join_heads(grad_queries), join_heads(grad_keys), join_heads(grad_values))


def shards(
    inputs,
    encoder,
    segments,
    enc_segments,
    self_query,
    self_key,
    self_value,
    self_output,
    cross_query,
    cross_key,
    cross_value,
    cross_output,
    gate_weight,
    up_weight,
    down_weight,
    self_gain,
    cross_gain,
    feed_gain,
    bias_table,
    cotangent,
):
    fetched = (
        lax.all_gather(self_query, "shard", axis=0, tiled=True),
        lax.all_gather(self_key, "shard", axis=0, tiled=True),
        lax.all_gather(self_value, "shard", axis=0, tiled=True),
        lax.all_gather(self_output, "shard", axis=0, tiled=True),
        lax.all_gather(cross_query, "shard", axis=0, tiled=True),
        lax.all_gather(cross_key, "shard", axis=0, tiled=True),
        lax.all_gather(cross_value, "shard", axis=0, tiled=True),
        lax.all_gather(cross_output, "shard", axis=0, tiled=True),
        lax.all_gather(gate_weight, "shard", axis=0, tiled=True),
        lax.all_gather(up_weight, "shard", axis=0, tiled=True),
        lax.all_gather(down_weight, "shard", axis=0, tiled=True),
        lax.all_gather(self_gain, "shard", axis=0, tiled=True),
        lax.all_gather(cross_gain, "shard", axis=0, tiled=True),
        lax.all_gather(feed_gain, "shard", axis=0, tiled=True),
        lax.all_gather(bias_table, "shard", axis=0, tiled=True),
    )
    (
        w_query,
        w_key,
        w_value,
        w_output,
        c_query,
        c_key,
        c_value,
        c_output,
        w_gate,
        w_up,
        w_down,
        g_self,
        g_cross,
        g_feed,
        table_full,
    ) = fetched
    gain_self = g_self.astype(jnp.float32)
    gain_cross = g_cross.astype(jnp.float32)
    gain_feed = g_feed.astype(jnp.float32)
    source = inputs[0].astype(jnp.float32)
    memory = encoder[0]
    segment_ids = segments[0]
    memory_ids = enc_segments[0]
    tokens_here = source.shape[0]
    length = segment_ids.shape[0]
    block_size = math.gcd(length, 512)
    block_count = length // block_size
    query_start = lax.axis_index("shard") * tokens_here
    query_ids = lax.dynamic_slice_in_dim(segment_ids, query_start, tokens_here)
    id_blocks = segment_ids.reshape(block_count, block_size)
    key_starts = jnp.arange(block_count, dtype=jnp.int32) * block_size
    cross_allowed = (query_ids[:, None] == memory_ids[None, :])[None]
    normed_self = rms_scale(source, gain_self).astype(jnp.bfloat16)
    query_heads = split_heads(product(normed_self, w_query).astype(jnp.bfloat16))
    key_local = product(normed_self, w_key).astype(jnp.bfloat16)
    value_local = product(normed_self, w_value).astype(jnp.bfloat16)
    keys_all, values_all = (
        lax.all_gather(key_local, "shard", axis=0, tiled=True),
        lax.all_gather(value_local, "shard", axis=0, tiled=True),
    )
    key_blocks = to_blocks(keys_all, block_count)
    value_blocks = to_blocks(values_all, block_count)
    logsum_self = self_logsum(
        query_heads, query_start, query_ids, table_full, key_blocks, id_blocks, key_starts
    )
    mixed_self = self_mix(
        query_heads,
        query_start,
        query_ids,
        table_full,
        key_blocks,
        value_blocks,
        id_blocks,
        key_starts,
        logsum_self,
    )
    joined_self = join_heads(mixed_self).astype(jnp.bfloat16)
    after_self = source + product(joined_self, w_output)
    normed_cross = rms_scale(after_self, gain_cross).astype(jnp.bfloat16)
    query_cross = split_heads(product(normed_cross, c_query).astype(jnp.bfloat16))
    key_cross_local = product(memory, c_key).astype(jnp.bfloat16)
    value_cross_local = product(memory, c_value).astype(jnp.bfloat16)
    keys_cross, values_cross = (
        lax.all_gather(key_cross_local, "shard", axis=0, tiled=True),
        lax.all_gather(value_cross_local, "shard", axis=0, tiled=True),
    )
    key_cross = split_heads(keys_cross)
    value_cross = split_heads(values_cross)
    mixed_cross, logsum_cross = cross_forward(query_cross, key_cross, value_cross, cross_allowed)
    joined_cross = join_heads(mixed_cross).astype(jnp.bfloat16)
    after_cross = after_self + product(joined_cross, c_output)
    normed_feed = rms_scale(after_cross, gain_feed).astype(jnp.bfloat16)
    gate_act = product(normed_feed, w_gate)
    up_act = product(normed_feed, w_up)
    hidden = (jax.nn.gelu(gate_act, approximate=True) * up_act).astype(jnp.bfloat16)
    outcome = after_cross + product(hidden, w_down)
    fetched = (
        lax.all_gather(self_query, "shard", axis=0, tiled=True),
        lax.all_gather(self_key, "shard", axis=0, tiled=True),
        lax.all_gather(self_value, "shard", axis=0, tiled=True),
        lax.all_gather(self_output, "shard", axis=0, tiled=True),
        lax.all_gather(cross_query, "shard", axis=0, tiled=True),
        lax.all_gather(cross_key, "shard", axis=0, tiled=True),
        lax.all_gather(cross_value, "shard", axis=0, tiled=True),
        lax.all_gather(cross_output, "shard", axis=0, tiled=True),
        lax.all_gather(gate_weight, "shard", axis=0, tiled=True),
        lax.all_gather(up_weight, "shard", axis=0, tiled=True),
        lax.all_gather(down_weight, "shard", axis=0, tiled=True),
        lax.all_gather(self_gain, "shard", axis=0, tiled=True),
        lax.all_gather(cross_gain, "shard", axis=0, tiled=True),
        lax.all_gather(feed_gain, "shard", axis=0, tiled=True),
        lax.all_gather(bias_table, "shard", axis=0, tiled=True),
    )
    (
        w_query,
        w_key,
        w_value,
        w_output,
        c_query,
        c_key,
        c_value,
        c_output,
        w_gate,
        w_up,
        w_down,
        g_self,
        g_cross,
        g_feed,
        table_full,
    ) = fetched
    gain_self = g_self.astype(jnp.float32)
    gain_cross = g_cross.astype(jnp.float32)
    gain_feed = g_feed.astype(jnp.float32)
    keys_all, values_all = (
        lax.all_gather(key_local, "shard", axis=0, tiled=True),
        lax.all_gather(value_local, "shard", axis=0, tiled=True),
    )
    key_blocks = to_blocks(keys_all, block_count)
    value_blocks = to_blocks(values_all, block_count)
    grad_out = cotangent[0].astype(jnp.float32)
    grad_down_in = cotangent[0]
    d_down = product_rows(hidden, grad_down_in)
    grad_hidden = product_cols(grad_down_in, w_down)

    def activation(gate_in, up_in):
        return jax.nn.gelu(gate_in, approximate=True) * up_in

    unused, pull = jax.vjp(activation, gate_act, up_act)
    grad_gate, grad_up = pull(grad_hidden)
    grad_gate = grad_gate.astype(jnp.bfloat16)
    grad_up = grad_up.astype(jnp.bfloat16)
    d_gate = product_rows(normed_feed, grad_gate)
    d_up = product_rows(normed_feed, grad_up)
    grad_normed_feed = product_cols(grad_gate, w_gate) + product_cols(grad_up, w_up)
    unused, pull = jax.vjp(rms_scale, after_cross, gain_feed)
    norm_part, d_feed_gain = pull(grad_normed_feed)
    grad_cross_total = grad_out + norm_part
    grad_cross_in = grad_cross_total.astype(jnp.bfloat16)
    d_c_output = product_rows(joined_cross, grad_cross_in)
    grad_mixed_cross = split_heads(product_cols(grad_cross_in, c_output).astype(jnp.bfloat16))
    grad_query_cross, grad_keys_cross, grad_values_cross = cross_backward(
        query_cross, key_cross, value_cross, cross_allowed, logsum_cross, grad_mixed_cross
    )
    grad_query_cross = grad_query_cross.astype(jnp.bfloat16)
    key_part, value_part = (
        lax.psum_scatter(
            grad_keys_cross.astype(jnp.bfloat16), "shard", scatter_dimension=0, tiled=True
        ).astype(jnp.float32),
        lax.psum_scatter(
            grad_values_cross.astype(jnp.bfloat16), "shard", scatter_dimension=0, tiled=True
        ).astype(jnp.float32),
    )
    grad_key_cross = key_part.astype(jnp.bfloat16)
    grad_value_cross = value_part.astype(jnp.bfloat16)
    d_c_query = product_rows(normed_cross, grad_query_cross)
    d_c_key = product_rows(memory, grad_key_cross)
    d_c_value = product_rows(memory, grad_value_cross)
    grad_memory = product_cols(grad_key_cross, c_key) + product_cols(grad_value_cross, c_value)
    grad_normed_cross = product_cols(grad_query_cross, c_query)
    unused, pull = jax.vjp(rms_scale, after_self, gain_cross)
    norm_part, d_cross_gain = pull(grad_normed_cross)
    grad_self_total = grad_cross_total + norm_part
    grad_self_in = grad_self_total.astype(jnp.bfloat16)
    d_output = product_rows(joined_self, grad_self_in)
    grad_mixed_self = split_heads(product_cols(grad_self_in, w_output).astype(jnp.bfloat16))
    grad_queries, d_table, grad_keys_full, grad_values_full = self_backward(
        query_heads,
        query_start,
        query_ids,
        table_full,
        key_blocks,
        value_blocks,
        id_blocks,
        key_starts,
        logsum_self,
        grad_mixed_self,
    )
    grad_query_self = grad_queries.astype(jnp.bfloat16)
    key_part, value_part = (
        lax.psum_scatter(
            grad_keys_full.astype(jnp.bfloat16), "shard", scatter_dimension=0, tiled=True
        ).astype(jnp.float32),
        lax.psum_scatter(
            grad_values_full.astype(jnp.bfloat16), "shard", scatter_dimension=0, tiled=True
        ).astype(jnp.float32),
    )
    grad_key_self = key_part.astype(jnp.bfloat16)
    grad_value_self = value_part.astype(jnp.bfloat16)
    d_query = product_rows(normed_self, grad_query_self)
    d_key = product_rows(normed_self, grad_key_self)
    d_value = product_rows(normed_self, grad_value_self)
    grad_normed_self = (
        product_cols(grad_query_self, w_query)
        + product_cols(grad_key_self, w_key)
        + product_cols(grad_value_self, w_value)
    )
    unused, pull = jax.vjp(rms_scale, source, gain_self)
    norm_part, d_self_gain = pull(grad_normed_self)
    grad_source = grad_self_total + norm_part
    summed = (
        lax.psum_scatter(
            d_query.astype(jnp.bfloat16), "shard", scatter_dimension=0, tiled=True
        ).astype(jnp.float32),
        lax.psum_scatter(
            d_key.astype(jnp.bfloat16), "shard", scatter_dimension=0, tiled=True
        ).astype(jnp.float32),
        lax.psum_scatter(
            d_value.astype(jnp.bfloat16), "shard", scatter_dimension=0, tiled=True
        ).astype(jnp.float32),
        lax.psum_scatter(
            d_output.astype(jnp.bfloat16), "shard", scatter_dimension=0, tiled=True
        ).astype(jnp.float32),
        lax.psum_scatter(
            d_c_query.astype(jnp.bfloat16), "shard", scatter_dimension=0, tiled=True
        ).astype(jnp.float32),
        lax.psum_scatter(
            d_c_key.astype(jnp.bfloat16), "shard", scatter_dimension=0, tiled=True
        ).astype(jnp.float32),
        lax.psum_scatter(
            d_c_value.astype(jnp.bfloat16), "shard", scatter_dimension=0, tiled=True
        ).astype(jnp.float32),
        lax.psum_scatter(
            d_c_output.astype(jnp.bfloat16), "shard", scatter_dimension=0, tiled=True
        ).astype(jnp.float32),
        lax.psum_scatter(
            d_gate.astype(jnp.bfloat16), "shard", scatter_dimension=0, tiled=True
        ).astype(jnp.float32),
        lax.psum_scatter(
            d_up.astype(jnp.bfloat16), "shard", scatter_dimension=0, tiled=True
        ).astype(jnp.float32),
        lax.psum_scatter(
            d_down.astype(jnp.bfloat16), "shard", scatter_dimension=0, tiled=True
        ).astype(jnp.float32),
        lax.psum_scatter(
            d_self_gain.astype(jnp.bfloat16), "shard", scatter_dimension=0, tiled=True
        ).astype(jnp.float32),
        lax.psum_scatter(
            d_cross_gain.astype(jnp.bfloat16), "shard", scatter_dimension=0, tiled=True
        ).astype(jnp.float32),
        lax.psum_scatter(
            d_feed_gain.astype(jnp.bfloat16), "shard", scatter_dimension=0, tiled=True
        ).astype(jnp.float32),
        lax.psum_scatter(
            d_table.astype(jnp.bfloat16), "shard", scatter_dimension=0, tiled=True
        ).astype(jnp.float32),
    )
    totals = (
        lax.psum(summed[0].astype(jnp.bfloat16), "rep").astype(jnp.float32),
        lax.psum(summed[1].astype(jnp.bfloat16), "rep").astype(jnp.float32),
        lax.psum(summed[2].astype(jnp.bfloat16), "rep").astype(jnp.float32),
        lax.psum(summed[3].astype(jnp.bfloat16), "rep").astype(jnp.float32),
        lax.psum(summed[4].astype(jnp.bfloat16), "rep").astype(jnp.float32),
        lax.psum(summed[5].astype(jnp.bfloat16), "rep").astype(jnp.float32),
        lax.psum(summed[6].astype(jnp.bfloat16), "rep").astype(jnp.float32),
        lax.psum(summed[7].astype(jnp.bfloat16), "rep").astype(jnp.float32),
        lax.psum(summed[8].astype(jnp.bfloat16), "rep").astype(jnp.float32),
        lax.psum(summed[9].astype(jnp.bfloat16), "rep").astype(jnp.float32),
        lax.psum(summed[10].astype(jnp.bfloat16), "rep").astype(jnp.float32),
        lax.psum(summed[11].astype(jnp.bfloat16), "rep").astype(jnp.float32),
        lax.psum(summed[12].astype(jnp.bfloat16), "rep").astype(jnp.float32),
        lax.psum(summed[13].astype(jnp.bfloat16), "rep").astype(jnp.float32),
        lax.psum(summed[14].astype(jnp.bfloat16), "rep").astype(jnp.float32),
    )
    return (
        outcome.astype(jnp.bfloat16)[None],
        grad_source[None],
        grad_memory[None],
        totals[0],
        totals[1],
        totals[2],
        totals[3],
        totals[4],
        totals[5],
        totals[6],
        totals[7],
        totals[8],
        totals[9],
        totals[10],
        totals[11],
        totals[12],
        totals[13],
        totals[14],
    )


def swap(value, axis, size, step):
    return lax.ppermute(value, axis, [(place, place ^ step) for place in range(size)])


def after(value, *others):
    return lax.optimization_barrier((value, *others))[0]


def run_kernel(name, body, ids, operands, results, scratch=()):
    whole = pl.BlockSpec(memory_space=pltpu.VMEM)
    return pl.pallas_call(
        body,
        out_shape=[jax.ShapeDtypeStruct(shape, kind) for shape, kind in results],
        in_specs=[pl.BlockSpec(memory_space=pltpu.SMEM)] + [whole] * len(operands),
        out_specs=[whole] * len(results),
        scratch_shapes=[pltpu.VMEM(shape, kind) for shape, kind in scratch],
        name=name,
    )(ids, *operands)


low_kind = jnp.bfloat16
full_kind = jnp.float32


def rows_at(place, size):
    return pl.ds(pl.multiple_of(place * size, size), size)


def put_blocks(index, blocks, target):
    size = blocks[0].shape[0]
    for step, block in enumerate(blocks):
        target[rows_at(index ^ step, size), :] = block[...]


def split_cores(index, partial, room, send, keep):
    core = index & 1
    size = send.shape[0]
    room[...] = partial
    keep[...] = room[rows_at(core, size), :]
    send[...] = room[rows_at(1 - core, size), :].astype(low_kind)


def join_cores(index, own, other, room):
    core = index & 1
    size = own.shape[0]
    room[rows_at(core, size), :] = own[...].astype(full_kind)
    room[rows_at(1 - core, size), :] = other[...].astype(full_kind)
    return room[...]


def inverse_rms(values):
    return lax.rsqrt(jnp.mean(values * values, axis=-1, keepdims=True) + epsilon)


def norm_backward(grad, values, gain):
    scale = inverse_rms(values)
    row = jnp.sum(grad * values * scale, axis=0, keepdims=True)
    scaled = grad * gain
    inner = jnp.mean(scaled * values, axis=-1, keepdims=True)
    return scale * scaled - values * (scale * scale * scale * inner), row


def bucket_rows(buckets, length):
    lanes = lax.broadcasted_iota(jnp.int32, (buckets, length), 1)
    distance = jnp.where(lanes == 0, 0, length - lanes)
    return (bucket_of(distance) == lax.broadcasted_iota(jnp.int32, (buckets, length), 0)).astype(
        full_kind
    )


def columns_body(ids, *refs):
    count = len(refs) - 4
    sources, targets = refs[:count], refs[count:]
    for place in range(4):

        @pl.when(ids[0] == place)
        def _():
            for step in range(4):
                start = 0
                for source in sources:
                    width = source.shape[1] // 4
                    begin = (place ^ step) * width
                    targets[step][:, start : start + width] = source[:, begin : begin + width]
                    start += width


def pack_body(ids, source, gain0, gain1, gain2, table, *refs):
    sources, packed, targets = refs[:3], refs[3], refs[4:]
    columns_body(ids, *sources, *targets)
    size, model = source.shape
    packed[:size, :] = source[...]
    rows = table.shape[0]
    line = [gain[...].astype(full_kind).reshape(1, -1) for gain in (gain0, gain1, gain2)]
    width = sum(piece.shape[1] for piece in line)
    line = jnp.concatenate(line + [jnp.zeros((1, model - width), full_kind)], axis=1)
    grid = jnp.concatenate(
        [table[...].astype(full_kind), jnp.zeros((rows, model - table.shape[1]), full_kind)], axis=1
    )
    lines = jnp.concatenate([line, jnp.zeros((7, model), full_kind), grid], axis=0)
    packed[size:, :] = lines.astype(low_kind)


def split_columns_body(ids, gate, up, own, send1, send2, send3):
    column = ids[1] & 1
    width = gate.shape[1] // 4
    half = send2.shape[0]
    for place in range(4):

        @pl.when(ids[0] == place)
        def _():
            for step, target in enumerate((own, send1, send2, send3)):
                begin = (place ^ step) * width
                rows = slice(None) if step < 2 else rows_at(column, half)
                for number, source in enumerate((gate, up)):
                    target[:, number * width : (number + 1) * width] = source[
                        rows, begin : begin + width
                    ]


def heads_of(matrix, number, part, wide):
    start = part * wide + number * HEAD_DIM
    return matrix[:, start : start + HEAD_DIM]


def softmax_rows(scores, allowed):
    scores = jnp.where(allowed, scores, masked_score)
    powers = jnp.exp(scores - jnp.max(scores, axis=-1, keepdims=True))
    return powers * (1.0 / jnp.sum(powers, axis=-1, keepdims=True))


def self_half(half, ids, source, weight, gains, rows, mapped_before, output, seg_col, seg_row, outs):
    normed_out, mapped_out, chances_out, mixed_out, send, keep, room = outs
    size = normed_out.shape[0]
    wide = output.shape[0]
    normed = (source * inverse_rms(source) * gains[0:1, :]).astype(low_kind)
    normed_out[...] = normed
    mapped = product(normed, weight).astype(low_kind)
    mapped_out[...] = mapped
    every = mapped if half == 0 else jnp.concatenate([mapped_before, mapped], axis=0)
    keys = every.shape[0]
    places = lax.broadcasted_iota(jnp.int32, (size, keys), 0) + half * size
    others = lax.broadcasted_iota(jnp.int32, (size, keys), 1)
    allowed = (places >= others) & (seg_col == seg_row[:, :keys])
    mixed = []
    for number in range(wide // HEAD_DIM):
        line = jnp.broadcast_to(rows[number : number + 1, :], (size, rows.shape[1]))
        bias = pltpu.roll(line, half * size, 1, stride=1, stride_axis=0)[:, :keys]
        scores = product_cols(heads_of(mapped, number, 0, wide), heads_of(every, number, 1, wide))
        chances = softmax_rows(scores + bias, allowed).astype(low_kind)
        chances_out[number] = chances
        mixed.append(product(chances, heads_of(every, number, 2, wide)))
    mixed = jnp.concatenate(mixed, axis=1).astype(low_kind)
    mixed_out[...] = mixed
    split_cores(ids[0], product(mixed, output), room, send, keep)


def self_first_body(
    ids, x0, x1, x2, x3, w0, w1, w2, w3, output, seg_col, seg_row,
    source_out, weight_out, gains_out, rows_out,
    normed_out, mapped_out, chances_out, mixed_out, send, keep,
    room, small, lines,
):
    index = ids[0]
    tokens = source_out.shape[0] // 4
    put_blocks(index, [block.at[:tokens] for block in (x0, x1, x2, x3)], source_out)
    put_blocks(index, (w0, w1, w2, w3), weight_out)
    for step, block in enumerate((x0, x1, x2, x3)):
        small[rows_at(index ^ step, 16), :] = block[tokens:, :].astype(full_kind)
    model = source_out.shape[1]
    part = model // 4
    for place in range(3):
        gains_out[place : place + 1, :] = jnp.concatenate(
            [small[16 * t : 16 * t + 1, part * place : part * (place + 1)] for t in range(4)],
            axis=1,
        )
    gains_out[3:8, :] = jnp.zeros((5, model), full_kind)
    table = jnp.concatenate([small[16 * t + 8 : 16 * t + 16, :128] for t in range(4)], axis=0)
    hot = bucket_rows(table.shape[0], rows_out.shape[1])
    lines[...] = product_rows(table.astype(low_kind), hot.astype(low_kind))
    heads_here = chances_out.shape[0]
    for number in range(heads_here):
        rows_out[number : number + 1, :] = lines[pl.ds(index * heads_here + number, 1), :]
    rows_out[heads_here:8, :] = jnp.zeros((8 - heads_here, rows_out.shape[1]), full_kind)
    size = normed_out.shape[0]
    self_half(
        0, ids, source_out[:size, :].astype(full_kind), weight_out[...], gains_out, rows_out, None,
        output[...], seg_col[:size, :], seg_row[...],
        (normed_out, mapped_out, chances_out, mixed_out, send, keep, room),
    )


def self_second_body(
    ids, source, weight, gains, rows, mapped_before, output, seg_col, seg_row,
    normed_out, mapped_out, chances_out, mixed_out, send, keep, room,
):
    size = normed_out.shape[0]
    self_half(
        1, ids, source[size:, :].astype(full_kind), weight[...], gains, rows, mapped_before[...],
        output[...], seg_col[size:, :], seg_row[...],
        (normed_out, mapped_out, chances_out, mixed_out, send, keep, room),
    )


def cross_keys_body(ids, e0, e1, e2, e3, w0, w1, w2, w3, memory_out, weight_out, mapped_out):
    put_blocks(ids[0], (e0, e1, e2, e3), memory_out)
    put_blocks(ids[0], (w0, w1, w2, w3), weight_out)
    wide = weight_out.shape[1] // 3
    mapped_out[...] = product(memory_out[...], weight_out[:, wide:]).astype(low_kind)


def cross_body(
    half, ids, source, own, other, gains, weight, mapped, output, seg_col, enc_row,
    after_out, normed_out, query_out, chances_out, mixed_out, send, keep, room,
):
    size = after_out.shape[0]
    wide = output.shape[0]
    start = half * size
    values = source[start : start + size, :].astype(full_kind) + join_cores(
        ids[0], own, other, room
    )
    after_out[...] = values
    normed = (values * inverse_rms(values) * gains[1:2, :]).astype(low_kind)
    normed_out[...] = normed
    query = product(normed, weight[:, :wide]).astype(low_kind)
    query_out[...] = query
    allowed = seg_col[start : start + size, :] == enc_row[...]
    every = mapped[...]
    mixed = []
    for number in range(wide // HEAD_DIM):
        scores = product_cols(heads_of(query, number, 0, wide), heads_of(every, number, 0, wide))
        chances = softmax_rows(scores, allowed).astype(low_kind)
        chances_out[number] = chances
        mixed.append(product(chances, heads_of(every, number, 1, wide)))
    mixed = jnp.concatenate(mixed, axis=1).astype(low_kind)
    mixed_out[...] = mixed
    split_cores(ids[0], product(mixed, output[...]), room, send, keep)


def feed_join_body(ids, w0, w1, w2, w2x, w3, w3x, g0, g1, g2, g3, weight_out, grad_out):
    index, column = ids[0], ids[1] & 1
    put_blocks(index, (w0, w1), weight_out)
    half = w2.shape[0]
    for step, mine, other in ((2, w2, w2x), (3, w3, w3x)):
        weight_out[rows_at(2 * (index ^ step) + column, half), :] = mine[...]
        weight_out[rows_at(2 * (index ^ step) + 1 - column, half), :] = other[...]
    put_blocks(ids[0], (g0, g1, g2, g3), grad_out)


def feed_body(half, ids, before, own, other, gains, weight, down, grad_out, *refs):
    parts = refs[:2] if half else ()
    after_out, normed_out, hidden_out, acts_out, *rest = refs[len(parts) :]
    size = after_out.shape[0]
    start = half * size
    units = down.shape[0]
    room = rest[-1]
    values = before[...] + join_cores(ids[0], own, other, room)
    after_out[...] = values
    normed = (values * inverse_rms(values) * gains[2:3, :]).astype(low_kind)
    normed_out[...] = normed
    acts = product(normed, weight[...])
    gate, up = acts[:, :units], acts[:, units:]
    root = math.sqrt(2 / math.pi)
    square = gate * gate
    bend = jnp.tanh(root * gate * (1.0 + 0.044715 * square))
    curve = 0.5 * gate * (1.0 + bend)
    slope = 0.5 * (1.0 + bend) + 0.5 * gate * (1.0 - bend * bend) * root * (
        1.0 + 3 * 0.044715 * square
    )
    hidden = (curve * up).astype(low_kind)
    hidden_out[...] = hidden
    grad_hidden = product_cols(grad_out[start : start + size, :], down[...])
    acts_out[:, :units] = (grad_hidden * up * slope).astype(low_kind)
    acts_out[:, units:] = (grad_hidden * curve).astype(low_kind)
    grad = product_cols(acts_out[...], weight[...])
    result = product(hidden, down[...])
    if half:
        send, keep, out_send, out_keep = rest[:4]
        for place, part in ((0, parts[0][...]), (1, grad)):
            split_cores(ids[0], part, room, send.at[place], keep.at[place])
        for place, part in ((0, parts[1][...]), (1, result)):
            split_cores(ids[0], part, room, out_send.at[place], out_keep.at[place])
    else:
        rest[0][...] = grad
        rest[1][...] = result


def rep_bits(ids):
    rep = ids[1]
    return rep & 1, (rep >> 1) & 1, rep >> 2


def chunk_targets(ids, keep_first, send_first, keep_second, send_second):
    column, low, unused = rep_bits(ids)
    for slot in range(4):
        high, middle = slot >> 1, slot & 1
        for target, bit in ((keep_first, column), (send_first, 1 - column)):
            yield target.at[slot], 4 * high + 2 * middle + bit, 0
        for target, bit in ((keep_second, low), (send_second, 1 - low)):
            yield target.at[slot], 4 * high + 2 * bit + middle, 1


def feed_weights_body(
    ids, normed0, normed1, acts0, acts1, hidden0, hidden1, grad_out,
    keep_first, send_first, keep_second, send_second, feed, down,
):
    size = normed0.shape[0]
    feed[...] = (
        product_rows(normed0[...], acts0[...]) + product_rows(normed1[...], acts1[...])
    ).astype(low_kind)
    down[...] = (
        product_rows(hidden0[...], grad_out[:size, :])
        + product_rows(hidden1[...], grad_out[size:, :])
    ).astype(low_kind)
    rows = feed.shape[0] // 2
    width = feed.shape[1] // 8
    small = down.shape[0] // 8
    lanes = down.shape[1] // 2
    for target, chunk, part in chunk_targets(ids, keep_first, send_first, keep_second, send_second):
        target[:rows, :] = feed[part * rows : (part + 1) * rows, rows_at(chunk, width)]
        for piece in range(lanes // width):
            start = part * lanes + piece * width
            target[rows + piece * small : rows + (piece + 1) * small, :] = down[
                rows_at(chunk, small), start : start + width
            ]


def store_small_chunks(ids, columns, output, buffers):
    small = output.shape[0] // 8
    lanes = output.shape[1] // 2
    quarter = columns.shape[0] // 4
    for target, chunk, part in chunk_targets(ids, *buffers):
        for place in range(2):
            start = (2 * part + place) * quarter + chunk * small
            target[place] = columns[pl.ds(pl.multiple_of(start, 8), small), :].astype(low_kind)
        target[2] = jnp.zeros(target.shape[1:], low_kind)
        target[2, :, :lanes] = output[
            pl.ds(pl.multiple_of(chunk * small, 8), small), part * lanes : (part + 1) * lanes
        ].astype(low_kind)


def halve_body(ids, keep_first, came_first, keep_second, came_second, *outs):
    new_first, send_first, new_second, send_second = outs
    column, low, unused = rep_bits(ids)
    for keep, came, new, send, bit in (
        (keep_first, came_first, new_first, send_first, low),
        (keep_second, came_second, new_second, send_second, column),
    ):
        for high in range(2):
            for target, place in ((new, 2 * high + bit), (send, 2 * high + 1 - bit)):
                total = keep[place].astype(full_kind) + came[place].astype(full_kind)
                target[high] = total.astype(target.dtype)


def quarter_body(ids, keep_first, came_first, keep_second, came_second, new, send):
    high = rep_bits(ids)[2]
    for part, (keep, came) in enumerate(((keep_first, came_first), (keep_second, came_second))):
        for target, place in ((new, high), (send, 1 - high)):
            total = keep[place].astype(full_kind) + came[place].astype(full_kind)
            target[part] = total.astype(target.dtype)


def trade_body(ids, keep, came, own, send1, send2, send3, rows, room):
    if len(keep.shape) == 3:
        quarter = room.shape[1]
        for part in range(2):
            total = (keep[part] + came[part].astype(full_kind)).astype(low_kind)
            room[2 * part] = total[:quarter]
            room[2 * part + 1] = total[quarter : 2 * quarter]
            rows[part] = total[2 * quarter :]
    else:
        for part in range(2):
            for place in range(3):
                total = (keep[part, place] + came[part, place].astype(full_kind)).astype(low_kind)
                if place < 2:
                    room[2 * part + place] = total
                else:
                    rows[part] = total
    for step, target in enumerate((own, send1, send2, send3)):
        target[...] = room[ids[0] ^ step]


def gather_body(ids, own, came1, came2, came3, rows, out):
    blocks = (own, came1, came2, came3, rows.at[0], rows.at[1])
    for number, block in enumerate(blocks):
        part, place = number // 3, number % 3
        if len(out.shape) == 3:
            size = block.shape[0]
            out[part, place * size : (place + 1) * size] = block[...]
        else:
            out[part, place] = block[...]


def pair_body(ids, mine, other, first, second):
    for place, source in enumerate((mine, other)):
        first[place] = source[0]
        second[place] = source[1]


def all_pieces(ids, firsts, seconds):
    for step in range(4):
        for high in range(2):
            chunk = ids[1] ^ (4 * high + step)
            yield firsts[step].at[high], seconds[step].at[high], high, chunk


def feed_out_body(ids, *refs):
    firsts, seconds, (gate, up, down) = refs[:4], refs[4:8], refs[8:]
    quarter = gate.shape[0]
    units = gate.shape[1] // 4
    small = down.shape[0] // 8
    high_bit = rep_bits(ids)[2]
    for first, second, high, chunk in all_pieces(ids, firsts, seconds):
        width = first.shape[1]
        for value in range(2):

            @pl.when(high_bit == value)
            def _():
                target = (gate, up)[value ^ high]
                for step in range(4):
                    block = second[:quarter] if step == 3 else first[step * quarter : (step + 1) * quarter]
                    start = (ids[0] ^ step) * units + (chunk & 3) * width
                    target[:, pl.ds(pl.multiple_of(start, width), width)] = block.astype(full_kind)

        for piece in range(down.shape[1] // width):
            begin = quarter + piece * small
            down[rows_at(chunk, small), piece * width : (piece + 1) * width] = second[
                begin : begin + small
            ].astype(full_kind)


def small_out_body(ids, *refs):
    firsts, seconds, outs, room = refs[:4], refs[4:8], refs[8:12], refs[12]
    small = room.shape[1] // 8
    lanes = outs[3].shape[1] // 2
    wide = outs[0].shape[0]
    for first, second, high, chunk in all_pieces(ids, firsts, seconds):
        where = pl.ds(pl.multiple_of(chunk * small, 8), small)
        for step in range(4):
            block = second[0] if step == 3 else first[step]
            room[step, where, :] = block.astype(full_kind)
        for part in range(2):
            outs[3][where, part * lanes : (part + 1) * lanes] = second[1 + part][:, :lanes].astype(
                full_kind
            )
    for place in range(4):
        for number in range(3):
            outs[number][:, place * wide : (place + 1) * wide] = room[
                ids[0] ^ place, :, number * wide : (number + 1) * wide
            ]


def attention_backward(grads, query, keys, values, chances, number):
    wide = grads.shape[1]
    grad = heads_of(grads, number, 0, wide)
    full = chances.astype(full_kind)
    grad_chances = product_cols(grad, heads_of(values, number, 0, wide))
    grad_scores = full * (grad_chances - jnp.sum(full * grad_chances, axis=-1, keepdims=True))
    rounded = grad_scores.astype(low_kind)
    return (
        grad_scores,
        product(rounded, heads_of(keys, number, 0, wide)).astype(low_kind),
        product_rows(rounded, heads_of(query, number, 0, wide)),
        product_rows(chances, grad),
    )


def join_halves(index, own, other, room):
    core = index & 1
    size = own.shape[1]
    for chip in range(2):
        room[rows_at(core + 2 * chip, size), :] = own[chip].astype(full_kind)
        room[rows_at(1 - core + 2 * chip, size), :] = other[chip].astype(full_kind)
    return room[...]


def cross_back_body(
    ids, grad_out, own, other, values0, values1, gains, output, query0, query1, chances0, chances1,
    mapped, weight, total_out, low_out, query_out, sums_out, row_out, send, keep, room,
):
    wide = output.shape[0]
    join_halves(ids[0], own, other, room)
    size = values0.shape[0]
    row = 0.0
    for half, values in ((0, values0), (1, values1)):
        part = slice(half * size, (half + 1) * size)
        grad, piece = norm_backward(room[part, :], values[...], gains[2:3, :])
        row = row + piece
        total = grad_out[part, :].astype(full_kind) + grad
        total_out[part, :] = total
        low_out[part, :] = total.astype(low_kind)
    row_out[...] = jnp.broadcast_to(row, row_out.shape)
    grad_mixed = product_cols(low_out[...], output[...]).astype(low_kind)
    every = mapped[...]
    query = jnp.concatenate([query0[...], query1[...]], axis=0)
    keys, values = [], []
    for number in range(wide // HEAD_DIM):
        chances = jnp.concatenate([chances0[number], chances1[number]], axis=0)
        unused, grad_query, grad_keys, grad_values = attention_backward(
            grad_mixed, query, every[:, :wide], every[:, wide:], chances, number
        )
        query_out[:, number * HEAD_DIM : (number + 1) * HEAD_DIM] = grad_query
        keys.append(grad_keys)
        values.append(grad_values)
    sums_out[...] = jnp.concatenate(keys + values, axis=1).astype(low_kind)
    scatter_cores(ids[0], product_cols(query_out[...], weight[:, :wide]), room, send, keep)


def cross_weights_body(
    ids, normed0, normed1, query, memory, sums, mixed0, mixed1, low, weight,
    keep_first, send_first, keep_second, send_second, send, keep, room, columns, output,
):
    wide = query.shape[1]
    size = normed0.shape[0]
    columns[:, :wide] = product_rows(normed0[...], query[:size, :]) + product_rows(
        normed1[...], query[size:, :]
    )
    columns[:, wide:] = product_rows(memory[...], sums[...])
    output[...] = product_rows(mixed0[...], low[:size, :]) + product_rows(mixed1[...], low[size:, :])
    store_small_chunks(ids, columns, output, (keep_first, send_first, keep_second, send_second))
    scatter_cores(ids[0], product_cols(sums[...], weight[:, wide:]), room, send, keep)


def scatter_cores(index, partial, room, send, keep):
    core = index & 1
    size = send.shape[1]
    room[...] = partial
    for chip in range(2):
        keep[chip] = room[rows_at(core + 2 * chip, size), :]
        send[chip] = room[rows_at(1 - core + 2 * chip, size), :].astype(low_kind)


def diagonal_sums(matrix):
    width = matrix.shape[1]
    size = matrix.shape[0]
    while size > 1:
        size //= 2
        matrix = matrix[:size] + pltpu.roll(matrix[size:], width - size, 1)
    return matrix


def self_back_body(
    ids, total, own, other, values0, values1, gains, output, mapped0, mapped1, chances0, chances1,
    total_out, low_out, query_out, sums_out, row_out, table_out, room,
):
    wide = output.shape[0]
    join_halves(ids[0], own, other, room)
    size = values0.shape[0]
    row = 0.0
    for half, values in ((0, values0), (1, values1)):
        part = slice(half * size, (half + 1) * size)
        grad, piece = norm_backward(room[part, :], values[...], gains[1:2, :])
        row = row + piece
        new_total = total[part, :] + grad
        total_out[part, :] = new_total
        low_out[part, :] = new_total.astype(low_kind)
    row_out[...] = jnp.broadcast_to(row, row_out.shape)
    grad_mixed = product_cols(low_out[...], output[...]).astype(low_kind)
    buckets = table_out.shape[0]
    hot = bucket_rows(buckets, 2 * size)
    every = jnp.concatenate([mapped0[...], mapped1[...]], axis=0)
    keys, values, columns = [], [], []
    for number in range(wide // HEAD_DIM):
        line = None
        for half, chances in ((1, chances1), (0, chances0)):
            part = slice(half * size, (half + 1) * size)
            seen = slice(0, (half + 1) * size)
            grad_scores, grad_query, grad_keys, grad_values = attention_backward(
                grad_mixed[part], every[part, :wide], every[seen, wide : 2 * wide],
                every[seen, 2 * wide :], chances[number], number,
            )
            query_out[part, number * HEAD_DIM : (number + 1) * HEAD_DIM] = grad_query
            if half:
                line = pltpu.roll(diagonal_sums(grad_scores), size, 1)
                keys.append(grad_keys)
                values.append(grad_values)
            else:
                empty = jnp.zeros((size, size), full_kind)
                line = line + diagonal_sums(jnp.concatenate([grad_scores, empty], axis=1))
                keys[-1] = jnp.concatenate([keys[-1][:size] + grad_keys, keys[-1][size:]], axis=0)
                values[-1] = jnp.concatenate(
                    [values[-1][:size] + grad_values, values[-1][size:]], axis=0
                )
        columns.append(jnp.sum(hot * line, axis=1, keepdims=True))
    sums_out[...] = jnp.concatenate(keys + values, axis=1).astype(low_kind)
    columns.append(jnp.zeros((buckets, 128 - len(columns)), full_kind))
    table_out[...] = jnp.concatenate(columns, axis=1)


def self_weights_body(
    ids, normed0, normed1, query, sums, mixed0, mixed1, low, weight,
    keep_first, send_first, keep_second, send_second, send, keep, room, columns, output, merged,
):
    wide = query.shape[1]
    size = normed0.shape[0]
    merged[:, :wide] = query[...]
    merged[:, wide:] = sums[...]
    columns[...] = product_rows(normed0[...], merged[:size, :]) + product_rows(
        normed1[...], merged[size:, :]
    )
    output[...] = product_rows(mixed0[...], low[:size, :]) + product_rows(mixed1[...], low[size:, :])
    store_small_chunks(ids, columns, output, (keep_first, send_first, keep_second, send_second))
    scatter_cores(ids[0], product_cols(merged[...], weight[...]), room, send, keep)


def finish_body(ids, source, mine, far, gains, total, cross_row, feed_row, table, grad_out, vector):
    index = ids[0]
    size, model = source.shape
    grad, row = norm_backward(
        mine[...] + far[...].astype(full_kind), source[...].astype(full_kind), gains[0:1, :]
    )
    grad_out[...] = total[rows_at(index, size), :] + grad
    lanes = lax.broadcasted_iota(jnp.int32, (1, model), 1)
    part = model // 4
    here = (lanes >= index * part) & (lanes < (index + 1) * part)
    pieces = []
    for line in (row, jnp.where(here, cross_row[0:1, :], 0.0), jnp.where(here, feed_row[0:1, :], 0.0)):
        pieces += [line[:, start : start + 128] for start in range(0, model, 128)]
    pieces += [jnp.zeros((-len(pieces) % 8, 128), full_kind)]
    vector[: vector.shape[0] - table.shape[0], :] = jnp.concatenate(pieces, axis=0)
    vector[vector.shape[0] - table.shape[0] :, :] = pltpu.roll(
        table[...], index * (HEADS // 4), 1
    )


def chip_pair_body(ids, keep, arrived, mine, other):
    chip = ids[0] >> 1
    mine[...] = keep[chip] + arrived[chip].astype(full_kind)
    other[...] = (keep[1 - chip] + arrived[1 - chip].astype(full_kind)).astype(low_kind)


class Kernels:
    def __init__(self, ids):
        self.ids = ids

    def __call__(self, name, body, operands, results, scratch=(), cover=()):
        outs = run_kernel(name, body, self.ids, operands, results, scratch)
        if cover:
            outs = after(tuple(outs), *cover)
        self.ids = after(self.ids, outs[0])
        return outs

    def wait(self, *values):
        self.ids = after(self.ids, *values)


def rep_swap(value, step):
    return swap(value, "rep", 8, step)


def shard_swap(value, step):
    return swap(value, "shard", 4, step)


class Reduction:
    def __init__(self, call, name, buffers):
        self.call, self.name = call, name
        self.keeps = (buffers[0], buffers[2])
        self.came = (rep_swap(buffers[1], 1), rep_swap(buffers[3], 2))
        self.shape = buffers[0].shape[1:]

    def halve(self, cover=()):
        results = []
        for unused in range(2):
            results += [((2,) + self.shape, full_kind), ((2,) + self.shape, low_kind)]
        outs = self.call(
            self.name + "_halve",
            halve_body,
            (self.keeps[0], self.came[0], self.keeps[1], self.came[1]),
            results,
            cover=cover,
        )
        self.keeps = (outs[0], outs[2])
        self.came = (rep_swap(outs[1], 2), rep_swap(outs[3], 1))

    def quarter(self, cover=()):
        shape = (2,) + self.shape
        self.keep, send = self.call(
            self.name + "_quarter",
            quarter_body,
            (self.keeps[0], self.came[0], self.keeps[1], self.came[1]),
            [(shape, full_kind), (shape, low_kind)],
            cover=cover,
        )
        self.last = rep_swap(send, 4)

    def trade(self, cover=()):
        block = (self.shape[0] // 3,) + self.shape[1:] if len(self.shape) == 2 else self.shape[1:]
        rows = (2,) + block
        own, *sends, self.rows = self.call(
            self.name + "_trade",
            trade_body,
            (self.keep, self.last),
            [(block, low_kind)] * 4 + [(rows, low_kind)],
            [((4,) + block, low_kind)],
            cover=cover,
        )
        self.blocks = [own] + [shard_swap(send, step) for step, send in zip((1, 2, 3), sends)]

    def gather(self, cover=()):
        (self.piece,) = self.call(
            self.name + "_gather",
            gather_body,
            (*self.blocks, self.rows),
            [((2,) + self.shape, low_kind)],
            cover=cover,
        )
        self.other = rep_swap(self.piece, 4)

    def pair(self, cover=()):
        shape = (2,) + self.shape
        first, second = self.call(
            self.name + "_pair", pair_body, (self.piece, self.other), [(shape, low_kind)] * 2, cover=cover
        )
        first_far, second_far = rep_swap(first, 2), rep_swap(second, 1)
        self.firsts = (first, rep_swap(first, 1), first_far, rep_swap(first_far, 1))
        self.seconds = (second, second_far, rep_swap(second, 2), rep_swap(second_far, 2))

    def finish(self, body, results, scratch=()):
        return self.call(
            self.name + "_out", body, (*self.firsts, *self.seconds), results, scratch
        )


class GroupSum:
    def __init__(self, send, keep):
        self.keep = keep
        self.came = shard_swap(send, 1)

    def add(self):
        self.pair = (self.keep + self.came.astype(full_kind)).astype(low_kind)
        self.far = shard_swap(self.pair, 2)
        return self.pair

    def total(self):
        own = (self.pair.astype(full_kind) + self.far.astype(full_kind)).astype(low_kind)
        self.results = (own, shard_swap(own, 1))
        return own


def sum_small(vector):
    for step in (1, 2):
        vector = vector + shard_swap(vector, step)
    for step in (1, 2, 4):
        vector = vector + rep_swap(vector, step)
    return vector


def split_shards(
    inputs,
    encoder,
    segments,
    enc_segments,
    self_query,
    self_key,
    self_value,
    self_output,
    cross_query,
    cross_key,
    cross_value,
    cross_output,
    gate_weight,
    up_weight,
    down_weight,
    self_gain,
    cross_gain,
    feed_gain,
    bias_table,
    cotangent,
):
    index = lax.axis_index("shard")
    rep = lax.axis_index("rep")
    call = Kernels(jnp.stack([index, rep]))
    tokens_here, model = inputs.shape[1:]
    length = 4 * tokens_here
    half_size = 2 * tokens_here
    heads_here = HEADS // 4
    wide = heads_here * HEAD_DIM
    units = down_weight.shape[0]
    memory_length = enc_segments.shape[1]
    small_rows = bias_table.shape[0]
    buckets = 4 * small_rows
    part = self_gain.shape[0]

    def blocks_of(*weights):
        width = sum(weight.shape[1] for weight in weights) // 4
        shape = (weights[0].shape[0], width)
        return call("columns", columns_body, weights, [(shape, low_kind)] * 4)

    def traded(blocks):
        return [blocks[0]] + [shard_swap(blocks[step], step) for step in range(1, 4)]

    column_shape = (part, 3 * wide)
    packed, *self_blocks = call(
        "pack",
        pack_body,
        (
            inputs[0], self_gain, cross_gain, feed_gain, bias_table, self_query, self_key,
            self_value,
        ),
        [((tokens_here + 16, model), low_kind)] + [(column_shape, low_kind)] * 4,
    )
    source_far = shard_swap(packed, 2)
    self_blocks = traded(self_blocks)
    cross_blocks = blocks_of(cross_query, cross_key, cross_value)
    feed_blocks = call(
        "feed_columns",
        split_columns_body,
        (gate_weight, up_weight),
        [((part, 2 * units), low_kind)] * 2 + [((part // 2, 2 * units), low_kind)] * 2,
    )
    source_far = after(source_far, feed_blocks[0])
    source_blocks = [packed, shard_swap(packed, 1), source_far, shard_swap(source_far, 1)]
    seg_row = segments
    seg_col = segments[0][:, None]
    enc_row = enc_segments
    call.wait(seg_col, self_blocks[2], self_blocks[3])
    cross_blocks = traded(after(tuple(cross_blocks), self_blocks[2], self_blocks[3]))
    room = [((half_size, model), full_kind)]
    whole_room = [((length, model), full_kind)]
    pieces = [((tokens_here, model), low_kind), ((tokens_here, model), full_kind)]
    two_pieces = [((2,) + shape, kind) for shape, kind in pieces]

    def self_results(keys):
        return [
            ((half_size, model), low_kind),
            ((half_size, 3 * wide), low_kind),
            ((heads_here, half_size, keys), low_kind),
            ((half_size, wide), low_kind),
        ] + pieces

    source, w_self, gains, rows, *first = call(
        "self_first",
        self_first_body,
        (*source_blocks, *self_blocks, self_output, seg_col, seg_row),
        [
            ((length, model), low_kind),
            ((model, 3 * wide), low_kind),
            ((8, model), full_kind),
            ((8, length), full_kind),
        ]
        + self_results(half_size),
        room + [((64, model), full_kind), ((128, length), full_kind)],
        cover=(cross_blocks[2],),
    )
    first_sum = GroupSum(*first[4:])
    memory_far = shard_swap(after(encoder[0], first[0]), 2)
    second = call(
        "self_second",
        self_second_body,
        (source, w_self, gains, rows, first[1], self_output, seg_col, seg_row),
        self_results(length),
        room,
        cover=(cross_blocks[3], first_sum.came),
    )
    second_sum = GroupSum(*second[4:])
    call.wait(first_sum.add())
    memory_blocks = [
        encoder[0], shard_swap(encoder[0], 1), memory_far, shard_swap(memory_far, 1)
    ]
    memory, w_cross, cross_mapped = call(
        "cross_keys",
        cross_keys_body,
        (*memory_blocks, *cross_blocks),
        [
            ((memory_length, model), low_kind),
            ((model, 3 * wide), low_kind),
            ((memory_length, 2 * wide), low_kind),
        ],
        cover=(second_sum.came,),
    )
    pair = second_sum.add()
    call.wait(pair)
    first_sum.total()
    feed_blocks = after(tuple(feed_blocks), pair)
    feed_near = shard_swap(feed_blocks[1], 1)
    feed_two = shard_swap(feed_blocks[2], 2)

    def cross_call(half, sums, cover):
        own, other = sums.results
        return call(
            "cross",
            functools.partial(cross_body, half),
            (source, own, other, gains, w_cross, cross_mapped, cross_output, seg_col, enc_row),
            [
                ((half_size, model), full_kind),
                ((half_size, model), low_kind),
                ((half_size, wide), low_kind),
                ((heads_here, half_size, memory_length), low_kind),
                ((half_size, wide), low_kind),
            ]
            + pieces,
            room,
            cover=cover,
        )

    cross0 = cross_call(0, first_sum, (second_sum.far, feed_two))
    cross_first = GroupSum(*cross0[5:])
    call.wait(second_sum.total())
    feed_two_other = rep_swap(feed_two, 1)
    feed_three = shard_swap(after(feed_blocks[3], cross0[0]), 3)
    grad_far = shard_swap(after(cotangent[0], cross0[0]), 2)
    cross1 = cross_call(1, second_sum, (feed_three, feed_two_other, cross_first.came))
    cross_second = GroupSum(*cross1[5:])
    call.wait(cross_first.add())
    feed_three_other = rep_swap(feed_three, 1)
    grad_blocks = [
        cotangent[0], shard_swap(cotangent[0], 1), grad_far, shard_swap(grad_far, 1)
    ]
    w_feed, grad_out = call(
        "feed_join",
        feed_join_body,
        (
            feed_blocks[0], feed_near, feed_two, feed_two_other, feed_three, feed_three_other,
            *grad_blocks,
        ),
        [((model, 2 * units), low_kind), ((length, model), low_kind)],
        cover=(cross_second.came,),
    )
    call.wait(cross_second.add())
    cross_first.total()

    def feed_call(half, sums, before, parts, tail, cover=()):
        own, other = sums.results
        return call(
            "feed",
            functools.partial(feed_body, half),
            (before, own, other, gains, w_feed, down_weight, grad_out) + parts,
            [
                ((half_size, model), full_kind),
                ((half_size, model), low_kind),
                ((half_size, units), low_kind),
                ((half_size, 2 * units), low_kind),
            ]
            + tail,
            room,
            cover=cover,
        )

    feed0 = feed_call(0, cross_first, cross0[0], (), room * 2, (cross_second.far,))
    cross_second.total()
    feed1 = feed_call(1, cross_second, cross1[0], (feed0[4], feed0[5]), two_pieces * 2)
    feed_sum = GroupSum(*feed1[4:6])
    out_came = shard_swap(feed1[6], 1)

    chunk = (model // 2 + units // 8 * (model // 2) // (2 * units // 8), 2 * units // 8)
    feed_grads = Reduction(
        call,
        "feed_grads",
        call(
            "feed_weights",
            feed_weights_body,
            (feed0[1], feed1[1], feed0[3], feed1[3], feed0[2], feed1[2], grad_out),
            [((4,) + chunk, low_kind)] * 4,
            [((model, 2 * units), low_kind), ((units, model), low_kind)],
            cover=(feed_sum.came, out_came),
        ),
    )
    call.wait(feed_sum.add())

    def scatter_pair(arrived, keep):
        mine, other = call(
            "chip_pair",
            chip_pair_body,
            (keep, arrived),
            [((tokens_here, model), full_kind), ((tokens_here, model), low_kind)],
        )
        return mine, shard_swap(other, 2)

    mine, far = scatter_pair(out_came, feed1[7])
    feed_sum.total()
    own_after = lax.dynamic_slice_in_dim(
        jnp.where(index < 2, feed0[0], feed1[0]), (index & 1) * tokens_here, tokens_here
    )
    outcome = (own_after + mine + far.astype(full_kind)).astype(low_kind)

    feed_grads.halve()
    total_cross, low_cross, query_cross, sums_cross, row_feed, *sends = call(
        "cross_back",
        cross_back_body,
        (
            grad_out, *feed_sum.results, feed0[0], feed1[0], gains, cross_output, cross0[2], cross1[2],
            cross0[3], cross1[3], cross_mapped, w_cross,
        ),
        [
            ((length, model), full_kind),
            ((length, model), low_kind),
            ((length, wide), low_kind),
            ((memory_length, 2 * wide), low_kind),
            ((8, model), full_kind),
        ]
        + two_pieces,
        whole_room,
        cover=feed_grads.came,
    )
    cross_sum = GroupSum(*sends)
    feed_grads.quarter(cover=(cross_sum.came,))
    call.wait(cross_sum.add())
    small_chunk = (3, wide // 8, 3 * wide)
    weight_room = [((model, 3 * wide), full_kind), ((wide, model), full_kind)]
    *buffers, send, keep = call(
        "cross_weights",
        cross_weights_body,
        (
            cross0[1], cross1[1], query_cross, memory, sums_cross, cross0[4], cross1[4], low_cross,
            w_cross,
        ),
        [((4,) + small_chunk, low_kind)] * 4 + two_pieces,
        whole_room + weight_room,
    )
    cross_grads = Reduction(call, "cross_grads", buffers)
    mine, far = scatter_pair(shard_swap(send, 1), keep)
    grad_memory = mine + far.astype(full_kind)
    call.wait(cross_sum.total())
    feed_grads.trade()
    total_self, low_self, query_self, sums_self, row_cross, table = call(
        "self_back",
        self_back_body,
        (
            total_cross, *cross_sum.results, cross0[0], cross1[0], gains, self_output, first[1], second[1],
            first[2], second[2],
        ),
        [
            ((length, model), full_kind),
            ((length, model), low_kind),
            ((length, wide), low_kind),
            ((length, 2 * wide), low_kind),
            ((8, model), full_kind),
            ((buckets, 128), full_kind),
        ],
        whole_room,
        cover=cross_grads.came + tuple(feed_grads.blocks[1:]),
    )
    feed_grads.gather()
    cross_grads.halve()
    *buffers, send, keep = call(
        "self_weights",
        self_weights_body,
        (first[0], second[0], query_self, sums_self, first[3], second[3], low_self, w_self),
        [((4,) + small_chunk, low_kind)] * 4 + two_pieces,
        whole_room + weight_room + [((length, 3 * wide), low_kind)],
        cover=cross_grads.came,
    )
    self_grads = Reduction(call, "self_grads", buffers)
    arrived = shard_swap(send, 1)
    cross_grads.quarter(cover=(arrived, feed_grads.other))
    mine, far = scatter_pair(arrived, keep)
    feed_grads.pair()
    self_grads.halve()
    cross_grads.trade()
    gain_rows = -(-3 * model // 1024) * 8
    grad_source, vector = call(
        "finish",
        finish_body,
        (inputs[0], mine, far, gains, total_self, row_cross, row_feed, table),
        [((tokens_here, model), full_kind), ((gain_rows + buckets, 128), full_kind)],
    )
    vector = sum_small(vector)
    self_grads.quarter()
    cross_grads.gather()
    self_grads.trade()
    cross_grads.pair()
    feed_out = feed_grads.finish(
        feed_out_body,
        [((part, 4 * units), full_kind)] * 2 + [((units, model), full_kind)],
    )
    self_grads.gather()
    small_results = [((part, model), full_kind)] * 3 + [((wide, model), full_kind)]
    out_room = [((4, wide, 3 * wide), full_kind)]
    cross_out = cross_grads.finish(small_out_body, small_results, out_room)
    self_grads.pair()
    self_out = self_grads.finish(small_out_body, small_results, out_room)

    gains_sum = vector[: 3 * model // 128].reshape(3, model)
    gains_here = lax.dynamic_slice_in_dim(gains_sum, index * part, part, 1)
    table_grad = lax.dynamic_slice_in_dim(
        vector[gain_rows:, :HEADS], index * small_rows, small_rows
    )
    return (
        outcome[None],
        grad_source[None],
        grad_memory[None],
        *self_out,
        *cross_out,
        *feed_out,
        gains_here[0],
        gains_here[1],
        gains_here[2],
        table_grad,
    )


def solution(mesh):
    in_specs = (
        P("rep", "shard", None),
        P("rep", "shard", None),
        P("rep", None),
        P("rep", None),
        P("shard", None),
        P("shard", None),
        P("shard", None),
        P("shard", None),
        P("shard", None),
        P("shard", None),
        P("shard", None),
        P("shard", None),
        P("shard", None),
        P("shard", None),
        P("shard", None),
        P("shard"),
        P("shard"),
        P("shard"),
        P("shard", None),
        P("rep", "shard", None),
    )
    out_specs = (
        P("rep", "shard", None),
        P("rep", "shard", None),
        P("rep", "shard", None),
        P("shard", None),
        P("shard", None),
        P("shard", None),
        P("shard", None),
        P("shard", None),
        P("shard", None),
        P("shard", None),
        P("shard", None),
        P("shard", None),
        P("shard", None),
        P("shard", None),
        P("shard"),
        P("shard"),
        P("shard"),
        P("shard", None),
    )
    split = mesh.shape["shard"] == 4 and mesh.shape["rep"] == 8
    body = split_shards if split else shards
    return jax.shard_map(body, mesh=mesh, in_specs=in_specs, out_specs=out_specs, check_vma=False)
```

```python
import functools
import math

import jax
import jax.numpy as jnp
from jax import lax
from jax.experimental import pallas as pl
from jax.experimental.pallas import tpu as pltpu
from jax.sharding import PartitionSpec as P

HEADS = 12
HEAD_DIM = 64


bucket_edges = [math.ceil(16 * 8 ** (number / 16)) for number in range(1, 16)]
epsilon = 1e-06
masked_score = -1000000000.0


def bucket_of(distance):
    far_part = sum(((distance >= border).astype(jnp.int32) for border in bucket_edges))
    return jnp.where(distance < 16, distance, 16 + far_part)


def rms_scale(values, scales):
    return values * lax.rsqrt(jnp.mean(values * values, axis=-1, keepdims=True) + epsilon) * scales


def product(former, latter):
    return jnp.dot(former, latter, preferred_element_type=jnp.float32)


def product_rows(former, latter):
    return lax.dot_general(
        former, latter, (((0,), (0,)), ((), ())), preferred_element_type=jnp.float32
    )


def product_cols(former, latter):
    return lax.dot_general(
        former, latter, (((1,), (1,)), ((), ())), preferred_element_type=jnp.float32
    )


def split_heads(matrix):
    return matrix.reshape(matrix.shape[0], HEADS, HEAD_DIM).transpose(1, 0, 2)


def join_heads(stacked):
    return stacked.transpose(1, 0, 2).reshape(stacked.shape[1], HEADS * HEAD_DIM)


def to_blocks(matrix, block_count):
    return matrix.reshape(block_count, -1, HEADS, HEAD_DIM).transpose(0, 2, 1, 3)


def from_blocks(stacked):
    return stacked.transpose(0, 2, 1, 3).reshape(-1, HEADS * HEAD_DIM)


def self_scores(queries, query_start, query_ids, table_full, key_rows, key_start, key_ids):
    query_count = queries.shape[1]
    key_count = key_rows.shape[1]
    query_places = query_start + jnp.arange(query_count, dtype=jnp.int32)
    key_places = key_start + jnp.arange(key_count, dtype=jnp.int32)
    buckets = bucket_of(jnp.maximum(query_places[:, None] - key_places[None, :], 0))
    one_hot = (
        buckets.reshape(1, -1) == jnp.arange(table_full.shape[0], dtype=jnp.int32)[:, None]
    ).astype(jnp.bfloat16)
    bias_block = jnp.einsum(
        "bn,bh->hn", one_hot, table_full, preferred_element_type=jnp.float32
    ).reshape(HEADS, query_count, key_count)
    scores = (
        jnp.einsum("hqd,hkd->hqk", queries, key_rows, preferred_element_type=jnp.float32)
        + bias_block
    )
    allowed = (query_places[:, None] >= key_places[None, :]) & (
        query_ids[:, None] == key_ids[None, :]
    )
    return (jnp.where(allowed[None], scores, masked_score), one_hot)


def self_logsum(queries, query_start, query_ids, table_full, key_blocks, id_blocks, key_starts):
    query_count = queries.shape[1]

    def advance(running, packed):
        largest, totals = running
        key_rows, key_ids, key_start = packed
        scores, unused = self_scores(
            queries, query_start, query_ids, table_full, key_rows, key_start, key_ids
        )
        newest = jnp.maximum(largest, jnp.max(scores, axis=-1, keepdims=True))
        totals = totals * jnp.exp(largest - newest) + jnp.sum(
            jnp.exp(scores - newest), axis=-1, keepdims=True
        )
        return ((newest, totals), None)

    initial = (
        jnp.full((HEADS, query_count, 1), -jnp.inf, jnp.float32),
        jnp.zeros((HEADS, query_count, 1), jnp.float32),
    )
    (largest, totals), unused = lax.scan(advance, initial, (key_blocks, id_blocks, key_starts))
    return largest + jnp.log(totals)


def self_mix(
    queries,
    query_start,
    query_ids,
    table_full,
    key_blocks,
    value_blocks,
    id_blocks,
    key_starts,
    logsum,
):

    def advance(accum, packed):
        key_rows, value_rows, key_ids, key_start = packed
        scores, unused = self_scores(
            queries, query_start, query_ids, table_full, key_rows, key_start, key_ids
        )
        weights = jnp.exp(scores - logsum).astype(jnp.bfloat16)
        return (
            accum
            + jnp.einsum("hqk,hkd->hqd", weights, value_rows, preferred_element_type=jnp.float32),
            None,
        )

    initial = jnp.zeros((HEADS, queries.shape[1], HEAD_DIM), jnp.float32)
    accum, unused = lax.scan(advance, initial, (key_blocks, value_blocks, id_blocks, key_starts))
    return accum


def self_backward(
    queries,
    query_start,
    query_ids,
    table_full,
    key_blocks,
    value_blocks,
    id_blocks,
    key_starts,
    logsum,
    grad_mixed,
):
    query_count = queries.shape[1]

    def dots(accum, packed):
        key_rows, value_rows, key_ids, key_start = packed
        scores, unused = self_scores(
            queries, query_start, query_ids, table_full, key_rows, key_start, key_ids
        )
        chances = jnp.exp(scores - logsum)
        grad_chances = jnp.einsum(
            "hqd,hkd->hqk", grad_mixed, value_rows, preferred_element_type=jnp.float32
        )
        return (accum + jnp.sum(chances * grad_chances, axis=-1, keepdims=True), None)

    row_dots, unused = lax.scan(
        dots,
        jnp.zeros((HEADS, query_count, 1), jnp.float32),
        (key_blocks, value_blocks, id_blocks, key_starts),
    )

    def advance(running, packed):
        grad_queries, grad_table = running
        key_rows, value_rows, key_ids, key_start = packed
        scores, one_hot = self_scores(
            queries, query_start, query_ids, table_full, key_rows, key_start, key_ids
        )
        chances = jnp.exp(scores - logsum)
        grad_chances = jnp.einsum(
            "hqd,hkd->hqk", grad_mixed, value_rows, preferred_element_type=jnp.float32
        )
        grad_scores = chances * (grad_chances - row_dots)
        rounded = grad_scores.astype(jnp.bfloat16)
        grad_values = jnp.einsum(
            "hqk,hqd->hkd",
            chances.astype(jnp.bfloat16),
            grad_mixed,
            preferred_element_type=jnp.float32,
        )
        grad_keys = jnp.einsum("hqk,hqd->hkd", rounded, queries, preferred_element_type=jnp.float32)
        grad_queries = grad_queries + jnp.einsum(
            "hqk,hkd->hqd", rounded, key_rows, preferred_element_type=jnp.float32
        )
        grad_table = grad_table + jnp.einsum(
            "bn,hn->bh",
            one_hot,
            grad_scores.reshape(HEADS, -1),
            precision=lax.Precision.HIGHEST,
            preferred_element_type=jnp.float32,
        )
        return ((grad_queries, grad_table), (grad_keys, grad_values))

    initial = (
        jnp.zeros((HEADS, query_count, HEAD_DIM), jnp.float32),
        jnp.zeros((table_full.shape[0], HEADS), jnp.float32),
    )
    (grad_queries, grad_table), (grad_keys, grad_values) = lax.scan(
        advance, initial, (key_blocks, value_blocks, id_blocks, key_starts)
    )
    return (join_heads(grad_queries), grad_table, from_blocks(grad_keys), from_blocks(grad_values))


def cross_forward(queries, key_heads, value_heads, allowed):
    scores = jnp.where(
        allowed,
        jnp.einsum("hqd,hkd->hqk", queries, key_heads, preferred_element_type=jnp.float32),
        masked_score,
    )
    largest = jnp.max(scores, axis=-1, keepdims=True)
    logsum = largest + jnp.log(jnp.sum(jnp.exp(scores - largest), axis=-1, keepdims=True))
    weights = jnp.exp(scores - logsum).astype(jnp.bfloat16)
    mixed = jnp.einsum("hqk,hkd->hqd", weights, value_heads, preferred_element_type=jnp.float32)
    return (mixed, logsum)


def cross_backward(queries, key_heads, value_heads, allowed, logsum, grad_mixed):
    scores = jnp.where(
        allowed,
        jnp.einsum("hqd,hkd->hqk", queries, key_heads, preferred_element_type=jnp.float32),
        masked_score,
    )
    chances = jnp.exp(scores - logsum)
    grad_values = jnp.einsum(
        "hqk,hqd->hkd", chances.astype(jnp.bfloat16), grad_mixed, preferred_element_type=jnp.float32
    )
    grad_chances = jnp.einsum(
        "hqd,hkd->hqk", grad_mixed, value_heads, preferred_element_type=jnp.float32
    )
    grad_scores = chances * (grad_chances - jnp.sum(chances * grad_chances, axis=-1, keepdims=True))
    rounded = grad_scores.astype(jnp.bfloat16)
    grad_queries = jnp.einsum(
        "hqk,hkd->hqd", rounded, key_heads, preferred_element_type=jnp.float32
    )
    grad_keys = jnp.einsum("hqk,hqd->hkd", rounded, queries, preferred_element_type=jnp.float32)
    return (join_heads(grad_queries), join_heads(grad_keys), join_heads(grad_values))


def shards(
    inputs,
    encoder,
    segments,
    enc_segments,
    self_query,
    self_key,
    self_value,
    self_output,
    cross_query,
    cross_key,
    cross_value,
    cross_output,
    gate_weight,
    up_weight,
    down_weight,
    self_gain,
    cross_gain,
    feed_gain,
    bias_table,
    cotangent,
):
    fetched = (
        lax.all_gather(self_query, "shard", axis=0, tiled=True),
        lax.all_gather(self_key, "shard", axis=0, tiled=True),
        lax.all_gather(self_value, "shard", axis=0, tiled=True),
        lax.all_gather(self_output, "shard", axis=0, tiled=True),
        lax.all_gather(cross_query, "shard", axis=0, tiled=True),
        lax.all_gather(cross_key, "shard", axis=0, tiled=True),
        lax.all_gather(cross_value, "shard", axis=0, tiled=True),
        lax.all_gather(cross_output, "shard", axis=0, tiled=True),
        lax.all_gather(gate_weight, "shard", axis=0, tiled=True),
        lax.all_gather(up_weight, "shard", axis=0, tiled=True),
        lax.all_gather(down_weight, "shard", axis=0, tiled=True),
        lax.all_gather(self_gain, "shard", axis=0, tiled=True),
        lax.all_gather(cross_gain, "shard", axis=0, tiled=True),
        lax.all_gather(feed_gain, "shard", axis=0, tiled=True),
        lax.all_gather(bias_table, "shard", axis=0, tiled=True),
    )
    (
        w_query,
        w_key,
        w_value,
        w_output,
        c_query,
        c_key,
        c_value,
        c_output,
        w_gate,
        w_up,
        w_down,
        g_self,
        g_cross,
        g_feed,
        table_full,
    ) = fetched
    gain_self = g_self.astype(jnp.float32)
    gain_cross = g_cross.astype(jnp.float32)
    gain_feed = g_feed.astype(jnp.float32)
    source = inputs[0].astype(jnp.float32)
    memory = encoder[0]
    segment_ids = segments[0]
    memory_ids = enc_segments[0]
    tokens_here = source.shape[0]
    length = segment_ids.shape[0]
    block_size = math.gcd(length, 512)
    block_count = length // block_size
    query_start = lax.axis_index("shard") * tokens_here
    query_ids = lax.dynamic_slice_in_dim(segment_ids, query_start, tokens_here)
    id_blocks = segment_ids.reshape(block_count, block_size)
    key_starts = jnp.arange(block_count, dtype=jnp.int32) * block_size
    cross_allowed = (query_ids[:, None] == memory_ids[None, :])[None]
    normed_self = rms_scale(source, gain_self).astype(jnp.bfloat16)
    query_heads = split_heads(product(normed_self, w_query).astype(jnp.bfloat16))
    key_local = product(normed_self, w_key).astype(jnp.bfloat16)
    value_local = product(normed_self, w_value).astype(jnp.bfloat16)
    keys_all, values_all = (
        lax.all_gather(key_local, "shard", axis=0, tiled=True),
        lax.all_gather(value_local, "shard", axis=0, tiled=True),
    )
    key_blocks = to_blocks(keys_all, block_count)
    value_blocks = to_blocks(values_all, block_count)
    logsum_self = self_logsum(
        query_heads, query_start, query_ids, table_full, key_blocks, id_blocks, key_starts
    )
    mixed_self = self_mix(
        query_heads,
        query_start,
        query_ids,
        table_full,
        key_blocks,
        value_blocks,
        id_blocks,
        key_starts,
        logsum_self,
    )
    joined_self = join_heads(mixed_self).astype(jnp.bfloat16)
    after_self = source + product(joined_self, w_output)
    normed_cross = rms_scale(after_self, gain_cross).astype(jnp.bfloat16)
    query_cross = split_heads(product(normed_cross, c_query).astype(jnp.bfloat16))
    key_cross_local = product(memory, c_key).astype(jnp.bfloat16)
    value_cross_local = product(memory, c_value).astype(jnp.bfloat16)
    keys_cross, values_cross = (
        lax.all_gather(key_cross_local, "shard", axis=0, tiled=True),
        lax.all_gather(value_cross_local, "shard", axis=0, tiled=True),
    )
    key_cross = split_heads(keys_cross)
    value_cross = split_heads(values_cross)
    mixed_cross, logsum_cross = cross_forward(query_cross, key_cross, value_cross, cross_allowed)
    joined_cross = join_heads(mixed_cross).astype(jnp.bfloat16)
    after_cross = after_self + product(joined_cross, c_output)
    normed_feed = rms_scale(after_cross, gain_feed).astype(jnp.bfloat16)
    gate_act = product(normed_feed, w_gate)
    up_act = product(normed_feed, w_up)
    hidden = (jax.nn.gelu(gate_act, approximate=True) * up_act).astype(jnp.bfloat16)
    outcome = after_cross + product(hidden, w_down)
    fetched = (
        lax.all_gather(self_query, "shard", axis=0, tiled=True),
        lax.all_gather(self_key, "shard", axis=0, tiled=True),
        lax.all_gather(self_value, "shard", axis=0, tiled=True),
        lax.all_gather(self_output, "shard", axis=0, tiled=True),
        lax.all_gather(cross_query, "shard", axis=0, tiled=True),
        lax.all_gather(cross_key, "shard", axis=0, tiled=True),
        lax.all_gather(cross_value, "shard", axis=0, tiled=True),
        lax.all_gather(cross_output, "shard", axis=0, tiled=True),
        lax.all_gather(gate_weight, "shard", axis=0, tiled=True),
        lax.all_gather(up_weight, "shard", axis=0, tiled=True),
        lax.all_gather(down_weight, "shard", axis=0, tiled=True),
        lax.all_gather(self_gain, "shard", axis=0, tiled=True),
        lax.all_gather(cross_gain, "shard", axis=0, tiled=True),
        lax.all_gather(feed_gain, "shard", axis=0, tiled=True),
        lax.all_gather(bias_table, "shard", axis=0, tiled=True),
    )
    (
        w_query,
        w_key,
        w_value,
        w_output,
        c_query,
        c_key,
        c_value,
        c_output,
        w_gate,
        w_up,
        w_down,
        g_self,
        g_cross,
        g_feed,
        table_full,
    ) = fetched
    gain_self = g_self.astype(jnp.float32)
    gain_cross = g_cross.astype(jnp.float32)
    gain_feed = g_feed.astype(jnp.float32)
    keys_all, values_all = (
        lax.all_gather(key_local, "shard", axis=0, tiled=True),
        lax.all_gather(value_local, "shard", axis=0, tiled=True),
    )
    key_blocks = to_blocks(keys_all, block_count)
    value_blocks = to_blocks(values_all, block_count)
    grad_out = cotangent[0].astype(jnp.float32)
    grad_down_in = cotangent[0]
    d_down = product_rows(hidden, grad_down_in)
    grad_hidden = product_cols(grad_down_in, w_down)

    def activation(gate_in, up_in):
        return jax.nn.gelu(gate_in, approximate=True) * up_in

    unused, pull = jax.vjp(activation, gate_act, up_act)
    grad_gate, grad_up = pull(grad_hidden)
    grad_gate = grad_gate.astype(jnp.bfloat16)
    grad_up = grad_up.astype(jnp.bfloat16)
    d_gate = product_rows(normed_feed, grad_gate)
    d_up = product_rows(normed_feed, grad_up)
    grad_normed_feed = product_cols(grad_gate, w_gate) + product_cols(grad_up, w_up)
    unused, pull = jax.vjp(rms_scale, after_cross, gain_feed)
    norm_part, d_feed_gain = pull(grad_normed_feed)
    grad_cross_total = grad_out + norm_part
    grad_cross_in = grad_cross_total.astype(jnp.bfloat16)
    d_c_output = product_rows(joined_cross, grad_cross_in)
    grad_mixed_cross = split_heads(product_cols(grad_cross_in, c_output).astype(jnp.bfloat16))
    grad_query_cross, grad_keys_cross, grad_values_cross = cross_backward(
        query_cross, key_cross, value_cross, cross_allowed, logsum_cross, grad_mixed_cross
    )
    grad_query_cross = grad_query_cross.astype(jnp.bfloat16)
    key_part, value_part = (
        lax.psum_scatter(
            grad_keys_cross.astype(jnp.bfloat16), "shard", scatter_dimension=0, tiled=True
        ).astype(jnp.float32),
        lax.psum_scatter(
            grad_values_cross.astype(jnp.bfloat16), "shard", scatter_dimension=0, tiled=True
        ).astype(jnp.float32),
    )
    grad_key_cross = key_part.astype(jnp.bfloat16)
    grad_value_cross = value_part.astype(jnp.bfloat16)
    d_c_query = product_rows(normed_cross, grad_query_cross)
    d_c_key = product_rows(memory, grad_key_cross)
    d_c_value = product_rows(memory, grad_value_cross)
    grad_memory = product_cols(grad_key_cross, c_key) + product_cols(grad_value_cross, c_value)
    grad_normed_cross = product_cols(grad_query_cross, c_query)
    unused, pull = jax.vjp(rms_scale, after_self, gain_cross)
    norm_part, d_cross_gain = pull(grad_normed_cross)
    grad_self_total = grad_cross_total + norm_part
    grad_self_in = grad_self_total.astype(jnp.bfloat16)
    d_output = product_rows(joined_self, grad_self_in)
    grad_mixed_self = split_heads(product_cols(grad_self_in, w_output).astype(jnp.bfloat16))
    grad_queries, d_table, grad_keys_full, grad_values_full = self_backward(
        query_heads,
        query_start,
        query_ids,
        table_full,
        key_blocks,
        value_blocks,
        id_blocks,
        key_starts,
        logsum_self,
        grad_mixed_self,
    )
    grad_query_self = grad_queries.astype(jnp.bfloat16)
    key_part, value_part = (
        lax.psum_scatter(
            grad_keys_full.astype(jnp.bfloat16), "shard", scatter_dimension=0, tiled=True
        ).astype(jnp.float32),
        lax.psum_scatter(
            grad_values_full.astype(jnp.bfloat16), "shard", scatter_dimension=0, tiled=True
        ).astype(jnp.float32),
    )
    grad_key_self = key_part.astype(jnp.bfloat16)
    grad_value_self = value_part.astype(jnp.bfloat16)
    d_query = product_rows(normed_self, grad_query_self)
    d_key = product_rows(normed_self, grad_key_self)
    d_value = product_rows(normed_self, grad_value_self)
    grad_normed_self = (
        product_cols(grad_query_self, w_query)
        + product_cols(grad_key_self, w_key)
        + product_cols(grad_value_self, w_value)
    )
    unused, pull = jax.vjp(rms_scale, source, gain_self)
    norm_part, d_self_gain = pull(grad_normed_self)
    grad_source = grad_self_total + norm_part
    summed = (
        lax.psum_scatter(
            d_query.astype(jnp.bfloat16), "shard", scatter_dimension=0, tiled=True
        ).astype(jnp.float32),
        lax.psum_scatter(
            d_key.astype(jnp.bfloat16), "shard", scatter_dimension=0, tiled=True
        ).astype(jnp.float32),
        lax.psum_scatter(
            d_value.astype(jnp.bfloat16), "shard", scatter_dimension=0, tiled=True
        ).astype(jnp.float32),
        lax.psum_scatter(
            d_output.astype(jnp.bfloat16), "shard", scatter_dimension=0, tiled=True
        ).astype(jnp.float32),
        lax.psum_scatter(
            d_c_query.astype(jnp.bfloat16), "shard", scatter_dimension=0, tiled=True
        ).astype(jnp.float32),
        lax.psum_scatter(
            d_c_key.astype(jnp.bfloat16), "shard", scatter_dimension=0, tiled=True
        ).astype(jnp.float32),
        lax.psum_scatter(
            d_c_value.astype(jnp.bfloat16), "shard", scatter_dimension=0, tiled=True
        ).astype(jnp.float32),
        lax.psum_scatter(
            d_c_output.astype(jnp.bfloat16), "shard", scatter_dimension=0, tiled=True
        ).astype(jnp.float32),
        lax.psum_scatter(
            d_gate.astype(jnp.bfloat16), "shard", scatter_dimension=0, tiled=True
        ).astype(jnp.float32),
        lax.psum_scatter(
            d_up.astype(jnp.bfloat16), "shard", scatter_dimension=0, tiled=True
        ).astype(jnp.float32),
        lax.psum_scatter(
            d_down.astype(jnp.bfloat16), "shard", scatter_dimension=0, tiled=True
        ).astype(jnp.float32),
        lax.psum_scatter(
            d_self_gain.astype(jnp.bfloat16), "shard", scatter_dimension=0, tiled=True
        ).astype(jnp.float32),
        lax.psum_scatter(
            d_cross_gain.astype(jnp.bfloat16), "shard", scatter_dimension=0, tiled=True
        ).astype(jnp.float32),
        lax.psum_scatter(
            d_feed_gain.astype(jnp.bfloat16), "shard", scatter_dimension=0, tiled=True
        ).astype(jnp.float32),
        lax.psum_scatter(
            d_table.astype(jnp.bfloat16), "shard", scatter_dimension=0, tiled=True
        ).astype(jnp.float32),
    )
    totals = (
        lax.psum(summed[0].astype(jnp.bfloat16), "rep").astype(jnp.float32),
        lax.psum(summed[1].astype(jnp.bfloat16), "rep").astype(jnp.float32),
        lax.psum(summed[2].astype(jnp.bfloat16), "rep").astype(jnp.float32),
        lax.psum(summed[3].astype(jnp.bfloat16), "rep").astype(jnp.float32),
        lax.psum(summed[4].astype(jnp.bfloat16), "rep").astype(jnp.float32),
        lax.psum(summed[5].astype(jnp.bfloat16), "rep").astype(jnp.float32),
        lax.psum(summed[6].astype(jnp.bfloat16), "rep").astype(jnp.float32),
        lax.psum(summed[7].astype(jnp.bfloat16), "rep").astype(jnp.float32),
        lax.psum(summed[8].astype(jnp.bfloat16), "rep").astype(jnp.float32),
        lax.psum(summed[9].astype(jnp.bfloat16), "rep").astype(jnp.float32),
        lax.psum(summed[10].astype(jnp.bfloat16), "rep").astype(jnp.float32),
        lax.psum(summed[11].astype(jnp.bfloat16), "rep").astype(jnp.float32),
        lax.psum(summed[12].astype(jnp.bfloat16), "rep").astype(jnp.float32),
        lax.psum(summed[13].astype(jnp.bfloat16), "rep").astype(jnp.float32),
        lax.psum(summed[14].astype(jnp.bfloat16), "rep").astype(jnp.float32),
    )
    return (
        outcome.astype(jnp.bfloat16)[None],
        grad_source[None],
        grad_memory[None],
        totals[0],
        totals[1],
        totals[2],
        totals[3],
        totals[4],
        totals[5],
        totals[6],
        totals[7],
        totals[8],
        totals[9],
        totals[10],
        totals[11],
        totals[12],
        totals[13],
        totals[14],
    )


def swap(value, axis, size, step):
    return lax.ppermute(value, axis, [(place, place ^ step) for place in range(size)])


def after(value, *others):
    return lax.optimization_barrier((value, *others))[0]


def run_kernel(name, body, ids, operands, results, scratch=()):
    whole = pl.BlockSpec(memory_space=pltpu.VMEM)
    return pl.pallas_call(
        body,
        out_shape=[jax.ShapeDtypeStruct(shape, kind) for shape, kind in results],
        in_specs=[pl.BlockSpec(memory_space=pltpu.SMEM)] + [whole] * len(operands),
        out_specs=[whole] * len(results),
        scratch_shapes=[pltpu.VMEM(shape, kind) for shape, kind in scratch],
        name=name,
    )(ids, *operands)


low_kind = jnp.bfloat16
full_kind = jnp.float32


def rows_at(place, size):
    return pl.ds(pl.multiple_of(place * size, size), size)


def put_blocks(index, blocks, target):
    size = blocks[0].shape[0]
    for step, block in enumerate(blocks):
        target[rows_at(index ^ step, size), :] = block[...]


def split_cores(index, partial, room, send, keep):
    core = index & 1
    size = send.shape[0]
    room[...] = partial
    keep[...] = room[rows_at(core, size), :]
    send[...] = room[rows_at(1 - core, size), :].astype(low_kind)


def join_cores(index, own, other, room):
    core = index & 1
    size = own.shape[0]
    room[rows_at(core, size), :] = own[...].astype(full_kind)
    room[rows_at(1 - core, size), :] = other[...].astype(full_kind)
    return room[...]


def inverse_rms(values):
    return lax.rsqrt(jnp.mean(values * values, axis=-1, keepdims=True) + epsilon)


def norm_backward(grad, values, gain):
    scale = inverse_rms(values)
    row = jnp.sum(grad * values * scale, axis=0, keepdims=True)
    scaled = grad * gain
    inner = jnp.mean(scaled * values, axis=-1, keepdims=True)
    return scale * scaled - values * (scale * scale * scale * inner), row


def bucket_rows(buckets, length):
    lanes = lax.broadcasted_iota(jnp.int32, (buckets, length), 1)
    distance = jnp.where(lanes == 0, 0, length - lanes)
    return (bucket_of(distance) == lax.broadcasted_iota(jnp.int32, (buckets, length), 0)).astype(
        full_kind
    )


def columns_body(ids, *refs):
    count = len(refs) - 4
    sources, targets = refs[:count], refs[count:]
    for place in range(4):

        @pl.when(ids[0] == place)
        def _():
            for step in range(4):
                start = 0
                for source in sources:
                    width = source.shape[1] // 4
                    begin = (place ^ step) * width
                    targets[step][:, start : start + width] = source[:, begin : begin + width]
                    start += width


def pack_body(ids, source, gain0, gain1, gain2, table, *refs):
    sources, packed, targets = refs[:3], refs[3], refs[4:]
    columns_body(ids, *sources, *targets)
    size, model = source.shape
    packed[:size, :] = source[...]
    rows = table.shape[0]
    line = [gain[...].astype(full_kind).reshape(1, -1) for gain in (gain0, gain1, gain2)]
    width = sum(piece.shape[1] for piece in line)
    line = jnp.concatenate(line + [jnp.zeros((1, model - width), full_kind)], axis=1)
    grid = jnp.concatenate(
        [table[...].astype(full_kind), jnp.zeros((rows, model - table.shape[1]), full_kind)], axis=1
    )
    lines = jnp.concatenate([line, jnp.zeros((7, model), full_kind), grid], axis=0)
    packed[size:, :] = lines.astype(low_kind)


def split_columns_body(ids, gate, up, own, send1, send2, send3):
    column = ids[1] & 1
    width = gate.shape[1] // 4
    half = send2.shape[0]
    for place in range(4):

        @pl.when(ids[0] == place)
        def _():
            for step, target in enumerate((own, send1, send2, send3)):
                begin = (place ^ step) * width
                rows = slice(None) if step < 2 else rows_at(column, half)
                for number, source in enumerate((gate, up)):
                    target[:, number * width : (number + 1) * width] = source[
                        rows, begin : begin + width
                    ]


def heads_of(matrix, number, part, wide):
    start = part * wide + number * HEAD_DIM
    return matrix[:, start : start + HEAD_DIM]


def softmax_rows(scores, allowed):
    scores = jnp.where(allowed, scores, masked_score)
    powers = jnp.exp(scores - jnp.max(scores, axis=-1, keepdims=True))
    return powers * (1.0 / jnp.sum(powers, axis=-1, keepdims=True))


def self_half(half, ids, source, weight, gains, rows, mapped_before, output, seg_col, seg_row, outs):
    normed_out, mapped_out, chances_out, mixed_out, send, keep, room = outs
    size = normed_out.shape[0]
    wide = output.shape[0]
    normed = (source * inverse_rms(source) * gains[0:1, :]).astype(low_kind)
    normed_out[...] = normed
    mapped = product(normed, weight).astype(low_kind)
    mapped_out[...] = mapped
    every = mapped if half == 0 else jnp.concatenate([mapped_before, mapped], axis=0)
    keys = every.shape[0]
    places = lax.broadcasted_iota(jnp.int32, (size, keys), 0) + half * size
    others = lax.broadcasted_iota(jnp.int32, (size, keys), 1)
    allowed = (places >= others) & (seg_col == seg_row[:, :keys])
    mixed = []
    for number in range(wide // HEAD_DIM):
        line = jnp.broadcast_to(rows[number : number + 1, :], (size, rows.shape[1]))
        bias = pltpu.roll(line, half * size, 1, stride=1, stride_axis=0)[:, :keys]
        scores = product_cols(heads_of(mapped, number, 0, wide), heads_of(every, number, 1, wide))
        chances = softmax_rows(scores + bias, allowed).astype(low_kind)
        chances_out[number] = chances
        mixed.append(product(chances, heads_of(every, number, 2, wide)))
    mixed = jnp.concatenate(mixed, axis=1).astype(low_kind)
    mixed_out[...] = mixed
    split_cores(ids[0], product(mixed, output), room, send, keep)


def self_first_body(
    ids, x0, x1, x2, x3, w0, w1, w2, w3, output, seg_col, seg_row,
    source_out, weight_out, gains_out, rows_out,
    normed_out, mapped_out, chances_out, mixed_out, send, keep,
    room, small, lines,
):
    index = ids[0]
    tokens = source_out.shape[0] // 4
    put_blocks(index, [block.at[:tokens] for block in (x0, x1, x2, x3)], source_out)
    put_blocks(index, (w0, w1, w2, w3), weight_out)
    for step, block in enumerate((x0, x1, x2, x3)):
        small[rows_at(index ^ step, 16), :] = block[tokens:, :].astype(full_kind)
    model = source_out.shape[1]
    part = model // 4
    for place in range(3):
        gains_out[place : place + 1, :] = jnp.concatenate(
            [small[16 * t : 16 * t + 1, part * place : part * (place + 1)] for t in range(4)],
            axis=1,
        )
    gains_out[3:8, :] = jnp.zeros((5, model), full_kind)
    table = jnp.concatenate([small[16 * t + 8 : 16 * t + 16, :128] for t in range(4)], axis=0)
    hot = bucket_rows(table.shape[0], rows_out.shape[1])
    lines[...] = product_rows(table.astype(low_kind), hot.astype(low_kind))
    heads_here = chances_out.shape[0]
    for number in range(heads_here):
        rows_out[number : number + 1, :] = lines[pl.ds(index * heads_here + number, 1), :]
    rows_out[heads_here:8, :] = jnp.zeros((8 - heads_here, rows_out.shape[1]), full_kind)
    size = normed_out.shape[0]
    self_half(
        0, ids, source_out[:size, :].astype(full_kind), weight_out[...], gains_out, rows_out, None,
        output[...], seg_col[:size, :], seg_row[...],
        (normed_out, mapped_out, chances_out, mixed_out, send, keep, room),
    )


def self_second_body(
    ids, source, weight, gains, rows, mapped_before, output, seg_col, seg_row,
    normed_out, mapped_out, chances_out, mixed_out, send, keep, room,
):
    size = normed_out.shape[0]
    self_half(
        1, ids, source[size:, :].astype(full_kind), weight[...], gains, rows, mapped_before[...],
        output[...], seg_col[size:, :], seg_row[...],
        (normed_out, mapped_out, chances_out, mixed_out, send, keep, room),
    )


def cross_keys_body(ids, e0, e1, e2, e3, w0, w1, w2, w3, memory_out, weight_out, mapped_out):
    put_blocks(ids[0], (e0, e1, e2, e3), memory_out)
    put_blocks(ids[0], (w0, w1, w2, w3), weight_out)
    wide = weight_out.shape[1] // 3
    mapped_out[...] = product(memory_out[...], weight_out[:, wide:]).astype(low_kind)


def cross_body(
    half, ids, source, own, other, gains, weight, mapped, output, seg_col, enc_row,
    after_out, normed_out, query_out, chances_out, mixed_out, send, keep, room,
):
    size = after_out.shape[0]
    wide = output.shape[0]
    start = half * size
    values = source[start : start + size, :].astype(full_kind) + join_cores(
        ids[0], own, other, room
    )
    after_out[...] = values
    normed = (values * inverse_rms(values) * gains[1:2, :]).astype(low_kind)
    normed_out[...] = normed
    query = product(normed, weight[:, :wide]).astype(low_kind)
    query_out[...] = query
    allowed = seg_col[start : start + size, :] == enc_row[...]
    every = mapped[...]
    mixed = []
    for number in range(wide // HEAD_DIM):
        scores = product_cols(heads_of(query, number, 0, wide), heads_of(every, number, 0, wide))
        chances = softmax_rows(scores, allowed).astype(low_kind)
        chances_out[number] = chances
        mixed.append(product(chances, heads_of(every, number, 1, wide)))
    mixed = jnp.concatenate(mixed, axis=1).astype(low_kind)
    mixed_out[...] = mixed
    split_cores(ids[0], product(mixed, output[...]), room, send, keep)


def feed_join_body(ids, w0, w1, w2, w2x, w3, w3x, g0, g1, g2, g3, weight_out, grad_out):
    index, column = ids[0], ids[1] & 1
    put_blocks(index, (w0, w1), weight_out)
    half = w2.shape[0]
    for step, mine, other in ((2, w2, w2x), (3, w3, w3x)):
        weight_out[rows_at(2 * (index ^ step) + column, half), :] = mine[...]
        weight_out[rows_at(2 * (index ^ step) + 1 - column, half), :] = other[...]
    put_blocks(ids[0], (g0, g1, g2, g3), grad_out)


def feed_body(half, ids, before, own, other, gains, weight, down, grad_out, *refs):
    parts = refs[:2] if half else ()
    after_out, normed_out, hidden_out, acts_out, *rest = refs[len(parts) :]
    size = after_out.shape[0]
    start = half * size
    units = down.shape[0]
    room = rest[-1]
    values = before[...] + join_cores(ids[0], own, other, room)
    after_out[...] = values
    normed = (values * inverse_rms(values) * gains[2:3, :]).astype(low_kind)
    normed_out[...] = normed
    acts = product(normed, weight[...])
    gate, up = acts[:, :units], acts[:, units:]
    root = math.sqrt(2 / math.pi)
    square = gate * gate
    bend = jnp.tanh(root * gate * (1.0 + 0.044715 * square))
    curve = 0.5 * gate * (1.0 + bend)
    slope = 0.5 * (1.0 + bend) + 0.5 * gate * (1.0 - bend * bend) * root * (
        1.0 + 3 * 0.044715 * square
    )
    hidden = (curve * up).astype(low_kind)
    hidden_out[...] = hidden
    grad_hidden = product_cols(grad_out[start : start + size, :], down[...])
    acts_out[:, :units] = (grad_hidden * up * slope).astype(low_kind)
    acts_out[:, units:] = (grad_hidden * curve).astype(low_kind)
    grad = product_cols(acts_out[...], weight[...])
    result = product(hidden, down[...])
    if half:
        send, keep, out_send, out_keep = rest[:4]
        for place, part in ((0, parts[0][...]), (1, grad)):
            split_cores(ids[0], part, room, send.at[place], keep.at[place])
        for place, part in ((0, parts[1][...]), (1, result)):
            split_cores(ids[0], part, room, out_send.at[place], out_keep.at[place])
    else:
        rest[0][...] = grad
        rest[1][...] = result


def rep_bits(ids):
    rep = ids[1]
    return rep & 1, (rep >> 1) & 1, rep >> 2


def chunk_targets(ids, keep_first, send_first, keep_second, send_second):
    column, low, unused = rep_bits(ids)
    for slot in range(4):
        high, middle = slot >> 1, slot & 1
        for target, bit in ((keep_first, column), (send_first, 1 - column)):
            yield target.at[slot], 4 * high + 2 * middle + bit, 0
        for target, bit in ((keep_second, low), (send_second, 1 - low)):
            yield target.at[slot], 4 * high + 2 * bit + middle, 1


def feed_weights_body(
    ids, normed0, normed1, acts0, acts1, hidden0, hidden1, grad_out,
    keep_first, send_first, keep_second, send_second, feed, down,
):
    size = normed0.shape[0]
    feed[...] = (
        product_rows(normed0[...], acts0[...]) + product_rows(normed1[...], acts1[...])
    ).astype(low_kind)
    down[...] = (
        product_rows(hidden0[...], grad_out[:size, :])
        + product_rows(hidden1[...], grad_out[size:, :])
    ).astype(low_kind)
    rows = feed.shape[0] // 4
    width = feed.shape[1] // 8
    small = down.shape[0] // 8
    lanes = down.shape[1] // 2
    for target, chunk, part in chunk_targets(ids, keep_first, send_first, keep_second, send_second):
        for place in range(2):
            start = (2 * part + place) * rows
            target[place] = feed[start : start + rows, rows_at(chunk, width)]
        for piece in range(lanes // width):
            start = part * lanes + piece * width
            target[2, piece * small : (piece + 1) * small, :] = down[
                rows_at(chunk, small), start : start + width
            ]


def store_small_chunks(ids, columns, output, buffers):
    small = output.shape[0] // 8
    lanes = output.shape[1] // 2
    quarter = columns.shape[0] // 4
    for target, chunk, part in chunk_targets(ids, *buffers):
        for place in range(2):
            start = (2 * part + place) * quarter + chunk * small
            target[place] = columns[pl.ds(pl.multiple_of(start, 8), small), :].astype(low_kind)
        target[2] = jnp.zeros(target.shape[1:], low_kind)
        target[2, :, :lanes] = output[
            pl.ds(pl.multiple_of(chunk * small, 8), small), part * lanes : (part + 1) * lanes
        ].astype(low_kind)


small_lanes = slice(3 * 128, 4 * 128)


def small_pieces(count, size):
    half = (count - size) // 2
    yield (0, 0), slice(0, size)
    yield (0, 1), slice(size, size + half)
    yield (1, 0), slice(size + half, count)


def halve_body(ids, keep_first, came_first, keep_second, came_second, *outs):
    new_first, send_first, new_second, send_second = outs
    column, low, unused = rep_bits(ids)
    for keep, came, new, send, bit in (
        (keep_first, came_first, new_first, send_first, low),
        (keep_second, came_second, new_second, send_second, column),
    ):
        for high in range(2):
            for target, place in ((new, 2 * high + bit), (send, 2 * high + 1 - bit)):
                total = keep[place].astype(full_kind) + came[place].astype(full_kind)
                target[high] = total.astype(target.dtype)


def quarter_body(ids, keep_first, came_first, keep_second, came_second, total):
    for part, (keep, came) in enumerate(((keep_first, came_first), (keep_second, came_second))):
        total[part] = (keep[...] + came[...].astype(full_kind)).astype(low_kind)


def quarter_small_body(
    ids, keep_first, came_first, keep_second, came_second, vector, near, far, across, total
):
    quarter_body(ids, keep_first, came_first, keep_second, came_second, total)
    lines = (vector[...] + near[...] + far[...] + across[...]).astype(low_kind)
    for (part, high), piece in small_pieces(lines.shape[0], total.shape[3]):
        total[part, high, 2, : piece.stop - piece.start, small_lanes] = lines[piece, :]


def trade_body(ids, mine, came, own, send1, send2, send3, rows, room):
    for part in range(2):
        for high in range(2):
            total = (
                mine[part, high].astype(full_kind) + came[part, high].astype(full_kind)
            ).astype(low_kind)
            room[2 * part, high] = total[0]
            room[2 * part + 1, high] = total[1]
            rows[part, high] = total[2]
    for step, target in enumerate((own, send1, send2, send3)):
        target[...] = room[ids[0] ^ step]


def gather_body(ids, own, came1, came2, came3, rows, first, second):
    for place, block in enumerate((own, came1, came2)):
        first[:, place] = block[...]
    for place, block in enumerate((came3, rows.at[0], rows.at[1])):
        second[:, place] = block[...]


def all_pieces(ids, firsts, seconds):
    for step in range(4):
        for high in range(2):
            chunk = 4 * high + ((ids[1] & 3) ^ step)
            yield firsts[step].at[high], seconds[step].at[high], high, chunk


def feed_out_body(ids, *refs):
    firsts, seconds, (gate, up, down) = refs[:4], refs[4:8], refs[8:]
    units = gate.shape[1] // 4
    small = down.shape[0] // 8
    for first, second, high, chunk in all_pieces(ids, firsts, seconds):
        width = first.shape[2]
        target = (gate, up)[high]
        for step in range(4):
            block = second[0] if step == 3 else first[step]
            start = (ids[0] ^ step) * units + (chunk & 3) * width
            target[:, pl.ds(pl.multiple_of(start, width), width)] = block.astype(full_kind)
        for piece in range(down.shape[1] // width):
            part, begin = piece // 3, piece % 3 * small
            down[rows_at(chunk, small), piece * width : (piece + 1) * width] = second[
                1 + part, begin : begin + small
            ].astype(full_kind)


def small_out_body(ids, *refs):
    firsts, seconds, outs, room = refs[:4], refs[4:8], refs[8:12], refs[-1]
    small = room.shape[1] // 8
    lanes = outs[3].shape[1] // 2
    wide = outs[0].shape[0]
    for first, second, high, chunk in all_pieces(ids, firsts, seconds):
        where = pl.ds(pl.multiple_of(chunk * small, 8), small)
        for step in range(4):
            block = second[0] if step == 3 else first[step]
            room[step, where, :] = block.astype(full_kind)
        for part in range(2):
            outs[3][where, part * lanes : (part + 1) * lanes] = second[1 + part][:, :lanes].astype(
                full_kind
            )
    for place in range(4):
        for number in range(3):
            outs[number][:, place * wide : (place + 1) * wide] = room[
                ids[0] ^ place, :, number * wide : (number + 1) * wide
            ]


def last_out_body(ids, *refs):
    *refs, vector, room, lines = refs
    small_out_body(ids, *refs, room)
    seconds = refs[4:8]
    for step, second in enumerate(seconds):
        place = (ids[1] & 3) ^ step
        for (part, high), piece in small_pieces(vector.shape[0], second.shape[2]):
            lines[place, piece, :] = second[
                high, 1 + part, : piece.stop - piece.start, small_lanes
            ].astype(full_kind)
    vector[...] = (lines[0] + lines[1]) + (lines[2] + lines[3])


def attention_backward(grads, query, keys, values, chances, number):
    wide = grads.shape[1]
    grad = heads_of(grads, number, 0, wide)
    full = chances.astype(full_kind)
    grad_chances = product_cols(grad, heads_of(values, number, 0, wide))
    grad_scores = full * (grad_chances - jnp.sum(full * grad_chances, axis=-1, keepdims=True))
    rounded = grad_scores.astype(low_kind)
    return (
        grad_scores,
        product(rounded, heads_of(keys, number, 0, wide)).astype(low_kind),
        product_rows(rounded, heads_of(query, number, 0, wide)),
        product_rows(chances, grad),
    )


def join_halves(index, own, other, room):
    core = index & 1
    size = own.shape[1]
    for chip in range(2):
        room[rows_at(core + 2 * chip, size), :] = own[chip].astype(full_kind)
        room[rows_at(1 - core + 2 * chip, size), :] = other[chip].astype(full_kind)
    return room[...]


def cross_back_body(
    ids, grad_out, own, other, values0, values1, gains, output, query0, query1, chances0, chances1,
    mapped, weight, total_out, low_out, query_out, sums_out, row_out, send, keep, room,
):
    wide = output.shape[0]
    join_halves(ids[0], own, other, room)
    size = values0.shape[0]
    row = 0.0
    for half, values in ((0, values0), (1, values1)):
        part = slice(half * size, (half + 1) * size)
        grad, piece = norm_backward(room[part, :], values[...], gains[2:3, :])
        row = row + piece
        total = grad_out[part, :].astype(full_kind) + grad
        total_out[part, :] = total
        low_out[part, :] = total.astype(low_kind)
    row_out[...] = jnp.broadcast_to(row, row_out.shape)
    grad_mixed = product_cols(low_out[...], output[...]).astype(low_kind)
    every = mapped[...]
    query = jnp.concatenate([query0[...], query1[...]], axis=0)
    keys, values = [], []
    for number in range(wide // HEAD_DIM):
        chances = jnp.concatenate([chances0[number], chances1[number]], axis=0)
        unused, grad_query, grad_keys, grad_values = attention_backward(
            grad_mixed, query, every[:, :wide], every[:, wide:], chances, number
        )
        query_out[:, number * HEAD_DIM : (number + 1) * HEAD_DIM] = grad_query
        keys.append(grad_keys)
        values.append(grad_values)
    sums_out[...] = jnp.concatenate(keys + values, axis=1).astype(low_kind)
    scatter_cores(ids[0], product_cols(query_out[...], weight[:, :wide]), room, send, keep)


def cross_weights_body(
    ids, normed0, normed1, query, memory, sums, mixed0, mixed1, low, weight,
    keep_first, send_first, keep_second, send_second, send, keep, room, columns, output,
):
    wide = query.shape[1]
    size = normed0.shape[0]
    columns[:, :wide] = product_rows(normed0[...], query[:size, :]) + product_rows(
        normed1[...], query[size:, :]
    )
    columns[:, wide:] = product_rows(memory[...], sums[...])
    output[...] = product_rows(mixed0[...], low[:size, :]) + product_rows(mixed1[...], low[size:, :])
    store_small_chunks(ids, columns, output, (keep_first, send_first, keep_second, send_second))
    scatter_cores(ids[0], product_cols(sums[...], weight[:, wide:]), room, send, keep)


def scatter_cores(index, partial, room, send, keep):
    core = index & 1
    size = send.shape[1]
    room[...] = partial
    for chip in range(2):
        keep[chip] = room[rows_at(core + 2 * chip, size), :]
        send[chip] = room[rows_at(1 - core + 2 * chip, size), :].astype(low_kind)


def diagonal_sums(matrix):
    width = matrix.shape[1]
    size = matrix.shape[0]
    while size > 1:
        size //= 2
        matrix = matrix[:size] + pltpu.roll(matrix[size:], width - size, 1)
    return matrix


def self_back_body(
    ids, total, own, other, values0, values1, gains, output, mapped0, mapped1, chances0, chances1,
    total_out, low_out, query_out, sums_out, row_out, table_out, room,
):
    wide = output.shape[0]
    join_halves(ids[0], own, other, room)
    size = values0.shape[0]
    row = 0.0
    for half, values in ((0, values0), (1, values1)):
        part = slice(half * size, (half + 1) * size)
        grad, piece = norm_backward(room[part, :], values[...], gains[1:2, :])
        row = row + piece
        new_total = total[part, :] + grad
        total_out[part, :] = new_total
        low_out[part, :] = new_total.astype(low_kind)
    row_out[...] = jnp.broadcast_to(row, row_out.shape)
    grad_mixed = product_cols(low_out[...], output[...]).astype(low_kind)
    buckets = table_out.shape[0]
    hot = bucket_rows(buckets, 2 * size)
    every = jnp.concatenate([mapped0[...], mapped1[...]], axis=0)
    keys, values, columns = [], [], []
    for number in range(wide // HEAD_DIM):
        line = None
        for half, chances in ((1, chances1), (0, chances0)):
            part = slice(half * size, (half + 1) * size)
            seen = slice(0, (half + 1) * size)
            grad_scores, grad_query, grad_keys, grad_values = attention_backward(
                grad_mixed[part], every[part, :wide], every[seen, wide : 2 * wide],
                every[seen, 2 * wide :], chances[number], number,
            )
            query_out[part, number * HEAD_DIM : (number + 1) * HEAD_DIM] = grad_query
            if half:
                line = pltpu.roll(diagonal_sums(grad_scores), size, 1)
                keys.append(grad_keys)
                values.append(grad_values)
            else:
                empty = jnp.zeros((size, size), full_kind)
                line = line + diagonal_sums(jnp.concatenate([grad_scores, empty], axis=1))
                keys[-1] = jnp.concatenate([keys[-1][:size] + grad_keys, keys[-1][size:]], axis=0)
                values[-1] = jnp.concatenate(
                    [values[-1][:size] + grad_values, values[-1][size:]], axis=0
                )
        columns.append(jnp.sum(hot * line, axis=1, keepdims=True))
    sums_out[...] = jnp.concatenate(keys + values, axis=1).astype(low_kind)
    columns.append(jnp.zeros((buckets, 128 - len(columns)), full_kind))
    table_out[...] = jnp.concatenate(columns, axis=1)


def self_weights_body(
    ids, normed0, normed1, query, sums, mixed0, mixed1, low, weight,
    keep_first, send_first, keep_second, send_second, send, keep, room, columns, output, merged,
):
    wide = query.shape[1]
    size = normed0.shape[0]
    merged[:, :wide] = query[...]
    merged[:, wide:] = sums[...]
    columns[...] = product_rows(normed0[...], merged[:size, :]) + product_rows(
        normed1[...], merged[size:, :]
    )
    output[...] = product_rows(mixed0[...], low[:size, :]) + product_rows(mixed1[...], low[size:, :])
    store_small_chunks(ids, columns, output, (keep_first, send_first, keep_second, send_second))
    scatter_cores(ids[0], product_cols(merged[...], weight[...]), room, send, keep)


def finish_body(ids, source, mine, far, gains, total, cross_row, feed_row, table, grad_out, vector):
    index = ids[0]
    size, model = source.shape
    grad, row = norm_backward(
        mine[...] + far[...].astype(full_kind), source[...].astype(full_kind), gains[0:1, :]
    )
    grad_out[...] = total[rows_at(index, size), :] + grad
    lanes = lax.broadcasted_iota(jnp.int32, (1, model), 1)
    part = model // 4
    here = (lanes >= index * part) & (lanes < (index + 1) * part)
    pieces = []
    for line in (row, jnp.where(here, cross_row[0:1, :], 0.0), jnp.where(here, feed_row[0:1, :], 0.0)):
        pieces += [line[:, start : start + 128] for start in range(0, model, 128)]
    pieces += [jnp.zeros((-len(pieces) % 8, 128), full_kind)]
    vector[: vector.shape[0] - table.shape[0], :] = jnp.concatenate(pieces, axis=0)
    vector[vector.shape[0] - table.shape[0] :, :] = pltpu.roll(
        table[...], index * (HEADS // 4), 1
    )


def chip_pair_body(ids, keep, arrived, mine, other):
    chip = ids[0] >> 1
    mine[...] = keep[chip] + arrived[chip].astype(full_kind)
    other[...] = (keep[1 - chip] + arrived[1 - chip].astype(full_kind)).astype(low_kind)


class Kernels:
    def __init__(self, ids):
        self.ids = ids

    def __call__(self, name, body, operands, results, scratch=(), cover=()):
        outs = run_kernel(name, body, self.ids, operands, results, scratch)
        if cover:
            outs = after(tuple(outs), *cover)
        self.ids = after(self.ids, outs[0])
        return outs

    def wait(self, *values):
        self.ids = after(self.ids, *values)


def rep_swap(value, step):
    return swap(value, "rep", 8, step)


def shard_swap(value, step):
    return swap(value, "shard", 4, step)


class Reduction:
    def __init__(self, call, name, buffers):
        self.call, self.name = call, name
        self.keeps = (buffers[0], buffers[2])
        self.came = (rep_swap(buffers[1], 1), rep_swap(buffers[3], 2))
        self.shape = buffers[0].shape[1:]

    def halve(self, cover=()):
        results = []
        for unused in range(2):
            results += [((2,) + self.shape, full_kind), ((2,) + self.shape, low_kind)]
        outs = self.call(
            self.name + "_halve",
            halve_body,
            (self.keeps[0], self.came[0], self.keeps[1], self.came[1]),
            results,
            cover=cover,
        )
        self.keeps = (outs[0], outs[2])
        self.came = (rep_swap(outs[1], 2), rep_swap(outs[3], 1))

    def quarter(self, cover=(), vectors=()):
        (self.total,) = self.call(
            self.name + "_quarter",
            quarter_small_body if vectors else quarter_body,
            (self.keeps[0], self.came[0], self.keeps[1], self.came[1]) + vectors,
            [((2, 2) + self.shape, low_kind)],
            cover=cover,
        )
        self.last = rep_swap(self.total, 4)

    def trade(self, cover=()):
        block = self.shape[1:]
        own, *sends, self.rows = self.call(
            self.name + "_trade",
            trade_body,
            (self.total, self.last),
            [((2,) + block, low_kind)] * 4 + [((2, 2) + block, low_kind)],
            [((4, 2) + block, low_kind)],
            cover=cover,
        )
        self.blocks = [own] + [shard_swap(send, step) for step, send in zip((1, 2, 3), sends)]

    def gather(self, cover=()):
        first, second = self.call(
            self.name + "_gather",
            gather_body,
            (*self.blocks, self.rows),
            [((2,) + self.shape, low_kind)] * 2,
            cover=cover,
        )
        first_far, second_far = rep_swap(first, 2), rep_swap(second, 1)
        self.far = (first_far, second_far)
        self.near = (rep_swap(first, 1), rep_swap(second, 2))
        self.firsts = (first, self.near[0], first_far, rep_swap(first_far, 1))
        self.seconds = (second, second_far, self.near[1], rep_swap(second_far, 2))

    def finish(self, body, results, scratch=(), cover=()):
        return self.call(
            self.name + "_out", body, (*self.firsts, *self.seconds), results, scratch, cover
        )


class GroupSum:
    def __init__(self, send, keep):
        self.keep = keep
        self.came = shard_swap(send, 1)

    def add(self):
        self.pair = (self.keep + self.came.astype(full_kind)).astype(low_kind)
        self.far = shard_swap(self.pair, 2)
        return self.pair

    def total(self):
        own = (self.pair.astype(full_kind) + self.far.astype(full_kind)).astype(low_kind)
        self.results = (own, shard_swap(own, 1))
        return own


def split_shards(
    inputs,
    encoder,
    segments,
    enc_segments,
    self_query,
    self_key,
    self_value,
    self_output,
    cross_query,
    cross_key,
    cross_value,
    cross_output,
    gate_weight,
    up_weight,
    down_weight,
    self_gain,
    cross_gain,
    feed_gain,
    bias_table,
    cotangent,
):
    index = lax.axis_index("shard")
    rep = lax.axis_index("rep")
    call = Kernels(jnp.stack([index, rep]))
    tokens_here, model = inputs.shape[1:]
    length = 4 * tokens_here
    half_size = 2 * tokens_here
    heads_here = HEADS // 4
    wide = heads_here * HEAD_DIM
    units = down_weight.shape[0]
    memory_length = enc_segments.shape[1]
    small_rows = bias_table.shape[0]
    buckets = 4 * small_rows
    part = self_gain.shape[0]

    def blocks_of(*weights):
        width = sum(weight.shape[1] for weight in weights) // 4
        shape = (weights[0].shape[0], width)
        return call("columns", columns_body, weights, [(shape, low_kind)] * 4)

    def traded(blocks):
        return [blocks[0]] + [shard_swap(blocks[step], step) for step in range(1, 4)]

    column_shape = (part, 3 * wide)
    packed, *self_blocks = call(
        "pack",
        pack_body,
        (
            inputs[0], self_gain, cross_gain, feed_gain, bias_table, self_query, self_key,
            self_value,
        ),
        [((tokens_here + 16, model), low_kind)] + [(column_shape, low_kind)] * 4,
    )
    source_far = shard_swap(packed, 2)
    self_blocks = traded(self_blocks)
    cross_blocks = blocks_of(cross_query, cross_key, cross_value)
    feed_blocks = call(
        "feed_columns",
        split_columns_body,
        (gate_weight, up_weight),
        [((part, 2 * units), low_kind)] * 2 + [((part // 2, 2 * units), low_kind)] * 2,
    )
    source_far = after(source_far, feed_blocks[0])
    source_blocks = [packed, shard_swap(packed, 1), source_far, shard_swap(source_far, 1)]
    seg_row = segments
    seg_col = segments[0][:, None]
    enc_row = enc_segments
    call.wait(seg_col, self_blocks[2], self_blocks[3])
    cross_blocks = traded(after(tuple(cross_blocks), self_blocks[2], self_blocks[3]))
    room = [((half_size, model), full_kind)]
    whole_room = [((length, model), full_kind)]
    pieces = [((tokens_here, model), low_kind), ((tokens_here, model), full_kind)]
    two_pieces = [((2,) + shape, kind) for shape, kind in pieces]

    def self_results(keys):
        return [
            ((half_size, model), low_kind),
            ((half_size, 3 * wide), low_kind),
            ((heads_here, half_size, keys), low_kind),
            ((half_size, wide), low_kind),
        ] + pieces

    source, w_self, gains, rows, *first = call(
        "self_first",
        self_first_body,
        (*source_blocks, *self_blocks, self_output, seg_col, seg_row),
        [
            ((length, model), low_kind),
            ((model, 3 * wide), low_kind),
            ((8, model), full_kind),
            ((8, length), full_kind),
        ]
        + self_results(half_size),
        room + [((64, model), full_kind), ((128, length), full_kind)],
        cover=(cross_blocks[2],),
    )
    first_sum = GroupSum(*first[4:])
    memory_far = shard_swap(after(encoder[0], first[0]), 2)
    second = call(
        "self_second",
        self_second_body,
        (source, w_self, gains, rows, first[1], self_output, seg_col, seg_row),
        self_results(length),
        room,
        cover=(cross_blocks[3], first_sum.came),
    )
    second_sum = GroupSum(*second[4:])
    call.wait(first_sum.add())
    memory_blocks = [
        encoder[0], shard_swap(encoder[0], 1), memory_far, shard_swap(memory_far, 1)
    ]
    memory, w_cross, cross_mapped = call(
        "cross_keys",
        cross_keys_body,
        (*memory_blocks, *cross_blocks),
        [
            ((memory_length, model), low_kind),
            ((model, 3 * wide), low_kind),
            ((memory_length, 2 * wide), low_kind),
        ],
        cover=(second_sum.came,),
    )
    pair = second_sum.add()
    call.wait(pair)
    first_sum.total()
    feed_blocks = after(tuple(feed_blocks), pair)
    feed_near = shard_swap(feed_blocks[1], 1)
    feed_two = shard_swap(feed_blocks[2], 2)

    def cross_call(half, sums, cover):
        own, other = sums.results
        return call(
            "cross",
            functools.partial(cross_body, half),
            (source, own, other, gains, w_cross, cross_mapped, cross_output, seg_col, enc_row),
            [
                ((half_size, model), full_kind),
                ((half_size, model), low_kind),
                ((half_size, wide), low_kind),
                ((heads_here, half_size, memory_length), low_kind),
                ((half_size, wide), low_kind),
            ]
            + pieces,
            room,
            cover=cover,
        )

    cross0 = cross_call(0, first_sum, (second_sum.far, feed_two))
    cross_first = GroupSum(*cross0[5:])
    call.wait(second_sum.total())
    feed_two_other = rep_swap(feed_two, 1)
    feed_three = shard_swap(after(feed_blocks[3], cross0[0]), 3)
    grad_far = shard_swap(after(cotangent[0], cross0[0]), 2)
    cross1 = cross_call(1, second_sum, (feed_three, feed_two_other, cross_first.came))
    cross_second = GroupSum(*cross1[5:])
    call.wait(cross_first.add())
    feed_three_other = rep_swap(feed_three, 1)
    grad_blocks = [
        cotangent[0], shard_swap(cotangent[0], 1), grad_far, shard_swap(grad_far, 1)
    ]
    w_feed, grad_out = call(
        "feed_join",
        feed_join_body,
        (
            feed_blocks[0], feed_near, feed_two, feed_two_other, feed_three, feed_three_other,
            *grad_blocks,
        ),
        [((model, 2 * units), low_kind), ((length, model), low_kind)],
        cover=(cross_second.came,),
    )
    call.wait(cross_second.add())
    cross_first.total()

    def feed_call(half, sums, before, parts, tail, cover=()):
        own, other = sums.results
        return call(
            "feed",
            functools.partial(feed_body, half),
            (before, own, other, gains, w_feed, down_weight, grad_out) + parts,
            [
                ((half_size, model), full_kind),
                ((half_size, model), low_kind),
                ((half_size, units), low_kind),
                ((half_size, 2 * units), low_kind),
            ]
            + tail,
            room,
            cover=cover,
        )

    feed0 = feed_call(0, cross_first, cross0[0], (), room * 2, (cross_second.far,))
    cross_second.total()
    feed1 = feed_call(1, cross_second, cross1[0], (feed0[4], feed0[5]), two_pieces * 2)
    feed_sum = GroupSum(*feed1[4:6])
    out_came = shard_swap(feed1[6], 1)

    chunk = (3, model // 4, 2 * units // 8)
    feed_grads = Reduction(
        call,
        "feed_grads",
        call(
            "feed_weights",
            feed_weights_body,
            (feed0[1], feed1[1], feed0[3], feed1[3], feed0[2], feed1[2], grad_out),
            [((4,) + chunk, low_kind)] * 4,
            [((model, 2 * units), low_kind), ((units, model), low_kind)],
            cover=(feed_sum.came, out_came),
        ),
    )
    call.wait(feed_sum.add())

    def scatter_pair(arrived, keep):
        mine, other = call(
            "chip_pair",
            chip_pair_body,
            (keep, arrived),
            [((tokens_here, model), full_kind), ((tokens_here, model), low_kind)],
        )
        return mine, shard_swap(other, 2)

    mine, far = scatter_pair(out_came, feed1[7])
    feed_sum.total()
    own_after = lax.dynamic_slice_in_dim(
        jnp.where(index < 2, feed0[0], feed1[0]), (index & 1) * tokens_here, tokens_here
    )
    outcome = (own_after + mine + far.astype(full_kind)).astype(low_kind)

    total_cross, low_cross, query_cross, sums_cross, row_feed, *sends = call(
        "cross_back",
        cross_back_body,
        (
            grad_out, *feed_sum.results, feed0[0], feed1[0], gains, cross_output, cross0[2], cross1[2],
            cross0[3], cross1[3], cross_mapped, w_cross,
        ),
        [
            ((length, model), full_kind),
            ((length, model), low_kind),
            ((length, wide), low_kind),
            ((memory_length, 2 * wide), low_kind),
            ((8, model), full_kind),
        ]
        + two_pieces,
        whole_room,
        cover=feed_grads.came,
    )
    cross_sum = GroupSum(*sends)
    feed_grads.halve(cover=(cross_sum.came,))
    call.wait(cross_sum.add())
    small_chunk = (3, wide // 8, 3 * wide)
    weight_room = [((model, 3 * wide), full_kind), ((wide, model), full_kind)]
    *buffers, send, keep = call(
        "cross_weights",
        cross_weights_body,
        (
            cross0[1], cross1[1], query_cross, memory, sums_cross, cross0[4], cross1[4], low_cross,
            w_cross,
        ),
        [((4,) + small_chunk, low_kind)] * 4 + two_pieces,
        whole_room + weight_room,
        cover=(cross_sum.far,) + feed_grads.came,
    )
    cross_grads = Reduction(call, "cross_grads", buffers)
    memory_came, memory_keep = shard_swap(send, 1), keep
    call.wait(cross_sum.total())
    feed_grads.quarter(cover=cross_sum.results)
    total_self, low_self, query_self, sums_self, row_cross, table = call(
        "self_back",
        self_back_body,
        (
            total_cross, *cross_sum.results, cross0[0], cross1[0], gains, self_output, first[1], second[1],
            first[2], second[2],
        ),
        [
            ((length, model), full_kind),
            ((length, model), low_kind),
            ((length, wide), low_kind),
            ((length, 2 * wide), low_kind),
            ((8, model), full_kind),
            ((buckets, 128), full_kind),
        ],
        whole_room,
        cover=(memory_came,),
    )
    *buffers, send, keep = call(
        "self_weights",
        self_weights_body,
        (first[0], second[0], query_self, sums_self, first[3], second[3], low_self, w_self),
        [((4,) + small_chunk, low_kind)] * 4 + two_pieces,
        whole_room + weight_room + [((length, 3 * wide), low_kind)],
        cover=cross_grads.came,
    )
    self_grads = Reduction(call, "self_grads", buffers)
    arrived = shard_swap(send, 1)
    cross_grads.halve(cover=(arrived,))
    mine, far = scatter_pair(arrived, keep)
    feed_grads.trade(cover=self_grads.came)
    self_grads.halve(cover=cross_grads.came + (far,))
    cross_grads.quarter(cover=tuple(feed_grads.blocks[1:]))
    gain_rows = -(-3 * model // 1024) * 8
    vector_kind = ((gain_rows + buckets, 128), full_kind)
    grad_source, vector = call(
        "finish",
        finish_body,
        (inputs[0], mine, far, gains, total_self, row_cross, row_feed, table),
        [((tokens_here, model), full_kind), vector_kind],
        cover=self_grads.came,
    )
    vectors = (vector,) + tuple(shard_swap(vector, step) for step in (1, 2, 3))
    feed_grads.gather(cover=vectors[1:])
    self_grads.quarter(vectors=vectors)
    memory_mine, memory_far = scatter_pair(memory_came, memory_keep)
    grad_memory = memory_mine + memory_far.astype(full_kind)
    cross_grads.trade(cover=feed_grads.far)
    cross_grads.gather()
    self_grads.trade(cover=cross_grads.far)
    small_results = [((part, model), full_kind)] * 3 + [((wide, model), full_kind)]
    out_room = [((4, wide, 3 * wide), full_kind)]
    cross_out = cross_grads.finish(
        small_out_body, small_results, out_room, tuple(self_grads.blocks[1:])
    )
    self_grads.gather()
    feed_out = feed_grads.finish(
        feed_out_body,
        [((part, 4 * units), full_kind)] * 2 + [((units, model), full_kind)],
        cover=self_grads.far + self_grads.near,
    )
    *self_out, vector = self_grads.finish(
        last_out_body,
        small_results + [vector_kind],
        out_room + [((4,) + vector_kind[0], full_kind)],
    )

    gains_sum = vector[: 3 * model // 128].reshape(3, model)
    gains_here = lax.dynamic_slice_in_dim(gains_sum, index * part, part, 1)
    table_grad = lax.dynamic_slice_in_dim(
        vector[gain_rows:, :HEADS], index * small_rows, small_rows
    )
    return (
        outcome[None],
        grad_source[None],
        grad_memory[None],
        *self_out,
        *cross_out,
        *feed_out,
        gains_here[0],
        gains_here[1],
        gains_here[2],
        table_grad,
    )


def solution(mesh):
    in_specs = (
        P("rep", "shard", None),
        P("rep", "shard", None),
        P("rep", None),
        P("rep", None),
        P("shard", None),
        P("shard", None),
        P("shard", None),
        P("shard", None),
        P("shard", None),
        P("shard", None),
        P("shard", None),
        P("shard", None),
        P("shard", None),
        P("shard", None),
        P("shard", None),
        P("shard"),
        P("shard"),
        P("shard"),
        P("shard", None),
        P("rep", "shard", None),
    )
    out_specs = (
        P("rep", "shard", None),
        P("rep", "shard", None),
        P("rep", "shard", None),
        P("shard", None),
        P("shard", None),
        P("shard", None),
        P("shard", None),
        P("shard", None),
        P("shard", None),
        P("shard", None),
        P("shard", None),
        P("shard", None),
        P("shard", None),
        P("shard", None),
        P("shard"),
        P("shard"),
        P("shard"),
        P("shard", None),
    )
    split = mesh.shape["shard"] == 4 and mesh.shape["rep"] == 8
    body = split_shards if split else shards
    return jax.shard_map(body, mesh=mesh, in_specs=in_specs, out_specs=out_specs, check_vma=False)
```

```python
import functools
import math

import jax
import jax.numpy as jnp
from jax import lax
from jax.experimental import pallas as pl
from jax.experimental.pallas import tpu as pltpu
from jax.sharding import PartitionSpec as P

HEADS = 12
HEAD_DIM = 64


bucket_edges = [math.ceil(16 * 8 ** (number / 16)) for number in range(1, 16)]
epsilon = 1e-06
masked_score = -1000000000.0


def bucket_of(distance):
    far_part = sum(((distance >= border).astype(jnp.int32) for border in bucket_edges))
    return jnp.where(distance < 16, distance, 16 + far_part)


def rms_scale(values, scales):
    return values * lax.rsqrt(jnp.mean(values * values, axis=-1, keepdims=True) + epsilon) * scales


def product(former, latter):
    return jnp.dot(former, latter, preferred_element_type=jnp.float32)


def product_rows(former, latter):
    return lax.dot_general(
        former, latter, (((0,), (0,)), ((), ())), preferred_element_type=jnp.float32
    )


def product_cols(former, latter):
    return lax.dot_general(
        former, latter, (((1,), (1,)), ((), ())), preferred_element_type=jnp.float32
    )


def split_heads(matrix):
    return matrix.reshape(matrix.shape[0], HEADS, HEAD_DIM).transpose(1, 0, 2)


def join_heads(stacked):
    return stacked.transpose(1, 0, 2).reshape(stacked.shape[1], HEADS * HEAD_DIM)


def to_blocks(matrix, block_count):
    return matrix.reshape(block_count, -1, HEADS, HEAD_DIM).transpose(0, 2, 1, 3)


def from_blocks(stacked):
    return stacked.transpose(0, 2, 1, 3).reshape(-1, HEADS * HEAD_DIM)


def self_scores(queries, query_start, query_ids, table_full, key_rows, key_start, key_ids):
    query_count = queries.shape[1]
    key_count = key_rows.shape[1]
    query_places = query_start + jnp.arange(query_count, dtype=jnp.int32)
    key_places = key_start + jnp.arange(key_count, dtype=jnp.int32)
    buckets = bucket_of(jnp.maximum(query_places[:, None] - key_places[None, :], 0))
    one_hot = (
        buckets.reshape(1, -1) == jnp.arange(table_full.shape[0], dtype=jnp.int32)[:, None]
    ).astype(jnp.bfloat16)
    bias_block = jnp.einsum(
        "bn,bh->hn", one_hot, table_full, preferred_element_type=jnp.float32
    ).reshape(HEADS, query_count, key_count)
    scores = (
        jnp.einsum("hqd,hkd->hqk", queries, key_rows, preferred_element_type=jnp.float32)
        + bias_block
    )
    allowed = (query_places[:, None] >= key_places[None, :]) & (
        query_ids[:, None] == key_ids[None, :]
    )
    return (jnp.where(allowed[None], scores, masked_score), one_hot)


def self_logsum(queries, query_start, query_ids, table_full, key_blocks, id_blocks, key_starts):
    query_count = queries.shape[1]

    def advance(running, packed):
        largest, totals = running
        key_rows, key_ids, key_start = packed
        scores, unused = self_scores(
            queries, query_start, query_ids, table_full, key_rows, key_start, key_ids
        )
        newest = jnp.maximum(largest, jnp.max(scores, axis=-1, keepdims=True))
        totals = totals * jnp.exp(largest - newest) + jnp.sum(
            jnp.exp(scores - newest), axis=-1, keepdims=True
        )
        return ((newest, totals), None)

    initial = (
        jnp.full((HEADS, query_count, 1), -jnp.inf, jnp.float32),
        jnp.zeros((HEADS, query_count, 1), jnp.float32),
    )
    (largest, totals), unused = lax.scan(advance, initial, (key_blocks, id_blocks, key_starts))
    return largest + jnp.log(totals)


def self_mix(
    queries,
    query_start,
    query_ids,
    table_full,
    key_blocks,
    value_blocks,
    id_blocks,
    key_starts,
    logsum,
):

    def advance(accum, packed):
        key_rows, value_rows, key_ids, key_start = packed
        scores, unused = self_scores(
            queries, query_start, query_ids, table_full, key_rows, key_start, key_ids
        )
        weights = jnp.exp(scores - logsum).astype(jnp.bfloat16)
        return (
            accum
            + jnp.einsum("hqk,hkd->hqd", weights, value_rows, preferred_element_type=jnp.float32),
            None,
        )

    initial = jnp.zeros((HEADS, queries.shape[1], HEAD_DIM), jnp.float32)
    accum, unused = lax.scan(advance, initial, (key_blocks, value_blocks, id_blocks, key_starts))
    return accum


def self_backward(
    queries,
    query_start,
    query_ids,
    table_full,
    key_blocks,
    value_blocks,
    id_blocks,
    key_starts,
    logsum,
    grad_mixed,
):
    query_count = queries.shape[1]

    def dots(accum, packed):
        key_rows, value_rows, key_ids, key_start = packed
        scores, unused = self_scores(
            queries, query_start, query_ids, table_full, key_rows, key_start, key_ids
        )
        chances = jnp.exp(scores - logsum)
        grad_chances = jnp.einsum(
            "hqd,hkd->hqk", grad_mixed, value_rows, preferred_element_type=jnp.float32
        )
        return (accum + jnp.sum(chances * grad_chances, axis=-1, keepdims=True), None)

    row_dots, unused = lax.scan(
        dots,
        jnp.zeros((HEADS, query_count, 1), jnp.float32),
        (key_blocks, value_blocks, id_blocks, key_starts),
    )

    def advance(running, packed):
        grad_queries, grad_table = running
        key_rows, value_rows, key_ids, key_start = packed
        scores, one_hot = self_scores(
            queries, query_start, query_ids, table_full, key_rows, key_start, key_ids
        )
        chances = jnp.exp(scores - logsum)
        grad_chances = jnp.einsum(
            "hqd,hkd->hqk", grad_mixed, value_rows, preferred_element_type=jnp.float32
        )
        grad_scores = chances * (grad_chances - row_dots)
        rounded = grad_scores.astype(jnp.bfloat16)
        grad_values = jnp.einsum(
            "hqk,hqd->hkd",
            chances.astype(jnp.bfloat16),
            grad_mixed,
            preferred_element_type=jnp.float32,
        )
        grad_keys = jnp.einsum("hqk,hqd->hkd", rounded, queries, preferred_element_type=jnp.float32)
        grad_queries = grad_queries + jnp.einsum(
            "hqk,hkd->hqd", rounded, key_rows, preferred_element_type=jnp.float32
        )
        grad_table = grad_table + jnp.einsum(
            "bn,hn->bh",
            one_hot,
            grad_scores.reshape(HEADS, -1),
            precision=lax.Precision.HIGHEST,
            preferred_element_type=jnp.float32,
        )
        return ((grad_queries, grad_table), (grad_keys, grad_values))

    initial = (
        jnp.zeros((HEADS, query_count, HEAD_DIM), jnp.float32),
        jnp.zeros((table_full.shape[0], HEADS), jnp.float32),
    )
    (grad_queries, grad_table), (grad_keys, grad_values) = lax.scan(
        advance, initial, (key_blocks, value_blocks, id_blocks, key_starts)
    )
    return (join_heads(grad_queries), grad_table, from_blocks(grad_keys), from_blocks(grad_values))


def cross_forward(queries, key_heads, value_heads, allowed):
    scores = jnp.where(
        allowed,
        jnp.einsum("hqd,hkd->hqk", queries, key_heads, preferred_element_type=jnp.float32),
        masked_score,
    )
    largest = jnp.max(scores, axis=-1, keepdims=True)
    logsum = largest + jnp.log(jnp.sum(jnp.exp(scores - largest), axis=-1, keepdims=True))
    weights = jnp.exp(scores - logsum).astype(jnp.bfloat16)
    mixed = jnp.einsum("hqk,hkd->hqd", weights, value_heads, preferred_element_type=jnp.float32)
    return (mixed, logsum)


def cross_backward(queries, key_heads, value_heads, allowed, logsum, grad_mixed):
    scores = jnp.where(
        allowed,
        jnp.einsum("hqd,hkd->hqk", queries, key_heads, preferred_element_type=jnp.float32),
        masked_score,
    )
    chances = jnp.exp(scores - logsum)
    grad_values = jnp.einsum(
        "hqk,hqd->hkd", chances.astype(jnp.bfloat16), grad_mixed, preferred_element_type=jnp.float32
    )
    grad_chances = jnp.einsum(
        "hqd,hkd->hqk", grad_mixed, value_heads, preferred_element_type=jnp.float32
    )
    grad_scores = chances * (grad_chances - jnp.sum(chances * grad_chances, axis=-1, keepdims=True))
    rounded = grad_scores.astype(jnp.bfloat16)
    grad_queries = jnp.einsum(
        "hqk,hkd->hqd", rounded, key_heads, preferred_element_type=jnp.float32
    )
    grad_keys = jnp.einsum("hqk,hqd->hkd", rounded, queries, preferred_element_type=jnp.float32)
    return (join_heads(grad_queries), join_heads(grad_keys), join_heads(grad_values))


def shards(
    inputs,
    encoder,
    segments,
    enc_segments,
    self_query,
    self_key,
    self_value,
    self_output,
    cross_query,
    cross_key,
    cross_value,
    cross_output,
    gate_weight,
    up_weight,
    down_weight,
    self_gain,
    cross_gain,
    feed_gain,
    bias_table,
    cotangent,
):
    fetched = (
        lax.all_gather(self_query, "shard", axis=0, tiled=True),
        lax.all_gather(self_key, "shard", axis=0, tiled=True),
        lax.all_gather(self_value, "shard", axis=0, tiled=True),
        lax.all_gather(self_output, "shard", axis=0, tiled=True),
        lax.all_gather(cross_query, "shard", axis=0, tiled=True),
        lax.all_gather(cross_key, "shard", axis=0, tiled=True),
        lax.all_gather(cross_value, "shard", axis=0, tiled=True),
        lax.all_gather(cross_output, "shard", axis=0, tiled=True),
        lax.all_gather(gate_weight, "shard", axis=0, tiled=True),
        lax.all_gather(up_weight, "shard", axis=0, tiled=True),
        lax.all_gather(down_weight, "shard", axis=0, tiled=True),
        lax.all_gather(self_gain, "shard", axis=0, tiled=True),
        lax.all_gather(cross_gain, "shard", axis=0, tiled=True),
        lax.all_gather(feed_gain, "shard", axis=0, tiled=True),
        lax.all_gather(bias_table, "shard", axis=0, tiled=True),
    )
    (
        w_query,
        w_key,
        w_value,
        w_output,
        c_query,
        c_key,
        c_value,
        c_output,
        w_gate,
        w_up,
        w_down,
        g_self,
        g_cross,
        g_feed,
        table_full,
    ) = fetched
    gain_self = g_self.astype(jnp.float32)
    gain_cross = g_cross.astype(jnp.float32)
    gain_feed = g_feed.astype(jnp.float32)
    source = inputs[0].astype(jnp.float32)
    memory = encoder[0]
    segment_ids = segments[0]
    memory_ids = enc_segments[0]
    tokens_here = source.shape[0]
    length = segment_ids.shape[0]
    block_size = math.gcd(length, 512)
    block_count = length // block_size
    query_start = lax.axis_index("shard") * tokens_here
    query_ids = lax.dynamic_slice_in_dim(segment_ids, query_start, tokens_here)
    id_blocks = segment_ids.reshape(block_count, block_size)
    key_starts = jnp.arange(block_count, dtype=jnp.int32) * block_size
    cross_allowed = (query_ids[:, None] == memory_ids[None, :])[None]
    normed_self = rms_scale(source, gain_self).astype(jnp.bfloat16)
    query_heads = split_heads(product(normed_self, w_query).astype(jnp.bfloat16))
    key_local = product(normed_self, w_key).astype(jnp.bfloat16)
    value_local = product(normed_self, w_value).astype(jnp.bfloat16)
    keys_all, values_all = (
        lax.all_gather(key_local, "shard", axis=0, tiled=True),
        lax.all_gather(value_local, "shard", axis=0, tiled=True),
    )
    key_blocks = to_blocks(keys_all, block_count)
    value_blocks = to_blocks(values_all, block_count)
    logsum_self = self_logsum(
        query_heads, query_start, query_ids, table_full, key_blocks, id_blocks, key_starts
    )
    mixed_self = self_mix(
        query_heads,
        query_start,
        query_ids,
        table_full,
        key_blocks,
        value_blocks,
        id_blocks,
        key_starts,
        logsum_self,
    )
    joined_self = join_heads(mixed_self).astype(jnp.bfloat16)
    after_self = source + product(joined_self, w_output)
    normed_cross = rms_scale(after_self, gain_cross).astype(jnp.bfloat16)
    query_cross = split_heads(product(normed_cross, c_query).astype(jnp.bfloat16))
    key_cross_local = product(memory, c_key).astype(jnp.bfloat16)
    value_cross_local = product(memory, c_value).astype(jnp.bfloat16)
    keys_cross, values_cross = (
        lax.all_gather(key_cross_local, "shard", axis=0, tiled=True),
        lax.all_gather(value_cross_local, "shard", axis=0, tiled=True),
    )
    key_cross = split_heads(keys_cross)
    value_cross = split_heads(values_cross)
    mixed_cross, logsum_cross = cross_forward(query_cross, key_cross, value_cross, cross_allowed)
    joined_cross = join_heads(mixed_cross).astype(jnp.bfloat16)
    after_cross = after_self + product(joined_cross, c_output)
    normed_feed = rms_scale(after_cross, gain_feed).astype(jnp.bfloat16)
    gate_act = product(normed_feed, w_gate)
    up_act = product(normed_feed, w_up)
    hidden = (jax.nn.gelu(gate_act, approximate=True) * up_act).astype(jnp.bfloat16)
    outcome = after_cross + product(hidden, w_down)
    fetched = (
        lax.all_gather(self_query, "shard", axis=0, tiled=True),
        lax.all_gather(self_key, "shard", axis=0, tiled=True),
        lax.all_gather(self_value, "shard", axis=0, tiled=True),
        lax.all_gather(self_output, "shard", axis=0, tiled=True),
        lax.all_gather(cross_query, "shard", axis=0, tiled=True),
        lax.all_gather(cross_key, "shard", axis=0, tiled=True),
        lax.all_gather(cross_value, "shard", axis=0, tiled=True),
        lax.all_gather(cross_output, "shard", axis=0, tiled=True),
        lax.all_gather(gate_weight, "shard", axis=0, tiled=True),
        lax.all_gather(up_weight, "shard", axis=0, tiled=True),
        lax.all_gather(down_weight, "shard", axis=0, tiled=True),
        lax.all_gather(self_gain, "shard", axis=0, tiled=True),
        lax.all_gather(cross_gain, "shard", axis=0, tiled=True),
        lax.all_gather(feed_gain, "shard", axis=0, tiled=True),
        lax.all_gather(bias_table, "shard", axis=0, tiled=True),
    )
    (
        w_query,
        w_key,
        w_value,
        w_output,
        c_query,
        c_key,
        c_value,
        c_output,
        w_gate,
        w_up,
        w_down,
        g_self,
        g_cross,
        g_feed,
        table_full,
    ) = fetched
    gain_self = g_self.astype(jnp.float32)
    gain_cross = g_cross.astype(jnp.float32)
    gain_feed = g_feed.astype(jnp.float32)
    keys_all, values_all = (
        lax.all_gather(key_local, "shard", axis=0, tiled=True),
        lax.all_gather(value_local, "shard", axis=0, tiled=True),
    )
    key_blocks = to_blocks(keys_all, block_count)
    value_blocks = to_blocks(values_all, block_count)
    grad_out = cotangent[0].astype(jnp.float32)
    grad_down_in = cotangent[0]
    d_down = product_rows(hidden, grad_down_in)
    grad_hidden = product_cols(grad_down_in, w_down)

    def activation(gate_in, up_in):
        return jax.nn.gelu(gate_in, approximate=True) * up_in

    unused, pull = jax.vjp(activation, gate_act, up_act)
    grad_gate, grad_up = pull(grad_hidden)
    grad_gate = grad_gate.astype(jnp.bfloat16)
    grad_up = grad_up.astype(jnp.bfloat16)
    d_gate = product_rows(normed_feed, grad_gate)
    d_up = product_rows(normed_feed, grad_up)
    grad_normed_feed = product_cols(grad_gate, w_gate) + product_cols(grad_up, w_up)
    unused, pull = jax.vjp(rms_scale, after_cross, gain_feed)
    norm_part, d_feed_gain = pull(grad_normed_feed)
    grad_cross_total = grad_out + norm_part
    grad_cross_in = grad_cross_total.astype(jnp.bfloat16)
    d_c_output = product_rows(joined_cross, grad_cross_in)
    grad_mixed_cross = split_heads(product_cols(grad_cross_in, c_output).astype(jnp.bfloat16))
    grad_query_cross, grad_keys_cross, grad_values_cross = cross_backward(
        query_cross, key_cross, value_cross, cross_allowed, logsum_cross, grad_mixed_cross
    )
    grad_query_cross = grad_query_cross.astype(jnp.bfloat16)
    key_part, value_part = (
        lax.psum_scatter(
            grad_keys_cross.astype(jnp.bfloat16), "shard", scatter_dimension=0, tiled=True
        ).astype(jnp.float32),
        lax.psum_scatter(
            grad_values_cross.astype(jnp.bfloat16), "shard", scatter_dimension=0, tiled=True
        ).astype(jnp.float32),
    )
    grad_key_cross = key_part.astype(jnp.bfloat16)
    grad_value_cross = value_part.astype(jnp.bfloat16)
    d_c_query = product_rows(normed_cross, grad_query_cross)
    d_c_key = product_rows(memory, grad_key_cross)
    d_c_value = product_rows(memory, grad_value_cross)
    grad_memory = product_cols(grad_key_cross, c_key) + product_cols(grad_value_cross, c_value)
    grad_normed_cross = product_cols(grad_query_cross, c_query)
    unused, pull = jax.vjp(rms_scale, after_self, gain_cross)
    norm_part, d_cross_gain = pull(grad_normed_cross)
    grad_self_total = grad_cross_total + norm_part
    grad_self_in = grad_self_total.astype(jnp.bfloat16)
    d_output = product_rows(joined_self, grad_self_in)
    grad_mixed_self = split_heads(product_cols(grad_self_in, w_output).astype(jnp.bfloat16))
    grad_queries, d_table, grad_keys_full, grad_values_full = self_backward(
        query_heads,
        query_start,
        query_ids,
        table_full,
        key_blocks,
        value_blocks,
        id_blocks,
        key_starts,
        logsum_self,
        grad_mixed_self,
    )
    grad_query_self = grad_queries.astype(jnp.bfloat16)
    key_part, value_part = (
        lax.psum_scatter(
            grad_keys_full.astype(jnp.bfloat16), "shard", scatter_dimension=0, tiled=True
        ).astype(jnp.float32),
        lax.psum_scatter(
            grad_values_full.astype(jnp.bfloat16), "shard", scatter_dimension=0, tiled=True
        ).astype(jnp.float32),
    )
    grad_key_self = key_part.astype(jnp.bfloat16)
    grad_value_self = value_part.astype(jnp.bfloat16)
    d_query = product_rows(normed_self, grad_query_self)
    d_key = product_rows(normed_self, grad_key_self)
    d_value = product_rows(normed_self, grad_value_self)
    grad_normed_self = (
        product_cols(grad_query_self, w_query)
        + product_cols(grad_key_self, w_key)
        + product_cols(grad_value_self, w_value)
    )
    unused, pull = jax.vjp(rms_scale, source, gain_self)
    norm_part, d_self_gain = pull(grad_normed_self)
    grad_source = grad_self_total + norm_part
    summed = (
        lax.psum_scatter(
            d_query.astype(jnp.bfloat16), "shard", scatter_dimension=0, tiled=True
        ).astype(jnp.float32),
        lax.psum_scatter(
            d_key.astype(jnp.bfloat16), "shard", scatter_dimension=0, tiled=True
        ).astype(jnp.float32),
        lax.psum_scatter(
            d_value.astype(jnp.bfloat16), "shard", scatter_dimension=0, tiled=True
        ).astype(jnp.float32),
        lax.psum_scatter(
            d_output.astype(jnp.bfloat16), "shard", scatter_dimension=0, tiled=True
        ).astype(jnp.float32),
        lax.psum_scatter(
            d_c_query.astype(jnp.bfloat16), "shard", scatter_dimension=0, tiled=True
        ).astype(jnp.float32),
        lax.psum_scatter(
            d_c_key.astype(jnp.bfloat16), "shard", scatter_dimension=0, tiled=True
        ).astype(jnp.float32),
        lax.psum_scatter(
            d_c_value.astype(jnp.bfloat16), "shard", scatter_dimension=0, tiled=True
        ).astype(jnp.float32),
        lax.psum_scatter(
            d_c_output.astype(jnp.bfloat16), "shard", scatter_dimension=0, tiled=True
        ).astype(jnp.float32),
        lax.psum_scatter(
            d_gate.astype(jnp.bfloat16), "shard", scatter_dimension=0, tiled=True
        ).astype(jnp.float32),
        lax.psum_scatter(
            d_up.astype(jnp.bfloat16), "shard", scatter_dimension=0, tiled=True
        ).astype(jnp.float32),
        lax.psum_scatter(
            d_down.astype(jnp.bfloat16), "shard", scatter_dimension=0, tiled=True
        ).astype(jnp.float32),
        lax.psum_scatter(
            d_self_gain.astype(jnp.bfloat16), "shard", scatter_dimension=0, tiled=True
        ).astype(jnp.float32),
        lax.psum_scatter(
            d_cross_gain.astype(jnp.bfloat16), "shard", scatter_dimension=0, tiled=True
        ).astype(jnp.float32),
        lax.psum_scatter(
            d_feed_gain.astype(jnp.bfloat16), "shard", scatter_dimension=0, tiled=True
        ).astype(jnp.float32),
        lax.psum_scatter(
            d_table.astype(jnp.bfloat16), "shard", scatter_dimension=0, tiled=True
        ).astype(jnp.float32),
    )
    totals = (
        lax.psum(summed[0].astype(jnp.bfloat16), "rep").astype(jnp.float32),
        lax.psum(summed[1].astype(jnp.bfloat16), "rep").astype(jnp.float32),
        lax.psum(summed[2].astype(jnp.bfloat16), "rep").astype(jnp.float32),
        lax.psum(summed[3].astype(jnp.bfloat16), "rep").astype(jnp.float32),
        lax.psum(summed[4].astype(jnp.bfloat16), "rep").astype(jnp.float32),
        lax.psum(summed[5].astype(jnp.bfloat16), "rep").astype(jnp.float32),
        lax.psum(summed[6].astype(jnp.bfloat16), "rep").astype(jnp.float32),
        lax.psum(summed[7].astype(jnp.bfloat16), "rep").astype(jnp.float32),
        lax.psum(summed[8].astype(jnp.bfloat16), "rep").astype(jnp.float32),
        lax.psum(summed[9].astype(jnp.bfloat16), "rep").astype(jnp.float32),
        lax.psum(summed[10].astype(jnp.bfloat16), "rep").astype(jnp.float32),
        lax.psum(summed[11].astype(jnp.bfloat16), "rep").astype(jnp.float32),
        lax.psum(summed[12].astype(jnp.bfloat16), "rep").astype(jnp.float32),
        lax.psum(summed[13].astype(jnp.bfloat16), "rep").astype(jnp.float32),
        lax.psum(summed[14].astype(jnp.bfloat16), "rep").astype(jnp.float32),
    )
    return (
        outcome.astype(jnp.bfloat16)[None],
        grad_source[None],
        grad_memory[None],
        totals[0],
        totals[1],
        totals[2],
        totals[3],
        totals[4],
        totals[5],
        totals[6],
        totals[7],
        totals[8],
        totals[9],
        totals[10],
        totals[11],
        totals[12],
        totals[13],
        totals[14],
    )


def swap(value, axis, size, step):
    return lax.ppermute(value, axis, [(place, place ^ step) for place in range(size)])


def after(value, *others):
    return lax.optimization_barrier((value, *others))[0]


def run_kernel(name, body, ids, operands, results, scratch=()):
    whole = pl.BlockSpec(memory_space=pltpu.VMEM)
    return pl.pallas_call(
        body,
        out_shape=[jax.ShapeDtypeStruct(shape, kind) for shape, kind in results],
        in_specs=[pl.BlockSpec(memory_space=pltpu.SMEM)] + [whole] * len(operands),
        out_specs=[whole] * len(results),
        scratch_shapes=[pltpu.VMEM(shape, kind) for shape, kind in scratch],
        name=name,
    )(ids, *operands)


low_kind = jnp.bfloat16
full_kind = jnp.float32


def rows_at(place, size):
    return pl.ds(pl.multiple_of(place * size, size), size)


def put_blocks(index, blocks, target):
    size = blocks[0].shape[0]
    for step, block in enumerate(blocks):
        target[rows_at(index ^ step, size), :] = block[...]


def split_cores(index, partial, room, send, keep):
    core = index & 1
    size = send.shape[0]
    room[...] = partial
    keep[...] = room[rows_at(core, size), :]
    send[...] = room[rows_at(1 - core, size), :].astype(low_kind)


def join_cores(index, own, other, room):
    core = index & 1
    size = own.shape[0]
    room[rows_at(core, size), :] = own[...].astype(full_kind)
    room[rows_at(1 - core, size), :] = other[...].astype(full_kind)
    return room[...]


def inverse_rms(values):
    return lax.rsqrt(jnp.mean(values * values, axis=-1, keepdims=True) + epsilon)


def norm_backward(grad, values, gain):
    scale = inverse_rms(values)
    row = jnp.sum(grad * values * scale, axis=0, keepdims=True)
    scaled = grad * gain
    inner = jnp.mean(scaled * values, axis=-1, keepdims=True)
    return scale * scaled - values * (scale * scale * scale * inner), row


def bucket_rows(buckets, length):
    lanes = lax.broadcasted_iota(jnp.int32, (buckets, length), 1)
    distance = jnp.where(lanes == 0, 0, length - lanes)
    return (bucket_of(distance) == lax.broadcasted_iota(jnp.int32, (buckets, length), 0)).astype(
        full_kind
    )


def columns_body(ids, *refs):
    count = len(refs) - 4
    sources, targets = refs[:count], refs[count:]
    for place in range(4):

        @pl.when(ids[0] == place)
        def _():
            for step in range(4):
                start = 0
                for source in sources:
                    width = source.shape[1] // 4
                    begin = (place ^ step) * width
                    targets[step][:, start : start + width] = source[:, begin : begin + width]
                    start += width


def pack_body(ids, source, gain0, gain1, gain2, table, *refs):
    sources, packed, targets = refs[:3], refs[3], refs[4:]
    columns_body(ids, *sources, *targets)
    size, model = source.shape
    packed[:size, :] = source[...]
    rows = table.shape[0]
    line = [gain[...].astype(full_kind).reshape(1, -1) for gain in (gain0, gain1, gain2)]
    width = sum(piece.shape[1] for piece in line)
    line = jnp.concatenate(line + [jnp.zeros((1, model - width), full_kind)], axis=1)
    grid = jnp.concatenate(
        [table[...].astype(full_kind), jnp.zeros((rows, model - table.shape[1]), full_kind)], axis=1
    )
    lines = jnp.concatenate([line, jnp.zeros((7, model), full_kind), grid], axis=0)
    packed[size:, :] = lines.astype(low_kind)


def split_columns_body(ids, gate, up, own, send1, send2, send3):
    column = ids[1] & 1
    width = gate.shape[1] // 4
    half = send2.shape[0]
    for place in range(4):

        @pl.when(ids[0] == place)
        def _():
            for step, target in enumerate((own, send1, send2, send3)):
                begin = (place ^ step) * width
                rows = slice(None) if step < 2 else rows_at(column, half)
                for number, source in enumerate((gate, up)):
                    target[:, number * width : (number + 1) * width] = source[
                        rows, begin : begin + width
                    ]


def heads_of(matrix, number, part, wide):
    start = part * wide + number * HEAD_DIM
    return matrix[:, start : start + HEAD_DIM]


def stack_heads(matrix, target, first):
    for number in range(matrix.shape[1] // HEAD_DIM):
        target[first + number, : matrix.shape[0], :] = matrix[
            :, number * HEAD_DIM : (number + 1) * HEAD_DIM
        ]


def joined_heads(source, first, count):
    return jnp.concatenate([source[first + number] for number in range(count)], axis=1)


def each_head(count, body):
    def step(number, unused):
        body(number)
        return unused

    lax.fori_loop(0, count, step, 0)


def softmax_rows(scores, allowed):
    scores = jnp.where(allowed, scores, masked_score)
    powers = jnp.exp(scores - jnp.max(scores, axis=-1, keepdims=True))
    return powers * (1.0 / jnp.sum(powers, axis=-1, keepdims=True))


def self_half(half, ids, source, weight, gains, rows, mapped_before, output, seg_col, seg_row, outs):
    normed_out, mapped_out, chances_out, mixed_out, send, keep, room, heads, joined = outs
    size = normed_out.shape[0]
    wide = output.shape[0]
    count = wide // HEAD_DIM
    normed = (source * inverse_rms(source) * gains[0:1, :]).astype(low_kind)
    normed_out[...] = normed
    mapped = product(normed, weight).astype(low_kind)
    mapped_out[...] = mapped
    every = mapped if half == 0 else jnp.concatenate([mapped_before, mapped], axis=0)
    keys = every.shape[0]
    places = lax.broadcasted_iota(jnp.int32, (size, keys), 0) + half * size
    others = lax.broadcasted_iota(jnp.int32, (size, keys), 1)
    allowed = (places >= others) & (seg_col == seg_row[:, :keys])
    stack_heads(mapped[:, :wide], heads, 0)
    stack_heads(every[:, wide:], heads, count)

    def one_head(number):
        line = jnp.broadcast_to(rows[pl.ds(number, 1), :], (size, rows.shape[1]))
        bias = pltpu.roll(line, half * size, 1, stride=1, stride_axis=0)[:, :keys]
        scores = product_cols(heads[number, :size, :], heads[count + number, :keys, :])
        chances = softmax_rows(scores + bias, allowed).astype(low_kind)
        chances_out[number] = chances
        joined[number] = product(chances, heads[2 * count + number, :keys, :]).astype(low_kind)

    each_head(count, one_head)
    mixed = joined_heads(joined, 0, count)
    mixed_out[...] = mixed
    split_cores(ids[0], product(mixed, output), room, send, keep)


def self_first_body(
    ids, x0, x1, x2, x3, w0, w1, w2, w3, output, seg_col, seg_row,
    source_out, weight_out, gains_out, rows_out,
    normed_out, mapped_out, chances_out, mixed_out, send, keep,
    room, heads, joined, small, lines,
):
    index = ids[0]
    tokens = source_out.shape[0] // 4
    put_blocks(index, [block.at[:tokens] for block in (x0, x1, x2, x3)], source_out)
    put_blocks(index, (w0, w1, w2, w3), weight_out)
    for step, block in enumerate((x0, x1, x2, x3)):
        small[rows_at(index ^ step, 16), :] = block[tokens:, :].astype(full_kind)
    model = source_out.shape[1]
    part = model // 4
    for place in range(3):
        gains_out[place : place + 1, :] = jnp.concatenate(
            [small[16 * t : 16 * t + 1, part * place : part * (place + 1)] for t in range(4)],
            axis=1,
        )
    gains_out[3:8, :] = jnp.zeros((5, model), full_kind)
    table = jnp.concatenate([small[16 * t + 8 : 16 * t + 16, :128] for t in range(4)], axis=0)
    hot = bucket_rows(table.shape[0], rows_out.shape[1])
    lines[...] = product_rows(table.astype(low_kind), hot.astype(low_kind))
    heads_here = chances_out.shape[0]
    for number in range(heads_here):
        rows_out[number : number + 1, :] = lines[pl.ds(index * heads_here + number, 1), :]
    rows_out[heads_here:8, :] = jnp.zeros((8 - heads_here, rows_out.shape[1]), full_kind)
    size = normed_out.shape[0]
    self_half(
        0, ids, source_out[:size, :].astype(full_kind), weight_out[...], gains_out, rows_out, None,
        output[...], seg_col[:size, :], seg_row[...],
        (normed_out, mapped_out, chances_out, mixed_out, send, keep, room, heads, joined),
    )


def self_second_body(
    ids, source, weight, gains, rows, mapped_before, output, seg_col, seg_row,
    normed_out, mapped_out, chances_out, mixed_out, send, keep, room, heads, joined,
):
    size = normed_out.shape[0]
    self_half(
        1, ids, source[size:, :].astype(full_kind), weight[...], gains, rows, mapped_before[...],
        output[...], seg_col[size:, :], seg_row[...],
        (normed_out, mapped_out, chances_out, mixed_out, send, keep, room, heads, joined),
    )


def cross_keys_body(ids, e0, e1, e2, e3, w0, w1, w2, w3, memory_out, weight_out, mapped_out):
    put_blocks(ids[0], (e0, e1, e2, e3), memory_out)
    put_blocks(ids[0], (w0, w1, w2, w3), weight_out)
    wide = weight_out.shape[1] // 3
    mapped_out[...] = product(memory_out[...], weight_out[:, wide:]).astype(low_kind)


def cross_body(
    half, ids, source, own, other, gains, weight, mapped, output, seg_col, enc_row,
    after_out, normed_out, query_out, chances_out, mixed_out, send, keep, room, heads, joined,
):
    size = after_out.shape[0]
    wide = output.shape[0]
    count = wide // HEAD_DIM
    start = half * size
    values = source[start : start + size, :].astype(full_kind) + join_cores(
        ids[0], own, other, room
    )
    after_out[...] = values
    normed = (values * inverse_rms(values) * gains[1:2, :]).astype(low_kind)
    normed_out[...] = normed
    query = product(normed, weight[:, :wide]).astype(low_kind)
    query_out[...] = query
    allowed = seg_col[start : start + size, :] == enc_row[...]
    stack_heads(query, heads, 0)
    stack_heads(mapped[...], heads, count)

    def one_head(number):
        scores = product_cols(heads[number, :size, :], heads[count + number])
        chances = softmax_rows(scores, allowed).astype(low_kind)
        chances_out[number] = chances
        joined[number] = product(chances, heads[2 * count + number]).astype(low_kind)

    each_head(count, one_head)
    mixed = joined_heads(joined, 0, count)
    mixed_out[...] = mixed
    split_cores(ids[0], product(mixed, output[...]), room, send, keep)


def feed_join_body(ids, w0, w1, w2, w2x, w3, w3x, g0, g1, g2, g3, weight_out, grad_out):
    index, column = ids[0], ids[1] & 1
    put_blocks(index, (w0, w1), weight_out)
    half = w2.shape[0]
    for step, mine, other in ((2, w2, w2x), (3, w3, w3x)):
        weight_out[rows_at(2 * (index ^ step) + column, half), :] = mine[...]
        weight_out[rows_at(2 * (index ^ step) + 1 - column, half), :] = other[...]
    put_blocks(ids[0], (g0, g1, g2, g3), grad_out)


def feed_body(half, ids, before, own, other, gains, weight, down, grad_out, *refs):
    parts = refs[:2] if half else ()
    after_out, normed_out, hidden_out, acts_out, *rest = refs[len(parts) :]
    size = after_out.shape[0]
    start = half * size
    units = down.shape[0]
    room = rest[-1]
    values = before[...] + join_cores(ids[0], own, other, room)
    after_out[...] = values
    normed = (values * inverse_rms(values) * gains[2:3, :]).astype(low_kind)
    normed_out[...] = normed
    acts = product(normed, weight[...])
    gate, up = acts[:, :units], acts[:, units:]
    root = math.sqrt(2 / math.pi)
    square = gate * gate
    bend = jnp.tanh(root * gate * (1.0 + 0.044715 * square))
    curve = 0.5 * gate * (1.0 + bend)
    slope = 0.5 * (1.0 + bend) + 0.5 * gate * (1.0 - bend * bend) * root * (
        1.0 + 3 * 0.044715 * square
    )
    hidden = (curve * up).astype(low_kind)
    hidden_out[...] = hidden
    grad_hidden = product_cols(grad_out[start : start + size, :], down[...])
    acts_out[:, :units] = (grad_hidden * up * slope).astype(low_kind)
    acts_out[:, units:] = (grad_hidden * curve).astype(low_kind)
    grad = product_cols(acts_out[...], weight[...])
    result = product(hidden, down[...])
    if half:
        send, keep, out_send, out_keep = rest[:4]
        for place, part in ((0, parts[0][...]), (1, grad)):
            split_cores(ids[0], part, room, send.at[place], keep.at[place])
        for place, part in ((0, parts[1][...]), (1, result)):
            split_cores(ids[0], part, room, out_send.at[place], out_keep.at[place])
    else:
        rest[0][...] = grad
        rest[1][...] = result


def rep_bits(ids):
    rep = ids[1]
    return rep & 1, (rep >> 1) & 1, rep >> 2


def each_chunk(ids, keep_first, send_first, keep_second, send_second, body):
    column, low, unused = rep_bits(ids)

    def step(slot, unused):
        high, middle = slot >> 1, slot & 1
        for target, bit in ((keep_first, column), (send_first, 1 - column)):
            body(target.at[slot], 4 * high + 2 * middle + bit, 0)
        for target, bit in ((keep_second, low), (send_second, 1 - low)):
            body(target.at[slot], 4 * high + 2 * bit + middle, 1)
        return unused

    lax.fori_loop(0, 4, step, 0)


def feed_weights_body(
    ids, normed0, normed1, acts0, acts1, hidden0, hidden1, grad_out,
    keep_first, send_first, keep_second, send_second, feed, down,
):
    size = normed0.shape[0]
    feed[...] = (
        product_rows(normed0[...], acts0[...]) + product_rows(normed1[...], acts1[...])
    ).astype(low_kind)
    down[...] = (
        product_rows(hidden0[...], grad_out[:size, :])
        + product_rows(hidden1[...], grad_out[size:, :])
    ).astype(low_kind)
    rows = feed.shape[0] // 4
    width = feed.shape[1] // 8
    small = down.shape[0] // 8
    lanes = down.shape[1] // 2

    def fill(target, chunk, part):
        for place in range(2):
            start = (2 * part + place) * rows
            target[place] = feed[start : start + rows, rows_at(chunk, width)]
        for piece in range(lanes // width):
            start = part * lanes + piece * width
            target[2, piece * small : (piece + 1) * small, :] = down[
                rows_at(chunk, small), start : start + width
            ]

    each_chunk(ids, keep_first, send_first, keep_second, send_second, fill)


def store_small_chunks(ids, columns, output, buffers):
    small = output.shape[0] // 8
    lanes = output.shape[1] // 2
    quarter = columns.shape[0] // 4

    def fill(target, chunk, part):
        for place in range(2):
            start = (2 * part + place) * quarter + chunk * small
            target[place] = columns[pl.ds(pl.multiple_of(start, 8), small), :].astype(low_kind)
        target[2] = jnp.zeros(target.shape[1:], low_kind)
        target[2, :, :lanes] = output[
            pl.ds(pl.multiple_of(chunk * small, 8), small), part * lanes : (part + 1) * lanes
        ].astype(low_kind)

    each_chunk(ids, *buffers, fill)


small_lanes = slice(3 * 128, 4 * 128)


def small_pieces(count, size):
    half = (count - size) // 2
    yield (0, 0), slice(0, size)
    yield (0, 1), slice(size, size + half)
    yield (1, 0), slice(size + half, count)


def halve_body(ids, keep_first, came_first, keep_second, came_second, *outs):
    new_first, send_first, new_second, send_second = outs
    column, low, unused = rep_bits(ids)
    for keep, came, new, send, bit in (
        (keep_first, came_first, new_first, send_first, low),
        (keep_second, came_second, new_second, send_second, column),
    ):
        for high in range(2):
            for target, place in ((new, 2 * high + bit), (send, 2 * high + 1 - bit)):
                total = keep[place].astype(full_kind) + came[place].astype(full_kind)
                target[high] = total.astype(target.dtype)


def quarter_body(ids, keep_first, came_first, keep_second, came_second, total):
    for part, (keep, came) in enumerate(((keep_first, came_first), (keep_second, came_second))):
        total[part] = (keep[...] + came[...].astype(full_kind)).astype(low_kind)


def quarter_small_body(
    ids, keep_first, came_first, keep_second, came_second, vector, near, far, across, total
):
    quarter_body(ids, keep_first, came_first, keep_second, came_second, total)
    lines = (vector[...] + near[...] + far[...] + across[...]).astype(low_kind)
    for (part, high), piece in small_pieces(lines.shape[0], total.shape[3]):
        total[part, high, 2, : piece.stop - piece.start, small_lanes] = lines[piece, :]


def trade_body(ids, mine, came, own, send1, send2, send3, rows, room):
    for part in range(2):
        for high in range(2):
            total = (
                mine[part, high].astype(full_kind) + came[part, high].astype(full_kind)
            ).astype(low_kind)
            room[2 * part, high] = total[0]
            room[2 * part + 1, high] = total[1]
            rows[part, high] = total[2]
    for step, target in enumerate((own, send1, send2, send3)):
        target[...] = room[ids[0] ^ step]


def gather_body(ids, own, came1, came2, came3, rows, first, second):
    for place, block in enumerate((own, came1, came2)):
        first[:, place] = block[...]
    for place, block in enumerate((came3, rows.at[0], rows.at[1])):
        second[:, place] = block[...]


def all_pieces(ids, firsts, seconds):
    for step in range(4):
        for high in range(2):
            chunk = 4 * high + ((ids[1] & 3) ^ step)
            yield firsts[step].at[high], seconds[step].at[high], high, chunk


def feed_out_body(ids, *refs):
    firsts, seconds, (gate, up, down) = refs[:4], refs[4:8], refs[8:]
    units = gate.shape[1] // 4
    small = down.shape[0] // 8
    for first, second, high, chunk in all_pieces(ids, firsts, seconds):
        width = first.shape[2]
        target = (gate, up)[high]
        for step in range(4):
            block = second[0] if step == 3 else first[step]
            start = (ids[0] ^ step) * units + (chunk & 3) * width
            target[:, pl.ds(pl.multiple_of(start, width), width)] = block.astype(full_kind)
        for piece in range(down.shape[1] // width):
            part, begin = piece // 3, piece % 3 * small
            down[rows_at(chunk, small), piece * width : (piece + 1) * width] = second[
                1 + part, begin : begin + small
            ].astype(full_kind)


def small_out_body(ids, *refs):
    firsts, seconds, outs, room = refs[:4], refs[4:8], refs[8:12], refs[-1]
    small = room.shape[1] // 8
    lanes = outs[3].shape[1] // 2
    wide = outs[0].shape[0]
    for first, second, high, chunk in all_pieces(ids, firsts, seconds):
        where = pl.ds(pl.multiple_of(chunk * small, 8), small)
        for step in range(4):
            block = second[0] if step == 3 else first[step]
            room[step, where, :] = block.astype(full_kind)
        for part in range(2):
            outs[3][where, part * lanes : (part + 1) * lanes] = second[1 + part][:, :lanes].astype(
                full_kind
            )
    for place in range(4):
        for number in range(3):
            outs[number][:, place * wide : (place + 1) * wide] = room[
                ids[0] ^ place, :, number * wide : (number + 1) * wide
            ]


def last_out_body(ids, *refs):
    *refs, vector, room, lines = refs
    small_out_body(ids, *refs, room)
    seconds = refs[4:8]
    for step, second in enumerate(seconds):
        place = (ids[1] & 3) ^ step
        for (part, high), piece in small_pieces(vector.shape[0], second.shape[2]):
            lines[place, piece, :] = second[
                high, 1 + part, : piece.stop - piece.start, small_lanes
            ].astype(full_kind)
    vector[...] = (lines[0] + lines[1]) + (lines[2] + lines[3])


def attention_backward(grad, query, keys, values, chances):
    full = chances.astype(full_kind)
    grad_chances = product_cols(grad, values)
    grad_scores = full * (grad_chances - jnp.sum(full * grad_chances, axis=-1, keepdims=True))
    rounded = grad_scores.astype(low_kind)
    return (
        grad_scores,
        product(rounded, keys).astype(low_kind),
        product_rows(rounded, query),
        product_rows(chances, grad),
    )


def join_halves(index, own, other, room):
    core = index & 1
    size = own.shape[1]
    for chip in range(2):
        room[rows_at(core + 2 * chip, size), :] = own[chip].astype(full_kind)
        room[rows_at(1 - core + 2 * chip, size), :] = other[chip].astype(full_kind)
    return room[...]


def cross_back_body(
    ids, grad_out, own, other, values0, values1, gains, output, query0, query1, chances0, chances1,
    mapped, weight, total_out, low_out, query_out, sums_out, row_out, send, keep, room, heads, joined,
):
    wide = output.shape[0]
    join_halves(ids[0], own, other, room)
    size = values0.shape[0]
    row = 0.0
    for half, values in ((0, values0), (1, values1)):
        part = slice(half * size, (half + 1) * size)
        grad, piece = norm_backward(room[part, :], values[...], gains[2:3, :])
        row = row + piece
        total = grad_out[part, :].astype(full_kind) + grad
        total_out[part, :] = total
        low_out[part, :] = total.astype(low_kind)
    row_out[...] = jnp.broadcast_to(row, row_out.shape)
    grad_mixed = product_cols(low_out[...], output[...]).astype(low_kind)
    count = wide // HEAD_DIM
    stack_heads(grad_mixed, heads, 0)
    stack_heads(jnp.concatenate([query0[...], query1[...]], axis=0), heads, count)
    stack_heads(mapped[...], heads, 2 * count)

    def one_head(number):
        chances = jnp.concatenate([chances0[number], chances1[number]], axis=0)
        unused, grad_query, grad_keys, grad_values = attention_backward(
            heads[number], heads[count + number], heads[2 * count + number],
            heads[3 * count + number], chances,
        )
        joined[number] = grad_query
        joined[count + number] = grad_keys.astype(low_kind)
        joined[2 * count + number] = grad_values.astype(low_kind)

    each_head(count, one_head)
    query_out[...] = joined_heads(joined, 0, count)
    sums_out[...] = joined_heads(joined, count, 2 * count)
    scatter_cores(ids[0], product_cols(query_out[...], weight[:, :wide]), room, send, keep)


def cross_weights_body(
    ids, normed0, normed1, query, memory, sums, mixed0, mixed1, low, weight,
    keep_first, send_first, keep_second, send_second, send, keep, room, columns, output,
):
    wide = query.shape[1]
    size = normed0.shape[0]
    columns[:, :wide] = product_rows(normed0[...], query[:size, :]) + product_rows(
        normed1[...], query[size:, :]
    )
    columns[:, wide:] = product_rows(memory[...], sums[...])
    output[...] = product_rows(mixed0[...], low[:size, :]) + product_rows(mixed1[...], low[size:, :])
    store_small_chunks(ids, columns, output, (keep_first, send_first, keep_second, send_second))
    scatter_cores(ids[0], product_cols(sums[...], weight[:, wide:]), room, send, keep)


def scatter_cores(index, partial, room, send, keep):
    core = index & 1
    size = send.shape[1]
    room[...] = partial
    for chip in range(2):
        keep[chip] = room[rows_at(core + 2 * chip, size), :]
        send[chip] = room[rows_at(1 - core + 2 * chip, size), :].astype(low_kind)


def diagonal_sums(matrix):
    width = matrix.shape[1]
    size = matrix.shape[0]
    while size > 1:
        size //= 2
        matrix = matrix[:size] + pltpu.roll(matrix[size:], width - size, 1)
    return matrix


def self_back_body(
    ids, total, own, other, values0, values1, gains, output, mapped0, mapped1, chances0, chances1,
    total_out, low_out, query_out, sums_out, row_out, table_out, room, heads, joined,
):
    wide = output.shape[0]
    join_halves(ids[0], own, other, room)
    size = values0.shape[0]
    row = 0.0
    for half, values in ((0, values0), (1, values1)):
        part = slice(half * size, (half + 1) * size)
        grad, piece = norm_backward(room[part, :], values[...], gains[1:2, :])
        row = row + piece
        new_total = total[part, :] + grad
        total_out[part, :] = new_total
        low_out[part, :] = new_total.astype(low_kind)
    row_out[...] = jnp.broadcast_to(row, row_out.shape)
    grad_mixed = product_cols(low_out[...], output[...]).astype(low_kind)
    buckets = table_out.shape[0]
    hot = bucket_rows(buckets, 2 * size)
    count = wide // HEAD_DIM
    stack_heads(grad_mixed, heads, 0)
    stack_heads(jnp.concatenate([mapped0[...], mapped1[...]], axis=0), heads, count)
    table_out[...] = jnp.zeros(table_out.shape, full_kind)

    def one_head(number):
        line = sums = None
        for half, chances in ((1, chances1), (0, chances0)):
            part = slice(half * size, (half + 1) * size)
            seen = slice(0, (half + 1) * size)
            grad_scores, grad_query, grad_keys, grad_values = attention_backward(
                heads[number, part, :], heads[count + number, part, :],
                heads[2 * count + number, seen, :], heads[3 * count + number, seen, :],
                chances[number],
            )
            joined[number, part, :] = grad_query
            if half:
                line = pltpu.roll(diagonal_sums(grad_scores), size, 1)
                sums = (grad_keys, grad_values)
            else:
                empty = jnp.zeros((size, size), full_kind)
                line = line + diagonal_sums(jnp.concatenate([grad_scores, empty], axis=1))
                for place, first, later in ((1, grad_keys, sums[0]), (2, grad_values, sums[1])):
                    joined[place * count + number, :size, :] = (later[:size] + first).astype(low_kind)
                    joined[place * count + number, size:, :] = later[size:].astype(low_kind)
        column = jnp.sum(hot * line, axis=1, keepdims=True)
        lanes = lax.broadcasted_iota(jnp.int32, table_out.shape, 1)
        table_out[...] += jnp.where(lanes == number, column, 0.0)

    each_head(count, one_head)
    query_out[...] = joined_heads(joined, 0, count)
    sums_out[...] = joined_heads(joined, count, 2 * count)


def self_weights_body(
    ids, normed0, normed1, query, sums, mixed0, mixed1, low, weight,
    keep_first, send_first, keep_second, send_second, send, keep, room, columns, output, merged,
):
    wide = query.shape[1]
    size = normed0.shape[0]
    merged[:, :wide] = query[...]
    merged[:, wide:] = sums[...]
    columns[...] = product_rows(normed0[...], merged[:size, :]) + product_rows(
        normed1[...], merged[size:, :]
    )
    output[...] = product_rows(mixed0[...], low[:size, :]) + product_rows(mixed1[...], low[size:, :])
    store_small_chunks(ids, columns, output, (keep_first, send_first, keep_second, send_second))
    scatter_cores(ids[0], product_cols(merged[...], weight[...]), room, send, keep)


def finish_body(ids, source, mine, far, gains, total, cross_row, feed_row, table, grad_out, vector):
    index = ids[0]
    size, model = source.shape
    grad, row = norm_backward(
        mine[...] + far[...].astype(full_kind), source[...].astype(full_kind), gains[0:1, :]
    )
    grad_out[...] = total[rows_at(index, size), :] + grad
    lanes = lax.broadcasted_iota(jnp.int32, (1, model), 1)
    part = model // 4
    here = (lanes >= index * part) & (lanes < (index + 1) * part)
    pieces = []
    for line in (row, jnp.where(here, cross_row[0:1, :], 0.0), jnp.where(here, feed_row[0:1, :], 0.0)):
        pieces += [line[:, start : start + 128] for start in range(0, model, 128)]
    pieces += [jnp.zeros((-len(pieces) % 8, 128), full_kind)]
    vector[: vector.shape[0] - table.shape[0], :] = jnp.concatenate(pieces, axis=0)
    vector[vector.shape[0] - table.shape[0] :, :] = pltpu.roll(
        table[...], index * (HEADS // 4), 1
    )


def chip_pair_body(ids, keep, arrived, mine, other):
    chip = ids[0] >> 1
    mine[...] = keep[chip] + arrived[chip].astype(full_kind)
    other[...] = (keep[1 - chip] + arrived[1 - chip].astype(full_kind)).astype(low_kind)


class Kernels:
    def __init__(self, ids):
        self.ids = ids

    def __call__(self, name, body, operands, results, scratch=(), cover=()):
        outs = run_kernel(name, body, self.ids, operands, results, scratch)
        if cover:
            outs = after(tuple(outs), *cover)
        self.ids = after(self.ids, outs[0])
        return outs

    def wait(self, *values):
        self.ids = after(self.ids, *values)


def rep_swap(value, step):
    return swap(value, "rep", 8, step)


def shard_swap(value, step):
    return swap(value, "shard", 4, step)


class Reduction:
    def __init__(self, call, name, buffers):
        self.call, self.name = call, name
        self.keeps = (buffers[0], buffers[2])
        self.came = (rep_swap(buffers[1], 1), rep_swap(buffers[3], 2))
        self.shape = buffers[0].shape[1:]

    def halve(self, cover=()):
        results = []
        for unused in range(2):
            results += [((2,) + self.shape, full_kind), ((2,) + self.shape, low_kind)]
        outs = self.call(
            self.name + "_halve",
            halve_body,
            (self.keeps[0], self.came[0], self.keeps[1], self.came[1]),
            results,
            cover=cover,
        )
        self.keeps = (outs[0], outs[2])
        self.came = (rep_swap(outs[1], 2), rep_swap(outs[3], 1))

    def quarter(self, cover=(), vectors=()):
        (self.total,) = self.call(
            self.name + "_quarter",
            quarter_small_body if vectors else quarter_body,
            (self.keeps[0], self.came[0], self.keeps[1], self.came[1]) + vectors,
            [((2, 2) + self.shape, low_kind)],
            cover=cover,
        )
        self.last = rep_swap(self.total, 4)

    def trade(self, cover=()):
        block = self.shape[1:]
        own, *sends, self.rows = self.call(
            self.name + "_trade",
            trade_body,
            (self.total, self.last),
            [((2,) + block, low_kind)] * 4 + [((2, 2) + block, low_kind)],
            [((4, 2) + block, low_kind)],
            cover=cover,
        )
        self.blocks = [own] + [shard_swap(send, step) for step, send in zip((1, 2, 3), sends)]

    def gather(self, cover=()):
        first, second = self.call(
            self.name + "_gather",
            gather_body,
            (*self.blocks, self.rows),
            [((2,) + self.shape, low_kind)] * 2,
            cover=cover,
        )
        first_far, second_far = rep_swap(first, 2), rep_swap(second, 1)
        self.far = (first_far, second_far)
        self.near = (rep_swap(first, 1), rep_swap(second, 2))
        self.firsts = (first, self.near[0], first_far, rep_swap(first_far, 1))
        self.seconds = (second, second_far, self.near[1], rep_swap(second_far, 2))

    def finish(self, body, results, scratch=(), cover=()):
        return self.call(
            self.name + "_out", body, (*self.firsts, *self.seconds), results, scratch, cover
        )


class GroupSum:
    def __init__(self, send, keep):
        self.keep = keep
        self.came = shard_swap(send, 1)

    def add(self):
        self.pair = (self.keep + self.came.astype(full_kind)).astype(low_kind)
        self.far = shard_swap(self.pair, 2)
        return self.pair

    def total(self):
        own = (self.pair.astype(full_kind) + self.far.astype(full_kind)).astype(low_kind)
        self.results = (own, shard_swap(own, 1))
        return own


def split_shards(
    inputs,
    encoder,
    segments,
    enc_segments,
    self_query,
    self_key,
    self_value,
    self_output,
    cross_query,
    cross_key,
    cross_value,
    cross_output,
    gate_weight,
    up_weight,
    down_weight,
    self_gain,
    cross_gain,
    feed_gain,
    bias_table,
    cotangent,
):
    index = lax.axis_index("shard")
    rep = lax.axis_index("rep")
    call = Kernels(jnp.stack([index, rep]))
    tokens_here, model = inputs.shape[1:]
    length = 4 * tokens_here
    half_size = 2 * tokens_here
    heads_here = HEADS // 4
    wide = heads_here * HEAD_DIM
    units = down_weight.shape[0]
    memory_length = enc_segments.shape[1]
    small_rows = bias_table.shape[0]
    buckets = 4 * small_rows
    part = self_gain.shape[0]

    def blocks_of(*weights):
        width = sum(weight.shape[1] for weight in weights) // 4
        shape = (weights[0].shape[0], width)
        return call("columns", columns_body, weights, [(shape, low_kind)] * 4)

    def traded(blocks):
        return [blocks[0]] + [shard_swap(blocks[step], step) for step in range(1, 4)]

    column_shape = (part, 3 * wide)
    packed, *self_blocks = call(
        "pack",
        pack_body,
        (
            inputs[0], self_gain, cross_gain, feed_gain, bias_table, self_query, self_key,
            self_value,
        ),
        [((tokens_here + 16, model), low_kind)] + [(column_shape, low_kind)] * 4,
    )
    source_far = shard_swap(packed, 2)
    self_blocks = traded(self_blocks)
    cross_blocks = blocks_of(cross_query, cross_key, cross_value)
    feed_blocks = call(
        "feed_columns",
        split_columns_body,
        (gate_weight, up_weight),
        [((part, 2 * units), low_kind)] * 2 + [((part // 2, 2 * units), low_kind)] * 2,
    )
    source_far = after(source_far, feed_blocks[0])
    source_blocks = [packed, shard_swap(packed, 1), source_far, shard_swap(source_far, 1)]
    seg_row = segments
    seg_col = segments[0][:, None]
    enc_row = enc_segments
    call.wait(seg_col, self_blocks[2], self_blocks[3])
    cross_blocks = traded(after(tuple(cross_blocks), self_blocks[2], self_blocks[3]))
    room = [((half_size, model), full_kind)]
    whole_room = [((length, model), full_kind)]

    def head_rooms(places, rows, outs):
        return [
            ((places * heads_here, max(length, memory_length), HEAD_DIM), low_kind),
            ((outs * heads_here, rows, HEAD_DIM), low_kind),
        ]

    pieces = [((tokens_here, model), low_kind), ((tokens_here, model), full_kind)]
    two_pieces = [((2,) + shape, kind) for shape, kind in pieces]

    def self_results(keys):
        return [
            ((half_size, model), low_kind),
            ((half_size, 3 * wide), low_kind),
            ((heads_here, half_size, keys), low_kind),
            ((half_size, wide), low_kind),
        ] + pieces

    source, w_self, gains, rows, *first = call(
        "self_first",
        self_first_body,
        (*source_blocks, *self_blocks, self_output, seg_col, seg_row),
        [
            ((length, model), low_kind),
            ((model, 3 * wide), low_kind),
            ((8, model), full_kind),
            ((8, length), full_kind),
        ]
        + self_results(half_size),
        room + head_rooms(3, half_size, 1) + [((64, model), full_kind), ((128, length), full_kind)],
        cover=(cross_blocks[2],),
    )
    first_sum = GroupSum(*first[4:])
    memory_far = shard_swap(after(encoder[0], first[0]), 2)
    second = call(
        "self_second",
        self_second_body,
        (source, w_self, gains, rows, first[1], self_output, seg_col, seg_row),
        self_results(length),
        room + head_rooms(3, half_size, 1),
        cover=(cross_blocks[3], first_sum.came),
    )
    second_sum = GroupSum(*second[4:])
    call.wait(first_sum.add())
    memory_blocks = [
        encoder[0], shard_swap(encoder[0], 1), memory_far, shard_swap(memory_far, 1)
    ]
    memory, w_cross, cross_mapped = call(
        "cross_keys",
        cross_keys_body,
        (*memory_blocks, *cross_blocks),
        [
            ((memory_length, model), low_kind),
            ((model, 3 * wide), low_kind),
            ((memory_length, 2 * wide), low_kind),
        ],
        cover=(second_sum.came,),
    )
    pair = second_sum.add()
    call.wait(pair)
    first_sum.total()
    feed_blocks = after(tuple(feed_blocks), pair)
    feed_near = shard_swap(feed_blocks[1], 1)
    feed_two = shard_swap(feed_blocks[2], 2)

    def cross_call(half, sums, cover):
        own, other = sums.results
        return call(
            "cross",
            functools.partial(cross_body, half),
            (source, own, other, gains, w_cross, cross_mapped, cross_output, seg_col, enc_row),
            [
                ((half_size, model), full_kind),
                ((half_size, model), low_kind),
                ((half_size, wide), low_kind),
                ((heads_here, half_size, memory_length), low_kind),
                ((half_size, wide), low_kind),
            ]
            + pieces,
            room + head_rooms(3, half_size, 1),
            cover=cover,
        )

    cross0 = cross_call(0, first_sum, (second_sum.far, feed_two))
    cross_first = GroupSum(*cross0[5:])
    call.wait(second_sum.total())
    feed_two_other = rep_swap(feed_two, 1)
    feed_three = shard_swap(after(feed_blocks[3], cross0[0]), 3)
    grad_far = shard_swap(after(cotangent[0], cross0[0]), 2)
    cross1 = cross_call(1, second_sum, (feed_three, feed_two_other, cross_first.came))
    cross_second = GroupSum(*cross1[5:])
    call.wait(cross_first.add())
    feed_three_other = rep_swap(feed_three, 1)
    grad_blocks = [
        cotangent[0], shard_swap(cotangent[0], 1), grad_far, shard_swap(grad_far, 1)
    ]
    w_feed, grad_out = call(
        "feed_join",
        feed_join_body,
        (
            feed_blocks[0], feed_near, feed_two, feed_two_other, feed_three, feed_three_other,
            *grad_blocks,
        ),
        [((model, 2 * units), low_kind), ((length, model), low_kind)],
        cover=(cross_second.came,),
    )
    call.wait(cross_second.add())
    cross_first.total()

    def feed_call(half, sums, before, parts, tail, cover=()):
        own, other = sums.results
        return call(
            "feed",
            functools.partial(feed_body, half),
            (before, own, other, gains, w_feed, down_weight, grad_out) + parts,
            [
                ((half_size, model), full_kind),
                ((half_size, model), low_kind),
                ((half_size, units), low_kind),
                ((half_size, 2 * units), low_kind),
            ]
            + tail,
            room,
            cover=cover,
        )

    feed0 = feed_call(0, cross_first, cross0[0], (), room * 2, (cross_second.far,))
    cross_second.total()
    feed1 = feed_call(1, cross_second, cross1[0], (feed0[4], feed0[5]), two_pieces * 2)
    feed_sum = GroupSum(*feed1[4:6])
    out_came = shard_swap(feed1[6], 1)

    chunk = (3, model // 4, 2 * units // 8)
    feed_grads = Reduction(
        call,
        "feed_grads",
        call(
            "feed_weights",
            feed_weights_body,
            (feed0[1], feed1[1], feed0[3], feed1[3], feed0[2], feed1[2], grad_out),
            [((4,) + chunk, low_kind)] * 4,
            [((model, 2 * units), low_kind), ((units, model), low_kind)],
            cover=(feed_sum.came, out_came),
        ),
    )
    call.wait(feed_sum.add())

    def scatter_pair(arrived, keep, cover=()):
        mine, other = call(
            "chip_pair",
            chip_pair_body,
            (keep, arrived),
            [((tokens_here, model), full_kind), ((tokens_here, model), low_kind)],
            cover=cover,
        )
        return mine, shard_swap(other, 2)

    mine, far = scatter_pair(out_came, feed1[7])
    feed_sum.total()
    own_after = lax.dynamic_slice_in_dim(
        jnp.where(index < 2, feed0[0], feed1[0]), (index & 1) * tokens_here, tokens_here
    )
    outcome = (own_after + mine + far.astype(full_kind)).astype(low_kind)

    total_cross, low_cross, query_cross, sums_cross, row_feed, *sends = call(
        "cross_back",
        cross_back_body,
        (
            grad_out, *feed_sum.results, feed0[0], feed1[0], gains, cross_output, cross0[2], cross1[2],
            cross0[3], cross1[3], cross_mapped, w_cross,
        ),
        [
            ((length, model), full_kind),
            ((length, model), low_kind),
            ((length, wide), low_kind),
            ((memory_length, 2 * wide), low_kind),
            ((8, model), full_kind),
        ]
        + two_pieces,
        whole_room + head_rooms(4, length, 3),
        cover=feed_grads.came,
    )
    cross_sum = GroupSum(*sends)
    feed_grads.halve(cover=(cross_sum.came,))
    call.wait(cross_sum.add())
    small_chunk = (3, wide // 8, 3 * wide)
    weight_room = [((model, 3 * wide), full_kind), ((wide, model), full_kind)]
    *buffers, send, keep = call(
        "cross_weights",
        cross_weights_body,
        (
            cross0[1], cross1[1], query_cross, memory, sums_cross, cross0[4], cross1[4], low_cross,
            w_cross,
        ),
        [((4,) + small_chunk, low_kind)] * 4 + two_pieces,
        whole_room + weight_room,
        cover=(cross_sum.far,) + feed_grads.came,
    )
    cross_grads = Reduction(call, "cross_grads", buffers)
    memory_came, memory_keep = shard_swap(send, 1), keep
    call.wait(cross_sum.total())
    feed_grads.quarter(cover=cross_sum.results)
    total_self, low_self, query_self, sums_self, row_cross, table = call(
        "self_back",
        self_back_body,
        (
            total_cross, *cross_sum.results, cross0[0], cross1[0], gains, self_output, first[1], second[1],
            first[2], second[2],
        ),
        [
            ((length, model), full_kind),
            ((length, model), low_kind),
            ((length, wide), low_kind),
            ((length, 2 * wide), low_kind),
            ((8, model), full_kind),
            ((buckets, 128), full_kind),
        ],
        whole_room + head_rooms(4, length, 3),
        cover=(memory_came,),
    )
    *buffers, send, keep = call(
        "self_weights",
        self_weights_body,
        (first[0], second[0], query_self, sums_self, first[3], second[3], low_self, w_self),
        [((4,) + small_chunk, low_kind)] * 4 + two_pieces,
        whole_room + weight_room + [((length, 3 * wide), low_kind)],
        cover=cross_grads.came,
    )
    self_grads = Reduction(call, "self_grads", buffers)
    arrived = shard_swap(send, 1)
    cross_grads.halve(cover=(arrived,))
    mine, far = scatter_pair(arrived, keep)
    feed_grads.trade(cover=self_grads.came)
    self_grads.halve(cover=cross_grads.came + (far,))
    cross_grads.quarter(cover=tuple(feed_grads.blocks[1:]))
    gain_rows = -(-3 * model // 1024) * 8
    vector_kind = ((gain_rows + buckets, 128), full_kind)
    grad_source, vector = call(
        "finish",
        finish_body,
        (inputs[0], mine, far, gains, total_self, row_cross, row_feed, table),
        [((tokens_here, model), full_kind), vector_kind],
        cover=self_grads.came,
    )
    vectors = (vector,) + tuple(shard_swap(vector, step) for step in (1, 2, 3))
    memory_mine, memory_far = scatter_pair(memory_came, memory_keep, vectors[1:])
    grad_memory = memory_mine + memory_far.astype(full_kind)
    self_grads.quarter(vectors=vectors)
    feed_grads.gather()
    cross_grads.trade()
    cross_grads.gather(cover=feed_grads.far)
    self_grads.trade(cover=cross_grads.far)
    feed_out = feed_grads.finish(
        feed_out_body,
        [((part, 4 * units), full_kind)] * 2 + [((units, model), full_kind)],
        cover=tuple(self_grads.blocks[1:]),
    )
    self_grads.gather()
    small_results = [((part, model), full_kind)] * 3 + [((wide, model), full_kind)]
    out_room = [((4, wide, 3 * wide), full_kind)]
    cross_out = cross_grads.finish(small_out_body, small_results, out_room, self_grads.far)
    *self_out, vector = self_grads.finish(
        last_out_body,
        small_results + [vector_kind],
        out_room + [((4,) + vector_kind[0], full_kind)],
    )

    gains_sum = vector[: 3 * model // 128].reshape(3, model)
    gains_here = lax.dynamic_slice_in_dim(gains_sum, index * part, part, 1)
    table_grad = lax.dynamic_slice_in_dim(
        vector[gain_rows:, :HEADS], index * small_rows, small_rows
    )
    return (
        outcome[None],
        grad_source[None],
        grad_memory[None],
        *self_out,
        *cross_out,
        *feed_out,
        gains_here[0],
        gains_here[1],
        gains_here[2],
        table_grad,
    )


def solution(mesh):
    in_specs = (
        P("rep", "shard", None),
        P("rep", "shard", None),
        P("rep", None),
        P("rep", None),
        P("shard", None),
        P("shard", None),
        P("shard", None),
        P("shard", None),
        P("shard", None),
        P("shard", None),
        P("shard", None),
        P("shard", None),
        P("shard", None),
        P("shard", None),
        P("shard", None),
        P("shard"),
        P("shard"),
        P("shard"),
        P("shard", None),
        P("rep", "shard", None),
    )
    out_specs = (
        P("rep", "shard", None),
        P("rep", "shard", None),
        P("rep", "shard", None),
        P("shard", None),
        P("shard", None),
        P("shard", None),
        P("shard", None),
        P("shard", None),
        P("shard", None),
        P("shard", None),
        P("shard", None),
        P("shard", None),
        P("shard", None),
        P("shard", None),
        P("shard"),
        P("shard"),
        P("shard"),
        P("shard", None),
    )
    split = mesh.shape["shard"] == 4 and mesh.shape["rep"] == 8
    body = split_shards if split else shards
    return jax.shard_map(body, mesh=mesh, in_specs=in_specs, out_specs=out_specs, check_vma=False)
```

```python
import functools
import math

import jax
import jax.numpy as jnp
from jax import lax
from jax.experimental import pallas as pl
from jax.experimental.pallas import tpu as pltpu
from jax.sharding import PartitionSpec as P

HEADS = 12
HEAD_DIM = 64


bucket_edges = [math.ceil(16 * 8 ** (number / 16)) for number in range(1, 16)]
epsilon = 1e-06
masked_score = -1000000000.0


def bucket_of(distance):
    far_part = sum(((distance >= border).astype(jnp.int32) for border in bucket_edges))
    return jnp.where(distance < 16, distance, 16 + far_part)


def rms_scale(values, scales):
    return values * lax.rsqrt(jnp.mean(values * values, axis=-1, keepdims=True) + epsilon) * scales


def product(former, latter):
    return jnp.dot(former, latter, preferred_element_type=jnp.float32)


def product_rows(former, latter):
    return lax.dot_general(
        former, latter, (((0,), (0,)), ((), ())), preferred_element_type=jnp.float32
    )


def product_cols(former, latter):
    return lax.dot_general(
        former, latter, (((1,), (1,)), ((), ())), preferred_element_type=jnp.float32
    )


def split_heads(matrix):
    return matrix.reshape(matrix.shape[0], HEADS, HEAD_DIM).transpose(1, 0, 2)


def join_heads(stacked):
    return stacked.transpose(1, 0, 2).reshape(stacked.shape[1], HEADS * HEAD_DIM)


def to_blocks(matrix, block_count):
    return matrix.reshape(block_count, -1, HEADS, HEAD_DIM).transpose(0, 2, 1, 3)


def from_blocks(stacked):
    return stacked.transpose(0, 2, 1, 3).reshape(-1, HEADS * HEAD_DIM)


def self_scores(queries, query_start, query_ids, table_full, key_rows, key_start, key_ids):
    query_count = queries.shape[1]
    key_count = key_rows.shape[1]
    query_places = query_start + jnp.arange(query_count, dtype=jnp.int32)
    key_places = key_start + jnp.arange(key_count, dtype=jnp.int32)
    buckets = bucket_of(jnp.maximum(query_places[:, None] - key_places[None, :], 0))
    one_hot = (
        buckets.reshape(1, -1) == jnp.arange(table_full.shape[0], dtype=jnp.int32)[:, None]
    ).astype(jnp.bfloat16)
    bias_block = jnp.einsum(
        "bn,bh->hn", one_hot, table_full, preferred_element_type=jnp.float32
    ).reshape(HEADS, query_count, key_count)
    scores = (
        jnp.einsum("hqd,hkd->hqk", queries, key_rows, preferred_element_type=jnp.float32)
        + bias_block
    )
    allowed = (query_places[:, None] >= key_places[None, :]) & (
        query_ids[:, None] == key_ids[None, :]
    )
    return (jnp.where(allowed[None], scores, masked_score), one_hot)


def self_logsum(queries, query_start, query_ids, table_full, key_blocks, id_blocks, key_starts):
    query_count = queries.shape[1]

    def advance(running, packed):
        largest, totals = running
        key_rows, key_ids, key_start = packed
        scores, unused = self_scores(
            queries, query_start, query_ids, table_full, key_rows, key_start, key_ids
        )
        newest = jnp.maximum(largest, jnp.max(scores, axis=-1, keepdims=True))
        totals = totals * jnp.exp(largest - newest) + jnp.sum(
            jnp.exp(scores - newest), axis=-1, keepdims=True
        )
        return ((newest, totals), None)

    initial = (
        jnp.full((HEADS, query_count, 1), -jnp.inf, jnp.float32),
        jnp.zeros((HEADS, query_count, 1), jnp.float32),
    )
    (largest, totals), unused = lax.scan(advance, initial, (key_blocks, id_blocks, key_starts))
    return largest + jnp.log(totals)


def self_mix(
    queries,
    query_start,
    query_ids,
    table_full,
    key_blocks,
    value_blocks,
    id_blocks,
    key_starts,
    logsum,
):

    def advance(accum, packed):
        key_rows, value_rows, key_ids, key_start = packed
        scores, unused = self_scores(
            queries, query_start, query_ids, table_full, key_rows, key_start, key_ids
        )
        weights = jnp.exp(scores - logsum).astype(jnp.bfloat16)
        return (
            accum
            + jnp.einsum("hqk,hkd->hqd", weights, value_rows, preferred_element_type=jnp.float32),
            None,
        )

    initial = jnp.zeros((HEADS, queries.shape[1], HEAD_DIM), jnp.float32)
    accum, unused = lax.scan(advance, initial, (key_blocks, value_blocks, id_blocks, key_starts))
    return accum


def self_backward(
    queries,
    query_start,
    query_ids,
    table_full,
    key_blocks,
    value_blocks,
    id_blocks,
    key_starts,
    logsum,
    grad_mixed,
):
    query_count = queries.shape[1]

    def dots(accum, packed):
        key_rows, value_rows, key_ids, key_start = packed
        scores, unused = self_scores(
            queries, query_start, query_ids, table_full, key_rows, key_start, key_ids
        )
        chances = jnp.exp(scores - logsum)
        grad_chances = jnp.einsum(
            "hqd,hkd->hqk", grad_mixed, value_rows, preferred_element_type=jnp.float32
        )
        return (accum + jnp.sum(chances * grad_chances, axis=-1, keepdims=True), None)

    row_dots, unused = lax.scan(
        dots,
        jnp.zeros((HEADS, query_count, 1), jnp.float32),
        (key_blocks, value_blocks, id_blocks, key_starts),
    )

    def advance(running, packed):
        grad_queries, grad_table = running
        key_rows, value_rows, key_ids, key_start = packed
        scores, one_hot = self_scores(
            queries, query_start, query_ids, table_full, key_rows, key_start, key_ids
        )
        chances = jnp.exp(scores - logsum)
        grad_chances = jnp.einsum(
            "hqd,hkd->hqk", grad_mixed, value_rows, preferred_element_type=jnp.float32
        )
        grad_scores = chances * (grad_chances - row_dots)
        rounded = grad_scores.astype(jnp.bfloat16)
        grad_values = jnp.einsum(
            "hqk,hqd->hkd",
            chances.astype(jnp.bfloat16),
            grad_mixed,
            preferred_element_type=jnp.float32,
        )
        grad_keys = jnp.einsum("hqk,hqd->hkd", rounded, queries, preferred_element_type=jnp.float32)
        grad_queries = grad_queries + jnp.einsum(
            "hqk,hkd->hqd", rounded, key_rows, preferred_element_type=jnp.float32
        )
        grad_table = grad_table + jnp.einsum(
            "bn,hn->bh",
            one_hot,
            grad_scores.reshape(HEADS, -1),
            precision=lax.Precision.HIGHEST,
            preferred_element_type=jnp.float32,
        )
        return ((grad_queries, grad_table), (grad_keys, grad_values))

    initial = (
        jnp.zeros((HEADS, query_count, HEAD_DIM), jnp.float32),
        jnp.zeros((table_full.shape[0], HEADS), jnp.float32),
    )
    (grad_queries, grad_table), (grad_keys, grad_values) = lax.scan(
        advance, initial, (key_blocks, value_blocks, id_blocks, key_starts)
    )
    return (join_heads(grad_queries), grad_table, from_blocks(grad_keys), from_blocks(grad_values))


def cross_forward(queries, key_heads, value_heads, allowed):
    scores = jnp.where(
        allowed,
        jnp.einsum("hqd,hkd->hqk", queries, key_heads, preferred_element_type=jnp.float32),
        masked_score,
    )
    largest = jnp.max(scores, axis=-1, keepdims=True)
    logsum = largest + jnp.log(jnp.sum(jnp.exp(scores - largest), axis=-1, keepdims=True))
    weights = jnp.exp(scores - logsum).astype(jnp.bfloat16)
    mixed = jnp.einsum("hqk,hkd->hqd", weights, value_heads, preferred_element_type=jnp.float32)
    return (mixed, logsum)


def cross_backward(queries, key_heads, value_heads, allowed, logsum, grad_mixed):
    scores = jnp.where(
        allowed,
        jnp.einsum("hqd,hkd->hqk", queries, key_heads, preferred_element_type=jnp.float32),
        masked_score,
    )
    chances = jnp.exp(scores - logsum)
    grad_values = jnp.einsum(
        "hqk,hqd->hkd", chances.astype(jnp.bfloat16), grad_mixed, preferred_element_type=jnp.float32
    )
    grad_chances = jnp.einsum(
        "hqd,hkd->hqk", grad_mixed, value_heads, preferred_element_type=jnp.float32
    )
    grad_scores = chances * (grad_chances - jnp.sum(chances * grad_chances, axis=-1, keepdims=True))
    rounded = grad_scores.astype(jnp.bfloat16)
    grad_queries = jnp.einsum(
        "hqk,hkd->hqd", rounded, key_heads, preferred_element_type=jnp.float32
    )
    grad_keys = jnp.einsum("hqk,hqd->hkd", rounded, queries, preferred_element_type=jnp.float32)
    return (join_heads(grad_queries), join_heads(grad_keys), join_heads(grad_values))


def shards(
    inputs,
    encoder,
    segments,
    enc_segments,
    self_query,
    self_key,
    self_value,
    self_output,
    cross_query,
    cross_key,
    cross_value,
    cross_output,
    gate_weight,
    up_weight,
    down_weight,
    self_gain,
    cross_gain,
    feed_gain,
    bias_table,
    cotangent,
):
    fetched = (
        lax.all_gather(self_query, "shard", axis=0, tiled=True),
        lax.all_gather(self_key, "shard", axis=0, tiled=True),
        lax.all_gather(self_value, "shard", axis=0, tiled=True),
        lax.all_gather(self_output, "shard", axis=0, tiled=True),
        lax.all_gather(cross_query, "shard", axis=0, tiled=True),
        lax.all_gather(cross_key, "shard", axis=0, tiled=True),
        lax.all_gather(cross_value, "shard", axis=0, tiled=True),
        lax.all_gather(cross_output, "shard", axis=0, tiled=True),
        lax.all_gather(gate_weight, "shard", axis=0, tiled=True),
        lax.all_gather(up_weight, "shard", axis=0, tiled=True),
        lax.all_gather(down_weight, "shard", axis=0, tiled=True),
        lax.all_gather(self_gain, "shard", axis=0, tiled=True),
        lax.all_gather(cross_gain, "shard", axis=0, tiled=True),
        lax.all_gather(feed_gain, "shard", axis=0, tiled=True),
        lax.all_gather(bias_table, "shard", axis=0, tiled=True),
    )
    (
        w_query,
        w_key,
        w_value,
        w_output,
        c_query,
        c_key,
        c_value,
        c_output,
        w_gate,
        w_up,
        w_down,
        g_self,
        g_cross,
        g_feed,
        table_full,
    ) = fetched
    gain_self = g_self.astype(jnp.float32)
    gain_cross = g_cross.astype(jnp.float32)
    gain_feed = g_feed.astype(jnp.float32)
    source = inputs[0].astype(jnp.float32)
    memory = encoder[0]
    segment_ids = segments[0]
    memory_ids = enc_segments[0]
    tokens_here = source.shape[0]
    length = segment_ids.shape[0]
    block_size = math.gcd(length, 512)
    block_count = length // block_size
    query_start = lax.axis_index("shard") * tokens_here
    query_ids = lax.dynamic_slice_in_dim(segment_ids, query_start, tokens_here)
    id_blocks = segment_ids.reshape(block_count, block_size)
    key_starts = jnp.arange(block_count, dtype=jnp.int32) * block_size
    cross_allowed = (query_ids[:, None] == memory_ids[None, :])[None]
    normed_self = rms_scale(source, gain_self).astype(jnp.bfloat16)
    query_heads = split_heads(product(normed_self, w_query).astype(jnp.bfloat16))
    key_local = product(normed_self, w_key).astype(jnp.bfloat16)
    value_local = product(normed_self, w_value).astype(jnp.bfloat16)
    keys_all, values_all = (
        lax.all_gather(key_local, "shard", axis=0, tiled=True),
        lax.all_gather(value_local, "shard", axis=0, tiled=True),
    )
    key_blocks = to_blocks(keys_all, block_count)
    value_blocks = to_blocks(values_all, block_count)
    logsum_self = self_logsum(
        query_heads, query_start, query_ids, table_full, key_blocks, id_blocks, key_starts
    )
    mixed_self = self_mix(
        query_heads,
        query_start,
        query_ids,
        table_full,
        key_blocks,
        value_blocks,
        id_blocks,
        key_starts,
        logsum_self,
    )
    joined_self = join_heads(mixed_self).astype(jnp.bfloat16)
    after_self = source + product(joined_self, w_output)
    normed_cross = rms_scale(after_self, gain_cross).astype(jnp.bfloat16)
    query_cross = split_heads(product(normed_cross, c_query).astype(jnp.bfloat16))
    key_cross_local = product(memory, c_key).astype(jnp.bfloat16)
    value_cross_local = product(memory, c_value).astype(jnp.bfloat16)
    keys_cross, values_cross = (
        lax.all_gather(key_cross_local, "shard", axis=0, tiled=True),
        lax.all_gather(value_cross_local, "shard", axis=0, tiled=True),
    )
    key_cross = split_heads(keys_cross)
    value_cross = split_heads(values_cross)
    mixed_cross, logsum_cross = cross_forward(query_cross, key_cross, value_cross, cross_allowed)
    joined_cross = join_heads(mixed_cross).astype(jnp.bfloat16)
    after_cross = after_self + product(joined_cross, c_output)
    normed_feed = rms_scale(after_cross, gain_feed).astype(jnp.bfloat16)
    gate_act = product(normed_feed, w_gate)
    up_act = product(normed_feed, w_up)
    hidden = (jax.nn.gelu(gate_act, approximate=True) * up_act).astype(jnp.bfloat16)
    outcome = after_cross + product(hidden, w_down)
    fetched = (
        lax.all_gather(self_query, "shard", axis=0, tiled=True),
        lax.all_gather(self_key, "shard", axis=0, tiled=True),
        lax.all_gather(self_value, "shard", axis=0, tiled=True),
        lax.all_gather(self_output, "shard", axis=0, tiled=True),
        lax.all_gather(cross_query, "shard", axis=0, tiled=True),
        lax.all_gather(cross_key, "shard", axis=0, tiled=True),
        lax.all_gather(cross_value, "shard", axis=0, tiled=True),
        lax.all_gather(cross_output, "shard", axis=0, tiled=True),
        lax.all_gather(gate_weight, "shard", axis=0, tiled=True),
        lax.all_gather(up_weight, "shard", axis=0, tiled=True),
        lax.all_gather(down_weight, "shard", axis=0, tiled=True),
        lax.all_gather(self_gain, "shard", axis=0, tiled=True),
        lax.all_gather(cross_gain, "shard", axis=0, tiled=True),
        lax.all_gather(feed_gain, "shard", axis=0, tiled=True),
        lax.all_gather(bias_table, "shard", axis=0, tiled=True),
    )
    (
        w_query,
        w_key,
        w_value,
        w_output,
        c_query,
        c_key,
        c_value,
        c_output,
        w_gate,
        w_up,
        w_down,
        g_self,
        g_cross,
        g_feed,
        table_full,
    ) = fetched
    gain_self = g_self.astype(jnp.float32)
    gain_cross = g_cross.astype(jnp.float32)
    gain_feed = g_feed.astype(jnp.float32)
    keys_all, values_all = (
        lax.all_gather(key_local, "shard", axis=0, tiled=True),
        lax.all_gather(value_local, "shard", axis=0, tiled=True),
    )
    key_blocks = to_blocks(keys_all, block_count)
    value_blocks = to_blocks(values_all, block_count)
    grad_out = cotangent[0].astype(jnp.float32)
    grad_down_in = cotangent[0]
    d_down = product_rows(hidden, grad_down_in)
    grad_hidden = product_cols(grad_down_in, w_down)

    def activation(gate_in, up_in):
        return jax.nn.gelu(gate_in, approximate=True) * up_in

    unused, pull = jax.vjp(activation, gate_act, up_act)
    grad_gate, grad_up = pull(grad_hidden)
    grad_gate = grad_gate.astype(jnp.bfloat16)
    grad_up = grad_up.astype(jnp.bfloat16)
    d_gate = product_rows(normed_feed, grad_gate)
    d_up = product_rows(normed_feed, grad_up)
    grad_normed_feed = product_cols(grad_gate, w_gate) + product_cols(grad_up, w_up)
    unused, pull = jax.vjp(rms_scale, after_cross, gain_feed)
    norm_part, d_feed_gain = pull(grad_normed_feed)
    grad_cross_total = grad_out + norm_part
    grad_cross_in = grad_cross_total.astype(jnp.bfloat16)
    d_c_output = product_rows(joined_cross, grad_cross_in)
    grad_mixed_cross = split_heads(product_cols(grad_cross_in, c_output).astype(jnp.bfloat16))
    grad_query_cross, grad_keys_cross, grad_values_cross = cross_backward(
        query_cross, key_cross, value_cross, cross_allowed, logsum_cross, grad_mixed_cross
    )
    grad_query_cross = grad_query_cross.astype(jnp.bfloat16)
    key_part, value_part = (
        lax.psum_scatter(
            grad_keys_cross.astype(jnp.bfloat16), "shard", scatter_dimension=0, tiled=True
        ).astype(jnp.float32),
        lax.psum_scatter(
            grad_values_cross.astype(jnp.bfloat16), "shard", scatter_dimension=0, tiled=True
        ).astype(jnp.float32),
    )
    grad_key_cross = key_part.astype(jnp.bfloat16)
    grad_value_cross = value_part.astype(jnp.bfloat16)
    d_c_query = product_rows(normed_cross, grad_query_cross)
    d_c_key = product_rows(memory, grad_key_cross)
    d_c_value = product_rows(memory, grad_value_cross)
    grad_memory = product_cols(grad_key_cross, c_key) + product_cols(grad_value_cross, c_value)
    grad_normed_cross = product_cols(grad_query_cross, c_query)
    unused, pull = jax.vjp(rms_scale, after_self, gain_cross)
    norm_part, d_cross_gain = pull(grad_normed_cross)
    grad_self_total = grad_cross_total + norm_part
    grad_self_in = grad_self_total.astype(jnp.bfloat16)
    d_output = product_rows(joined_self, grad_self_in)
    grad_mixed_self = split_heads(product_cols(grad_self_in, w_output).astype(jnp.bfloat16))
    grad_queries, d_table, grad_keys_full, grad_values_full = self_backward(
        query_heads,
        query_start,
        query_ids,
        table_full,
        key_blocks,
        value_blocks,
        id_blocks,
        key_starts,
        logsum_self,
        grad_mixed_self,
    )
    grad_query_self = grad_queries.astype(jnp.bfloat16)
    key_part, value_part = (
        lax.psum_scatter(
            grad_keys_full.astype(jnp.bfloat16), "shard", scatter_dimension=0, tiled=True
        ).astype(jnp.float32),
        lax.psum_scatter(
            grad_values_full.astype(jnp.bfloat16), "shard", scatter_dimension=0, tiled=True
        ).astype(jnp.float32),
    )
    grad_key_self = key_part.astype(jnp.bfloat16)
    grad_value_self = value_part.astype(jnp.bfloat16)
    d_query = product_rows(normed_self, grad_query_self)
    d_key = product_rows(normed_self, grad_key_self)
    d_value = product_rows(normed_self, grad_value_self)
    grad_normed_self = (
        product_cols(grad_query_self, w_query)
        + product_cols(grad_key_self, w_key)
        + product_cols(grad_value_self, w_value)
    )
    unused, pull = jax.vjp(rms_scale, source, gain_self)
    norm_part, d_self_gain = pull(grad_normed_self)
    grad_source = grad_self_total + norm_part
    summed = (
        lax.psum_scatter(
            d_query.astype(jnp.bfloat16), "shard", scatter_dimension=0, tiled=True
        ).astype(jnp.float32),
        lax.psum_scatter(
            d_key.astype(jnp.bfloat16), "shard", scatter_dimension=0, tiled=True
        ).astype(jnp.float32),
        lax.psum_scatter(
            d_value.astype(jnp.bfloat16), "shard", scatter_dimension=0, tiled=True
        ).astype(jnp.float32),
        lax.psum_scatter(
            d_output.astype(jnp.bfloat16), "shard", scatter_dimension=0, tiled=True
        ).astype(jnp.float32),
        lax.psum_scatter(
            d_c_query.astype(jnp.bfloat16), "shard", scatter_dimension=0, tiled=True
        ).astype(jnp.float32),
        lax.psum_scatter(
            d_c_key.astype(jnp.bfloat16), "shard", scatter_dimension=0, tiled=True
        ).astype(jnp.float32),
        lax.psum_scatter(
            d_c_value.astype(jnp.bfloat16), "shard", scatter_dimension=0, tiled=True
        ).astype(jnp.float32),
        lax.psum_scatter(
            d_c_output.astype(jnp.bfloat16), "shard", scatter_dimension=0, tiled=True
        ).astype(jnp.float32),
        lax.psum_scatter(
            d_gate.astype(jnp.bfloat16), "shard", scatter_dimension=0, tiled=True
        ).astype(jnp.float32),
        lax.psum_scatter(
            d_up.astype(jnp.bfloat16), "shard", scatter_dimension=0, tiled=True
        ).astype(jnp.float32),
        lax.psum_scatter(
            d_down.astype(jnp.bfloat16), "shard", scatter_dimension=0, tiled=True
        ).astype(jnp.float32),
        lax.psum_scatter(
            d_self_gain.astype(jnp.bfloat16), "shard", scatter_dimension=0, tiled=True
        ).astype(jnp.float32),
        lax.psum_scatter(
            d_cross_gain.astype(jnp.bfloat16), "shard", scatter_dimension=0, tiled=True
        ).astype(jnp.float32),
        lax.psum_scatter(
            d_feed_gain.astype(jnp.bfloat16), "shard", scatter_dimension=0, tiled=True
        ).astype(jnp.float32),
        lax.psum_scatter(
            d_table.astype(jnp.bfloat16), "shard", scatter_dimension=0, tiled=True
        ).astype(jnp.float32),
    )
    totals = (
        lax.psum(summed[0].astype(jnp.bfloat16), "rep").astype(jnp.float32),
        lax.psum(summed[1].astype(jnp.bfloat16), "rep").astype(jnp.float32),
        lax.psum(summed[2].astype(jnp.bfloat16), "rep").astype(jnp.float32),
        lax.psum(summed[3].astype(jnp.bfloat16), "rep").astype(jnp.float32),
        lax.psum(summed[4].astype(jnp.bfloat16), "rep").astype(jnp.float32),
        lax.psum(summed[5].astype(jnp.bfloat16), "rep").astype(jnp.float32),
        lax.psum(summed[6].astype(jnp.bfloat16), "rep").astype(jnp.float32),
        lax.psum(summed[7].astype(jnp.bfloat16), "rep").astype(jnp.float32),
        lax.psum(summed[8].astype(jnp.bfloat16), "rep").astype(jnp.float32),
        lax.psum(summed[9].astype(jnp.bfloat16), "rep").astype(jnp.float32),
        lax.psum(summed[10].astype(jnp.bfloat16), "rep").astype(jnp.float32),
        lax.psum(summed[11].astype(jnp.bfloat16), "rep").astype(jnp.float32),
        lax.psum(summed[12].astype(jnp.bfloat16), "rep").astype(jnp.float32),
        lax.psum(summed[13].astype(jnp.bfloat16), "rep").astype(jnp.float32),
        lax.psum(summed[14].astype(jnp.bfloat16), "rep").astype(jnp.float32),
    )
    return (
        outcome.astype(jnp.bfloat16)[None],
        grad_source[None],
        grad_memory[None],
        totals[0],
        totals[1],
        totals[2],
        totals[3],
        totals[4],
        totals[5],
        totals[6],
        totals[7],
        totals[8],
        totals[9],
        totals[10],
        totals[11],
        totals[12],
        totals[13],
        totals[14],
    )


def swap(value, axis, size, step):
    return lax.ppermute(value, axis, [(place, place ^ step) for place in range(size)])


def after(value, *others):
    return lax.optimization_barrier((value, *others))[0]


def run_kernel(name, body, ids, operands, results, scratch=()):
    whole = pl.BlockSpec(memory_space=pltpu.VMEM)
    return pl.pallas_call(
        body,
        out_shape=[jax.ShapeDtypeStruct(shape, kind) for shape, kind in results],
        in_specs=[pl.BlockSpec(memory_space=pltpu.SMEM)] + [whole] * len(operands),
        out_specs=[whole] * len(results),
        scratch_shapes=[pltpu.VMEM(shape, kind) for shape, kind in scratch],
        name=name,
    )(ids, *operands)


low_kind = jnp.bfloat16
full_kind = jnp.float32


def rows_at(place, size):
    return pl.ds(pl.multiple_of(place * size, size), size)


def put_blocks(index, blocks, target):
    size = blocks[0].shape[0]
    for step, block in enumerate(blocks):
        target[rows_at(index ^ step, size), :] = block[...]


def split_cores(index, partial, room, send, keep):
    core = index & 1
    size = send.shape[0]
    room[...] = partial
    keep[...] = room[rows_at(core, size), :]
    send[...] = room[rows_at(1 - core, size), :].astype(low_kind)


def join_cores(index, own, other, room):
    core = index & 1
    size = own.shape[0]
    room[rows_at(core, size), :] = own[...].astype(full_kind)
    room[rows_at(1 - core, size), :] = other[...].astype(full_kind)
    return room[...]


def inverse_rms(values):
    return lax.rsqrt(jnp.mean(values * values, axis=-1, keepdims=True) + epsilon)


def norm_backward(grad, values, gain):
    scale = inverse_rms(values)
    row = jnp.sum(grad * values * scale, axis=0, keepdims=True)
    scaled = grad * gain
    inner = jnp.mean(scaled * values, axis=-1, keepdims=True)
    return scale * scaled - values * (scale * scale * scale * inner), row


def bucket_rows(buckets, length):
    lanes = lax.broadcasted_iota(jnp.int32, (buckets, length), 1)
    distance = jnp.where(lanes == 0, 0, length - lanes)
    return (bucket_of(distance) == lax.broadcasted_iota(jnp.int32, (buckets, length), 0)).astype(
        full_kind
    )


def columns_body(ids, *refs):
    count = len(refs) - 4
    sources, targets = refs[:count], refs[count:]
    for place in range(4):

        @pl.when(ids[0] == place)
        def _():
            for step in range(4):
                start = 0
                for source in sources:
                    width = source.shape[1] // 4
                    begin = (place ^ step) * width
                    targets[step][:, start : start + width] = source[:, begin : begin + width]
                    start += width


def pack_body(ids, source, gain0, gain1, gain2, table, *refs):
    sources, packed, targets = refs[:3], refs[3], refs[4:]
    columns_body(ids, *sources, *targets)
    size, model = source.shape
    packed[:size, :] = source[...]
    rows = table.shape[0]
    line = [gain[...].astype(full_kind).reshape(1, -1) for gain in (gain0, gain1, gain2)]
    width = sum(piece.shape[1] for piece in line)
    line = jnp.concatenate(line + [jnp.zeros((1, model - width), full_kind)], axis=1)
    grid = jnp.concatenate(
        [table[...].astype(full_kind), jnp.zeros((rows, model - table.shape[1]), full_kind)], axis=1
    )
    lines = jnp.concatenate([line, jnp.zeros((7, model), full_kind), grid], axis=0)
    packed[size:, :] = lines.astype(low_kind)


def split_columns_body(ids, gate, up, own, send1, send2, send3):
    column = ids[1] & 1
    width = gate.shape[1] // 4
    half = send2.shape[0]
    for place in range(4):

        @pl.when(ids[0] == place)
        def _():
            for step, target in enumerate((own, send1, send2, send3)):
                begin = (place ^ step) * width
                rows = slice(None) if step < 2 else rows_at(column, half)
                for number, source in enumerate((gate, up)):
                    target[:, number * width : (number + 1) * width] = source[
                        rows, begin : begin + width
                    ]


def heads_of(matrix, number, part, wide):
    start = part * wide + number * HEAD_DIM
    return matrix[:, start : start + HEAD_DIM]


def stack_heads(matrix, target, first):
    for number in range(matrix.shape[1] // HEAD_DIM):
        target[first + number, : matrix.shape[0], :] = matrix[
            :, number * HEAD_DIM : (number + 1) * HEAD_DIM
        ]


def joined_heads(source, first, count):
    return jnp.concatenate([source[first + number] for number in range(count)], axis=1)


def each_head(count, body):
    def step(number, unused):
        body(number)
        return unused

    lax.fori_loop(0, count, step, 0)


def softmax_rows(scores, allowed):
    scores = jnp.where(allowed, scores, masked_score)
    powers = jnp.exp(scores - jnp.max(scores, axis=-1, keepdims=True))
    return powers * (1.0 / jnp.sum(powers, axis=-1, keepdims=True))


def self_half(half, ids, source, weight, gains, rows, mapped_before, output, seg_col, seg_row, outs):
    normed_out, mapped_out, chances_out, mixed_out, send, keep, room, heads, joined = outs
    size = normed_out.shape[0]
    wide = output.shape[0]
    count = wide // HEAD_DIM
    normed = (source * inverse_rms(source) * gains[0:1, :]).astype(low_kind)
    normed_out[...] = normed
    mapped = product(normed, weight).astype(low_kind)
    mapped_out[...] = mapped
    every = mapped if half == 0 else jnp.concatenate([mapped_before, mapped], axis=0)
    keys = every.shape[0]
    places = lax.broadcasted_iota(jnp.int32, (size, keys), 0) + half * size
    others = lax.broadcasted_iota(jnp.int32, (size, keys), 1)
    allowed = (places >= others) & (seg_col == seg_row[:, :keys])
    stack_heads(mapped[:, :wide], heads, 0)
    stack_heads(every[:, wide:], heads, count)

    def one_head(number):
        line = jnp.broadcast_to(rows[pl.ds(number, 1), :], (size, rows.shape[1]))
        bias = pltpu.roll(line, half * size, 1, stride=1, stride_axis=0)[:, :keys]
        scores = product_cols(heads[number, :size, :], heads[count + number, :keys, :])
        chances = softmax_rows(scores + bias, allowed).astype(low_kind)
        chances_out[number] = chances
        joined[number] = product(chances, heads[2 * count + number, :keys, :]).astype(low_kind)

    each_head(count, one_head)
    mixed = joined_heads(joined, 0, count)
    mixed_out[...] = mixed
    split_cores(ids[0], product(mixed, output), room, send, keep)


def self_first_body(
    ids, x0, x1, x2, x3, w0, w1, w2, w3, output, seg_col, seg_row,
    source_out, weight_out, gains_out, rows_out,
    normed_out, mapped_out, chances_out, mixed_out, send, keep,
    room, heads, joined, small, lines,
):
    index = ids[0]
    tokens = source_out.shape[0] // 4
    put_blocks(index, [block.at[:tokens] for block in (x0, x1, x2, x3)], source_out)
    put_blocks(index, (w0, w1, w2, w3), weight_out)
    for step, block in enumerate((x0, x1, x2, x3)):
        small[rows_at(index ^ step, 16), :] = block[tokens:, :].astype(full_kind)
    model = source_out.shape[1]
    part = model // 4
    for place in range(3):
        gains_out[place : place + 1, :] = jnp.concatenate(
            [small[16 * t : 16 * t + 1, part * place : part * (place + 1)] for t in range(4)],
            axis=1,
        )
    gains_out[3:8, :] = jnp.zeros((5, model), full_kind)
    table = jnp.concatenate([small[16 * t + 8 : 16 * t + 16, :128] for t in range(4)], axis=0)
    hot = bucket_rows(table.shape[0], rows_out.shape[1])
    lines[...] = product_rows(table.astype(low_kind), hot.astype(low_kind))
    heads_here = chances_out.shape[0]
    for number in range(heads_here):
        rows_out[number : number + 1, :] = lines[pl.ds(index * heads_here + number, 1), :]
    rows_out[heads_here:8, :] = jnp.zeros((8 - heads_here, rows_out.shape[1]), full_kind)
    size = normed_out.shape[0]
    self_half(
        0, ids, source_out[:size, :].astype(full_kind), weight_out[...], gains_out, rows_out, None,
        output[...], seg_col[:size, :], seg_row[...],
        (normed_out, mapped_out, chances_out, mixed_out, send, keep, room, heads, joined),
    )


def self_second_body(
    ids, source, weight, gains, rows, mapped_before, output, seg_col, seg_row,
    normed_out, mapped_out, chances_out, mixed_out, send, keep, room, heads, joined,
):
    size = normed_out.shape[0]
    self_half(
        1, ids, source[size:, :].astype(full_kind), weight[...], gains, rows, mapped_before[...],
        output[...], seg_col[size:, :], seg_row[...],
        (normed_out, mapped_out, chances_out, mixed_out, send, keep, room, heads, joined),
    )


def cross_keys_body(ids, e0, e1, e2, e3, w0, w1, w2, w3, memory_out, weight_out, mapped_out):
    put_blocks(ids[0], (e0, e1, e2, e3), memory_out)
    put_blocks(ids[0], (w0, w1, w2, w3), weight_out)
    wide = weight_out.shape[1] // 3
    mapped_out[...] = product(memory_out[...], weight_out[:, wide:]).astype(low_kind)


def cross_body(
    half, ids, source, own, other, gains, weight, mapped, output, seg_col, enc_row,
    after_out, normed_out, query_out, chances_out, mixed_out, send, keep, room, heads, joined,
):
    size = after_out.shape[0]
    wide = output.shape[0]
    count = wide // HEAD_DIM
    start = half * size
    values = source[start : start + size, :].astype(full_kind) + join_cores(
        ids[0], own, other, room
    )
    after_out[...] = values
    normed = (values * inverse_rms(values) * gains[1:2, :]).astype(low_kind)
    normed_out[...] = normed
    query = product(normed, weight[:, :wide]).astype(low_kind)
    query_out[...] = query
    allowed = seg_col[start : start + size, :] == enc_row[...]
    stack_heads(query, heads, 0)
    stack_heads(mapped[...], heads, count)

    def one_head(number):
        scores = product_cols(heads[number, :size, :], heads[count + number])
        chances = softmax_rows(scores, allowed).astype(low_kind)
        chances_out[number] = chances
        joined[number] = product(chances, heads[2 * count + number]).astype(low_kind)

    each_head(count, one_head)
    mixed = joined_heads(joined, 0, count)
    mixed_out[...] = mixed
    split_cores(ids[0], product(mixed, output[...]), room, send, keep)


def feed_join_body(ids, w0, w1, w2, w2x, w3, w3x, g0, g1, g2, g3, weight_out, grad_out):
    index, column = ids[0], ids[1] & 1
    put_blocks(index, (w0, w1), weight_out)
    half = w2.shape[0]
    for step, mine, other in ((2, w2, w2x), (3, w3, w3x)):
        weight_out[rows_at(2 * (index ^ step) + column, half), :] = mine[...]
        weight_out[rows_at(2 * (index ^ step) + 1 - column, half), :] = other[...]
    put_blocks(ids[0], (g0, g1, g2, g3), grad_out)


def feed_body(half, ids, before, own, other, gains, weight, down, grad_out, *refs):
    parts = refs[:2] if half else ()
    after_out, normed_out, hidden_out, acts_out, *rest = refs[len(parts) :]
    size = after_out.shape[0]
    start = half * size
    units = down.shape[0]
    room = rest[-1]
    values = before[...] + join_cores(ids[0], own, other, room)
    after_out[...] = values
    normed = (values * inverse_rms(values) * gains[2:3, :]).astype(low_kind)
    normed_out[...] = normed
    acts = product(normed, weight[...])
    gate, up = acts[:, :units], acts[:, units:]
    root = math.sqrt(2 / math.pi)
    square = gate * gate
    bend = jnp.tanh(root * gate * (1.0 + 0.044715 * square))
    curve = 0.5 * gate * (1.0 + bend)
    slope = 0.5 * (1.0 + bend) + 0.5 * gate * (1.0 - bend * bend) * root * (
        1.0 + 3 * 0.044715 * square
    )
    hidden = (curve * up).astype(low_kind)
    hidden_out[...] = hidden
    grad_hidden = product_cols(grad_out[start : start + size, :], down[...])
    acts_out[:, :units] = (grad_hidden * up * slope).astype(low_kind)
    acts_out[:, units:] = (grad_hidden * curve).astype(low_kind)
    grad = product_cols(acts_out[...], weight[...])
    result = product(hidden, down[...])
    if half:
        send, keep, out_send, out_keep = rest[:4]
        for place, part in ((0, parts[0][...]), (1, grad)):
            split_cores(ids[0], part, room, send.at[place], keep.at[place])
        for place, part in ((0, parts[1][...]), (1, result)):
            split_cores(ids[0], part, room, out_send.at[place], out_keep.at[place])
    else:
        rest[0][...] = grad
        rest[1][...] = result


def rep_bits(ids):
    rep = ids[1]
    return rep & 1, (rep >> 1) & 1, rep >> 2


def each_chunk(ids, keep_first, send_first, keep_second, send_second, body):
    column, low, unused = rep_bits(ids)

    def step(slot, unused):
        high, middle = slot >> 1, slot & 1
        for target, bit in ((keep_first, column), (send_first, 1 - column)):
            body(target.at[slot], 4 * high + 2 * middle + bit, 0)
        for target, bit in ((keep_second, low), (send_second, 1 - low)):
            body(target.at[slot], 4 * high + 2 * bit + middle, 1)
        return unused

    lax.fori_loop(0, 4, step, 0)


def feed_weights_body(
    ids, normed0, normed1, acts0, acts1, hidden0, hidden1, grad_out,
    keep_first, send_first, keep_second, send_second, feed, down,
):
    size = normed0.shape[0]
    feed[...] = (
        product_rows(normed0[...], acts0[...]) + product_rows(normed1[...], acts1[...])
    ).astype(low_kind)
    down[...] = (
        product_rows(hidden0[...], grad_out[:size, :])
        + product_rows(hidden1[...], grad_out[size:, :])
    ).astype(low_kind)
    rows = feed.shape[0] // 4
    width = feed.shape[1] // 8
    small = down.shape[0] // 8
    lanes = down.shape[1] // 2

    def fill(target, chunk, part):
        for place in range(2):
            start = (2 * part + place) * rows
            target[place] = feed[start : start + rows, rows_at(chunk, width)]
        for piece in range(lanes // width):
            start = part * lanes + piece * width
            target[2, piece * small : (piece + 1) * small, :] = down[
                rows_at(chunk, small), start : start + width
            ]

    each_chunk(ids, keep_first, send_first, keep_second, send_second, fill)


def store_small_chunks(ids, columns, output, buffers):
    small = output.shape[0] // 8
    lanes = output.shape[1] // 2
    quarter = columns.shape[0] // 4

    def fill(target, chunk, part):
        for place in range(2):
            start = (2 * part + place) * quarter + chunk * small
            target[place] = columns[pl.ds(pl.multiple_of(start, 8), small), :].astype(low_kind)
        target[2] = jnp.zeros(target.shape[1:], low_kind)
        target[2, :, :lanes] = output[
            pl.ds(pl.multiple_of(chunk * small, 8), small), part * lanes : (part + 1) * lanes
        ].astype(low_kind)

    each_chunk(ids, *buffers, fill)


small_lanes = slice(3 * 128, 4 * 128)


def small_pieces(count, size):
    half = (count - size) // 2
    yield (0, 0), slice(0, size)
    yield (0, 1), slice(size, size + half)
    yield (1, 0), slice(size + half, count)


def halve_body(ids, keep_first, came_first, keep_second, came_second, *outs):
    new_first, send_first, new_second, send_second = outs
    column, low, unused = rep_bits(ids)
    for keep, came, new, send, bit in (
        (keep_first, came_first, new_first, send_first, low),
        (keep_second, came_second, new_second, send_second, column),
    ):
        for high in range(2):
            for target, place in ((new, 2 * high + bit), (send, 2 * high + 1 - bit)):
                total = keep[place].astype(full_kind) + came[place].astype(full_kind)
                target[high] = total.astype(target.dtype)


def quarter_body(ids, keep_first, came_first, keep_second, came_second, total):
    for part, (keep, came) in enumerate(((keep_first, came_first), (keep_second, came_second))):
        total[part] = (keep[...] + came[...].astype(full_kind)).astype(low_kind)


def quarter_small_body(
    ids, keep_first, came_first, keep_second, came_second, vector, near, far, across, total
):
    quarter_body(ids, keep_first, came_first, keep_second, came_second, total)
    lines = (vector[...] + near[...] + far[...] + across[...]).astype(low_kind)
    for (part, high), piece in small_pieces(lines.shape[0], total.shape[3]):
        total[part, high, 2, : piece.stop - piece.start, small_lanes] = lines[piece, :]


def trade_body(ids, mine, came, own, send1, send2, send3, rows, room):
    for part in range(2):
        for high in range(2):
            total = (
                mine[part, high].astype(full_kind) + came[part, high].astype(full_kind)
            ).astype(low_kind)
            room[2 * part, high] = total[0]
            room[2 * part + 1, high] = total[1]
            rows[part, high] = total[2]
    for step, target in enumerate((own, send1, send2, send3)):
        target[...] = room[ids[0] ^ step]


def gather_body(ids, own, came1, came2, came3, rows, first, second):
    for place, block in enumerate((own, came1, came2)):
        first[:, place] = block[...]
    for place, block in enumerate((came3, rows.at[0], rows.at[1])):
        second[:, place] = block[...]


def all_pieces(ids, firsts, seconds):
    for step in range(4):
        for high in range(2):
            chunk = 4 * high + ((ids[1] & 3) ^ step)
            yield firsts[step].at[high], seconds[step].at[high], high, chunk


def feed_out_body(ids, *refs):
    firsts, seconds, (gate, up, down) = refs[:4], refs[4:8], refs[8:]
    units = gate.shape[1] // 4
    small = down.shape[0] // 8
    for first, second, high, chunk in all_pieces(ids, firsts, seconds):
        width = first.shape[2]
        target = (gate, up)[high]
        for step in range(4):
            block = second[0] if step == 3 else first[step]
            start = (ids[0] ^ step) * units + (chunk & 3) * width
            target[:, pl.ds(pl.multiple_of(start, width), width)] = block.astype(full_kind)
        for piece in range(down.shape[1] // width):
            part, begin = piece // 3, piece % 3 * small
            down[rows_at(chunk, small), piece * width : (piece + 1) * width] = second[
                1 + part, begin : begin + small
            ].astype(full_kind)


def small_out_body(ids, *refs):
    firsts, seconds, outs, room = refs[:4], refs[4:8], refs[8:12], refs[-1]
    small = room.shape[1] // 8
    lanes = outs[3].shape[1] // 2
    wide = outs[0].shape[0]
    for first, second, high, chunk in all_pieces(ids, firsts, seconds):
        where = pl.ds(pl.multiple_of(chunk * small, 8), small)
        for step in range(4):
            block = second[0] if step == 3 else first[step]
            room[step, where, :] = block.astype(full_kind)
        for part in range(2):
            outs[3][where, part * lanes : (part + 1) * lanes] = second[1 + part][:, :lanes].astype(
                full_kind
            )
    for place in range(4):
        for number in range(3):
            outs[number][:, place * wide : (place + 1) * wide] = room[
                ids[0] ^ place, :, number * wide : (number + 1) * wide
            ]


def last_out_body(ids, *refs):
    *refs, vector, room, lines = refs
    small_out_body(ids, *refs, room)
    seconds = refs[4:8]
    for step, second in enumerate(seconds):
        place = (ids[1] & 3) ^ step
        for (part, high), piece in small_pieces(vector.shape[0], second.shape[2]):
            lines[place, piece, :] = second[
                high, 1 + part, : piece.stop - piece.start, small_lanes
            ].astype(full_kind)
    vector[...] = (lines[0] + lines[1]) + (lines[2] + lines[3])


def attention_backward(grad, query, keys, values, chances):
    full = chances.astype(full_kind)
    grad_chances = product_cols(grad, values)
    grad_scores = full * (grad_chances - jnp.sum(full * grad_chances, axis=-1, keepdims=True))
    rounded = grad_scores.astype(low_kind)
    return (
        grad_scores,
        product(rounded, keys).astype(low_kind),
        product_rows(rounded, query),
        product_rows(chances, grad),
    )


def join_halves(index, own, other, room):
    core = index & 1
    size = own.shape[1]
    for chip in range(2):
        room[rows_at(core + 2 * chip, size), :] = own[chip].astype(full_kind)
        room[rows_at(1 - core + 2 * chip, size), :] = other[chip].astype(full_kind)
    return room[...]


def cross_back_body(
    ids, grad_out, own, other, values0, values1, gains, output, query0, query1, chances0, chances1,
    mapped, weight, total_out, low_out, query_out, sums_out, row_out, send, keep, room, heads, joined,
):
    wide = output.shape[0]
    join_halves(ids[0], own, other, room)
    size = values0.shape[0]
    row = 0.0
    for half, values in ((0, values0), (1, values1)):
        part = slice(half * size, (half + 1) * size)
        grad, piece = norm_backward(room[part, :], values[...], gains[2:3, :])
        row = row + piece
        total = grad_out[part, :].astype(full_kind) + grad
        total_out[part, :] = total
        low_out[part, :] = total.astype(low_kind)
    row_out[...] = jnp.broadcast_to(row, row_out.shape)
    grad_mixed = product_cols(low_out[...], output[...]).astype(low_kind)
    count = wide // HEAD_DIM
    stack_heads(grad_mixed, heads, 0)
    stack_heads(jnp.concatenate([query0[...], query1[...]], axis=0), heads, count)
    stack_heads(mapped[...], heads, 2 * count)

    def one_head(number):
        chances = jnp.concatenate([chances0[number], chances1[number]], axis=0)
        unused, grad_query, grad_keys, grad_values = attention_backward(
            heads[number], heads[count + number], heads[2 * count + number],
            heads[3 * count + number], chances,
        )
        joined[number] = grad_query
        joined[count + number] = grad_keys.astype(low_kind)
        joined[2 * count + number] = grad_values.astype(low_kind)

    each_head(count, one_head)
    query_out[...] = joined_heads(joined, 0, count)
    sums_out[...] = joined_heads(joined, count, 2 * count)
    scatter_cores(ids[0], product_cols(query_out[...], weight[:, :wide]), room, send, keep)


def cross_weights_body(
    ids, normed0, normed1, query, memory, sums, mixed0, mixed1, low, weight,
    keep_first, send_first, keep_second, send_second, send, keep, room, columns, output,
):
    wide = query.shape[1]
    size = normed0.shape[0]
    columns[:, :wide] = product_rows(normed0[...], query[:size, :]) + product_rows(
        normed1[...], query[size:, :]
    )
    columns[:, wide:] = product_rows(memory[...], sums[...])
    output[...] = product_rows(mixed0[...], low[:size, :]) + product_rows(mixed1[...], low[size:, :])
    store_small_chunks(ids, columns, output, (keep_first, send_first, keep_second, send_second))
    scatter_cores(ids[0], product_cols(sums[...], weight[:, wide:]), room, send, keep)


def scatter_cores(index, partial, room, send, keep):
    core = index & 1
    size = send.shape[1]
    room[...] = partial
    for chip in range(2):
        keep[chip] = room[rows_at(core + 2 * chip, size), :]
        send[chip] = room[rows_at(1 - core + 2 * chip, size), :].astype(low_kind)


def diagonal_sums(matrix):
    width = matrix.shape[1]
    size = matrix.shape[0]
    while size > 1:
        size //= 2
        matrix = matrix[:size] + pltpu.roll(matrix[size:], width - size, 1)
    return matrix


def self_back_body(
    ids, total, own, other, values0, values1, gains, output, mapped0, mapped1, chances0, chances1,
    total_out, low_out, query_out, sums_out, row_out, table_out, room, heads, joined,
):
    wide = output.shape[0]
    join_halves(ids[0], own, other, room)
    size = values0.shape[0]
    row = 0.0
    for half, values in ((0, values0), (1, values1)):
        part = slice(half * size, (half + 1) * size)
        grad, piece = norm_backward(room[part, :], values[...], gains[1:2, :])
        row = row + piece
        new_total = total[part, :] + grad
        total_out[part, :] = new_total
        low_out[part, :] = new_total.astype(low_kind)
    row_out[...] = jnp.broadcast_to(row, row_out.shape)
    grad_mixed = product_cols(low_out[...], output[...]).astype(low_kind)
    buckets = table_out.shape[0]
    hot = bucket_rows(buckets, 2 * size)
    count = wide // HEAD_DIM
    stack_heads(grad_mixed, heads, 0)
    stack_heads(jnp.concatenate([mapped0[...], mapped1[...]], axis=0), heads, count)
    table_out[...] = jnp.zeros(table_out.shape, full_kind)

    def one_head(number):
        line = sums = None
        for half, chances in ((1, chances1), (0, chances0)):
            part = slice(half * size, (half + 1) * size)
            seen = slice(0, (half + 1) * size)
            grad_scores, grad_query, grad_keys, grad_values = attention_backward(
                heads[number, part, :], heads[count + number, part, :],
                heads[2 * count + number, seen, :], heads[3 * count + number, seen, :],
                chances[number],
            )
            joined[number, part, :] = grad_query
            if half:
                line = pltpu.roll(diagonal_sums(grad_scores), size, 1)
                sums = (grad_keys, grad_values)
            else:
                empty = jnp.zeros((size, size), full_kind)
                line = line + diagonal_sums(jnp.concatenate([grad_scores, empty], axis=1))
                for place, first, later in ((1, grad_keys, sums[0]), (2, grad_values, sums[1])):
                    joined[place * count + number, :size, :] = (later[:size] + first).astype(low_kind)
                    joined[place * count + number, size:, :] = later[size:].astype(low_kind)
        column = jnp.sum(hot * line, axis=1, keepdims=True)
        lanes = lax.broadcasted_iota(jnp.int32, table_out.shape, 1)
        table_out[...] += jnp.where(lanes == number, column, 0.0)

    each_head(count, one_head)
    query_out[...] = joined_heads(joined, 0, count)
    sums_out[...] = joined_heads(joined, count, 2 * count)


def self_weights_body(
    ids, normed0, normed1, query, sums, mixed0, mixed1, low, weight,
    keep_first, send_first, keep_second, send_second, send, keep, room, columns, output, merged,
):
    wide = query.shape[1]
    size = normed0.shape[0]
    merged[:, :wide] = query[...]
    merged[:, wide:] = sums[...]
    columns[...] = product_rows(normed0[...], merged[:size, :]) + product_rows(
        normed1[...], merged[size:, :]
    )
    output[...] = product_rows(mixed0[...], low[:size, :]) + product_rows(mixed1[...], low[size:, :])
    store_small_chunks(ids, columns, output, (keep_first, send_first, keep_second, send_second))
    scatter_cores(ids[0], product_cols(merged[...], weight[...]), room, send, keep)


def finish_body(ids, source, mine, far, gains, total, cross_row, feed_row, table, grad_out, vector):
    index = ids[0]
    size, model = source.shape
    grad, row = norm_backward(
        mine[...] + far[...].astype(full_kind), source[...].astype(full_kind), gains[0:1, :]
    )
    grad_out[...] = total[rows_at(index, size), :] + grad
    lanes = lax.broadcasted_iota(jnp.int32, (1, model), 1)
    part = model // 4
    here = (lanes >= index * part) & (lanes < (index + 1) * part)
    pieces = []
    for line in (row, jnp.where(here, cross_row[0:1, :], 0.0), jnp.where(here, feed_row[0:1, :], 0.0)):
        pieces += [line[:, start : start + 128] for start in range(0, model, 128)]
    pieces += [jnp.zeros((-len(pieces) % 8, 128), full_kind)]
    vector[: vector.shape[0] - table.shape[0], :] = jnp.concatenate(pieces, axis=0)
    vector[vector.shape[0] - table.shape[0] :, :] = pltpu.roll(
        table[...], index * (HEADS // 4), 1
    )


def chip_pair_body(ids, keep, arrived, mine, other):
    chip = ids[0] >> 1
    mine[...] = keep[chip] + arrived[chip].astype(full_kind)
    other[...] = (keep[1 - chip] + arrived[1 - chip].astype(full_kind)).astype(low_kind)


class Kernels:
    def __init__(self, ids):
        self.ids = ids

    def __call__(self, name, body, operands, results, scratch=(), cover=()):
        outs = run_kernel(name, body, self.ids, operands, results, scratch)
        if cover:
            outs = after(tuple(outs), *cover)
        self.ids = after(self.ids, outs[0])
        return outs

    def wait(self, *values):
        self.ids = after(self.ids, *values)


def rep_swap(value, step):
    return swap(value, "rep", 8, step)


def shard_swap(value, step):
    return swap(value, "shard", 4, step)


class Reduction:
    def __init__(self, call, name, buffers):
        self.call, self.name = call, name
        self.keeps = (buffers[0], buffers[2])
        self.came = (rep_swap(buffers[1], 1), rep_swap(buffers[3], 2))
        self.shape = buffers[0].shape[1:]

    def halve(self, cover=()):
        results = []
        for unused in range(2):
            results += [((2,) + self.shape, full_kind), ((2,) + self.shape, low_kind)]
        outs = self.call(
            self.name + "_halve",
            halve_body,
            (self.keeps[0], self.came[0], self.keeps[1], self.came[1]),
            results,
            cover=cover,
        )
        self.keeps = (outs[0], outs[2])
        self.came = (rep_swap(outs[1], 2), rep_swap(outs[3], 1))

    def quarter(self, cover=(), vectors=()):
        (self.total,) = self.call(
            self.name + "_quarter",
            quarter_small_body if vectors else quarter_body,
            (self.keeps[0], self.came[0], self.keeps[1], self.came[1]) + vectors,
            [((2, 2) + self.shape, low_kind)],
            cover=cover,
        )
        self.last = rep_swap(self.total, 4)

    def trade(self, cover=()):
        block = self.shape[1:]
        own, *sends, self.rows = self.call(
            self.name + "_trade",
            trade_body,
            (self.total, self.last),
            [((2,) + block, low_kind)] * 4 + [((2, 2) + block, low_kind)],
            [((4, 2) + block, low_kind)],
            cover=cover,
        )
        self.blocks = [own] + [shard_swap(send, step) for step, send in zip((1, 2, 3), sends)]

    def gather(self, cover=()):
        first, second = self.call(
            self.name + "_gather",
            gather_body,
            (*self.blocks, self.rows),
            [((2,) + self.shape, low_kind)] * 2,
            cover=cover,
        )
        first_far, second_far = rep_swap(first, 2), rep_swap(second, 1)
        self.far = (first_far, second_far)
        self.near = (rep_swap(first, 1), rep_swap(second, 2))
        self.firsts = (first, self.near[0], first_far, rep_swap(first_far, 1))
        self.seconds = (second, second_far, self.near[1], rep_swap(second_far, 2))

    def finish(self, body, results, scratch=(), cover=()):
        return self.call(
            self.name + "_out", body, (*self.firsts, *self.seconds), results, scratch, cover
        )


class GroupSum:
    def __init__(self, send, keep):
        self.keep = keep
        self.came = shard_swap(send, 1)

    def add(self):
        self.pair = (self.keep + self.came.astype(full_kind)).astype(low_kind)
        self.far = shard_swap(self.pair, 2)
        return self.pair

    def hold(self, value):
        self.far = after(self.far, value)

    def total(self):
        own = (self.pair.astype(full_kind) + self.far.astype(full_kind)).astype(low_kind)
        self.results = (own, shard_swap(own, 1))
        return own


def split_shards(
    inputs,
    encoder,
    segments,
    enc_segments,
    self_query,
    self_key,
    self_value,
    self_output,
    cross_query,
    cross_key,
    cross_value,
    cross_output,
    gate_weight,
    up_weight,
    down_weight,
    self_gain,
    cross_gain,
    feed_gain,
    bias_table,
    cotangent,
):
    index = lax.axis_index("shard")
    rep = lax.axis_index("rep")
    call = Kernels(jnp.stack([index, rep]))
    tokens_here, model = inputs.shape[1:]
    length = 4 * tokens_here
    half_size = 2 * tokens_here
    heads_here = HEADS // 4
    wide = heads_here * HEAD_DIM
    units = down_weight.shape[0]
    memory_length = enc_segments.shape[1]
    small_rows = bias_table.shape[0]
    buckets = 4 * small_rows
    part = self_gain.shape[0]

    def blocks_of(*weights):
        width = sum(weight.shape[1] for weight in weights) // 4
        shape = (weights[0].shape[0], width)
        return call("columns", columns_body, weights, [(shape, low_kind)] * 4)

    def traded(blocks):
        return [blocks[0]] + [shard_swap(blocks[step], step) for step in range(1, 4)]

    column_shape = (part, 3 * wide)
    packed, *self_blocks = call(
        "pack",
        pack_body,
        (
            inputs[0], self_gain, cross_gain, feed_gain, bias_table, self_query, self_key,
            self_value,
        ),
        [((tokens_here + 16, model), low_kind)] + [(column_shape, low_kind)] * 4,
    )
    source_far = shard_swap(packed, 2)
    self_blocks = traded(self_blocks)
    cross_blocks = blocks_of(cross_query, cross_key, cross_value)
    feed_blocks = call(
        "feed_columns",
        split_columns_body,
        (gate_weight, up_weight),
        [((part, 2 * units), low_kind)] * 2 + [((part // 2, 2 * units), low_kind)] * 2,
    )
    source_far = after(source_far, feed_blocks[0])
    source_blocks = [packed, shard_swap(packed, 1), source_far, shard_swap(source_far, 1)]
    seg_row = segments
    seg_col = segments[0][:, None]
    enc_row = enc_segments
    call.wait(seg_col, self_blocks[2], self_blocks[3])
    cross_blocks = traded(after(tuple(cross_blocks), self_blocks[2], self_blocks[3]))
    room = [((half_size, model), full_kind)]
    whole_room = [((length, model), full_kind)]

    def head_rooms(places, rows, outs):
        return [
            ((places * heads_here, max(length, memory_length), HEAD_DIM), low_kind),
            ((outs * heads_here, rows, HEAD_DIM), low_kind),
        ]

    pieces = [((tokens_here, model), low_kind), ((tokens_here, model), full_kind)]
    two_pieces = [((2,) + shape, kind) for shape, kind in pieces]

    def self_results(keys):
        return [
            ((half_size, model), low_kind),
            ((half_size, 3 * wide), low_kind),
            ((heads_here, half_size, keys), low_kind),
            ((half_size, wide), low_kind),
        ] + pieces

    source, w_self, gains, rows, *first = call(
        "self_first",
        self_first_body,
        (*source_blocks, *self_blocks, self_output, seg_col, seg_row),
        [
            ((length, model), low_kind),
            ((model, 3 * wide), low_kind),
            ((8, model), full_kind),
            ((8, length), full_kind),
        ]
        + self_results(half_size),
        room + head_rooms(3, half_size, 1) + [((64, model), full_kind), ((128, length), full_kind)],
        cover=(cross_blocks[2], cross_blocks[3]),
    )
    first_sum = GroupSum(*first[4:])
    memory_far = shard_swap(after(encoder[0], first[0]), 2)
    second = call(
        "self_second",
        self_second_body,
        (source, w_self, gains, rows, first[1], self_output, seg_col, seg_row),
        self_results(length),
        room + head_rooms(3, half_size, 1),
        cover=(first_sum.came,),
    )
    second_sum = GroupSum(*second[4:])
    call.wait(first_sum.add())
    memory_blocks = [
        encoder[0], shard_swap(encoder[0], 1), memory_far, shard_swap(memory_far, 1)
    ]
    memory, w_cross, cross_mapped = call(
        "cross_keys",
        cross_keys_body,
        (*memory_blocks, *cross_blocks),
        [
            ((memory_length, model), low_kind),
            ((model, 3 * wide), low_kind),
            ((memory_length, 2 * wide), low_kind),
        ],
        cover=(second_sum.came,),
    )
    pair = second_sum.add()
    call.wait(pair)
    first_sum.total()
    feed_blocks = after(tuple(feed_blocks), pair)
    feed_near = shard_swap(feed_blocks[1], 1)
    feed_two = shard_swap(feed_blocks[2], 2)

    def cross_call(half, sums, cover):
        own, other = sums.results
        return call(
            "cross",
            functools.partial(cross_body, half),
            (source, own, other, gains, w_cross, cross_mapped, cross_output, seg_col, enc_row),
            [
                ((half_size, model), full_kind),
                ((half_size, model), low_kind),
                ((half_size, wide), low_kind),
                ((heads_here, half_size, memory_length), low_kind),
                ((half_size, wide), low_kind),
            ]
            + pieces,
            room + head_rooms(3, half_size, 1),
            cover=cover,
        )

    grad_far = shard_swap(after(cotangent[0], cross_mapped), 2)
    cross0 = cross_call(0, first_sum, (second_sum.far, feed_two, grad_far))
    cross_first = GroupSum(*cross0[5:])
    call.wait(second_sum.total())
    feed_two_other = rep_swap(feed_two, 1)
    feed_three = shard_swap(after(feed_blocks[3], cross0[0]), 3)
    cross1 = cross_call(1, second_sum, (feed_three, feed_two_other, cross_first.came))
    cross_second = GroupSum(*cross1[5:])
    call.wait(cross_first.add())
    feed_three_other = rep_swap(feed_three, 1)
    grad_blocks = [
        cotangent[0], shard_swap(cotangent[0], 1), grad_far, shard_swap(grad_far, 1)
    ]
    w_feed, grad_out = call(
        "feed_join",
        feed_join_body,
        (
            feed_blocks[0], feed_near, feed_two, feed_two_other, feed_three, feed_three_other,
            *grad_blocks,
        ),
        [((model, 2 * units), low_kind), ((length, model), low_kind)],
        cover=(cross_second.came,),
    )
    call.wait(cross_second.add())
    cross_first.total()
    cross_second.hold(w_feed)

    def feed_call(half, sums, before, parts, tail, cover=()):
        own, other = sums.results
        return call(
            "feed",
            functools.partial(feed_body, half),
            (before, own, other, gains, w_feed, down_weight, grad_out) + parts,
            [
                ((half_size, model), full_kind),
                ((half_size, model), low_kind),
                ((half_size, units), low_kind),
                ((half_size, 2 * units), low_kind),
            ]
            + tail,
            room,
            cover=cover,
        )

    feed0 = feed_call(0, cross_first, cross0[0], (), room * 2, (cross_second.far,))
    cross_second.total()
    feed1 = feed_call(1, cross_second, cross1[0], (feed0[4], feed0[5]), two_pieces * 2)
    feed_sum = GroupSum(*feed1[4:6])
    out_came = shard_swap(feed1[6], 1)

    chunk = (3, model // 4, 2 * units // 8)
    feed_grads = Reduction(
        call,
        "feed_grads",
        call(
            "feed_weights",
            feed_weights_body,
            (feed0[1], feed1[1], feed0[3], feed1[3], feed0[2], feed1[2], grad_out),
            [((4,) + chunk, low_kind)] * 4,
            [((model, 2 * units), low_kind), ((units, model), low_kind)],
            cover=(feed_sum.came, out_came),
        ),
    )
    call.wait(feed_sum.add())

    def scatter_pair(arrived, keep, cover=()):
        mine, other = call(
            "chip_pair",
            chip_pair_body,
            (keep, arrived),
            [((tokens_here, model), full_kind), ((tokens_here, model), low_kind)],
            cover=cover,
        )
        return mine, shard_swap(other, 2)

    mine, out_far = scatter_pair(out_came, feed1[7])
    feed_sum.total()
    own_after = lax.dynamic_slice_in_dim(
        jnp.where(index < 2, feed0[0], feed1[0]), (index & 1) * tokens_here, tokens_here
    )
    outcome = (own_after + mine + out_far.astype(full_kind)).astype(low_kind)

    total_cross, low_cross, query_cross, sums_cross, row_feed, *sends = call(
        "cross_back",
        cross_back_body,
        (
            grad_out, *feed_sum.results, feed0[0], feed1[0], gains, cross_output, cross0[2], cross1[2],
            cross0[3], cross1[3], cross_mapped, w_cross,
        ),
        [
            ((length, model), full_kind),
            ((length, model), low_kind),
            ((length, wide), low_kind),
            ((memory_length, 2 * wide), low_kind),
            ((8, model), full_kind),
        ]
        + two_pieces,
        whole_room + head_rooms(4, length, 3),
        cover=feed_grads.came + (out_far,),
    )
    cross_sum = GroupSum(*sends)
    feed_grads.halve(cover=(cross_sum.came,))
    call.wait(cross_sum.add())
    small_chunk = (3, wide // 8, 3 * wide)
    weight_room = [((model, 3 * wide), full_kind), ((wide, model), full_kind)]
    *buffers, send, keep = call(
        "cross_weights",
        cross_weights_body,
        (
            cross0[1], cross1[1], query_cross, memory, sums_cross, cross0[4], cross1[4], low_cross,
            w_cross,
        ),
        [((4,) + small_chunk, low_kind)] * 4 + two_pieces,
        whole_room + weight_room,
        cover=(cross_sum.far,) + feed_grads.came,
    )
    cross_sum.hold(keep)
    cross_grads = Reduction(call, "cross_grads", buffers)
    memory_came, memory_keep = shard_swap(send, 1), keep
    call.wait(cross_sum.total())
    feed_grads.quarter(cover=cross_sum.results)
    total_self, low_self, query_self, sums_self, row_cross, table = call(
        "self_back",
        self_back_body,
        (
            total_cross, *cross_sum.results, cross0[0], cross1[0], gains, self_output, first[1], second[1],
            first[2], second[2],
        ),
        [
            ((length, model), full_kind),
            ((length, model), low_kind),
            ((length, wide), low_kind),
            ((length, 2 * wide), low_kind),
            ((8, model), full_kind),
            ((buckets, 128), full_kind),
        ],
        whole_room + head_rooms(4, length, 3),
        cover=(memory_came,),
    )
    *buffers, send, keep = call(
        "self_weights",
        self_weights_body,
        (first[0], second[0], query_self, sums_self, first[3], second[3], low_self, w_self),
        [((4,) + small_chunk, low_kind)] * 4 + two_pieces,
        whole_room + weight_room + [((length, 3 * wide), low_kind)],
        cover=cross_grads.came,
    )
    self_grads = Reduction(call, "self_grads", buffers)
    arrived = shard_swap(send, 1)
    cross_grads.halve(cover=(arrived,))
    mine, far = scatter_pair(arrived, keep)
    feed_grads.trade(cover=self_grads.came)
    call.wait(outcome)
    self_grads.halve(cover=cross_grads.came + (far,))
    cross_grads.quarter(cover=tuple(feed_grads.blocks[1:]))
    gain_rows = -(-3 * model // 1024) * 8
    vector_kind = ((gain_rows + buckets, 128), full_kind)
    grad_source, vector = call(
        "finish",
        finish_body,
        (inputs[0], mine, far, gains, total_self, row_cross, row_feed, table),
        [((tokens_here, model), full_kind), vector_kind],
        cover=self_grads.came,
    )
    vectors = (vector,) + tuple(shard_swap(vector, step) for step in (1, 2, 3))
    memory_mine, memory_far = scatter_pair(memory_came, memory_keep, vectors[1:])
    grad_memory = memory_mine + memory_far.astype(full_kind)
    self_grads.quarter(vectors=vectors)
    feed_grads.gather()
    cross_grads.trade()
    cross_grads.gather(cover=feed_grads.far)
    self_grads.trade(cover=cross_grads.far)
    feed_out = feed_grads.finish(
        feed_out_body,
        [((part, 4 * units), full_kind)] * 2 + [((units, model), full_kind)],
        cover=tuple(self_grads.blocks[1:]),
    )
    self_grads.gather()
    small_results = [((part, model), full_kind)] * 3 + [((wide, model), full_kind)]
    out_room = [((4, wide, 3 * wide), full_kind)]
    cross_out = cross_grads.finish(small_out_body, small_results, out_room, self_grads.far)
    *self_out, vector = self_grads.finish(
        last_out_body,
        small_results + [vector_kind],
        out_room + [((4,) + vector_kind[0], full_kind)],
    )

    gains_sum = vector[: 3 * model // 128].reshape(3, model)
    gains_here = lax.dynamic_slice_in_dim(gains_sum, index * part, part, 1)
    table_grad = lax.dynamic_slice_in_dim(
        vector[gain_rows:, :HEADS], index * small_rows, small_rows
    )
    return (
        outcome[None],
        grad_source[None],
        grad_memory[None],
        *self_out,
        *cross_out,
        *feed_out,
        gains_here[0],
        gains_here[1],
        gains_here[2],
        table_grad,
    )


def solution(mesh):
    in_specs = (
        P("rep", "shard", None),
        P("rep", "shard", None),
        P("rep", None),
        P("rep", None),
        P("shard", None),
        P("shard", None),
        P("shard", None),
        P("shard", None),
        P("shard", None),
        P("shard", None),
        P("shard", None),
        P("shard", None),
        P("shard", None),
        P("shard", None),
        P("shard", None),
        P("shard"),
        P("shard"),
        P("shard"),
        P("shard", None),
        P("rep", "shard", None),
    )
    out_specs = (
        P("rep", "shard", None),
        P("rep", "shard", None),
        P("rep", "shard", None),
        P("shard", None),
        P("shard", None),
        P("shard", None),
        P("shard", None),
        P("shard", None),
        P("shard", None),
        P("shard", None),
        P("shard", None),
        P("shard", None),
        P("shard", None),
        P("shard", None),
        P("shard"),
        P("shard"),
        P("shard"),
        P("shard", None),
    )
    split = mesh.shape["shard"] == 4 and mesh.shape["rep"] == 8
    body = split_shards if split else shards
    return jax.shard_map(body, mesh=mesh, in_specs=in_specs, out_specs=out_specs, check_vma=False)
```

```python
import functools
import math

import jax
import jax.numpy as jnp
from jax import lax
from jax.experimental import pallas as pl
from jax.experimental.pallas import tpu as pltpu
from jax.sharding import PartitionSpec as P

HEADS = 12
HEAD_DIM = 64


bucket_edges = [math.ceil(16 * 8 ** (number / 16)) for number in range(1, 16)]
epsilon = 1e-06
masked_score = -1000000000.0


def bucket_of(distance):
    far_part = sum(((distance >= border).astype(jnp.int32) for border in bucket_edges))
    return jnp.where(distance < 16, distance, 16 + far_part)


def rms_scale(values, scales):
    return values * lax.rsqrt(jnp.mean(values * values, axis=-1, keepdims=True) + epsilon) * scales


def product(former, latter):
    return jnp.dot(former, latter, preferred_element_type=jnp.float32)


def product_rows(former, latter):
    return lax.dot_general(
        former, latter, (((0,), (0,)), ((), ())), preferred_element_type=jnp.float32
    )


def product_cols(former, latter):
    return lax.dot_general(
        former, latter, (((1,), (1,)), ((), ())), preferred_element_type=jnp.float32
    )


def split_heads(matrix):
    return matrix.reshape(matrix.shape[0], HEADS, HEAD_DIM).transpose(1, 0, 2)


def join_heads(stacked):
    return stacked.transpose(1, 0, 2).reshape(stacked.shape[1], HEADS * HEAD_DIM)


def to_blocks(matrix, block_count):
    return matrix.reshape(block_count, -1, HEADS, HEAD_DIM).transpose(0, 2, 1, 3)


def from_blocks(stacked):
    return stacked.transpose(0, 2, 1, 3).reshape(-1, HEADS * HEAD_DIM)


def self_scores(queries, query_start, query_ids, table_full, key_rows, key_start, key_ids):
    query_count = queries.shape[1]
    key_count = key_rows.shape[1]
    query_places = query_start + jnp.arange(query_count, dtype=jnp.int32)
    key_places = key_start + jnp.arange(key_count, dtype=jnp.int32)
    buckets = bucket_of(jnp.maximum(query_places[:, None] - key_places[None, :], 0))
    one_hot = (
        buckets.reshape(1, -1) == jnp.arange(table_full.shape[0], dtype=jnp.int32)[:, None]
    ).astype(jnp.bfloat16)
    bias_block = jnp.einsum(
        "bn,bh->hn", one_hot, table_full, preferred_element_type=jnp.float32
    ).reshape(HEADS, query_count, key_count)
    scores = (
        jnp.einsum("hqd,hkd->hqk", queries, key_rows, preferred_element_type=jnp.float32)
        + bias_block
    )
    allowed = (query_places[:, None] >= key_places[None, :]) & (
        query_ids[:, None] == key_ids[None, :]
    )
    return (jnp.where(allowed[None], scores, masked_score), one_hot)


def self_logsum(queries, query_start, query_ids, table_full, key_blocks, id_blocks, key_starts):
    query_count = queries.shape[1]

    def advance(running, packed):
        largest, totals = running
        key_rows, key_ids, key_start = packed
        scores, unused = self_scores(
            queries, query_start, query_ids, table_full, key_rows, key_start, key_ids
        )
        newest = jnp.maximum(largest, jnp.max(scores, axis=-1, keepdims=True))
        totals = totals * jnp.exp(largest - newest) + jnp.sum(
            jnp.exp(scores - newest), axis=-1, keepdims=True
        )
        return ((newest, totals), None)

    initial = (
        jnp.full((HEADS, query_count, 1), -jnp.inf, jnp.float32),
        jnp.zeros((HEADS, query_count, 1), jnp.float32),
    )
    (largest, totals), unused = lax.scan(advance, initial, (key_blocks, id_blocks, key_starts))
    return largest + jnp.log(totals)


def self_mix(
    queries,
    query_start,
    query_ids,
    table_full,
    key_blocks,
    value_blocks,
    id_blocks,
    key_starts,
    logsum,
):

    def advance(accum, packed):
        key_rows, value_rows, key_ids, key_start = packed
        scores, unused = self_scores(
            queries, query_start, query_ids, table_full, key_rows, key_start, key_ids
        )
        weights = jnp.exp(scores - logsum).astype(jnp.bfloat16)
        return (
            accum
            + jnp.einsum("hqk,hkd->hqd", weights, value_rows, preferred_element_type=jnp.float32),
            None,
        )

    initial = jnp.zeros((HEADS, queries.shape[1], HEAD_DIM), jnp.float32)
    accum, unused = lax.scan(advance, initial, (key_blocks, value_blocks, id_blocks, key_starts))
    return accum


def self_backward(
    queries,
    query_start,
    query_ids,
    table_full,
    key_blocks,
    value_blocks,
    id_blocks,
    key_starts,
    logsum,
    grad_mixed,
):
    query_count = queries.shape[1]

    def dots(accum, packed):
        key_rows, value_rows, key_ids, key_start = packed
        scores, unused = self_scores(
            queries, query_start, query_ids, table_full, key_rows, key_start, key_ids
        )
        chances = jnp.exp(scores - logsum)
        grad_chances = jnp.einsum(
            "hqd,hkd->hqk", grad_mixed, value_rows, preferred_element_type=jnp.float32
        )
        return (accum + jnp.sum(chances * grad_chances, axis=-1, keepdims=True), None)

    row_dots, unused = lax.scan(
        dots,
        jnp.zeros((HEADS, query_count, 1), jnp.float32),
        (key_blocks, value_blocks, id_blocks, key_starts),
    )

    def advance(running, packed):
        grad_queries, grad_table = running
        key_rows, value_rows, key_ids, key_start = packed
        scores, one_hot = self_scores(
            queries, query_start, query_ids, table_full, key_rows, key_start, key_ids
        )
        chances = jnp.exp(scores - logsum)
        grad_chances = jnp.einsum(
            "hqd,hkd->hqk", grad_mixed, value_rows, preferred_element_type=jnp.float32
        )
        grad_scores = chances * (grad_chances - row_dots)
        rounded = grad_scores.astype(jnp.bfloat16)
        grad_values = jnp.einsum(
            "hqk,hqd->hkd",
            chances.astype(jnp.bfloat16),
            grad_mixed,
            preferred_element_type=jnp.float32,
        )
        grad_keys = jnp.einsum("hqk,hqd->hkd", rounded, queries, preferred_element_type=jnp.float32)
        grad_queries = grad_queries + jnp.einsum(
            "hqk,hkd->hqd", rounded, key_rows, preferred_element_type=jnp.float32
        )
        grad_table = grad_table + jnp.einsum(
            "bn,hn->bh",
            one_hot,
            grad_scores.reshape(HEADS, -1),
            precision=lax.Precision.HIGHEST,
            preferred_element_type=jnp.float32,
        )
        return ((grad_queries, grad_table), (grad_keys, grad_values))

    initial = (
        jnp.zeros((HEADS, query_count, HEAD_DIM), jnp.float32),
        jnp.zeros((table_full.shape[0], HEADS), jnp.float32),
    )
    (grad_queries, grad_table), (grad_keys, grad_values) = lax.scan(
        advance, initial, (key_blocks, value_blocks, id_blocks, key_starts)
    )
    return (join_heads(grad_queries), grad_table, from_blocks(grad_keys), from_blocks(grad_values))


def cross_forward(queries, key_heads, value_heads, allowed):
    scores = jnp.where(
        allowed,
        jnp.einsum("hqd,hkd->hqk", queries, key_heads, preferred_element_type=jnp.float32),
        masked_score,
    )
    largest = jnp.max(scores, axis=-1, keepdims=True)
    logsum = largest + jnp.log(jnp.sum(jnp.exp(scores - largest), axis=-1, keepdims=True))
    weights = jnp.exp(scores - logsum).astype(jnp.bfloat16)
    mixed = jnp.einsum("hqk,hkd->hqd", weights, value_heads, preferred_element_type=jnp.float32)
    return (mixed, logsum)


def cross_backward(queries, key_heads, value_heads, allowed, logsum, grad_mixed):
    scores = jnp.where(
        allowed,
        jnp.einsum("hqd,hkd->hqk", queries, key_heads, preferred_element_type=jnp.float32),
        masked_score,
    )
    chances = jnp.exp(scores - logsum)
    grad_values = jnp.einsum(
        "hqk,hqd->hkd", chances.astype(jnp.bfloat16), grad_mixed, preferred_element_type=jnp.float32
    )
    grad_chances = jnp.einsum(
        "hqd,hkd->hqk", grad_mixed, value_heads, preferred_element_type=jnp.float32
    )
    grad_scores = chances * (grad_chances - jnp.sum(chances * grad_chances, axis=-1, keepdims=True))
    rounded = grad_scores.astype(jnp.bfloat16)
    grad_queries = jnp.einsum(
        "hqk,hkd->hqd", rounded, key_heads, preferred_element_type=jnp.float32
    )
    grad_keys = jnp.einsum("hqk,hqd->hkd", rounded, queries, preferred_element_type=jnp.float32)
    return (join_heads(grad_queries), join_heads(grad_keys), join_heads(grad_values))


def shards(
    inputs,
    encoder,
    segments,
    enc_segments,
    self_query,
    self_key,
    self_value,
    self_output,
    cross_query,
    cross_key,
    cross_value,
    cross_output,
    gate_weight,
    up_weight,
    down_weight,
    self_gain,
    cross_gain,
    feed_gain,
    bias_table,
    cotangent,
):
    fetched = (
        lax.all_gather(self_query, "shard", axis=0, tiled=True),
        lax.all_gather(self_key, "shard", axis=0, tiled=True),
        lax.all_gather(self_value, "shard", axis=0, tiled=True),
        lax.all_gather(self_output, "shard", axis=0, tiled=True),
        lax.all_gather(cross_query, "shard", axis=0, tiled=True),
        lax.all_gather(cross_key, "shard", axis=0, tiled=True),
        lax.all_gather(cross_value, "shard", axis=0, tiled=True),
        lax.all_gather(cross_output, "shard", axis=0, tiled=True),
        lax.all_gather(gate_weight, "shard", axis=0, tiled=True),
        lax.all_gather(up_weight, "shard", axis=0, tiled=True),
        lax.all_gather(down_weight, "shard", axis=0, tiled=True),
        lax.all_gather(self_gain, "shard", axis=0, tiled=True),
        lax.all_gather(cross_gain, "shard", axis=0, tiled=True),
        lax.all_gather(feed_gain, "shard", axis=0, tiled=True),
        lax.all_gather(bias_table, "shard", axis=0, tiled=True),
    )
    (
        w_query,
        w_key,
        w_value,
        w_output,
        c_query,
        c_key,
        c_value,
        c_output,
        w_gate,
        w_up,
        w_down,
        g_self,
        g_cross,
        g_feed,
        table_full,
    ) = fetched
    gain_self = g_self.astype(jnp.float32)
    gain_cross = g_cross.astype(jnp.float32)
    gain_feed = g_feed.astype(jnp.float32)
    source = inputs[0].astype(jnp.float32)
    memory = encoder[0]
    segment_ids = segments[0]
    memory_ids = enc_segments[0]
    tokens_here = source.shape[0]
    length = segment_ids.shape[0]
    block_size = math.gcd(length, 512)
    block_count = length // block_size
    query_start = lax.axis_index("shard") * tokens_here
    query_ids = lax.dynamic_slice_in_dim(segment_ids, query_start, tokens_here)
    id_blocks = segment_ids.reshape(block_count, block_size)
    key_starts = jnp.arange(block_count, dtype=jnp.int32) * block_size
    cross_allowed = (query_ids[:, None] == memory_ids[None, :])[None]
    normed_self = rms_scale(source, gain_self).astype(jnp.bfloat16)
    query_heads = split_heads(product(normed_self, w_query).astype(jnp.bfloat16))
    key_local = product(normed_self, w_key).astype(jnp.bfloat16)
    value_local = product(normed_self, w_value).astype(jnp.bfloat16)
    keys_all, values_all = (
        lax.all_gather(key_local, "shard", axis=0, tiled=True),
        lax.all_gather(value_local, "shard", axis=0, tiled=True),
    )
    key_blocks = to_blocks(keys_all, block_count)
    value_blocks = to_blocks(values_all, block_count)
    logsum_self = self_logsum(
        query_heads, query_start, query_ids, table_full, key_blocks, id_blocks, key_starts
    )
    mixed_self = self_mix(
        query_heads,
        query_start,
        query_ids,
        table_full,
        key_blocks,
        value_blocks,
        id_blocks,
        key_starts,
        logsum_self,
    )
    joined_self = join_heads(mixed_self).astype(jnp.bfloat16)
    after_self = source + product(joined_self, w_output)
    normed_cross = rms_scale(after_self, gain_cross).astype(jnp.bfloat16)
    query_cross = split_heads(product(normed_cross, c_query).astype(jnp.bfloat16))
    key_cross_local = product(memory, c_key).astype(jnp.bfloat16)
    value_cross_local = product(memory, c_value).astype(jnp.bfloat16)
    keys_cross, values_cross = (
        lax.all_gather(key_cross_local, "shard", axis=0, tiled=True),
        lax.all_gather(value_cross_local, "shard", axis=0, tiled=True),
    )
    key_cross = split_heads(keys_cross)
    value_cross = split_heads(values_cross)
    mixed_cross, logsum_cross = cross_forward(query_cross, key_cross, value_cross, cross_allowed)
    joined_cross = join_heads(mixed_cross).astype(jnp.bfloat16)
    after_cross = after_self + product(joined_cross, c_output)
    normed_feed = rms_scale(after_cross, gain_feed).astype(jnp.bfloat16)
    gate_act = product(normed_feed, w_gate)
    up_act = product(normed_feed, w_up)
    hidden = (jax.nn.gelu(gate_act, approximate=True) * up_act).astype(jnp.bfloat16)
    outcome = after_cross + product(hidden, w_down)
    fetched = (
        lax.all_gather(self_query, "shard", axis=0, tiled=True),
        lax.all_gather(self_key, "shard", axis=0, tiled=True),
        lax.all_gather(self_value, "shard", axis=0, tiled=True),
        lax.all_gather(self_output, "shard", axis=0, tiled=True),
        lax.all_gather(cross_query, "shard", axis=0, tiled=True),
        lax.all_gather(cross_key, "shard", axis=0, tiled=True),
        lax.all_gather(cross_value, "shard", axis=0, tiled=True),
        lax.all_gather(cross_output, "shard", axis=0, tiled=True),
        lax.all_gather(gate_weight, "shard", axis=0, tiled=True),
        lax.all_gather(up_weight, "shard", axis=0, tiled=True),
        lax.all_gather(down_weight, "shard", axis=0, tiled=True),
        lax.all_gather(self_gain, "shard", axis=0, tiled=True),
        lax.all_gather(cross_gain, "shard", axis=0, tiled=True),
        lax.all_gather(feed_gain, "shard", axis=0, tiled=True),
        lax.all_gather(bias_table, "shard", axis=0, tiled=True),
    )
    (
        w_query,
        w_key,
        w_value,
        w_output,
        c_query,
        c_key,
        c_value,
        c_output,
        w_gate,
        w_up,
        w_down,
        g_self,
        g_cross,
        g_feed,
        table_full,
    ) = fetched
    gain_self = g_self.astype(jnp.float32)
    gain_cross = g_cross.astype(jnp.float32)
    gain_feed = g_feed.astype(jnp.float32)
    keys_all, values_all = (
        lax.all_gather(key_local, "shard", axis=0, tiled=True),
        lax.all_gather(value_local, "shard", axis=0, tiled=True),
    )
    key_blocks = to_blocks(keys_all, block_count)
    value_blocks = to_blocks(values_all, block_count)
    grad_out = cotangent[0].astype(jnp.float32)
    grad_down_in = cotangent[0]
    d_down = product_rows(hidden, grad_down_in)
    grad_hidden = product_cols(grad_down_in, w_down)

    def activation(gate_in, up_in):
        return jax.nn.gelu(gate_in, approximate=True) * up_in

    unused, pull = jax.vjp(activation, gate_act, up_act)
    grad_gate, grad_up = pull(grad_hidden)
    grad_gate = grad_gate.astype(jnp.bfloat16)
    grad_up = grad_up.astype(jnp.bfloat16)
    d_gate = product_rows(normed_feed, grad_gate)
    d_up = product_rows(normed_feed, grad_up)
    grad_normed_feed = product_cols(grad_gate, w_gate) + product_cols(grad_up, w_up)
    unused, pull = jax.vjp(rms_scale, after_cross, gain_feed)
    norm_part, d_feed_gain = pull(grad_normed_feed)
    grad_cross_total = grad_out + norm_part
    grad_cross_in = grad_cross_total.astype(jnp.bfloat16)
    d_c_output = product_rows(joined_cross, grad_cross_in)
    grad_mixed_cross = split_heads(product_cols(grad_cross_in, c_output).astype(jnp.bfloat16))
    grad_query_cross, grad_keys_cross, grad_values_cross = cross_backward(
        query_cross, key_cross, value_cross, cross_allowed, logsum_cross, grad_mixed_cross
    )
    grad_query_cross = grad_query_cross.astype(jnp.bfloat16)
    key_part, value_part = (
        lax.psum_scatter(
            grad_keys_cross.astype(jnp.bfloat16), "shard", scatter_dimension=0, tiled=True
        ).astype(jnp.float32),
        lax.psum_scatter(
            grad_values_cross.astype(jnp.bfloat16), "shard", scatter_dimension=0, tiled=True
        ).astype(jnp.float32),
    )
    grad_key_cross = key_part.astype(jnp.bfloat16)
    grad_value_cross = value_part.astype(jnp.bfloat16)
    d_c_query = product_rows(normed_cross, grad_query_cross)
    d_c_key = product_rows(memory, grad_key_cross)
    d_c_value = product_rows(memory, grad_value_cross)
    grad_memory = product_cols(grad_key_cross, c_key) + product_cols(grad_value_cross, c_value)
    grad_normed_cross = product_cols(grad_query_cross, c_query)
    unused, pull = jax.vjp(rms_scale, after_self, gain_cross)
    norm_part, d_cross_gain = pull(grad_normed_cross)
    grad_self_total = grad_cross_total + norm_part
    grad_self_in = grad_self_total.astype(jnp.bfloat16)
    d_output = product_rows(joined_self, grad_self_in)
    grad_mixed_self = split_heads(product_cols(grad_self_in, w_output).astype(jnp.bfloat16))
    grad_queries, d_table, grad_keys_full, grad_values_full = self_backward(
        query_heads,
        query_start,
        query_ids,
        table_full,
        key_blocks,
        value_blocks,
        id_blocks,
        key_starts,
        logsum_self,
        grad_mixed_self,
    )
    grad_query_self = grad_queries.astype(jnp.bfloat16)
    key_part, value_part = (
        lax.psum_scatter(
            grad_keys_full.astype(jnp.bfloat16), "shard", scatter_dimension=0, tiled=True
        ).astype(jnp.float32),
        lax.psum_scatter(
            grad_values_full.astype(jnp.bfloat16), "shard", scatter_dimension=0, tiled=True
        ).astype(jnp.float32),
    )
    grad_key_self = key_part.astype(jnp.bfloat16)
    grad_value_self = value_part.astype(jnp.bfloat16)
    d_query = product_rows(normed_self, grad_query_self)
    d_key = product_rows(normed_self, grad_key_self)
    d_value = product_rows(normed_self, grad_value_self)
    grad_normed_self = (
        product_cols(grad_query_self, w_query)
        + product_cols(grad_key_self, w_key)
        + product_cols(grad_value_self, w_value)
    )
    unused, pull = jax.vjp(rms_scale, source, gain_self)
    norm_part, d_self_gain = pull(grad_normed_self)
    grad_source = grad_self_total + norm_part
    summed = (
        lax.psum_scatter(
            d_query.astype(jnp.bfloat16), "shard", scatter_dimension=0, tiled=True
        ).astype(jnp.float32),
        lax.psum_scatter(
            d_key.astype(jnp.bfloat16), "shard", scatter_dimension=0, tiled=True
        ).astype(jnp.float32),
        lax.psum_scatter(
            d_value.astype(jnp.bfloat16), "shard", scatter_dimension=0, tiled=True
        ).astype(jnp.float32),
        lax.psum_scatter(
            d_output.astype(jnp.bfloat16), "shard", scatter_dimension=0, tiled=True
        ).astype(jnp.float32),
        lax.psum_scatter(
            d_c_query.astype(jnp.bfloat16), "shard", scatter_dimension=0, tiled=True
        ).astype(jnp.float32),
        lax.psum_scatter(
            d_c_key.astype(jnp.bfloat16), "shard", scatter_dimension=0, tiled=True
        ).astype(jnp.float32),
        lax.psum_scatter(
            d_c_value.astype(jnp.bfloat16), "shard", scatter_dimension=0, tiled=True
        ).astype(jnp.float32),
        lax.psum_scatter(
            d_c_output.astype(jnp.bfloat16), "shard", scatter_dimension=0, tiled=True
        ).astype(jnp.float32),
        lax.psum_scatter(
            d_gate.astype(jnp.bfloat16), "shard", scatter_dimension=0, tiled=True
        ).astype(jnp.float32),
        lax.psum_scatter(
            d_up.astype(jnp.bfloat16), "shard", scatter_dimension=0, tiled=True
        ).astype(jnp.float32),
        lax.psum_scatter(
            d_down.astype(jnp.bfloat16), "shard", scatter_dimension=0, tiled=True
        ).astype(jnp.float32),
        lax.psum_scatter(
            d_self_gain.astype(jnp.bfloat16), "shard", scatter_dimension=0, tiled=True
        ).astype(jnp.float32),
        lax.psum_scatter(
            d_cross_gain.astype(jnp.bfloat16), "shard", scatter_dimension=0, tiled=True
        ).astype(jnp.float32),
        lax.psum_scatter(
            d_feed_gain.astype(jnp.bfloat16), "shard", scatter_dimension=0, tiled=True
        ).astype(jnp.float32),
        lax.psum_scatter(
            d_table.astype(jnp.bfloat16), "shard", scatter_dimension=0, tiled=True
        ).astype(jnp.float32),
    )
    totals = (
        lax.psum(summed[0].astype(jnp.bfloat16), "rep").astype(jnp.float32),
        lax.psum(summed[1].astype(jnp.bfloat16), "rep").astype(jnp.float32),
        lax.psum(summed[2].astype(jnp.bfloat16), "rep").astype(jnp.float32),
        lax.psum(summed[3].astype(jnp.bfloat16), "rep").astype(jnp.float32),
        lax.psum(summed[4].astype(jnp.bfloat16), "rep").astype(jnp.float32),
        lax.psum(summed[5].astype(jnp.bfloat16), "rep").astype(jnp.float32),
        lax.psum(summed[6].astype(jnp.bfloat16), "rep").astype(jnp.float32),
        lax.psum(summed[7].astype(jnp.bfloat16), "rep").astype(jnp.float32),
        lax.psum(summed[8].astype(jnp.bfloat16), "rep").astype(jnp.float32),
        lax.psum(summed[9].astype(jnp.bfloat16), "rep").astype(jnp.float32),
        lax.psum(summed[10].astype(jnp.bfloat16), "rep").astype(jnp.float32),
        lax.psum(summed[11].astype(jnp.bfloat16), "rep").astype(jnp.float32),
        lax.psum(summed[12].astype(jnp.bfloat16), "rep").astype(jnp.float32),
        lax.psum(summed[13].astype(jnp.bfloat16), "rep").astype(jnp.float32),
        lax.psum(summed[14].astype(jnp.bfloat16), "rep").astype(jnp.float32),
    )
    return (
        outcome.astype(jnp.bfloat16)[None],
        grad_source[None],
        grad_memory[None],
        totals[0],
        totals[1],
        totals[2],
        totals[3],
        totals[4],
        totals[5],
        totals[6],
        totals[7],
        totals[8],
        totals[9],
        totals[10],
        totals[11],
        totals[12],
        totals[13],
        totals[14],
    )


def swap(value, axis, size, step):
    return lax.ppermute(value, axis, [(place, place ^ step) for place in range(size)])


def after(value, *others):
    return lax.optimization_barrier((value, *others))[0]


def run_kernel(name, body, ids, operands, results, scratch=()):
    whole = pl.BlockSpec(memory_space=pltpu.VMEM)
    return pl.pallas_call(
        body,
        out_shape=[jax.ShapeDtypeStruct(shape, kind) for shape, kind in results],
        in_specs=[pl.BlockSpec(memory_space=pltpu.SMEM)] + [whole] * len(operands),
        out_specs=[whole] * len(results),
        scratch_shapes=[pltpu.VMEM(shape, kind) for shape, kind in scratch],
        name=name,
    )(ids, *operands)


low_kind = jnp.bfloat16
full_kind = jnp.float32


def rows_at(place, size):
    return pl.ds(pl.multiple_of(place * size, size), size)


def put_blocks(index, blocks, target):
    size = blocks[0].shape[0]
    for step, block in enumerate(blocks):
        target[rows_at(index ^ step, size), :] = block[...]


def split_cores(index, partial, room, send, keep):
    core = index & 1
    size = send.shape[0]
    room[...] = partial
    keep[...] = room[rows_at(core, size), :]
    send[...] = room[rows_at(1 - core, size), :].astype(low_kind)


def join_cores(index, own, other, room):
    core = index & 1
    size = own.shape[0]
    room[rows_at(core, size), :] = own[...].astype(full_kind)
    room[rows_at(1 - core, size), :] = other[...].astype(full_kind)
    return room[...]


def inverse_rms(values):
    return lax.rsqrt(jnp.mean(values * values, axis=-1, keepdims=True) + epsilon)


def norm_backward(grad, values, gain):
    scale = inverse_rms(values)
    row = jnp.sum(grad * values * scale, axis=0, keepdims=True)
    scaled = grad * gain
    inner = jnp.mean(scaled * values, axis=-1, keepdims=True)
    return scale * scaled - values * (scale * scale * scale * inner), row


def bucket_rows(buckets, length):
    lanes = lax.broadcasted_iota(jnp.int32, (buckets, length), 1)
    distance = jnp.where(lanes == 0, 0, length - lanes)
    return (bucket_of(distance) == lax.broadcasted_iota(jnp.int32, (buckets, length), 0)).astype(
        full_kind
    )


def columns_body(ids, *refs):
    count = len(refs) - 4
    sources, targets = refs[:count], refs[count:]
    for place in range(4):

        @pl.when(ids[0] == place)
        def _():
            for step in range(4):
                start = 0
                for source in sources:
                    width = source.shape[1] // 4
                    begin = (place ^ step) * width
                    targets[step][:, start : start + width] = source[:, begin : begin + width]
                    start += width


def pack_body(ids, source, gain0, gain1, gain2, table, *refs):
    sources, packed, targets = refs[:3], refs[3], refs[4:]
    columns_body(ids, *sources, *targets)
    size, model = source.shape
    packed[:size, :] = source[...]
    rows = table.shape[0]
    line = [gain[...].astype(full_kind).reshape(1, -1) for gain in (gain0, gain1, gain2)]
    width = sum(piece.shape[1] for piece in line)
    line = jnp.concatenate(line + [jnp.zeros((1, model - width), full_kind)], axis=1)
    grid = jnp.concatenate(
        [table[...].astype(full_kind), jnp.zeros((rows, model - table.shape[1]), full_kind)], axis=1
    )
    lines = jnp.concatenate([line, jnp.zeros((7, model), full_kind), grid], axis=0)
    packed[size:, :] = lines.astype(low_kind)


def split_columns_body(ids, gate, up, own, send1, send2, send3):
    column = ids[1] & 1
    width = gate.shape[1] // 4
    half = send2.shape[0]
    for place in range(4):

        @pl.when(ids[0] == place)
        def _():
            for step, target in enumerate((own, send1, send2, send3)):
                begin = (place ^ step) * width
                rows = slice(None) if step < 2 else rows_at(column, half)
                for number, source in enumerate((gate, up)):
                    target[:, number * width : (number + 1) * width] = source[
                        rows, begin : begin + width
                    ]


def heads_of(matrix, number, part, wide):
    start = part * wide + number * HEAD_DIM
    return matrix[:, start : start + HEAD_DIM]


def stack_heads(matrix, target, first):
    for number in range(matrix.shape[1] // HEAD_DIM):
        target[first + number, : matrix.shape[0], :] = matrix[
            :, number * HEAD_DIM : (number + 1) * HEAD_DIM
        ]


def joined_heads(source, first, count):
    return jnp.concatenate([source[first + number] for number in range(count)], axis=1)


def each_head(count, body):
    def step(number, unused):
        body(number)
        return unused

    lax.fori_loop(0, count, step, 0)


def softmax_rows(scores, allowed):
    scores = jnp.where(allowed, scores, masked_score)
    powers = jnp.exp(scores - jnp.max(scores, axis=-1, keepdims=True))
    return powers * (1.0 / jnp.sum(powers, axis=-1, keepdims=True))


def self_half(half, ids, source, weight, gains, rows, mapped_before, output, seg_col, seg_row, outs):
    normed_out, mapped_out, chances_out, mixed_out, send, keep, room, heads, joined = outs
    size = normed_out.shape[0]
    wide = output.shape[0]
    count = wide // HEAD_DIM
    normed = (source * inverse_rms(source) * gains[0:1, :]).astype(low_kind)
    normed_out[...] = normed
    mapped = product(normed, weight).astype(low_kind)
    mapped_out[...] = mapped
    every = mapped if half == 0 else jnp.concatenate([mapped_before, mapped], axis=0)
    keys = every.shape[0]
    places = lax.broadcasted_iota(jnp.int32, (size, keys), 0) + half * size
    others = lax.broadcasted_iota(jnp.int32, (size, keys), 1)
    allowed = (places >= others) & (seg_col == seg_row[:, :keys])
    stack_heads(mapped[:, :wide], heads, 0)
    stack_heads(every[:, wide:], heads, count)

    def one_head(number):
        line = jnp.broadcast_to(rows[pl.ds(number, 1), :], (size, rows.shape[1]))
        bias = pltpu.roll(line, half * size, 1, stride=1, stride_axis=0)[:, :keys]
        scores = product_cols(heads[number, :size, :], heads[count + number, :keys, :])
        chances = softmax_rows(scores + bias, allowed).astype(low_kind)
        chances_out[number] = chances
        joined[number] = product(chances, heads[2 * count + number, :keys, :]).astype(low_kind)

    each_head(count, one_head)
    mixed = joined_heads(joined, 0, count)
    mixed_out[...] = mixed
    split_cores(ids[0], product(mixed, output), room, send, keep)


def self_first_body(
    ids, x0, x1, x2, x3, w0, w1, w2, w3, output, seg_col, seg_row,
    source_out, weight_out, gains_out, rows_out,
    normed_out, mapped_out, chances_out, mixed_out, send, keep,
    room, heads, joined, small, lines,
):
    index = ids[0]
    tokens = source_out.shape[0] // 4
    put_blocks(index, [block.at[:tokens] for block in (x0, x1, x2, x3)], source_out)
    put_blocks(index, (w0, w1, w2, w3), weight_out)
    for step, block in enumerate((x0, x1, x2, x3)):
        small[rows_at(index ^ step, 16), :] = block[tokens:, :].astype(full_kind)
    model = source_out.shape[1]
    part = model // 4
    for place in range(3):
        gains_out[place : place + 1, :] = jnp.concatenate(
            [small[16 * t : 16 * t + 1, part * place : part * (place + 1)] for t in range(4)],
            axis=1,
        )
    gains_out[3:8, :] = jnp.zeros((5, model), full_kind)
    table = jnp.concatenate([small[16 * t + 8 : 16 * t + 16, :128] for t in range(4)], axis=0)
    hot = bucket_rows(table.shape[0], rows_out.shape[1])
    lines[...] = product_rows(table.astype(low_kind), hot.astype(low_kind))
    heads_here = chances_out.shape[0]
    for number in range(heads_here):
        rows_out[number : number + 1, :] = lines[pl.ds(index * heads_here + number, 1), :]
    rows_out[heads_here:8, :] = jnp.zeros((8 - heads_here, rows_out.shape[1]), full_kind)
    size = normed_out.shape[0]
    self_half(
        0, ids, source_out[:size, :].astype(full_kind), weight_out[...], gains_out, rows_out, None,
        output[...], seg_col[:size, :], seg_row[...],
        (normed_out, mapped_out, chances_out, mixed_out, send, keep, room, heads, joined),
    )


def self_second_body(
    ids, source, weight, gains, rows, mapped_before, output, seg_col, seg_row,
    normed_out, mapped_out, chances_out, mixed_out, send, keep, room, heads, joined,
):
    size = normed_out.shape[0]
    self_half(
        1, ids, source[size:, :].astype(full_kind), weight[...], gains, rows, mapped_before[...],
        output[...], seg_col[size:, :], seg_row[...],
        (normed_out, mapped_out, chances_out, mixed_out, send, keep, room, heads, joined),
    )


def cross_keys_body(ids, e0, e1, e2, e3, w0, w1, w2, w3, memory_out, weight_out, mapped_out):
    put_blocks(ids[0], (e0, e1, e2, e3), memory_out)
    put_blocks(ids[0], (w0, w1, w2, w3), weight_out)
    wide = weight_out.shape[1] // 3
    mapped_out[...] = product(memory_out[...], weight_out[:, wide:]).astype(low_kind)


def cross_body(
    half, ids, source, own, other, gains, weight, mapped, output, seg_col, enc_row,
    after_out, normed_out, query_out, chances_out, mixed_out, send, keep, room, heads, joined,
):
    size = after_out.shape[0]
    wide = output.shape[0]
    count = wide // HEAD_DIM
    start = half * size
    values = source[start : start + size, :].astype(full_kind) + join_cores(
        ids[0], own, other, room
    )
    after_out[...] = values
    normed = (values * inverse_rms(values) * gains[1:2, :]).astype(low_kind)
    normed_out[...] = normed
    query = product(normed, weight[:, :wide]).astype(low_kind)
    query_out[...] = query
    allowed = seg_col[start : start + size, :] == enc_row[...]
    stack_heads(query, heads, 0)
    stack_heads(mapped[...], heads, count)

    def one_head(number):
        scores = product_cols(heads[number, :size, :], heads[count + number])
        chances = softmax_rows(scores, allowed).astype(low_kind)
        chances_out[number] = chances
        joined[number] = product(chances, heads[2 * count + number]).astype(low_kind)

    each_head(count, one_head)
    mixed = joined_heads(joined, 0, count)
    mixed_out[...] = mixed
    split_cores(ids[0], product(mixed, output[...]), room, send, keep)


def feed_join_body(ids, w0, w1, w2, w2x, w3, w3x, g0, g1, g2, g3, weight_out, grad_out):
    index, column = ids[0], ids[1] & 1
    put_blocks(index, (w0, w1), weight_out)
    half = w2.shape[0]
    for step, mine, other in ((2, w2, w2x), (3, w3, w3x)):
        weight_out[rows_at(2 * (index ^ step) + column, half), :] = mine[...]
        weight_out[rows_at(2 * (index ^ step) + 1 - column, half), :] = other[...]
    put_blocks(ids[0], (g0, g1, g2, g3), grad_out)


def feed_body(half, ids, before, own, other, gains, weight, down, grad_out, *refs):
    parts = refs[:2] if half else ()
    after_out, normed_out, hidden_out, acts_out, *rest = refs[len(parts) :]
    size = after_out.shape[0]
    start = half * size
    units = down.shape[0]
    room = rest[-1]
    values = before[...] + join_cores(ids[0], own, other, room)
    after_out[...] = values
    normed = (values * inverse_rms(values) * gains[2:3, :]).astype(low_kind)
    normed_out[...] = normed
    acts = product(normed, weight[...])
    gate, up = acts[:, :units], acts[:, units:]
    root = math.sqrt(2 / math.pi)
    square = gate * gate
    bend = jnp.tanh(root * gate * (1.0 + 0.044715 * square))
    curve = 0.5 * gate * (1.0 + bend)
    slope = 0.5 * (1.0 + bend) + 0.5 * gate * (1.0 - bend * bend) * root * (
        1.0 + 3 * 0.044715 * square
    )
    hidden = (curve * up).astype(low_kind)
    hidden_out[...] = hidden
    grad_hidden = product_cols(grad_out[start : start + size, :], down[...])
    acts_out[:, :units] = (grad_hidden * up * slope).astype(low_kind)
    acts_out[:, units:] = (grad_hidden * curve).astype(low_kind)
    grad = product_cols(acts_out[...], weight[...])
    result = product(hidden, down[...])
    if half:
        send, keep, out_send, out_keep = rest[:4]
        for place, part in ((0, parts[0][...]), (1, grad)):
            split_cores(ids[0], part, room, send.at[place], keep.at[place])
        for place, part in ((0, parts[1][...]), (1, result)):
            split_cores(ids[0], part, room, out_send.at[place], out_keep.at[place])
    else:
        rest[0][...] = grad
        rest[1][...] = result


def rep_bits(ids):
    rep = ids[1]
    return rep & 1, (rep >> 1) & 1, rep >> 2


def each_chunk(ids, keep_first, send_first, keep_second, send_second, body):
    column, low, unused = rep_bits(ids)

    def step(slot, unused):
        high, middle = slot >> 1, slot & 1
        for target, bit in ((keep_first, column), (send_first, 1 - column)):
            body(target.at[slot], 4 * high + 2 * middle + bit, 0)
        for target, bit in ((keep_second, low), (send_second, 1 - low)):
            body(target.at[slot], 4 * high + 2 * bit + middle, 1)
        return unused

    lax.fori_loop(0, 4, step, 0)


def feed_weights_body(
    ids, normed0, normed1, acts0, acts1, hidden0, hidden1, grad_out,
    keep_first, send_first, keep_second, send_second, feed, down,
):
    size = normed0.shape[0]
    feed[...] = (
        product_rows(normed0[...], acts0[...]) + product_rows(normed1[...], acts1[...])
    ).astype(low_kind)
    down[...] = (
        product_rows(hidden0[...], grad_out[:size, :])
        + product_rows(hidden1[...], grad_out[size:, :])
    ).astype(low_kind)
    rows = feed.shape[0] // 4
    width = feed.shape[1] // 8
    small = down.shape[0] // 8
    lanes = down.shape[1] // 2

    def fill(target, chunk, part):
        for place in range(2):
            start = (2 * part + place) * rows
            target[place] = feed[start : start + rows, rows_at(chunk, width)]
        for piece in range(lanes // width):
            start = part * lanes + piece * width
            target[2, piece * small : (piece + 1) * small, :] = down[
                rows_at(chunk, small), start : start + width
            ]

    each_chunk(ids, keep_first, send_first, keep_second, send_second, fill)


def store_small_chunks(ids, columns, output, buffers):
    small = output.shape[0] // 8
    lanes = output.shape[1] // 2
    quarter = columns.shape[0] // 4

    def fill(target, chunk, part):
        for place in range(2):
            start = (2 * part + place) * quarter + chunk * small
            target[place] = columns[pl.ds(pl.multiple_of(start, 8), small), :].astype(low_kind)
        target[2] = jnp.zeros(target.shape[1:], low_kind)
        target[2, :, :lanes] = output[
            pl.ds(pl.multiple_of(chunk * small, 8), small), part * lanes : (part + 1) * lanes
        ].astype(low_kind)

    each_chunk(ids, *buffers, fill)


small_lanes = slice(3 * 128, 4 * 128)


def small_pieces(count, size):
    half = (count - size) // 2
    yield (0, 0), slice(0, size)
    yield (0, 1), slice(size, size + half)
    yield (1, 0), slice(size + half, count)


def halve_body(ids, keep_first, came_first, keep_second, came_second, *outs):
    new_first, send_first, new_second, send_second = outs
    column, low, unused = rep_bits(ids)
    for keep, came, new, send, bit in (
        (keep_first, came_first, new_first, send_first, low),
        (keep_second, came_second, new_second, send_second, column),
    ):
        for high in range(2):
            for target, place in ((new, 2 * high + bit), (send, 2 * high + 1 - bit)):
                total = keep[place].astype(full_kind) + came[place].astype(full_kind)
                target[high] = total.astype(target.dtype)


def quarter_body(ids, keep_first, came_first, keep_second, came_second, total):
    for part, (keep, came) in enumerate(((keep_first, came_first), (keep_second, came_second))):
        total[part] = (keep[...] + came[...].astype(full_kind)).astype(low_kind)


def quarter_small_body(
    ids, keep_first, came_first, keep_second, came_second, vector, near, far, across, total
):
    quarter_body(ids, keep_first, came_first, keep_second, came_second, total)
    lines = (vector[...] + near[...] + far[...] + across[...]).astype(low_kind)
    for (part, high), piece in small_pieces(lines.shape[0], total.shape[3]):
        total[part, high, 2, : piece.stop - piece.start, small_lanes] = lines[piece, :]


def trade_body(ids, mine, came, own, send1, send2, send3, rows, room):
    for part in range(2):
        for high in range(2):
            total = (
                mine[part, high].astype(full_kind) + came[part, high].astype(full_kind)
            ).astype(low_kind)
            room[2 * part, high] = total[0]
            room[2 * part + 1, high] = total[1]
            rows[part, high] = total[2]
    for step, target in enumerate((own, send1, send2, send3)):
        target[...] = room[ids[0] ^ step]


def gather_body(ids, own, came1, came2, came3, rows, first, second):
    for place, block in enumerate((own, came1, came2)):
        first[:, place] = block[...]
    for place, block in enumerate((came3, rows.at[0], rows.at[1])):
        second[:, place] = block[...]


def all_pieces(ids, firsts, seconds):
    for step in range(4):
        for high in range(2):
            chunk = 4 * high + ((ids[1] & 3) ^ step)
            yield firsts[step].at[high], seconds[step].at[high], high, chunk


def feed_out_body(ids, *refs):
    firsts, seconds, (gate, up, down) = refs[:4], refs[4:8], refs[8:]
    units = gate.shape[1] // 4
    small = down.shape[0] // 8
    for first, second, high, chunk in all_pieces(ids, firsts, seconds):
        width = first.shape[2]
        target = (gate, up)[high]
        for step in range(4):
            block = second[0] if step == 3 else first[step]
            start = (ids[0] ^ step) * units + (chunk & 3) * width
            target[:, pl.ds(pl.multiple_of(start, width), width)] = block.astype(full_kind)
        for piece in range(down.shape[1] // width):
            part, begin = piece // 3, piece % 3 * small
            down[rows_at(chunk, small), piece * width : (piece + 1) * width] = second[
                1 + part, begin : begin + small
            ].astype(full_kind)


def small_out_body(ids, *refs):
    firsts, seconds, outs, room = refs[:4], refs[4:8], refs[8:12], refs[-1]
    small = room.shape[1] // 8
    lanes = outs[3].shape[1] // 2
    wide = outs[0].shape[0]
    for first, second, high, chunk in all_pieces(ids, firsts, seconds):
        where = pl.ds(pl.multiple_of(chunk * small, 8), small)
        for step in range(4):
            block = second[0] if step == 3 else first[step]
            room[step, where, :] = block.astype(full_kind)
        for part in range(2):
            outs[3][where, part * lanes : (part + 1) * lanes] = second[1 + part][:, :lanes].astype(
                full_kind
            )
    for place in range(4):
        for number in range(3):
            outs[number][:, place * wide : (place + 1) * wide] = room[
                ids[0] ^ place, :, number * wide : (number + 1) * wide
            ]


def last_out_body(ids, *refs):
    *refs, gain0, gain1, gain2, table, room, lines, vector = refs
    small_out_body(ids, *refs, room)
    seconds = refs[4:8]
    for step, second in enumerate(seconds):
        place = (ids[1] & 3) ^ step
        for (part, high), piece in small_pieces(vector.shape[0], second.shape[2]):
            lines[place, piece, :] = second[
                high, 1 + part, : piece.stop - piece.start, small_lanes
            ].astype(full_kind)
    vector[...] = (lines[0] + lines[1]) + (lines[2] + lines[3])
    size = gain0.shape[0]
    count = 4 * size // 128
    for number, gain in enumerate((gain0, gain1, gain2)):
        line = jnp.concatenate(
            [vector[number * count + row : number * count + row + 1, :] for row in range(count)],
            axis=1,
        )
        for place in range(4):

            @pl.when(ids[0] == place)
            def _():
                gain[...] = line[:, place * size : (place + 1) * size].reshape(size)

    rows, heads = table.shape
    start = vector.shape[0] - 4 * rows + ids[0] * rows
    table[...] = vector[pl.ds(pl.multiple_of(start, rows), rows), :heads]


def attention_backward(grad, query, keys, values, chances):
    full = chances.astype(full_kind)
    grad_chances = product_cols(grad, values)
    grad_scores = full * (grad_chances - jnp.sum(full * grad_chances, axis=-1, keepdims=True))
    rounded = grad_scores.astype(low_kind)
    return (
        grad_scores,
        product(rounded, keys).astype(low_kind),
        product_rows(rounded, query),
        product_rows(chances, grad),
    )


def join_halves(index, own, other, room):
    core = index & 1
    size = own.shape[1]
    for chip in range(2):
        room[rows_at(core + 2 * chip, size), :] = own[chip].astype(full_kind)
        room[rows_at(1 - core + 2 * chip, size), :] = other[chip].astype(full_kind)
    return room[...]


def cross_back_body(
    ids, grad_out, own, other, values0, values1, gains, output, query0, query1, chances0, chances1,
    mapped, weight, total_out, low_out, query_out, sums_out, row_out, send, keep, room, heads, joined,
):
    wide = output.shape[0]
    join_halves(ids[0], own, other, room)
    size = values0.shape[0]
    row = 0.0
    for half, values in ((0, values0), (1, values1)):
        part = slice(half * size, (half + 1) * size)
        grad, piece = norm_backward(room[part, :], values[...], gains[2:3, :])
        row = row + piece
        total = grad_out[part, :].astype(full_kind) + grad
        total_out[part, :] = total
        low_out[part, :] = total.astype(low_kind)
    row_out[...] = jnp.broadcast_to(row, row_out.shape)
    grad_mixed = product_cols(low_out[...], output[...]).astype(low_kind)
    count = wide // HEAD_DIM
    stack_heads(grad_mixed, heads, 0)
    stack_heads(jnp.concatenate([query0[...], query1[...]], axis=0), heads, count)
    stack_heads(mapped[...], heads, 2 * count)

    def one_head(number):
        chances = jnp.concatenate([chances0[number], chances1[number]], axis=0)
        unused, grad_query, grad_keys, grad_values = attention_backward(
            heads[number], heads[count + number], heads[2 * count + number],
            heads[3 * count + number], chances,
        )
        joined[number] = grad_query
        joined[count + number] = grad_keys.astype(low_kind)
        joined[2 * count + number] = grad_values.astype(low_kind)

    each_head(count, one_head)
    query_out[...] = joined_heads(joined, 0, count)
    sums_out[...] = joined_heads(joined, count, 2 * count)
    scatter_cores(ids[0], product_cols(query_out[...], weight[:, :wide]), room, send, keep)


def cross_weights_body(
    ids, normed0, normed1, query, memory, sums, mixed0, mixed1, low, weight,
    keep_first, send_first, keep_second, send_second, send, keep, room, columns, output,
):
    wide = query.shape[1]
    size = normed0.shape[0]
    columns[:, :wide] = product_rows(normed0[...], query[:size, :]) + product_rows(
        normed1[...], query[size:, :]
    )
    columns[:, wide:] = product_rows(memory[...], sums[...])
    output[...] = product_rows(mixed0[...], low[:size, :]) + product_rows(mixed1[...], low[size:, :])
    store_small_chunks(ids, columns, output, (keep_first, send_first, keep_second, send_second))
    scatter_cores(ids[0], product_cols(sums[...], weight[:, wide:]), room, send, keep)


def scatter_cores(index, partial, room, send, keep):
    core = index & 1
    size = send.shape[1]
    room[...] = partial
    for chip in range(2):
        keep[chip] = room[rows_at(core + 2 * chip, size), :]
        send[chip] = room[rows_at(1 - core + 2 * chip, size), :].astype(low_kind)


def diagonal_sums(matrix):
    width = matrix.shape[1]
    size = matrix.shape[0]
    while size > 1:
        size //= 2
        matrix = matrix[:size] + pltpu.roll(matrix[size:], width - size, 1)
    return matrix


def self_back_body(
    ids, total, own, other, values0, values1, gains, output, mapped0, mapped1, chances0, chances1,
    total_out, low_out, query_out, sums_out, row_out, table_out, room, heads, joined,
):
    wide = output.shape[0]
    join_halves(ids[0], own, other, room)
    size = values0.shape[0]
    row = 0.0
    for half, values in ((0, values0), (1, values1)):
        part = slice(half * size, (half + 1) * size)
        grad, piece = norm_backward(room[part, :], values[...], gains[1:2, :])
        row = row + piece
        new_total = total[part, :] + grad
        total_out[part, :] = new_total
        low_out[part, :] = new_total.astype(low_kind)
    row_out[...] = jnp.broadcast_to(row, row_out.shape)
    grad_mixed = product_cols(low_out[...], output[...]).astype(low_kind)
    buckets = table_out.shape[0]
    hot = bucket_rows(buckets, 2 * size)
    count = wide // HEAD_DIM
    stack_heads(grad_mixed, heads, 0)
    stack_heads(jnp.concatenate([mapped0[...], mapped1[...]], axis=0), heads, count)
    table_out[...] = jnp.zeros(table_out.shape, full_kind)

    def one_head(number):
        line = sums = None
        for half, chances in ((1, chances1), (0, chances0)):
            part = slice(half * size, (half + 1) * size)
            seen = slice(0, (half + 1) * size)
            grad_scores, grad_query, grad_keys, grad_values = attention_backward(
                heads[number, part, :], heads[count + number, part, :],
                heads[2 * count + number, seen, :], heads[3 * count + number, seen, :],
                chances[number],
            )
            joined[number, part, :] = grad_query
            if half:
                line = pltpu.roll(diagonal_sums(grad_scores), size, 1)
                sums = (grad_keys, grad_values)
            else:
                empty = jnp.zeros((size, size), full_kind)
                line = line + diagonal_sums(jnp.concatenate([grad_scores, empty], axis=1))
                for place, first, later in ((1, grad_keys, sums[0]), (2, grad_values, sums[1])):
                    joined[place * count + number, :size, :] = (later[:size] + first).astype(low_kind)
                    joined[place * count + number, size:, :] = later[size:].astype(low_kind)
        column = jnp.sum(hot * line, axis=1, keepdims=True)
        lanes = lax.broadcasted_iota(jnp.int32, table_out.shape, 1)
        table_out[...] += jnp.where(lanes == number, column, 0.0)

    each_head(count, one_head)
    query_out[...] = joined_heads(joined, 0, count)
    sums_out[...] = joined_heads(joined, count, 2 * count)


def self_weights_body(
    ids, normed0, normed1, query, sums, mixed0, mixed1, low, weight,
    keep_first, send_first, keep_second, send_second, send, keep, room, columns, output, merged,
):
    wide = query.shape[1]
    size = normed0.shape[0]
    merged[:, :wide] = query[...]
    merged[:, wide:] = sums[...]
    columns[...] = product_rows(normed0[...], merged[:size, :]) + product_rows(
        normed1[...], merged[size:, :]
    )
    output[...] = product_rows(mixed0[...], low[:size, :]) + product_rows(mixed1[...], low[size:, :])
    store_small_chunks(ids, columns, output, (keep_first, send_first, keep_second, send_second))
    scatter_cores(ids[0], product_cols(merged[...], weight[...]), room, send, keep)


def finish_body(ids, source, mine, far, gains, total, cross_row, feed_row, table, grad_out, vector):
    index = ids[0]
    size, model = source.shape
    grad, row = norm_backward(
        mine[...] + far[...].astype(full_kind), source[...].astype(full_kind), gains[0:1, :]
    )
    grad_out[...] = total[rows_at(index, size), :] + grad
    lanes = lax.broadcasted_iota(jnp.int32, (1, model), 1)
    part = model // 4
    here = (lanes >= index * part) & (lanes < (index + 1) * part)
    pieces = []
    for line in (row, jnp.where(here, cross_row[0:1, :], 0.0), jnp.where(here, feed_row[0:1, :], 0.0)):
        pieces += [line[:, start : start + 128] for start in range(0, model, 128)]
    pieces += [jnp.zeros((-len(pieces) % 8, 128), full_kind)]
    vector[: vector.shape[0] - table.shape[0], :] = jnp.concatenate(pieces, axis=0)
    vector[vector.shape[0] - table.shape[0] :, :] = pltpu.roll(
        table[...], index * (HEADS // 4), 1
    )


def chip_pair_body(ids, keep, arrived, mine, other):
    chip = ids[0] >> 1
    mine[...] = keep[chip] + arrived[chip].astype(full_kind)
    other[...] = (keep[1 - chip] + arrived[1 - chip].astype(full_kind)).astype(low_kind)


class Kernels:
    def __init__(self, ids):
        self.ids = ids

    def __call__(self, name, body, operands, results, scratch=(), cover=()):
        outs = run_kernel(name, body, self.ids, operands, results, scratch)
        if cover:
            outs = after(tuple(outs), *cover)
        self.ids = after(self.ids, outs[0])
        return outs

    def wait(self, *values):
        self.ids = after(self.ids, *values)


def rep_swap(value, step):
    return swap(value, "rep", 8, step)


def shard_swap(value, step):
    return swap(value, "shard", 4, step)


class Reduction:
    def __init__(self, call, name, buffers):
        self.call, self.name = call, name
        self.keeps = (buffers[0], buffers[2])
        self.came = (rep_swap(buffers[1], 1), rep_swap(buffers[3], 2))
        self.shape = buffers[0].shape[1:]

    def halve(self, cover=()):
        results = []
        for unused in range(2):
            results += [((2,) + self.shape, full_kind), ((2,) + self.shape, low_kind)]
        outs = self.call(
            self.name + "_halve",
            halve_body,
            (self.keeps[0], self.came[0], self.keeps[1], self.came[1]),
            results,
            cover=cover,
        )
        self.keeps = (outs[0], outs[2])
        self.came = (rep_swap(outs[1], 2), rep_swap(outs[3], 1))

    def quarter(self, cover=(), vectors=()):
        (self.total,) = self.call(
            self.name + "_quarter",
            quarter_small_body if vectors else quarter_body,
            (self.keeps[0], self.came[0], self.keeps[1], self.came[1]) + vectors,
            [((2, 2) + self.shape, low_kind)],
            cover=cover,
        )
        self.last = rep_swap(self.total, 4)

    def trade(self, cover=()):
        block = self.shape[1:]
        own, *sends, self.rows = self.call(
            self.name + "_trade",
            trade_body,
            (self.total, self.last),
            [((2,) + block, low_kind)] * 4 + [((2, 2) + block, low_kind)],
            [((4, 2) + block, low_kind)],
            cover=cover,
        )
        self.blocks = [own] + [shard_swap(send, step) for step, send in zip((1, 2, 3), sends)]

    def gather(self, cover=()):
        first, second = self.call(
            self.name + "_gather",
            gather_body,
            (*self.blocks, self.rows),
            [((2,) + self.shape, low_kind)] * 2,
            cover=cover,
        )
        first_far, second_far = rep_swap(first, 2), rep_swap(second, 1)
        self.far = (first_far, second_far)
        self.near = (rep_swap(first, 1), rep_swap(second, 2))
        self.firsts = (first, self.near[0], first_far, rep_swap(first_far, 1))
        self.seconds = (second, second_far, self.near[1], rep_swap(second_far, 2))

    def finish(self, body, results, scratch=(), cover=()):
        return self.call(
            self.name + "_out", body, (*self.firsts, *self.seconds), results, scratch, cover
        )


class GroupSum:
    def __init__(self, send, keep):
        self.keep = keep
        self.came = shard_swap(send, 1)

    def add(self):
        self.pair = (self.keep + self.came.astype(full_kind)).astype(low_kind)
        self.far = shard_swap(self.pair, 2)
        return self.pair

    def hold(self, value):
        self.far = after(self.far, value)

    def total(self):
        own = (self.pair.astype(full_kind) + self.far.astype(full_kind)).astype(low_kind)
        self.results = (own, shard_swap(own, 1))
        return own


def split_shards(
    inputs,
    encoder,
    segments,
    enc_segments,
    self_query,
    self_key,
    self_value,
    self_output,
    cross_query,
    cross_key,
    cross_value,
    cross_output,
    gate_weight,
    up_weight,
    down_weight,
    self_gain,
    cross_gain,
    feed_gain,
    bias_table,
    cotangent,
):
    index = lax.axis_index("shard")
    rep = lax.axis_index("rep")
    call = Kernels(jnp.stack([index, rep]))
    tokens_here, model = inputs.shape[1:]
    length = 4 * tokens_here
    half_size = 2 * tokens_here
    heads_here = HEADS // 4
    wide = heads_here * HEAD_DIM
    units = down_weight.shape[0]
    memory_length = enc_segments.shape[1]
    small_rows = bias_table.shape[0]
    buckets = 4 * small_rows
    part = self_gain.shape[0]

    def blocks_of(*weights):
        width = sum(weight.shape[1] for weight in weights) // 4
        shape = (weights[0].shape[0], width)
        return call("columns", columns_body, weights, [(shape, low_kind)] * 4)

    def traded(blocks):
        return [blocks[0]] + [shard_swap(blocks[step], step) for step in range(1, 4)]

    column_shape = (part, 3 * wide)
    packed, *self_blocks = call(
        "pack",
        pack_body,
        (
            inputs[0], self_gain, cross_gain, feed_gain, bias_table, self_query, self_key,
            self_value,
        ),
        [((tokens_here + 16, model), low_kind)] + [(column_shape, low_kind)] * 4,
    )
    source_far = shard_swap(packed, 2)
    self_blocks = traded(self_blocks)
    cross_blocks = blocks_of(cross_query, cross_key, cross_value)
    feed_blocks = call(
        "feed_columns",
        split_columns_body,
        (gate_weight, up_weight),
        [((part, 2 * units), low_kind)] * 2 + [((part // 2, 2 * units), low_kind)] * 2,
    )
    source_far = after(source_far, feed_blocks[0])
    source_blocks = [packed, shard_swap(packed, 1), source_far, shard_swap(source_far, 1)]
    seg_row = segments
    seg_col = segments[0][:, None]
    enc_row = enc_segments
    call.wait(seg_col, self_blocks[2], self_blocks[3])
    cross_blocks = traded(after(tuple(cross_blocks), self_blocks[2], self_blocks[3]))
    room = [((half_size, model), full_kind)]
    whole_room = [((length, model), full_kind)]

    def head_rooms(places, rows, outs):
        return [
            ((places * heads_here, max(length, memory_length), HEAD_DIM), low_kind),
            ((outs * heads_here, rows, HEAD_DIM), low_kind),
        ]

    pieces = [((tokens_here, model), low_kind), ((tokens_here, model), full_kind)]
    two_pieces = [((2,) + shape, kind) for shape, kind in pieces]

    def self_results(keys):
        return [
            ((half_size, model), low_kind),
            ((half_size, 3 * wide), low_kind),
            ((heads_here, half_size, keys), low_kind),
            ((half_size, wide), low_kind),
        ] + pieces

    source, w_self, gains, rows, *first = call(
        "self_first",
        self_first_body,
        (*source_blocks, *self_blocks, self_output, seg_col, seg_row),
        [
            ((length, model), low_kind),
            ((model, 3 * wide), low_kind),
            ((8, model), full_kind),
            ((8, length), full_kind),
        ]
        + self_results(half_size),
        room + head_rooms(3, half_size, 1) + [((64, model), full_kind), ((128, length), full_kind)],
        cover=(cross_blocks[2], cross_blocks[3]),
    )
    first_sum = GroupSum(*first[4:])
    memory_far = shard_swap(after(encoder[0], first[0]), 2)
    second = call(
        "self_second",
        self_second_body,
        (source, w_self, gains, rows, first[1], self_output, seg_col, seg_row),
        self_results(length),
        room + head_rooms(3, half_size, 1),
        cover=(first_sum.came,),
    )
    second_sum = GroupSum(*second[4:])
    call.wait(first_sum.add())
    memory_blocks = [
        encoder[0], shard_swap(encoder[0], 1), memory_far, shard_swap(memory_far, 1)
    ]
    memory, w_cross, cross_mapped = call(
        "cross_keys",
        cross_keys_body,
        (*memory_blocks, *cross_blocks),
        [
            ((memory_length, model), low_kind),
            ((model, 3 * wide), low_kind),
            ((memory_length, 2 * wide), low_kind),
        ],
        cover=(second_sum.came,),
    )
    pair = second_sum.add()
    call.wait(pair)
    first_sum.total()
    feed_blocks = after(tuple(feed_blocks), pair)
    feed_near = shard_swap(feed_blocks[1], 1)
    feed_two = shard_swap(feed_blocks[2], 2)

    def cross_call(half, sums, cover):
        own, other = sums.results
        return call(
            "cross",
            functools.partial(cross_body, half),
            (source, own, other, gains, w_cross, cross_mapped, cross_output, seg_col, enc_row),
            [
                ((half_size, model), full_kind),
                ((half_size, model), low_kind),
                ((half_size, wide), low_kind),
                ((heads_here, half_size, memory_length), low_kind),
                ((half_size, wide), low_kind),
            ]
            + pieces,
            room + head_rooms(3, half_size, 1),
            cover=cover,
        )

    grad_far = shard_swap(after(cotangent[0], cross_mapped), 2)
    cross0 = cross_call(0, first_sum, (second_sum.far, feed_two, grad_far))
    cross_first = GroupSum(*cross0[5:])
    call.wait(second_sum.total())
    feed_two_other = rep_swap(feed_two, 1)
    feed_three = shard_swap(after(feed_blocks[3], cross0[0]), 3)
    cross1 = cross_call(1, second_sum, (feed_three, feed_two_other, cross_first.came))
    cross_second = GroupSum(*cross1[5:])
    call.wait(cross_first.add())
    feed_three_other = rep_swap(feed_three, 1)
    grad_blocks = [
        cotangent[0], shard_swap(cotangent[0], 1), grad_far, shard_swap(grad_far, 1)
    ]
    w_feed, grad_out = call(
        "feed_join",
        feed_join_body,
        (
            feed_blocks[0], feed_near, feed_two, feed_two_other, feed_three, feed_three_other,
            *grad_blocks,
        ),
        [((model, 2 * units), low_kind), ((length, model), low_kind)],
        cover=(cross_second.came,),
    )
    call.wait(cross_second.add())
    cross_first.total()
    cross_second.hold(w_feed)

    def feed_call(half, sums, before, parts, tail, cover=()):
        own, other = sums.results
        return call(
            "feed",
            functools.partial(feed_body, half),
            (before, own, other, gains, w_feed, down_weight, grad_out) + parts,
            [
                ((half_size, model), full_kind),
                ((half_size, model), low_kind),
                ((half_size, units), low_kind),
                ((half_size, 2 * units), low_kind),
            ]
            + tail,
            room,
            cover=cover,
        )

    feed0 = feed_call(0, cross_first, cross0[0], (), room * 2, (cross_second.far,))
    cross_second.total()
    feed1 = feed_call(1, cross_second, cross1[0], (feed0[4], feed0[5]), two_pieces * 2)
    feed_sum = GroupSum(*feed1[4:6])
    out_came = shard_swap(feed1[6], 1)

    chunk = (3, model // 4, 2 * units // 8)
    feed_grads = Reduction(
        call,
        "feed_grads",
        call(
            "feed_weights",
            feed_weights_body,
            (feed0[1], feed1[1], feed0[3], feed1[3], feed0[2], feed1[2], grad_out),
            [((4,) + chunk, low_kind)] * 4,
            [((model, 2 * units), low_kind), ((units, model), low_kind)],
            cover=(feed_sum.came, out_came),
        ),
    )
    call.wait(feed_sum.add())

    def scatter_pair(arrived, keep, cover=()):
        mine, other = call(
            "chip_pair",
            chip_pair_body,
            (keep, arrived),
            [((tokens_here, model), full_kind), ((tokens_here, model), low_kind)],
            cover=cover,
        )
        return mine, shard_swap(other, 2)

    mine, out_far = scatter_pair(out_came, feed1[7])
    feed_sum.total()
    own_after = lax.dynamic_slice_in_dim(
        jnp.where(index < 2, feed0[0], feed1[0]), (index & 1) * tokens_here, tokens_here
    )
    outcome = (own_after + mine + out_far.astype(full_kind)).astype(low_kind)

    total_cross, low_cross, query_cross, sums_cross, row_feed, *sends = call(
        "cross_back",
        cross_back_body,
        (
            grad_out, *feed_sum.results, feed0[0], feed1[0], gains, cross_output, cross0[2], cross1[2],
            cross0[3], cross1[3], cross_mapped, w_cross,
        ),
        [
            ((length, model), full_kind),
            ((length, model), low_kind),
            ((length, wide), low_kind),
            ((memory_length, 2 * wide), low_kind),
            ((8, model), full_kind),
        ]
        + two_pieces,
        whole_room + head_rooms(4, length, 3),
        cover=feed_grads.came + (out_far,),
    )
    cross_sum = GroupSum(*sends)
    feed_grads.halve(cover=(cross_sum.came,))
    call.wait(cross_sum.add())
    small_chunk = (3, wide // 8, 3 * wide)
    weight_room = [((model, 3 * wide), full_kind), ((wide, model), full_kind)]
    *buffers, send, keep = call(
        "cross_weights",
        cross_weights_body,
        (
            cross0[1], cross1[1], query_cross, memory, sums_cross, cross0[4], cross1[4], low_cross,
            w_cross,
        ),
        [((4,) + small_chunk, low_kind)] * 4 + two_pieces,
        whole_room + weight_room,
        cover=(cross_sum.far,) + feed_grads.came,
    )
    cross_sum.hold(keep)
    cross_grads = Reduction(call, "cross_grads", buffers)
    memory_came, memory_keep = shard_swap(send, 1), keep
    call.wait(cross_sum.total())
    feed_grads.quarter(cover=cross_sum.results)
    total_self, low_self, query_self, sums_self, row_cross, table = call(
        "self_back",
        self_back_body,
        (
            total_cross, *cross_sum.results, cross0[0], cross1[0], gains, self_output, first[1], second[1],
            first[2], second[2],
        ),
        [
            ((length, model), full_kind),
            ((length, model), low_kind),
            ((length, wide), low_kind),
            ((length, 2 * wide), low_kind),
            ((8, model), full_kind),
            ((buckets, 128), full_kind),
        ],
        whole_room + head_rooms(4, length, 3),
        cover=(memory_came,),
    )
    *buffers, send, keep = call(
        "self_weights",
        self_weights_body,
        (first[0], second[0], query_self, sums_self, first[3], second[3], low_self, w_self),
        [((4,) + small_chunk, low_kind)] * 4 + two_pieces,
        whole_room + weight_room + [((length, 3 * wide), low_kind)],
        cover=cross_grads.came,
    )
    self_grads = Reduction(call, "self_grads", buffers)
    arrived = shard_swap(send, 1)
    cross_grads.halve(cover=(arrived,))
    mine, far = scatter_pair(arrived, keep)
    feed_grads.trade(cover=self_grads.came)
    call.wait(outcome)
    self_grads.halve(cover=cross_grads.came + (far,))
    cross_grads.quarter(cover=tuple(feed_grads.blocks[1:]))
    gain_rows = -(-3 * model // 1024) * 8
    vector_kind = ((gain_rows + buckets, 128), full_kind)
    grad_source, vector = call(
        "finish",
        finish_body,
        (inputs[0], mine, far, gains, total_self, row_cross, row_feed, table),
        [((tokens_here, model), full_kind), vector_kind],
        cover=self_grads.came,
    )
    vectors = (vector,) + tuple(shard_swap(vector, step) for step in (1, 2, 3))
    memory_mine, memory_far = scatter_pair(memory_came, memory_keep, vectors[1:])
    grad_memory = memory_mine + memory_far.astype(full_kind)
    self_grads.quarter(vectors=vectors)
    feed_grads.gather()
    cross_grads.trade()
    cross_grads.gather(cover=feed_grads.far)
    self_grads.trade(cover=cross_grads.far)
    feed_out = feed_grads.finish(
        feed_out_body,
        [((part, 4 * units), full_kind)] * 2 + [((units, model), full_kind)],
        cover=tuple(self_grads.blocks[1:]),
    )
    self_grads.gather()
    small_results = [((part, model), full_kind)] * 3 + [((wide, model), full_kind)]
    out_room = [((4, wide, 3 * wide), full_kind)]
    cross_out = cross_grads.finish(small_out_body, small_results, out_room, self_grads.far)
    *self_out, gain0, gain1, gain2, table_grad = self_grads.finish(
        last_out_body,
        small_results + [((part,), full_kind)] * 3 + [((small_rows, HEADS), full_kind)],
        out_room + [((4,) + vector_kind[0], full_kind), vector_kind],
    )

    return (
        outcome[None],
        grad_source[None],
        grad_memory[None],
        *self_out,
        *cross_out,
        *feed_out,
        gain0,
        gain1,
        gain2,
        table_grad,
    )


def solution(mesh):
    in_specs = (
        P("rep", "shard", None),
        P("rep", "shard", None),
        P("rep", None),
        P("rep", None),
        P("shard", None),
        P("shard", None),
        P("shard", None),
        P("shard", None),
        P("shard", None),
        P("shard", None),
        P("shard", None),
        P("shard", None),
        P("shard", None),
        P("shard", None),
        P("shard", None),
        P("shard"),
        P("shard"),
        P("shard"),
        P("shard", None),
        P("rep", "shard", None),
    )
    out_specs = (
        P("rep", "shard", None),
        P("rep", "shard", None),
        P("rep", "shard", None),
        P("shard", None),
        P("shard", None),
        P("shard", None),
        P("shard", None),
        P("shard", None),
        P("shard", None),
        P("shard", None),
        P("shard", None),
        P("shard", None),
        P("shard", None),
        P("shard", None),
        P("shard"),
        P("shard"),
        P("shard"),
        P("shard", None),
    )
    split = mesh.shape["shard"] == 4 and mesh.shape["rep"] == 8
    body = split_shards if split else shards
    return jax.shard_map(body, mesh=mesh, in_specs=in_specs, out_specs=out_specs, check_vma=False)
```

```python
import functools
import math

import jax
import jax.numpy as jnp
from jax import lax
from jax.experimental import pallas as pl
from jax.experimental.pallas import tpu as pltpu
from jax.sharding import PartitionSpec as P

HEADS = 12
HEAD_DIM = 64


bucket_edges = [math.ceil(16 * 8 ** (number / 16)) for number in range(1, 16)]
epsilon = 1e-06
masked_score = -1000000000.0


def bucket_of(distance):
    far_part = sum(((distance >= border).astype(jnp.int32) for border in bucket_edges))
    return jnp.where(distance < 16, distance, 16 + far_part)


def rms_scale(values, scales):
    return values * lax.rsqrt(jnp.mean(values * values, axis=-1, keepdims=True) + epsilon) * scales


def product(former, latter):
    return jnp.dot(former, latter, preferred_element_type=jnp.float32)


def product_rows(former, latter):
    return lax.dot_general(
        former, latter, (((0,), (0,)), ((), ())), preferred_element_type=jnp.float32
    )


def product_cols(former, latter):
    return lax.dot_general(
        former, latter, (((1,), (1,)), ((), ())), preferred_element_type=jnp.float32
    )


def split_heads(matrix):
    return matrix.reshape(matrix.shape[0], HEADS, HEAD_DIM).transpose(1, 0, 2)


def join_heads(stacked):
    return stacked.transpose(1, 0, 2).reshape(stacked.shape[1], HEADS * HEAD_DIM)


def to_blocks(matrix, block_count):
    return matrix.reshape(block_count, -1, HEADS, HEAD_DIM).transpose(0, 2, 1, 3)


def from_blocks(stacked):
    return stacked.transpose(0, 2, 1, 3).reshape(-1, HEADS * HEAD_DIM)


def self_scores(queries, query_start, query_ids, table_full, key_rows, key_start, key_ids):
    query_count = queries.shape[1]
    key_count = key_rows.shape[1]
    query_places = query_start + jnp.arange(query_count, dtype=jnp.int32)
    key_places = key_start + jnp.arange(key_count, dtype=jnp.int32)
    buckets = bucket_of(jnp.maximum(query_places[:, None] - key_places[None, :], 0))
    one_hot = (
        buckets.reshape(1, -1) == jnp.arange(table_full.shape[0], dtype=jnp.int32)[:, None]
    ).astype(jnp.bfloat16)
    bias_block = jnp.einsum(
        "bn,bh->hn", one_hot, table_full, preferred_element_type=jnp.float32
    ).reshape(HEADS, query_count, key_count)
    scores = (
        jnp.einsum("hqd,hkd->hqk", queries, key_rows, preferred_element_type=jnp.float32)
        + bias_block
    )
    allowed = (query_places[:, None] >= key_places[None, :]) & (
        query_ids[:, None] == key_ids[None, :]
    )
    return (jnp.where(allowed[None], scores, masked_score), one_hot)


def self_logsum(queries, query_start, query_ids, table_full, key_blocks, id_blocks, key_starts):
    query_count = queries.shape[1]

    def advance(running, packed):
        largest, totals = running
        key_rows, key_ids, key_start = packed
        scores, unused = self_scores(
            queries, query_start, query_ids, table_full, key_rows, key_start, key_ids
        )
        newest = jnp.maximum(largest, jnp.max(scores, axis=-1, keepdims=True))
        totals = totals * jnp.exp(largest - newest) + jnp.sum(
            jnp.exp(scores - newest), axis=-1, keepdims=True
        )
        return ((newest, totals), None)

    initial = (
        jnp.full((HEADS, query_count, 1), -jnp.inf, jnp.float32),
        jnp.zeros((HEADS, query_count, 1), jnp.float32),
    )
    (largest, totals), unused = lax.scan(advance, initial, (key_blocks, id_blocks, key_starts))
    return largest + jnp.log(totals)


def self_mix(
    queries,
    query_start,
    query_ids,
    table_full,
    key_blocks,
    value_blocks,
    id_blocks,
    key_starts,
    logsum,
):

    def advance(accum, packed):
        key_rows, value_rows, key_ids, key_start = packed
        scores, unused = self_scores(
            queries, query_start, query_ids, table_full, key_rows, key_start, key_ids
        )
        weights = jnp.exp(scores - logsum).astype(jnp.bfloat16)
        return (
            accum
            + jnp.einsum("hqk,hkd->hqd", weights, value_rows, preferred_element_type=jnp.float32),
            None,
        )

    initial = jnp.zeros((HEADS, queries.shape[1], HEAD_DIM), jnp.float32)
    accum, unused = lax.scan(advance, initial, (key_blocks, value_blocks, id_blocks, key_starts))
    return accum


def self_backward(
    queries,
    query_start,
    query_ids,
    table_full,
    key_blocks,
    value_blocks,
    id_blocks,
    key_starts,
    logsum,
    grad_mixed,
):
    query_count = queries.shape[1]

    def dots(accum, packed):
        key_rows, value_rows, key_ids, key_start = packed
        scores, unused = self_scores(
            queries, query_start, query_ids, table_full, key_rows, key_start, key_ids
        )
        chances = jnp.exp(scores - logsum)
        grad_chances = jnp.einsum(
            "hqd,hkd->hqk", grad_mixed, value_rows, preferred_element_type=jnp.float32
        )
        return (accum + jnp.sum(chances * grad_chances, axis=-1, keepdims=True), None)

    row_dots, unused = lax.scan(
        dots,
        jnp.zeros((HEADS, query_count, 1), jnp.float32),
        (key_blocks, value_blocks, id_blocks, key_starts),
    )

    def advance(running, packed):
        grad_queries, grad_table = running
        key_rows, value_rows, key_ids, key_start = packed
        scores, one_hot = self_scores(
            queries, query_start, query_ids, table_full, key_rows, key_start, key_ids
        )
        chances = jnp.exp(scores - logsum)
        grad_chances = jnp.einsum(
            "hqd,hkd->hqk", grad_mixed, value_rows, preferred_element_type=jnp.float32
        )
        grad_scores = chances * (grad_chances - row_dots)
        rounded = grad_scores.astype(jnp.bfloat16)
        grad_values = jnp.einsum(
            "hqk,hqd->hkd",
            chances.astype(jnp.bfloat16),
            grad_mixed,
            preferred_element_type=jnp.float32,
        )
        grad_keys = jnp.einsum("hqk,hqd->hkd", rounded, queries, preferred_element_type=jnp.float32)
        grad_queries = grad_queries + jnp.einsum(
            "hqk,hkd->hqd", rounded, key_rows, preferred_element_type=jnp.float32
        )
        grad_table = grad_table + jnp.einsum(
            "bn,hn->bh",
            one_hot,
            grad_scores.reshape(HEADS, -1),
            precision=lax.Precision.HIGHEST,
            preferred_element_type=jnp.float32,
        )
        return ((grad_queries, grad_table), (grad_keys, grad_values))

    initial = (
        jnp.zeros((HEADS, query_count, HEAD_DIM), jnp.float32),
        jnp.zeros((table_full.shape[0], HEADS), jnp.float32),
    )
    (grad_queries, grad_table), (grad_keys, grad_values) = lax.scan(
        advance, initial, (key_blocks, value_blocks, id_blocks, key_starts)
    )
    return (join_heads(grad_queries), grad_table, from_blocks(grad_keys), from_blocks(grad_values))


def cross_forward(queries, key_heads, value_heads, allowed):
    scores = jnp.where(
        allowed,
        jnp.einsum("hqd,hkd->hqk", queries, key_heads, preferred_element_type=jnp.float32),
        masked_score,
    )
    largest = jnp.max(scores, axis=-1, keepdims=True)
    logsum = largest + jnp.log(jnp.sum(jnp.exp(scores - largest), axis=-1, keepdims=True))
    weights = jnp.exp(scores - logsum).astype(jnp.bfloat16)
    mixed = jnp.einsum("hqk,hkd->hqd", weights, value_heads, preferred_element_type=jnp.float32)
    return (mixed, logsum)


def cross_backward(queries, key_heads, value_heads, allowed, logsum, grad_mixed):
    scores = jnp.where(
        allowed,
        jnp.einsum("hqd,hkd->hqk", queries, key_heads, preferred_element_type=jnp.float32),
        masked_score,
    )
    chances = jnp.exp(scores - logsum)
    grad_values = jnp.einsum(
        "hqk,hqd->hkd", chances.astype(jnp.bfloat16), grad_mixed, preferred_element_type=jnp.float32
    )
    grad_chances = jnp.einsum(
        "hqd,hkd->hqk", grad_mixed, value_heads, preferred_element_type=jnp.float32
    )
    grad_scores = chances * (grad_chances - jnp.sum(chances * grad_chances, axis=-1, keepdims=True))
    rounded = grad_scores.astype(jnp.bfloat16)
    grad_queries = jnp.einsum(
        "hqk,hkd->hqd", rounded, key_heads, preferred_element_type=jnp.float32
    )
    grad_keys = jnp.einsum("hqk,hqd->hkd", rounded, queries, preferred_element_type=jnp.float32)
    return (join_heads(grad_queries), join_heads(grad_keys), join_heads(grad_values))


def shards(
    inputs,
    encoder,
    segments,
    enc_segments,
    self_query,
    self_key,
    self_value,
    self_output,
    cross_query,
    cross_key,
    cross_value,
    cross_output,
    gate_weight,
    up_weight,
    down_weight,
    self_gain,
    cross_gain,
    feed_gain,
    bias_table,
    cotangent,
):
    fetched = (
        lax.all_gather(self_query, "shard", axis=0, tiled=True),
        lax.all_gather(self_key, "shard", axis=0, tiled=True),
        lax.all_gather(self_value, "shard", axis=0, tiled=True),
        lax.all_gather(self_output, "shard", axis=0, tiled=True),
        lax.all_gather(cross_query, "shard", axis=0, tiled=True),
        lax.all_gather(cross_key, "shard", axis=0, tiled=True),
        lax.all_gather(cross_value, "shard", axis=0, tiled=True),
        lax.all_gather(cross_output, "shard", axis=0, tiled=True),
        lax.all_gather(gate_weight, "shard", axis=0, tiled=True),
        lax.all_gather(up_weight, "shard", axis=0, tiled=True),
        lax.all_gather(down_weight, "shard", axis=0, tiled=True),
        lax.all_gather(self_gain, "shard", axis=0, tiled=True),
        lax.all_gather(cross_gain, "shard", axis=0, tiled=True),
        lax.all_gather(feed_gain, "shard", axis=0, tiled=True),
        lax.all_gather(bias_table, "shard", axis=0, tiled=True),
    )
    (
        w_query,
        w_key,
        w_value,
        w_output,
        c_query,
        c_key,
        c_value,
        c_output,
        w_gate,
        w_up,
        w_down,
        g_self,
        g_cross,
        g_feed,
        table_full,
    ) = fetched
    gain_self = g_self.astype(jnp.float32)
    gain_cross = g_cross.astype(jnp.float32)
    gain_feed = g_feed.astype(jnp.float32)
    source = inputs[0].astype(jnp.float32)
    memory = encoder[0]
    segment_ids = segments[0]
    memory_ids = enc_segments[0]
    tokens_here = source.shape[0]
    length = segment_ids.shape[0]
    block_size = math.gcd(length, 512)
    block_count = length // block_size
    query_start = lax.axis_index("shard") * tokens_here
    query_ids = lax.dynamic_slice_in_dim(segment_ids, query_start, tokens_here)
    id_blocks = segment_ids.reshape(block_count, block_size)
    key_starts = jnp.arange(block_count, dtype=jnp.int32) * block_size
    cross_allowed = (query_ids[:, None] == memory_ids[None, :])[None]
    normed_self = rms_scale(source, gain_self).astype(jnp.bfloat16)
    query_heads = split_heads(product(normed_self, w_query).astype(jnp.bfloat16))
    key_local = product(normed_self, w_key).astype(jnp.bfloat16)
    value_local = product(normed_self, w_value).astype(jnp.bfloat16)
    keys_all, values_all = (
        lax.all_gather(key_local, "shard", axis=0, tiled=True),
        lax.all_gather(value_local, "shard", axis=0, tiled=True),
    )
    key_blocks = to_blocks(keys_all, block_count)
    value_blocks = to_blocks(values_all, block_count)
    logsum_self = self_logsum(
        query_heads, query_start, query_ids, table_full, key_blocks, id_blocks, key_starts
    )
    mixed_self = self_mix(
        query_heads,
        query_start,
        query_ids,
        table_full,
        key_blocks,
        value_blocks,
        id_blocks,
        key_starts,
        logsum_self,
    )
    joined_self = join_heads(mixed_self).astype(jnp.bfloat16)
    after_self = source + product(joined_self, w_output)
    normed_cross = rms_scale(after_self, gain_cross).astype(jnp.bfloat16)
    query_cross = split_heads(product(normed_cross, c_query).astype(jnp.bfloat16))
    key_cross_local = product(memory, c_key).astype(jnp.bfloat16)
    value_cross_local = product(memory, c_value).astype(jnp.bfloat16)
    keys_cross, values_cross = (
        lax.all_gather(key_cross_local, "shard", axis=0, tiled=True),
        lax.all_gather(value_cross_local, "shard", axis=0, tiled=True),
    )
    key_cross = split_heads(keys_cross)
    value_cross = split_heads(values_cross)
    mixed_cross, logsum_cross = cross_forward(query_cross, key_cross, value_cross, cross_allowed)
    joined_cross = join_heads(mixed_cross).astype(jnp.bfloat16)
    after_cross = after_self + product(joined_cross, c_output)
    normed_feed = rms_scale(after_cross, gain_feed).astype(jnp.bfloat16)
    gate_act = product(normed_feed, w_gate)
    up_act = product(normed_feed, w_up)
    hidden = (jax.nn.gelu(gate_act, approximate=True) * up_act).astype(jnp.bfloat16)
    outcome = after_cross + product(hidden, w_down)
    fetched = (
        lax.all_gather(self_query, "shard", axis=0, tiled=True),
        lax.all_gather(self_key, "shard", axis=0, tiled=True),
        lax.all_gather(self_value, "shard", axis=0, tiled=True),
        lax.all_gather(self_output, "shard", axis=0, tiled=True),
        lax.all_gather(cross_query, "shard", axis=0, tiled=True),
        lax.all_gather(cross_key, "shard", axis=0, tiled=True),
        lax.all_gather(cross_value, "shard", axis=0, tiled=True),
        lax.all_gather(cross_output, "shard", axis=0, tiled=True),
        lax.all_gather(gate_weight, "shard", axis=0, tiled=True),
        lax.all_gather(up_weight, "shard", axis=0, tiled=True),
        lax.all_gather(down_weight, "shard", axis=0, tiled=True),
        lax.all_gather(self_gain, "shard", axis=0, tiled=True),
        lax.all_gather(cross_gain, "shard", axis=0, tiled=True),
        lax.all_gather(feed_gain, "shard", axis=0, tiled=True),
        lax.all_gather(bias_table, "shard", axis=0, tiled=True),
    )
    (
        w_query,
        w_key,
        w_value,
        w_output,
        c_query,
        c_key,
        c_value,
        c_output,
        w_gate,
        w_up,
        w_down,
        g_self,
        g_cross,
        g_feed,
        table_full,
    ) = fetched
    gain_self = g_self.astype(jnp.float32)
    gain_cross = g_cross.astype(jnp.float32)
    gain_feed = g_feed.astype(jnp.float32)
    keys_all, values_all = (
        lax.all_gather(key_local, "shard", axis=0, tiled=True),
        lax.all_gather(value_local, "shard", axis=0, tiled=True),
    )
    key_blocks = to_blocks(keys_all, block_count)
    value_blocks = to_blocks(values_all, block_count)
    grad_out = cotangent[0].astype(jnp.float32)
    grad_down_in = cotangent[0]
    d_down = product_rows(hidden, grad_down_in)
    grad_hidden = product_cols(grad_down_in, w_down)

    def activation(gate_in, up_in):
        return jax.nn.gelu(gate_in, approximate=True) * up_in

    unused, pull = jax.vjp(activation, gate_act, up_act)
    grad_gate, grad_up = pull(grad_hidden)
    grad_gate = grad_gate.astype(jnp.bfloat16)
    grad_up = grad_up.astype(jnp.bfloat16)
    d_gate = product_rows(normed_feed, grad_gate)
    d_up = product_rows(normed_feed, grad_up)
    grad_normed_feed = product_cols(grad_gate, w_gate) + product_cols(grad_up, w_up)
    unused, pull = jax.vjp(rms_scale, after_cross, gain_feed)
    norm_part, d_feed_gain = pull(grad_normed_feed)
    grad_cross_total = grad_out + norm_part
    grad_cross_in = grad_cross_total.astype(jnp.bfloat16)
    d_c_output = product_rows(joined_cross, grad_cross_in)
    grad_mixed_cross = split_heads(product_cols(grad_cross_in, c_output).astype(jnp.bfloat16))
    grad_query_cross, grad_keys_cross, grad_values_cross = cross_backward(
        query_cross, key_cross, value_cross, cross_allowed, logsum_cross, grad_mixed_cross
    )
    grad_query_cross = grad_query_cross.astype(jnp.bfloat16)
    key_part, value_part = (
        lax.psum_scatter(
            grad_keys_cross.astype(jnp.bfloat16), "shard", scatter_dimension=0, tiled=True
        ).astype(jnp.float32),
        lax.psum_scatter(
            grad_values_cross.astype(jnp.bfloat16), "shard", scatter_dimension=0, tiled=True
        ).astype(jnp.float32),
    )
    grad_key_cross = key_part.astype(jnp.bfloat16)
    grad_value_cross = value_part.astype(jnp.bfloat16)
    d_c_query = product_rows(normed_cross, grad_query_cross)
    d_c_key = product_rows(memory, grad_key_cross)
    d_c_value = product_rows(memory, grad_value_cross)
    grad_memory = product_cols(grad_key_cross, c_key) + product_cols(grad_value_cross, c_value)
    grad_normed_cross = product_cols(grad_query_cross, c_query)
    unused, pull = jax.vjp(rms_scale, after_self, gain_cross)
    norm_part, d_cross_gain = pull(grad_normed_cross)
    grad_self_total = grad_cross_total + norm_part
    grad_self_in = grad_self_total.astype(jnp.bfloat16)
    d_output = product_rows(joined_self, grad_self_in)
    grad_mixed_self = split_heads(product_cols(grad_self_in, w_output).astype(jnp.bfloat16))
    grad_queries, d_table, grad_keys_full, grad_values_full = self_backward(
        query_heads,
        query_start,
        query_ids,
        table_full,
        key_blocks,
        value_blocks,
        id_blocks,
        key_starts,
        logsum_self,
        grad_mixed_self,
    )
    grad_query_self = grad_queries.astype(jnp.bfloat16)
    key_part, value_part = (
        lax.psum_scatter(
            grad_keys_full.astype(jnp.bfloat16), "shard", scatter_dimension=0, tiled=True
        ).astype(jnp.float32),
        lax.psum_scatter(
            grad_values_full.astype(jnp.bfloat16), "shard", scatter_dimension=0, tiled=True
        ).astype(jnp.float32),
    )
    grad_key_self = key_part.astype(jnp.bfloat16)
    grad_value_self = value_part.astype(jnp.bfloat16)
    d_query = product_rows(normed_self, grad_query_self)
    d_key = product_rows(normed_self, grad_key_self)
    d_value = product_rows(normed_self, grad_value_self)
    grad_normed_self = (
        product_cols(grad_query_self, w_query)
        + product_cols(grad_key_self, w_key)
        + product_cols(grad_value_self, w_value)
    )
    unused, pull = jax.vjp(rms_scale, source, gain_self)
    norm_part, d_self_gain = pull(grad_normed_self)
    grad_source = grad_self_total + norm_part
    summed = (
        lax.psum_scatter(
            d_query.astype(jnp.bfloat16), "shard", scatter_dimension=0, tiled=True
        ).astype(jnp.float32),
        lax.psum_scatter(
            d_key.astype(jnp.bfloat16), "shard", scatter_dimension=0, tiled=True
        ).astype(jnp.float32),
        lax.psum_scatter(
            d_value.astype(jnp.bfloat16), "shard", scatter_dimension=0, tiled=True
        ).astype(jnp.float32),
        lax.psum_scatter(
            d_output.astype(jnp.bfloat16), "shard", scatter_dimension=0, tiled=True
        ).astype(jnp.float32),
        lax.psum_scatter(
            d_c_query.astype(jnp.bfloat16), "shard", scatter_dimension=0, tiled=True
        ).astype(jnp.float32),
        lax.psum_scatter(
            d_c_key.astype(jnp.bfloat16), "shard", scatter_dimension=0, tiled=True
        ).astype(jnp.float32),
        lax.psum_scatter(
            d_c_value.astype(jnp.bfloat16), "shard", scatter_dimension=0, tiled=True
        ).astype(jnp.float32),
        lax.psum_scatter(
            d_c_output.astype(jnp.bfloat16), "shard", scatter_dimension=0, tiled=True
        ).astype(jnp.float32),
        lax.psum_scatter(
            d_gate.astype(jnp.bfloat16), "shard", scatter_dimension=0, tiled=True
        ).astype(jnp.float32),
        lax.psum_scatter(
            d_up.astype(jnp.bfloat16), "shard", scatter_dimension=0, tiled=True
        ).astype(jnp.float32),
        lax.psum_scatter(
            d_down.astype(jnp.bfloat16), "shard", scatter_dimension=0, tiled=True
        ).astype(jnp.float32),
        lax.psum_scatter(
            d_self_gain.astype(jnp.bfloat16), "shard", scatter_dimension=0, tiled=True
        ).astype(jnp.float32),
        lax.psum_scatter(
            d_cross_gain.astype(jnp.bfloat16), "shard", scatter_dimension=0, tiled=True
        ).astype(jnp.float32),
        lax.psum_scatter(
            d_feed_gain.astype(jnp.bfloat16), "shard", scatter_dimension=0, tiled=True
        ).astype(jnp.float32),
        lax.psum_scatter(
            d_table.astype(jnp.bfloat16), "shard", scatter_dimension=0, tiled=True
        ).astype(jnp.float32),
    )
    totals = (
        lax.psum(summed[0].astype(jnp.bfloat16), "rep").astype(jnp.float32),
        lax.psum(summed[1].astype(jnp.bfloat16), "rep").astype(jnp.float32),
        lax.psum(summed[2].astype(jnp.bfloat16), "rep").astype(jnp.float32),
        lax.psum(summed[3].astype(jnp.bfloat16), "rep").astype(jnp.float32),
        lax.psum(summed[4].astype(jnp.bfloat16), "rep").astype(jnp.float32),
        lax.psum(summed[5].astype(jnp.bfloat16), "rep").astype(jnp.float32),
        lax.psum(summed[6].astype(jnp.bfloat16), "rep").astype(jnp.float32),
        lax.psum(summed[7].astype(jnp.bfloat16), "rep").astype(jnp.float32),
        lax.psum(summed[8].astype(jnp.bfloat16), "rep").astype(jnp.float32),
        lax.psum(summed[9].astype(jnp.bfloat16), "rep").astype(jnp.float32),
        lax.psum(summed[10].astype(jnp.bfloat16), "rep").astype(jnp.float32),
        lax.psum(summed[11].astype(jnp.bfloat16), "rep").astype(jnp.float32),
        lax.psum(summed[12].astype(jnp.bfloat16), "rep").astype(jnp.float32),
        lax.psum(summed[13].astype(jnp.bfloat16), "rep").astype(jnp.float32),
        lax.psum(summed[14].astype(jnp.bfloat16), "rep").astype(jnp.float32),
    )
    return (
        outcome.astype(jnp.bfloat16)[None],
        grad_source[None],
        grad_memory[None],
        totals[0],
        totals[1],
        totals[2],
        totals[3],
        totals[4],
        totals[5],
        totals[6],
        totals[7],
        totals[8],
        totals[9],
        totals[10],
        totals[11],
        totals[12],
        totals[13],
        totals[14],
    )


def swap(value, axis, size, step):
    return lax.ppermute(value, axis, [(place, place ^ step) for place in range(size)])


def after(value, *others):
    return lax.optimization_barrier((value, *others))[0]


def run_kernel(name, body, ids, operands, results, scratch=()):
    whole = pl.BlockSpec(memory_space=pltpu.VMEM)
    return pl.pallas_call(
        body,
        out_shape=[jax.ShapeDtypeStruct(shape, kind) for shape, kind in results],
        in_specs=[pl.BlockSpec(memory_space=pltpu.SMEM)] + [whole] * len(operands),
        out_specs=[whole] * len(results),
        scratch_shapes=[pltpu.VMEM(shape, kind) for shape, kind in scratch],
        name=name,
    )(ids, *operands)


low_kind = jnp.bfloat16
full_kind = jnp.float32


def rows_at(place, size):
    return pl.ds(pl.multiple_of(place * size, size), size)


def put_blocks(index, blocks, target):
    size = blocks[0].shape[0]
    for step, block in enumerate(blocks):
        target[rows_at(index ^ step, size), :] = block[...]


def split_cores(index, partial, room, send, keep):
    core = index & 1
    size = send.shape[0]
    room[...] = partial
    keep[...] = room[rows_at(core, size), :]
    send[...] = room[rows_at(1 - core, size), :].astype(low_kind)


def join_cores(index, own, other, room):
    core = index & 1
    size = own.shape[0]
    room[rows_at(core, size), :] = own[...].astype(full_kind)
    room[rows_at(1 - core, size), :] = other[...].astype(full_kind)
    return room[...]


def inverse_rms(values):
    return lax.rsqrt(jnp.mean(values * values, axis=-1, keepdims=True) + epsilon)


def norm_backward(grad, values, gain):
    scale = inverse_rms(values)
    row = jnp.sum(grad * values * scale, axis=0, keepdims=True)
    scaled = grad * gain
    inner = jnp.mean(scaled * values, axis=-1, keepdims=True)
    return scale * scaled - values * (scale * scale * scale * inner), row


def bucket_rows(buckets, length):
    lanes = lax.broadcasted_iota(jnp.int32, (buckets, length), 1)
    distance = jnp.where(lanes == 0, 0, length - lanes)
    return (bucket_of(distance) == lax.broadcasted_iota(jnp.int32, (buckets, length), 0)).astype(
        full_kind
    )


def columns_body(ids, *refs):
    count = len(refs) - 4
    sources, targets = refs[:count], refs[count:]
    for place in range(4):

        @pl.when(ids[0] == place)
        def _():
            for step in range(4):
                start = 0
                for source in sources:
                    width = source.shape[1] // 4
                    begin = (place ^ step) * width
                    targets[step][:, start : start + width] = source[:, begin : begin + width]
                    start += width


def pack_body(ids, source, gain0, gain1, gain2, table, *refs):
    sources, packed, targets = refs[:3], refs[3], refs[4:]
    columns_body(ids, *sources, *targets)
    size, model = source.shape
    packed[:size, :] = source[...]
    rows = table.shape[0]
    line = [gain[...].astype(full_kind).reshape(1, -1) for gain in (gain0, gain1, gain2)]
    width = sum(piece.shape[1] for piece in line)
    line = jnp.concatenate(line + [jnp.zeros((1, model - width), full_kind)], axis=1)
    grid = jnp.concatenate(
        [table[...].astype(full_kind), jnp.zeros((rows, model - table.shape[1]), full_kind)], axis=1
    )
    lines = jnp.concatenate([line, jnp.zeros((7, model), full_kind), grid], axis=0)
    packed[size:, :] = lines.astype(low_kind)


def split_columns_body(ids, gate, up, own, send1, send2, send3):
    column = ids[1] & 1
    width = gate.shape[1] // 4
    half = send2.shape[0]
    for place in range(4):

        @pl.when(ids[0] == place)
        def _():
            for step, target in enumerate((own, send1, send2, send3)):
                begin = (place ^ step) * width
                rows = slice(None) if step < 2 else rows_at(column, half)
                for number, source in enumerate((gate, up)):
                    target[:, number * width : (number + 1) * width] = source[
                        rows, begin : begin + width
                    ]


def heads_of(matrix, number, part, wide):
    start = part * wide + number * HEAD_DIM
    return matrix[:, start : start + HEAD_DIM]


def stack_heads(matrix, target, first):
    for number in range(matrix.shape[1] // HEAD_DIM):
        target[first + number, : matrix.shape[0], :] = matrix[
            :, number * HEAD_DIM : (number + 1) * HEAD_DIM
        ]


def joined_heads(source, first, count):
    return jnp.concatenate([source[first + number] for number in range(count)], axis=1)


def each_head(count, body):
    def step(number, unused):
        body(number)
        return unused

    lax.fori_loop(0, count, step, 0)


def softmax_rows(scores, allowed):
    scores = jnp.where(allowed, scores, masked_score)
    powers = jnp.exp(scores - jnp.max(scores, axis=-1, keepdims=True))
    return powers * (1.0 / jnp.sum(powers, axis=-1, keepdims=True))


def self_half(half, ids, source, weight, gains, rows, mapped_before, output, seg_col, seg_row, outs):
    normed_out, mapped_out, chances_out, mixed_out, send, keep, room, heads, joined = outs
    size = normed_out.shape[0]
    wide = output.shape[0]
    count = wide // HEAD_DIM
    normed = (source * inverse_rms(source) * gains[0:1, :]).astype(low_kind)
    normed_out[...] = normed
    mapped = product(normed, weight).astype(low_kind)
    mapped_out[...] = mapped
    every = mapped if half == 0 else jnp.concatenate([mapped_before, mapped], axis=0)
    keys = every.shape[0]
    places = lax.broadcasted_iota(jnp.int32, (size, keys), 0) + half * size
    others = lax.broadcasted_iota(jnp.int32, (size, keys), 1)
    allowed = (places >= others) & (seg_col == seg_row[:, :keys])
    stack_heads(mapped[:, :wide], heads, 0)
    stack_heads(every[:, wide:], heads, count)

    def one_head(number):
        line = jnp.broadcast_to(rows[pl.ds(number, 1), :], (size, rows.shape[1]))
        bias = pltpu.roll(line, half * size, 1, stride=1, stride_axis=0)[:, :keys]
        scores = product_cols(heads[number, :size, :], heads[count + number, :keys, :])
        chances = softmax_rows(scores + bias, allowed).astype(low_kind)
        chances_out[number] = chances
        joined[number] = product(chances, heads[2 * count + number, :keys, :]).astype(low_kind)

    each_head(count, one_head)
    mixed = joined_heads(joined, 0, count)
    mixed_out[...] = mixed
    split_cores(ids[0], product(mixed, output), room, send, keep)


def self_first_body(
    ids, x0, x1, x2, x3, w0, w1, w2, w3, output, seg_col, seg_row,
    source_out, weight_out, gains_out, rows_out,
    normed_out, mapped_out, chances_out, mixed_out, send, keep,
    room, heads, joined, small, lines,
):
    index = ids[0]
    tokens = source_out.shape[0] // 4
    put_blocks(index, [block.at[:tokens] for block in (x0, x1, x2, x3)], source_out)
    put_blocks(index, (w0, w1, w2, w3), weight_out)
    for step, block in enumerate((x0, x1, x2, x3)):
        small[rows_at(index ^ step, 16), :] = block[tokens:, :].astype(full_kind)
    model = source_out.shape[1]
    part = model // 4
    for place in range(3):
        gains_out[place : place + 1, :] = jnp.concatenate(
            [small[16 * t : 16 * t + 1, part * place : part * (place + 1)] for t in range(4)],
            axis=1,
        )
    gains_out[3:8, :] = jnp.zeros((5, model), full_kind)
    table = jnp.concatenate([small[16 * t + 8 : 16 * t + 16, :128] for t in range(4)], axis=0)
    hot = bucket_rows(table.shape[0], rows_out.shape[1])
    lines[...] = product_rows(table.astype(low_kind), hot.astype(low_kind))
    heads_here = chances_out.shape[0]
    for number in range(heads_here):
        rows_out[number : number + 1, :] = lines[pl.ds(index * heads_here + number, 1), :]
    rows_out[heads_here:8, :] = jnp.zeros((8 - heads_here, rows_out.shape[1]), full_kind)
    size = normed_out.shape[0]
    self_half(
        0, ids, source_out[:size, :].astype(full_kind), weight_out[...], gains_out, rows_out, None,
        output[...], seg_col[:size, :], seg_row[...],
        (normed_out, mapped_out, chances_out, mixed_out, send, keep, room, heads, joined),
    )


def self_second_body(
    ids, source, weight, gains, rows, mapped_before, output, seg_col, seg_row,
    normed_out, mapped_out, chances_out, mixed_out, send, keep, room, heads, joined,
):
    size = normed_out.shape[0]
    self_half(
        1, ids, source[size:, :].astype(full_kind), weight[...], gains, rows, mapped_before[...],
        output[...], seg_col[size:, :], seg_row[...],
        (normed_out, mapped_out, chances_out, mixed_out, send, keep, room, heads, joined),
    )


def cross_keys_body(ids, e0, e1, e2, e3, w0, w1, w2, w3, memory_out, weight_out, mapped_out):
    put_blocks(ids[0], (e0, e1, e2, e3), memory_out)
    put_blocks(ids[0], (w0, w1, w2, w3), weight_out)
    wide = weight_out.shape[1] // 3
    mapped_out[...] = product(memory_out[...], weight_out[:, wide:]).astype(low_kind)


def cross_body(
    half, ids, source, own, other, gains, weight, mapped, output, seg_col, enc_row,
    after_out, normed_out, query_out, chances_out, mixed_out, send, keep, room, heads, joined,
):
    size = after_out.shape[0]
    wide = output.shape[0]
    count = wide // HEAD_DIM
    start = half * size
    values = source[start : start + size, :].astype(full_kind) + join_cores(
        ids[0], own, other, room
    )
    after_out[...] = values
    normed = (values * inverse_rms(values) * gains[1:2, :]).astype(low_kind)
    normed_out[...] = normed
    query = product(normed, weight[:, :wide]).astype(low_kind)
    query_out[...] = query
    allowed = seg_col[start : start + size, :] == enc_row[...]
    stack_heads(query, heads, 0)
    stack_heads(mapped[...], heads, count)

    def one_head(number):
        scores = product_cols(heads[number, :size, :], heads[count + number])
        chances = softmax_rows(scores, allowed).astype(low_kind)
        chances_out[number] = chances
        joined[number] = product(chances, heads[2 * count + number]).astype(low_kind)

    each_head(count, one_head)
    mixed = joined_heads(joined, 0, count)
    mixed_out[...] = mixed
    split_cores(ids[0], product(mixed, output[...]), room, send, keep)


def feed_join_body(ids, w0, w1, w2, w2x, w3, w3x, g0, g1, g2, g3, weight_out, grad_out):
    index, column = ids[0], ids[1] & 1
    put_blocks(index, (w0, w1), weight_out)
    half = w2.shape[0]
    for step, mine, other in ((2, w2, w2x), (3, w3, w3x)):
        weight_out[rows_at(2 * (index ^ step) + column, half), :] = mine[...]
        weight_out[rows_at(2 * (index ^ step) + 1 - column, half), :] = other[...]
    put_blocks(ids[0], (g0, g1, g2, g3), grad_out)


def feed_body(half, ids, before, own, other, gains, weight, down, grad_out, *refs):
    parts = refs[:2] if half else ()
    after_out, normed_out, hidden_out, acts_out, *rest = refs[len(parts) :]
    size = after_out.shape[0]
    start = half * size
    units = down.shape[0]
    room = rest[-1]
    values = before[...] + join_cores(ids[0], own, other, room)
    after_out[...] = values
    normed = (values * inverse_rms(values) * gains[2:3, :]).astype(low_kind)
    normed_out[...] = normed
    acts = product(normed, weight[...])
    gate, up = acts[:, :units], acts[:, units:]
    root = math.sqrt(2 / math.pi)
    square = gate * gate
    bend = jnp.tanh(root * gate * (1.0 + 0.044715 * square))
    curve = 0.5 * gate * (1.0 + bend)
    slope = 0.5 * (1.0 + bend) + 0.5 * gate * (1.0 - bend * bend) * root * (
        1.0 + 3 * 0.044715 * square
    )
    hidden = (curve * up).astype(low_kind)
    hidden_out[...] = hidden
    grad_hidden = product_cols(grad_out[start : start + size, :], down[...])
    acts_out[:, :units] = (grad_hidden * up * slope).astype(low_kind)
    acts_out[:, units:] = (grad_hidden * curve).astype(low_kind)
    grad = product_cols(acts_out[...], weight[...])
    result = product(hidden, down[...])
    if half:
        send, keep, out_send, out_keep = rest[:4]
        for place, part in ((0, parts[0][...]), (1, grad)):
            split_cores(ids[0], part, room, send.at[place], keep.at[place])
        for place, part in ((0, parts[1][...]), (1, result)):
            split_cores(ids[0], part, room, out_send.at[place], out_keep.at[place])
    else:
        rest[0][...] = grad
        rest[1][...] = result


def rep_bits(ids):
    rep = ids[1]
    return rep & 1, (rep >> 1) & 1, rep >> 2


def each_chunk(ids, keep_first, send_first, keep_second, send_second, body):
    column, low, unused = rep_bits(ids)

    def step(slot, unused):
        high, middle = slot >> 1, slot & 1
        for target, bit in ((keep_first, column), (send_first, 1 - column)):
            body(target.at[slot], 4 * high + 2 * middle + bit, 0)
        for target, bit in ((keep_second, low), (send_second, 1 - low)):
            body(target.at[slot], 4 * high + 2 * bit + middle, 1)
        return unused

    lax.fori_loop(0, 4, step, 0)


def feed_weights_body(
    ids, normed0, normed1, acts0, acts1, hidden0, hidden1, grad_out,
    keep_first, send_first, keep_second, send_second, feed, down,
):
    size = normed0.shape[0]
    feed[...] = (
        product_rows(normed0[...], acts0[...]) + product_rows(normed1[...], acts1[...])
    ).astype(low_kind)
    down[...] = (
        product_rows(hidden0[...], grad_out[:size, :])
        + product_rows(hidden1[...], grad_out[size:, :])
    ).astype(low_kind)
    rows = feed.shape[0] // 4
    width = feed.shape[1] // 8
    small = down.shape[0] // 8
    lanes = down.shape[1] // 2

    def fill(target, chunk, part):
        for place in range(2):
            start = (2 * part + place) * rows
            target[place] = feed[start : start + rows, rows_at(chunk, width)]
        for piece in range(lanes // width):
            start = part * lanes + piece * width
            target[2, piece * small : (piece + 1) * small, :] = down[
                rows_at(chunk, small), start : start + width
            ]

    each_chunk(ids, keep_first, send_first, keep_second, send_second, fill)


def store_small_chunks(ids, columns, output, buffers):
    small = output.shape[0] // 8
    lanes = output.shape[1] // 2
    quarter = columns.shape[0] // 4

    def fill(target, chunk, part):
        for place in range(2):
            start = (2 * part + place) * quarter + chunk * small
            target[place] = columns[pl.ds(pl.multiple_of(start, 8), small), :].astype(low_kind)
        target[2] = jnp.zeros(target.shape[1:], low_kind)
        target[2, :, :lanes] = output[
            pl.ds(pl.multiple_of(chunk * small, 8), small), part * lanes : (part + 1) * lanes
        ].astype(low_kind)

    each_chunk(ids, *buffers, fill)


small_lanes = slice(3 * 128, 4 * 128)


def small_pieces(count, size):
    half = (count - size) // 2
    yield (0, 0), slice(0, size)
    yield (0, 1), slice(size, size + half)
    yield (1, 0), slice(size + half, count)


def halve_body(ids, keep_first, came_first, keep_second, came_second, *outs):
    new_first, send_first, new_second, send_second = outs
    column, low, unused = rep_bits(ids)
    for keep, came, new, send, bit in (
        (keep_first, came_first, new_first, send_first, low),
        (keep_second, came_second, new_second, send_second, column),
    ):
        for high in range(2):
            for target, place in ((new, 2 * high + bit), (send, 2 * high + 1 - bit)):
                total = keep[place].astype(full_kind) + came[place].astype(full_kind)
                target[high] = total.astype(target.dtype)


def quarter_body(ids, keep_first, came_first, keep_second, came_second, total):
    for part, (keep, came) in enumerate(((keep_first, came_first), (keep_second, came_second))):
        total[part] = (keep[...] + came[...].astype(full_kind)).astype(low_kind)


def quarter_small_body(
    ids, keep_first, came_first, keep_second, came_second, vector, near, far, across, total
):
    quarter_body(ids, keep_first, came_first, keep_second, came_second, total)
    lines = (vector[...] + near[...] + far[...] + across[...]).astype(low_kind)
    for (part, high), piece in small_pieces(lines.shape[0], total.shape[3]):
        total[part, high, 2, : piece.stop - piece.start, small_lanes] = lines[piece, :]


def trade_body(ids, mine, came, own, send1, send2, send3, rows, room):
    for part in range(2):
        for high in range(2):
            total = (
                mine[part, high].astype(full_kind) + came[part, high].astype(full_kind)
            ).astype(low_kind)
            room[2 * part, high] = total[0]
            room[2 * part + 1, high] = total[1]
            rows[part, high] = total[2]
    for step, target in enumerate((own, send1, send2, send3)):
        target[...] = room[ids[0] ^ step]


def gather_body(ids, own, came1, came2, came3, rows, first, second):
    for place, block in enumerate((own, came1, came2)):
        first[:, place] = block[...]
    for place, block in enumerate((came3, rows.at[0], rows.at[1])):
        second[:, place] = block[...]


def all_pieces(ids, firsts, seconds):
    for step in range(4):
        for high in range(2):
            chunk = 4 * high + ((ids[1] & 3) ^ step)
            yield firsts[step].at[high], seconds[step].at[high], high, chunk


def feed_out_body(ids, *refs):
    firsts, seconds, (gate, up, down) = refs[:4], refs[4:8], refs[8:]
    units = gate.shape[1] // 4
    small = down.shape[0] // 8
    for first, second, high, chunk in all_pieces(ids, firsts, seconds):
        width = first.shape[2]
        target = (gate, up)[high]
        for step in range(4):
            block = second[0] if step == 3 else first[step]
            start = (ids[0] ^ step) * units + (chunk & 3) * width
            target[:, pl.ds(pl.multiple_of(start, width), width)] = block.astype(full_kind)
        for piece in range(down.shape[1] // width):
            part, begin = piece // 3, piece % 3 * small
            down[rows_at(chunk, small), piece * width : (piece + 1) * width] = second[
                1 + part, begin : begin + small
            ].astype(full_kind)


def small_out_body(ids, *refs):
    firsts, seconds, outs, room = refs[:4], refs[4:8], refs[8:12], refs[-1]
    small = room.shape[1] // 8
    lanes = outs[3].shape[1] // 2
    wide = outs[0].shape[0]
    for first, second, high, chunk in all_pieces(ids, firsts, seconds):
        where = pl.ds(pl.multiple_of(chunk * small, 8), small)
        for step in range(4):
            block = second[0] if step == 3 else first[step]
            room[step, where, :] = block.astype(full_kind)
        for part in range(2):
            outs[3][where, part * lanes : (part + 1) * lanes] = second[1 + part][:, :lanes].astype(
                full_kind
            )
    for place in range(4):
        for number in range(3):
            outs[number][:, place * wide : (place + 1) * wide] = room[
                ids[0] ^ place, :, number * wide : (number + 1) * wide
            ]


def last_out_body(ids, *refs):
    *refs, gain0, gain1, gain2, table, room, lines, vector = refs
    small_out_body(ids, *refs, room)
    seconds = refs[4:8]
    for step, second in enumerate(seconds):
        place = (ids[1] & 3) ^ step
        for (part, high), piece in small_pieces(vector.shape[0], second.shape[2]):
            lines[place, piece, :] = second[
                high, 1 + part, : piece.stop - piece.start, small_lanes
            ].astype(full_kind)
    vector[...] = (lines[0] + lines[1]) + (lines[2] + lines[3])
    size = gain0.shape[0]
    count = 4 * size // 128
    for number, gain in enumerate((gain0, gain1, gain2)):
        line = jnp.concatenate(
            [vector[number * count + row : number * count + row + 1, :] for row in range(count)],
            axis=1,
        )
        for place in range(4):

            @pl.when(ids[0] == place)
            def _():
                gain[...] = line[:, place * size : (place + 1) * size].reshape(size)

    rows, heads = table.shape
    start = vector.shape[0] - 4 * rows + ids[0] * rows
    table[...] = vector[pl.ds(pl.multiple_of(start, rows), rows), :heads]


def attention_backward(grad, query, keys, values, chances):
    full = chances.astype(full_kind)
    grad_chances = product_cols(grad, values)
    grad_scores = full * (grad_chances - jnp.sum(full * grad_chances, axis=-1, keepdims=True))
    rounded = grad_scores.astype(low_kind)
    return (
        grad_scores,
        product(rounded, keys).astype(low_kind),
        product_rows(rounded, query),
        product_rows(chances, grad),
    )


def join_halves(index, own, other, room):
    core = index & 1
    size = own.shape[1]
    for chip in range(2):
        room[rows_at(core + 2 * chip, size), :] = own[chip].astype(full_kind)
        room[rows_at(1 - core + 2 * chip, size), :] = other[chip].astype(full_kind)
    return room[...]


def cross_back_body(
    ids, grad_out, own, other, values0, values1, gains, output, query0, query1, chances0, chances1,
    mapped, weight, total_out, low_out, query_out, sums_out, row_out, send, keep, room, heads, joined,
):
    wide = output.shape[0]
    join_halves(ids[0], own, other, room)
    size = values0.shape[0]
    row = 0.0
    for half, values in ((0, values0), (1, values1)):
        part = slice(half * size, (half + 1) * size)
        grad, piece = norm_backward(room[part, :], values[...], gains[2:3, :])
        row = row + piece
        total = grad_out[part, :].astype(full_kind) + grad
        total_out[part, :] = total
        low_out[part, :] = total.astype(low_kind)
    row_out[...] = jnp.broadcast_to(row, row_out.shape)
    grad_mixed = product_cols(low_out[...], output[...]).astype(low_kind)
    count = wide // HEAD_DIM
    stack_heads(grad_mixed, heads, 0)
    stack_heads(jnp.concatenate([query0[...], query1[...]], axis=0), heads, count)
    stack_heads(mapped[...], heads, 2 * count)

    def one_head(number):
        chances = jnp.concatenate([chances0[number], chances1[number]], axis=0)
        unused, grad_query, grad_keys, grad_values = attention_backward(
            heads[number], heads[count + number], heads[2 * count + number],
            heads[3 * count + number], chances,
        )
        joined[number] = grad_query
        joined[count + number] = grad_keys.astype(low_kind)
        joined[2 * count + number] = grad_values.astype(low_kind)

    each_head(count, one_head)
    query_out[...] = joined_heads(joined, 0, count)
    sums_out[...] = joined_heads(joined, count, 2 * count)
    scatter_cores(ids[0], product_cols(query_out[...], weight[:, :wide]), room, send, keep)


def cross_weights_body(
    ids, normed0, normed1, query, memory, sums, mixed0, mixed1, low, weight,
    keep_first, send_first, keep_second, send_second, send, keep, room, columns, output,
):
    wide = query.shape[1]
    size = normed0.shape[0]
    columns[:, :wide] = product_rows(normed0[...], query[:size, :]) + product_rows(
        normed1[...], query[size:, :]
    )
    columns[:, wide:] = product_rows(memory[...], sums[...])
    output[...] = product_rows(mixed0[...], low[:size, :]) + product_rows(mixed1[...], low[size:, :])
    store_small_chunks(ids, columns, output, (keep_first, send_first, keep_second, send_second))
    scatter_cores(ids[0], product_cols(sums[...], weight[:, wide:]), room, send, keep)


def scatter_cores(index, partial, room, send, keep):
    core = index & 1
    size = send.shape[1]
    room[...] = partial
    for chip in range(2):
        keep[chip] = room[rows_at(core + 2 * chip, size), :]
        send[chip] = room[rows_at(1 - core + 2 * chip, size), :].astype(low_kind)


def diagonal_sums(matrix):
    width = matrix.shape[1]
    size = matrix.shape[0]
    while size > 1:
        size //= 2
        matrix = matrix[:size] + pltpu.roll(matrix[size:], width - size, 1)
    return matrix


def self_back_body(
    ids, total, own, other, values0, values1, gains, output, mapped0, mapped1, chances0, chances1,
    total_out, low_out, query_out, sums_out, row_out, table_out, room, heads, joined,
):
    wide = output.shape[0]
    join_halves(ids[0], own, other, room)
    size = values0.shape[0]
    row = 0.0
    for half, values in ((0, values0), (1, values1)):
        part = slice(half * size, (half + 1) * size)
        grad, piece = norm_backward(room[part, :], values[...], gains[1:2, :])
        row = row + piece
        new_total = total[part, :] + grad
        total_out[part, :] = new_total
        low_out[part, :] = new_total.astype(low_kind)
    row_out[...] = jnp.broadcast_to(row, row_out.shape)
    grad_mixed = product_cols(low_out[...], output[...]).astype(low_kind)
    buckets = table_out.shape[0]
    hot = bucket_rows(buckets, 2 * size)
    count = wide // HEAD_DIM
    stack_heads(grad_mixed, heads, 0)
    stack_heads(jnp.concatenate([mapped0[...], mapped1[...]], axis=0), heads, count)
    table_out[...] = jnp.zeros(table_out.shape, full_kind)

    def one_head(number):
        line = sums = None
        for half, chances in ((1, chances1), (0, chances0)):
            part = slice(half * size, (half + 1) * size)
            seen = slice(0, (half + 1) * size)
            grad_scores, grad_query, grad_keys, grad_values = attention_backward(
                heads[number, part, :], heads[count + number, part, :],
                heads[2 * count + number, seen, :], heads[3 * count + number, seen, :],
                chances[number],
            )
            joined[number, part, :] = grad_query
            if half:
                line = pltpu.roll(diagonal_sums(grad_scores), size, 1)
                sums = (grad_keys, grad_values)
            else:
                empty = jnp.zeros((size, size), full_kind)
                line = line + diagonal_sums(jnp.concatenate([grad_scores, empty], axis=1))
                for place, first, later in ((1, grad_keys, sums[0]), (2, grad_values, sums[1])):
                    joined[place * count + number, :size, :] = (later[:size] + first).astype(low_kind)
                    joined[place * count + number, size:, :] = later[size:].astype(low_kind)
        column = jnp.sum(hot * line, axis=1, keepdims=True)
        lanes = lax.broadcasted_iota(jnp.int32, table_out.shape, 1)
        table_out[...] += jnp.where(lanes == number, column, 0.0)

    each_head(count, one_head)
    query_out[...] = joined_heads(joined, 0, count)
    sums_out[...] = joined_heads(joined, count, 2 * count)


def self_weights_body(
    ids, normed0, normed1, query, sums, mixed0, mixed1, low, weight,
    keep_first, send_first, keep_second, send_second, send, keep, room, columns, output, merged,
):
    wide = query.shape[1]
    size = normed0.shape[0]
    merged[:, :wide] = query[...]
    merged[:, wide:] = sums[...]
    columns[...] = product_rows(normed0[...], merged[:size, :]) + product_rows(
        normed1[...], merged[size:, :]
    )
    output[...] = product_rows(mixed0[...], low[:size, :]) + product_rows(mixed1[...], low[size:, :])
    store_small_chunks(ids, columns, output, (keep_first, send_first, keep_second, send_second))
    scatter_cores(ids[0], product_cols(merged[...], weight[...]), room, send, keep)


def finish_body(ids, source, mine, far, gains, total, cross_row, feed_row, table, grad_out, vector):
    index = ids[0]
    size, model = source.shape
    grad, row = norm_backward(
        mine[...] + far[...].astype(full_kind), source[...].astype(full_kind), gains[0:1, :]
    )
    grad_out[...] = total[rows_at(index, size), :] + grad
    lanes = lax.broadcasted_iota(jnp.int32, (1, model), 1)
    part = model // 4
    here = (lanes >= index * part) & (lanes < (index + 1) * part)
    pieces = []
    for line in (row, jnp.where(here, cross_row[0:1, :], 0.0), jnp.where(here, feed_row[0:1, :], 0.0)):
        pieces += [line[:, start : start + 128] for start in range(0, model, 128)]
    pieces += [jnp.zeros((-len(pieces) % 8, 128), full_kind)]
    vector[: vector.shape[0] - table.shape[0], :] = jnp.concatenate(pieces, axis=0)
    vector[vector.shape[0] - table.shape[0] :, :] = pltpu.roll(
        table[...], index * (HEADS // 4), 1
    )


def chip_pair_body(ids, keep, arrived, mine, other):
    chip = ids[0] >> 1
    mine[...] = keep[chip] + arrived[chip].astype(full_kind)
    other[...] = (keep[1 - chip] + arrived[1 - chip].astype(full_kind)).astype(low_kind)


class Kernels:
    def __init__(self, ids):
        self.ids = ids

    def __call__(self, name, body, operands, results, scratch=(), cover=()):
        outs = run_kernel(name, body, self.ids, operands, results, scratch)
        if cover:
            outs = after(tuple(outs), *cover)
        self.ids = after(self.ids, outs[0])
        return outs

    def wait(self, *values):
        self.ids = after(self.ids, *values)


def rep_swap(value, step):
    return swap(value, "rep", 8, step)


def shard_swap(value, step):
    return swap(value, "shard", 4, step)


class Reduction:
    def __init__(self, call, name, buffers):
        self.call, self.name = call, name
        self.keeps = (buffers[0], buffers[2])
        self.came = (rep_swap(buffers[1], 1), rep_swap(buffers[3], 2))
        self.shape = buffers[0].shape[1:]

    def halve(self, cover=()):
        results = []
        for unused in range(2):
            results += [((2,) + self.shape, full_kind), ((2,) + self.shape, low_kind)]
        outs = self.call(
            self.name + "_halve",
            halve_body,
            (self.keeps[0], self.came[0], self.keeps[1], self.came[1]),
            results,
            cover=cover,
        )
        self.keeps = (outs[0], outs[2])
        self.came = (rep_swap(outs[1], 2), rep_swap(outs[3], 1))

    def quarter(self, cover=(), vectors=()):
        (self.total,) = self.call(
            self.name + "_quarter",
            quarter_small_body if vectors else quarter_body,
            (self.keeps[0], self.came[0], self.keeps[1], self.came[1]) + vectors,
            [((2, 2) + self.shape, low_kind)],
            cover=cover,
        )
        self.last = rep_swap(self.total, 4)

    def trade(self, cover=()):
        block = self.shape[1:]
        own, *sends, self.rows = self.call(
            self.name + "_trade",
            trade_body,
            (self.total, self.last),
            [((2,) + block, low_kind)] * 4 + [((2, 2) + block, low_kind)],
            [((4, 2) + block, low_kind)],
            cover=cover,
        )
        self.blocks = [own] + [shard_swap(send, step) for step, send in zip((1, 2, 3), sends)]

    def gather(self, cover=()):
        first, second = self.call(
            self.name + "_gather",
            gather_body,
            (*self.blocks, self.rows),
            [((2,) + self.shape, low_kind)] * 2,
            cover=cover,
        )
        first_far, second_far = rep_swap(first, 2), rep_swap(second, 1)
        self.far = (first_far, second_far)
        self.near = (rep_swap(first, 1), rep_swap(second, 2))
        self.firsts = (first, self.near[0], first_far, rep_swap(first_far, 1))
        self.seconds = (second, second_far, self.near[1], rep_swap(second_far, 2))

    def finish(self, body, results, scratch=(), cover=()):
        return self.call(
            self.name + "_out", body, (*self.firsts, *self.seconds), results, scratch, cover
        )


class GroupSum:
    def __init__(self, send, keep):
        self.keep = keep
        self.came = shard_swap(send, 1)

    def add(self):
        self.pair = (self.keep + self.came.astype(full_kind)).astype(low_kind)
        self.far = shard_swap(self.pair, 2)
        return self.pair

    def hold(self, value):
        self.far = after(self.far, value)

    def total(self):
        own = (self.pair.astype(full_kind) + self.far.astype(full_kind)).astype(low_kind)
        self.results = (own, shard_swap(own, 1))
        return own


def split_shards(
    inputs,
    encoder,
    segments,
    enc_segments,
    self_query,
    self_key,
    self_value,
    self_output,
    cross_query,
    cross_key,
    cross_value,
    cross_output,
    gate_weight,
    up_weight,
    down_weight,
    self_gain,
    cross_gain,
    feed_gain,
    bias_table,
    cotangent,
):
    index = lax.axis_index("shard")
    rep = lax.axis_index("rep")
    call = Kernels(jnp.stack([index, rep]))
    tokens_here, model = inputs.shape[1:]
    length = 4 * tokens_here
    half_size = 2 * tokens_here
    heads_here = HEADS // 4
    wide = heads_here * HEAD_DIM
    units = down_weight.shape[0]
    memory_length = enc_segments.shape[1]
    small_rows = bias_table.shape[0]
    buckets = 4 * small_rows
    part = self_gain.shape[0]

    def blocks_of(*weights):
        width = sum(weight.shape[1] for weight in weights) // 4
        shape = (weights[0].shape[0], width)
        return call("columns", columns_body, weights, [(shape, low_kind)] * 4)

    def traded(blocks):
        return [blocks[0]] + [shard_swap(blocks[step], step) for step in range(1, 4)]

    column_shape = (part, 3 * wide)
    packed, *self_blocks = call(
        "pack",
        pack_body,
        (
            inputs[0], self_gain, cross_gain, feed_gain, bias_table, self_query, self_key,
            self_value,
        ),
        [((tokens_here + 16, model), low_kind)] + [(column_shape, low_kind)] * 4,
    )
    source_far = shard_swap(packed, 2)
    self_blocks = traded(self_blocks)
    cross_blocks = blocks_of(cross_query, cross_key, cross_value)
    feed_blocks = call(
        "feed_columns",
        split_columns_body,
        (gate_weight, up_weight),
        [((part, 2 * units), low_kind)] * 2 + [((part // 2, 2 * units), low_kind)] * 2,
    )
    source_far = after(source_far, feed_blocks[0])
    source_blocks = [packed, shard_swap(packed, 1), source_far, shard_swap(source_far, 1)]
    seg_row = segments
    seg_col = segments[0][:, None]
    enc_row = enc_segments
    call.wait(seg_col, self_blocks[2], self_blocks[3])
    cross_blocks = traded(after(tuple(cross_blocks), self_blocks[2], self_blocks[3]))
    room = [((half_size, model), full_kind)]
    whole_room = [((length, model), full_kind)]

    def head_rooms(places, rows, outs):
        return [
            ((places * heads_here, max(length, memory_length), HEAD_DIM), low_kind),
            ((outs * heads_here, rows, HEAD_DIM), low_kind),
        ]

    pieces = [((tokens_here, model), low_kind), ((tokens_here, model), full_kind)]
    two_pieces = [((2,) + shape, kind) for shape, kind in pieces]

    def self_results(keys):
        return [
            ((half_size, model), low_kind),
            ((half_size, 3 * wide), low_kind),
            ((heads_here, half_size, keys), low_kind),
            ((half_size, wide), low_kind),
        ] + pieces

    source, w_self, gains, rows, *first = call(
        "self_first",
        self_first_body,
        (*source_blocks, *self_blocks, self_output, seg_col, seg_row),
        [
            ((length, model), low_kind),
            ((model, 3 * wide), low_kind),
            ((8, model), full_kind),
            ((8, length), full_kind),
        ]
        + self_results(half_size),
        room + head_rooms(3, half_size, 1) + [((64, model), full_kind), ((128, length), full_kind)],
        cover=(cross_blocks[2], cross_blocks[3]),
    )
    first_sum = GroupSum(*first[4:])
    memory_far = shard_swap(after(encoder[0], first[0]), 2)
    second = call(
        "self_second",
        self_second_body,
        (source, w_self, gains, rows, first[1], self_output, seg_col, seg_row),
        self_results(length),
        room + head_rooms(3, half_size, 1),
        cover=(first_sum.came,),
    )
    second_sum = GroupSum(*second[4:])
    call.wait(first_sum.add())
    memory_blocks = [
        encoder[0], shard_swap(encoder[0], 1), memory_far, shard_swap(memory_far, 1)
    ]
    memory, w_cross, cross_mapped = call(
        "cross_keys",
        cross_keys_body,
        (*memory_blocks, *cross_blocks),
        [
            ((memory_length, model), low_kind),
            ((model, 3 * wide), low_kind),
            ((memory_length, 2 * wide), low_kind),
        ],
        cover=(second_sum.came,),
    )
    pair = second_sum.add()
    call.wait(pair)
    first_sum.total()
    feed_blocks = after(tuple(feed_blocks), pair)
    feed_near = shard_swap(feed_blocks[1], 1)
    feed_two = shard_swap(feed_blocks[2], 2)

    def cross_call(half, sums, cover):
        own, other = sums.results
        return call(
            "cross",
            functools.partial(cross_body, half),
            (source, own, other, gains, w_cross, cross_mapped, cross_output, seg_col, enc_row),
            [
                ((half_size, model), full_kind),
                ((half_size, model), low_kind),
                ((half_size, wide), low_kind),
                ((heads_here, half_size, memory_length), low_kind),
                ((half_size, wide), low_kind),
            ]
            + pieces,
            room + head_rooms(3, half_size, 1),
            cover=cover,
        )

    grad_far = shard_swap(after(cotangent[0], cross_mapped), 2)
    cross0 = cross_call(0, first_sum, (second_sum.far, feed_two, grad_far))
    cross_first = GroupSum(*cross0[5:])
    call.wait(second_sum.total())
    feed_two_other = rep_swap(feed_two, 1)
    feed_three = shard_swap(after(feed_blocks[3], cross0[0]), 3)
    cross1 = cross_call(1, second_sum, (feed_three, feed_two_other, cross_first.came))
    cross_second = GroupSum(*cross1[5:])
    call.wait(cross_first.add())
    feed_three_other = rep_swap(feed_three, 1)
    grad_blocks = [
        cotangent[0], shard_swap(cotangent[0], 1), grad_far, shard_swap(grad_far, 1)
    ]
    w_feed, grad_out = call(
        "feed_join",
        feed_join_body,
        (
            feed_blocks[0], feed_near, feed_two, feed_two_other, feed_three, feed_three_other,
            *grad_blocks,
        ),
        [((model, 2 * units), low_kind), ((length, model), low_kind)],
        cover=(cross_second.came,),
    )
    call.wait(cross_second.add())
    cross_first.total()
    cross_second.hold(w_feed)

    def feed_call(half, sums, before, parts, tail, cover=()):
        own, other = sums.results
        return call(
            "feed",
            functools.partial(feed_body, half),
            (before, own, other, gains, w_feed, down_weight, grad_out) + parts,
            [
                ((half_size, model), full_kind),
                ((half_size, model), low_kind),
                ((half_size, units), low_kind),
                ((half_size, 2 * units), low_kind),
            ]
            + tail,
            room,
            cover=cover,
        )

    feed0 = feed_call(0, cross_first, cross0[0], (), room * 2, (cross_second.far,))
    cross_second.total()
    feed1 = feed_call(1, cross_second, cross1[0], (feed0[4], feed0[5]), two_pieces * 2)
    feed_sum = GroupSum(*feed1[4:6])
    out_came = shard_swap(feed1[6], 1)

    chunk = (3, model // 4, 2 * units // 8)
    feed_grads = Reduction(
        call,
        "feed_grads",
        call(
            "feed_weights",
            feed_weights_body,
            (feed0[1], feed1[1], feed0[3], feed1[3], feed0[2], feed1[2], grad_out),
            [((4,) + chunk, low_kind)] * 4,
            [((model, 2 * units), low_kind), ((units, model), low_kind)],
            cover=(feed_sum.came, out_came),
        ),
    )
    call.wait(feed_sum.add())

    def scatter_pair(arrived, keep, cover=()):
        mine, other = call(
            "chip_pair",
            chip_pair_body,
            (keep, arrived),
            [((tokens_here, model), full_kind), ((tokens_here, model), low_kind)],
            cover=cover,
        )
        return mine, shard_swap(other, 2)

    mine, out_far = scatter_pair(out_came, feed1[7])
    feed_sum.total()
    own_after = lax.dynamic_slice_in_dim(
        jnp.where(index < 2, feed0[0], feed1[0]), (index & 1) * tokens_here, tokens_here
    )
    outcome = (own_after + mine + out_far.astype(full_kind)).astype(low_kind)

    total_cross, low_cross, query_cross, sums_cross, row_feed, *sends = call(
        "cross_back",
        cross_back_body,
        (
            grad_out, *feed_sum.results, feed0[0], feed1[0], gains, cross_output, cross0[2], cross1[2],
            cross0[3], cross1[3], cross_mapped, w_cross,
        ),
        [
            ((length, model), full_kind),
            ((length, model), low_kind),
            ((length, wide), low_kind),
            ((memory_length, 2 * wide), low_kind),
            ((8, model), full_kind),
        ]
        + two_pieces,
        whole_room + head_rooms(4, length, 3),
        cover=feed_grads.came + (out_far,),
    )
    cross_sum = GroupSum(*sends)
    feed_grads.halve(cover=(cross_sum.came,))
    call.wait(cross_sum.add())
    small_chunk = (3, wide // 8, 3 * wide)
    weight_room = [((model, 3 * wide), full_kind), ((wide, model), full_kind)]
    *buffers, send, keep = call(
        "cross_weights",
        cross_weights_body,
        (
            cross0[1], cross1[1], query_cross, memory, sums_cross, cross0[4], cross1[4], low_cross,
            w_cross,
        ),
        [((4,) + small_chunk, low_kind)] * 4 + two_pieces,
        whole_room + weight_room,
        cover=(cross_sum.far,) + feed_grads.came,
    )
    cross_sum.hold(keep)
    cross_grads = Reduction(call, "cross_grads", buffers)
    memory_came, memory_keep = shard_swap(send, 1), keep
    call.wait(cross_sum.total())
    feed_grads.quarter(cover=cross_sum.results)
    total_self, low_self, query_self, sums_self, row_cross, table = call(
        "self_back",
        self_back_body,
        (
            total_cross, *cross_sum.results, cross0[0], cross1[0], gains, self_output, first[1], second[1],
            first[2], second[2],
        ),
        [
            ((length, model), full_kind),
            ((length, model), low_kind),
            ((length, wide), low_kind),
            ((length, 2 * wide), low_kind),
            ((8, model), full_kind),
            ((buckets, 128), full_kind),
        ],
        whole_room + head_rooms(4, length, 3),
        cover=(memory_came,),
    )
    *buffers, send, keep = call(
        "self_weights",
        self_weights_body,
        (first[0], second[0], query_self, sums_self, first[3], second[3], low_self, w_self),
        [((4,) + small_chunk, low_kind)] * 4 + two_pieces,
        whole_room + weight_room + [((length, 3 * wide), low_kind)],
        cover=cross_grads.came,
    )
    self_grads = Reduction(call, "self_grads", buffers)
    arrived = shard_swap(send, 1)
    cross_grads.halve(cover=(arrived,))
    mine, far = scatter_pair(arrived, keep)
    feed_grads.trade(cover=self_grads.came)
    call.wait(outcome)
    self_grads.halve(cover=cross_grads.came + (far,))
    cross_grads.quarter(cover=tuple(feed_grads.blocks[1:]))
    gain_rows = -(-3 * model // 1024) * 8
    vector_kind = ((gain_rows + buckets, 128), full_kind)
    grad_source, vector = call(
        "finish",
        finish_body,
        (inputs[0], mine, far, gains, total_self, row_cross, row_feed, table),
        [((tokens_here, model), full_kind), vector_kind],
        cover=self_grads.came,
    )
    vectors = (vector,) + tuple(shard_swap(vector, step) for step in (1, 2, 3))
    memory_mine, memory_far = scatter_pair(memory_came, memory_keep, vectors[1:])
    grad_memory = memory_mine + memory_far.astype(full_kind)
    self_grads.quarter(vectors=vectors)
    feed_grads.gather()
    cross_grads.trade()
    call.wait(grad_memory)
    cross_grads.gather(cover=feed_grads.far)
    self_grads.trade(cover=cross_grads.far)
    feed_out = feed_grads.finish(
        feed_out_body,
        [((part, 4 * units), full_kind)] * 2 + [((units, model), full_kind)],
        cover=tuple(self_grads.blocks[1:]),
    )
    self_grads.gather()
    small_results = [((part, model), full_kind)] * 3 + [((wide, model), full_kind)]
    out_room = [((4, wide, 3 * wide), full_kind)]
    cross_out = cross_grads.finish(small_out_body, small_results, out_room, self_grads.far)
    *self_out, gain0, gain1, gain2, table_grad = self_grads.finish(
        last_out_body,
        small_results + [((part,), full_kind)] * 3 + [((small_rows, HEADS), full_kind)],
        out_room + [((4,) + vector_kind[0], full_kind), vector_kind],
    )

    return (
        outcome[None],
        grad_source[None],
        grad_memory[None],
        *self_out,
        *cross_out,
        *feed_out,
        gain0,
        gain1,
        gain2,
        table_grad,
    )


def solution(mesh):
    in_specs = (
        P("rep", "shard", None),
        P("rep", "shard", None),
        P("rep", None),
        P("rep", None),
        P("shard", None),
        P("shard", None),
        P("shard", None),
        P("shard", None),
        P("shard", None),
        P("shard", None),
        P("shard", None),
        P("shard", None),
        P("shard", None),
        P("shard", None),
        P("shard", None),
        P("shard"),
        P("shard"),
        P("shard"),
        P("shard", None),
        P("rep", "shard", None),
    )
    out_specs = (
        P("rep", "shard", None),
        P("rep", "shard", None),
        P("rep", "shard", None),
        P("shard", None),
        P("shard", None),
        P("shard", None),
        P("shard", None),
        P("shard", None),
        P("shard", None),
        P("shard", None),
        P("shard", None),
        P("shard", None),
        P("shard", None),
        P("shard", None),
        P("shard"),
        P("shard"),
        P("shard"),
        P("shard", None),
    )
    split = mesh.shape["shard"] == 4 and mesh.shape["rep"] == 8
    body = split_shards if split else shards
    return jax.shard_map(body, mesh=mesh, in_specs=in_specs, out_specs=out_specs, check_vma=False)
```
